32 devices in a mesh: row: 8 (over z, y), col: 4 (over x, core).
Axes of the slice: x: 2, y: 2, z: 4, core: 2. Of those that a mesh axis runs over, the one named last changes fastest.
Arguments:
- tokens_in: bfloat16 [10240, 1024], P('row', 'col'), may hold values from -6 to 6
- grad_out: bfloat16 [10240, 1024], P('row', 'col'), may hold values from -6 to 6
- keep_mask: int32 [32, 256], P('row'), may hold values 0 or 1
- adapter_index: int32 [32], P('row'), may hold values from 0 to 7
- ln_gain: float32 [2, 1024], replicated, may hold values from 0.25 to 1.75
- ln_shift: float32 [2, 1024], replicated, may hold values from -1.8 to 1.8
- w_qkv: bfloat16 [3, 1024, 1024], P(None, 'row', 'col'), may hold values from -0.1875 to 0.1875
- bias_qv: bfloat16 [2, 1024], P(None, 'col'), may hold values from -1.796875 to 1.796875
- w_proj: bfloat16 [1024, 1024], P('col', 'row'), may hold values from -1.5 to 1.5
- w_fc1: bfloat16 [1024, 4096], P('row', 'col'), may hold values from -0.1875 to 0.1875
- bias_fc1: bfloat16 [4096], P('col'), may hold values from -1.796875 to 1.796875
- w_fc2: bfloat16 [4096, 1024], P('col', 'row'), may hold values from -0.09375 to 0.09375
- bias_out: bfloat16 [2, 1024], replicated, may hold values from -1.796875 to 1.796875
- qkv_down: bfloat16 [8, 16, 1024], replicated, may hold values from -0.1875 to 0.1875
- qkv_up: bfloat16 [8, 16, 3, 1024], replicated, may hold values from -0.75 to 0.75
- proj_down: bfloat16 [8, 16, 1024], replicated, may hold values from -1.5 to 1.5
- proj_up: bfloat16 [8, 16, 1024], replicated, may hold values from -0.75 to 0.75
- fc1_down: bfloat16 [8, 16, 1024], replicated, may hold values from -0.1875 to 0.1875
- fc1_up: bfloat16 [8, 16, 4096], replicated, may hold values from -0.75 to 0.75
- fc2_down: bfloat16 [8, 16, 4096], replicated, may hold values from -0.09375 to 0.09375
- fc2_up: bfloat16 [8, 16, 1024], replicated, may hold values from -0.75 to 0.75
Outputs:
- layer_out: bfloat16 [10240, 1024], P('row', 'col')
- grad_in: bfloat16 [10240, 1024], P('row', 'col')
- grad_qkv_down: float32 [8, 16, 1024], replicated
- grad_qkv_up: float32 [8, 16, 3, 1024], replicated
- grad_proj_down: float32 [8, 16, 1024], replicated
- grad_proj_up: float32 [8, 16, 1024], replicated
- grad_fc1_down: float32 [8, 16, 1024], replicated
- grad_fc1_up: float32 [8, 16, 4096], replicated
- grad_fc2_down: float32 [8, 16, 4096], replicated
- grad_fc2_up: float32 [8, 16, 1024], replicated
The draws below stay inside these ranges and needn't reach their ends.
All inputs are finite; a program needn't handle non-finite values. No bound on the sum of `keep_mask` on one device may be relied on, other than what follows from the above.
Results may differ from the reference program's by a relative error of at most 0.013.
Values may be sent and summed in bfloat16 or wider, within the bound.
No kernel may reach another device: no remote copies, remote signals or barrier semaphores. Data moves between devices by JAX's collectives and lax.ppermute only.
A program may use at most 192 MiB of HBM per device.

```python
import jax
import jax.numpy as jnp
from jax import lax

D = 1024
H = 16
HD = 64
FF = 4096
BUF = 64
SLOTS = 256
R = 16
NA = 8
IMG_ROW = 4
SEQ = 320
IMAGES = 32
TOKENS = 10240
N_ROW = 8


def plant(entries, key, smallest, top_value):
    longest = entries.shape.index(max(entries.shape))
    spots = []
    for shift in (0, 1):
        where = [jax.random.randint(jax.random.fold_in(key, axis), (), 0, length) for axis, length in enumerate(entries.shape)]
        where[longest] = (where[longest] + shift) % entries.shape[longest]
        spots.append(tuple(where))
    return entries.at[spots[0]].set(smallest).at[spots[1]].set(top_value)


def block_levels(own_key, extent, cuts, smallest, top_value):
    def one(axis_at, shards_of):
        heights = jax.random.uniform(jax.random.fold_in(jax.random.fold_in(own_key, 6), axis_at), (shards_of,), jnp.float32, smallest / len(cuts), top_value / len(cuts))
        return jnp.repeat(jnp.exp(heights), extent[axis_at] // shards_of).reshape((-1,) + (1,) * (len(extent) - axis_at - 1))

    factor_of = one(*cuts[0])
    for cut in cuts[1:]:
        factor_of = factor_of * one(*cut)
    return factor_of


def bell_draw(own_key, shape, spread, most, shards=(), held_as=jnp.bfloat16):
    gain = block_levels(own_key, shape, shards, -0.22, 0.18) if shards else 1.0
    entries = jax.random.normal(own_key, shape, jnp.float32) * spread * gain
    return jnp.minimum(jnp.maximum(entries, -most), most).astype(held_as)


def setup_inputs(seed: int = 0) -> dict:
    splits = jax.random.split(jax.random.key(seed), 22)
    return {
        "tokens_in": bell_draw(splits[0], (TOKENS, D), 1.0, 6.0, ((0, 8), (1, 4))),
        "grad_out": bell_draw(splits[1], (TOKENS, D), 1.0, 6.0, ((0, 8), (1, 4))),
        "keep_mask": plant((jax.random.randint(splits[2], (IMAGES, SLOTS), 0, 3) < 1).astype(jnp.int32), jax.random.fold_in(splits[2], 1), 0, 1),
        "adapter_index": plant(jax.random.randint(splits[3], (IMAGES,), 0, NA), jax.random.fold_in(splits[3], 1), 0, NA - 1).astype(jnp.int32),
        "ln_gain": jnp.clip(1.0 + 0.15 * jax.random.normal(splits[4], (2, D), jnp.float32), 0.25, 1.75),
        "ln_shift": bell_draw(splits[5], (2, D), 0.3, 1.8, (), jnp.float32),
        "w_qkv": bell_draw(splits[6], (3, D, D), D ** -0.5, 0.1875, ((1, 8), (2, 4))),
        "bias_qv": bell_draw(splits[7], (2, D), 0.3, 1.796875, ((1, 4),)),
        "w_proj": bell_draw(splits[8], (D, D), (max(D // 64, 1)) ** -0.5, 1.5, ((0, 4), (1, 8))),
        "w_fc1": bell_draw(splits[9], (D, FF), D ** -0.5, 0.1875, ((0, 8), (1, 4))),
        "bias_fc1": bell_draw(splits[10], (FF,), 0.3, 1.796875, ((0, 4),)),
        "w_fc2": bell_draw(splits[11], (FF, D), FF ** -0.5, 0.09375, ((0, 4), (1, 8))),
        "bias_out": bell_draw(splits[12], (2, D), 0.3, 1.796875),
        "qkv_down": bell_draw(splits[13], (NA, R, D), D ** -0.5, 0.1875),
        "qkv_up": bell_draw(splits[14], (NA, R, 3, D), (4 * R) ** -0.5, 0.75),
        "proj_down": bell_draw(splits[15], (NA, R, D), (max(D // 64, 1)) ** -0.5, 1.5),
        "proj_up": bell_draw(splits[16], (NA, R, D), (4 * R) ** -0.5, 0.75),
        "fc1_down": bell_draw(splits[17], (NA, R, D), D ** -0.5, 0.1875),
        "fc1_up": bell_draw(splits[18], (NA, R, FF), (4 * R) ** -0.5, 0.75),
        "fc2_down": bell_draw(splits[19], (NA, R, FF), FF ** -0.5, 0.09375),
        "fc2_up": bell_draw(splits[20], (NA, R, D), (4 * R) ** -0.5, 0.75),
    }


highest = lax.Precision.HIGHEST

@jax.custom_vjp
def low(v):
    return lax.optimization_barrier(v.astype(jnp.bfloat16)).astype(jnp.float32)

@jax.custom_vjp
def low_back(v):
    return v

def low_keep(v):
    return (low(v), None)

def low_pass(kept, grad):
    return (grad,)

def back_keep(v):
    return (v, None)

def back_low(kept, grad):
    return (low(grad),)
low.defvjp(low_keep, low_pass)
low_back.defvjp(back_keep, back_low)

def matmul(left_side, right_side):
    return jnp.dot(left_side, right_side, precision=highest, preferred_element_type=jnp.float32)

def normalize(values, gain_row, shift_row):
    row_mean = lax.optimization_barrier(jnp.mean(values, axis=-1, keepdims=True))
    centered = values - row_mean
    variance = lax.optimization_barrier(jnp.mean(centered * centered, axis=-1, keepdims=True))
    return centered * lax.rsqrt(variance + 1e-06) * gain_row + shift_row

def adapted(inputs, weight, down_map, up_map, select):
    latent = matmul(inputs, down_map.reshape(NA * R, -1).T) * select
    return matmul(inputs, weight) + matmul(latent, up_map.reshape(NA * R, -1))

def encoder_layer(hidden, qkv_down, qkv_up, proj_down, proj_up, fc1_down, fc1_up, fc2_down, fc2_up, frozen, keep_rows, select, key_open):
    ln_gain, ln_shift, w_qkv, bias_qv, w_proj, w_fc1, bias_fc1, w_fc2, bias_out = frozen
    images = key_open.shape[0]
    normed_one = low(normalize(hidden, ln_gain[0], ln_shift[0]))
    projected = [adapted(normed_one, w_qkv[section], qkv_down, qkv_up[:, :, section, :], select) for section in range(3)]
    queries = low(low_back(projected[0] + bias_qv[0]))
    key_side = low(low_back(projected[1]))
    value_side = low(low_back(projected[2] + bias_qv[1]))
    head_shape = (images, SEQ, H, HD)
    scores = jnp.einsum('gqhd,gkhd->ghqk', queries.reshape(head_shape), key_side.reshape(head_shape), precision=highest) * 0.125
    scores = low_back(scores)
    scores = jnp.where(key_open[:, None, None, :], scores, -1e+30)
    top_score = lax.optimization_barrier(jnp.max(scores, axis=-1, keepdims=True))
    exponent = jnp.exp(scores - top_score)
    soft_low = low(exponent / lax.optimization_barrier(jnp.sum(exponent, axis=-1, keepdims=True)))
    attended = jnp.einsum('ghqk,gkhd->gqhd', soft_low, value_side.reshape(head_shape), precision=highest)
    attended = low(low_back(attended.reshape(images * SEQ, D)))
    branch = low_back(adapted(attended, w_proj, proj_down, proj_up, select) + bias_out[0])
    middle = hidden + branch
    normed_two = low(normalize(middle, ln_gain[1], ln_shift[1]))
    pre_gelu = low_back(adapted(normed_two, w_fc1, fc1_down, fc1_up, select) + bias_fc1)
    activated = low(jax.nn.gelu(pre_gelu, approximate=False))
    result = low_back(adapted(activated, w_fc2, fc2_down, fc2_up, select) + bias_out[1])
    return keep_rows * (middle + result)

def reference(tokens_in, grad_out, keep_mask, adapter_index, ln_gain, ln_shift, w_qkv, bias_qv, w_proj, w_fc1, bias_fc1, w_fc2, bias_out, qkv_down, qkv_up, proj_down, proj_up, fc1_down, fc1_up, fc2_down, fc2_up):
    group_count = 1
    while group_count * 2 <= N_ROW and IMG_ROW * SEQ * group_count * 2 <= 4096:
        group_count = group_count * 2
    per_step = IMG_ROW * group_count
    step_count = IMAGES // per_step
    frozen = (ln_gain.astype(jnp.float32), ln_shift.astype(jnp.float32), w_qkv.astype(jnp.float32), bias_qv.astype(jnp.float32), w_proj.astype(jnp.float32), w_fc1.astype(jnp.float32), bias_fc1.astype(jnp.float32), w_fc2.astype(jnp.float32), bias_out.astype(jnp.float32))
    adapters = tuple((matrix.astype(jnp.float32) for matrix in (qkv_down, qkv_up, proj_down, proj_up, fc1_down, fc1_up, fc2_down, fc2_up)))
    inputs_all = tokens_in.reshape(step_count, per_step * SEQ, D)
    grads_all = grad_out.reshape(step_count, per_step * SEQ, D)
    keeps_all = keep_mask.reshape(step_count, per_step, SLOTS)
    owners_all = adapter_index.reshape(step_count, per_step)
    column_ids = jnp.arange(NA * R, dtype=jnp.int32) // R

    def one_step(totals, sliced):
        block_in, block_grad, block_keep, block_owner = sliced
        keep_full = jnp.concatenate([jnp.ones((per_step, BUF), jnp.int32), block_keep], axis=1)
        key_open = keep_full > 0
        keep_rows = keep_full.reshape(per_step * SEQ, 1).astype(jnp.float32)
        owner_rows = jnp.broadcast_to(block_owner[:, None], (per_step, SEQ)).reshape(per_step * SEQ, 1)
        select = (owner_rows == column_ids[None, :]).astype(jnp.float32)

        def forward(hidden, *weights):
            return encoder_layer(hidden, *weights, frozen, keep_rows, select, key_open)
        layer_out, pullback = jax.vjp(forward, block_in.astype(jnp.float32), *adapters)
        cotangents = pullback(block_grad.astype(jnp.float32))
        totals = tuple((running + addend for running, addend in zip(totals, cotangents[1:])))
        return (totals, (layer_out.astype(jnp.bfloat16), cotangents[0].astype(jnp.bfloat16)))
    initial = tuple((jnp.zeros_like(matrix) for matrix in adapters))
    totals, (outs_all, grads_in) = lax.scan(one_step, initial, (inputs_all, grads_all, keeps_all, owners_all))
    return (outs_all.reshape(TOKENS, D), grads_in.reshape(TOKENS, D), totals[0], totals[1], totals[2], totals[3], totals[4], totals[5], totals[6], totals[7])
```

```python
import jax
import jax.numpy as jnp
from jax import lax
from jax.sharding import PartitionSpec as P

D = 1024
H = 16
HD = 64
FF = 4096
BUF = 64
R = 16
NA = 8
SEQ = 320
BF = jnp.bfloat16
F32 = jnp.float32
BOTH = ("row", "col")


def norm_parts(values):
    row_mean = jnp.mean(values, axis=-1, keepdims=True)
    centered = values - row_mean
    variance = jnp.mean(centered * centered, axis=-1, keepdims=True)
    inverse = lax.rsqrt(variance + 1e-06)
    return (centered * inverse, inverse)


def norm_back(grad_normed, gain_row, unit_rows, inverse):
    scaled = grad_normed * gain_row
    first_mean = jnp.mean(scaled, axis=-1, keepdims=True)
    second_mean = jnp.mean(scaled * unit_rows, axis=-1, keepdims=True)
    return inverse * (scaled - first_mean - unit_rows * second_mean)


def gelu_slope(pre_gelu):
    cumulative = 0.5 * (1.0 + lax.erf(pre_gelu * 0.7071067811865476))
    return cumulative + pre_gelu * jnp.exp(-0.5 * pre_gelu * pre_gelu) * 0.3989422804014327


def dot(formula, left_side, right_side):
    return jnp.einsum(formula, left_side, right_side, preferred_element_type=F32)


def low(values):
    return values.astype(BF)


def exchange(block, axis, bit, rows, cols):
    stride = (1 << bit) * (cols if axis == "row" else 1)
    pairs = [(i, i ^ stride) for i in range(rows * cols)]
    return lax.ppermute(block, BOTH, pairs)


def joined(block, axis, bit, rows, cols, index, dim):
    other = exchange(block, axis, bit, rows, cols)
    is_high = ((index >> bit) & 1) == 1
    first = jnp.where(is_high, other, block)
    second = jnp.where(is_high, block, other)
    return jnp.stack([first, second], axis=dim)


def gather_blocks(shard, col_first):
    rows, cols = lax.axis_size("row"), lax.axis_size("col")
    row_bits = rows.bit_length() - 1
    col_bits = cols.bit_length() - 1
    row_index = lax.axis_index("row")
    order = [("row", b) for b in range(row_bits - 1, -1, -1)]
    wide = [("col", b) for b in range(col_bits - 1, 0, -1)]
    if col_first:
        order = order[:-1] + wide + order[-1:]
    else:
        order = order + wide
    order = order + [("col", 0)]
    held = [(0, shard)]
    depth = 0
    for axis, bit in order:
        if axis == "row":
            held = [
                (j, joined(block, axis, bit, rows, cols, row_index, depth)) for j, block in held
            ]
            depth += 1
            if bit == 0:
                held = [(j, block.reshape(-1, shard.shape[-1])) for j, block in held]
        else:
            held = held + [
                (j ^ (1 << bit), exchange(block, axis, bit, rows, cols)) for j, block in held
            ]
    return [block for _, block in sorted(held, key=lambda pair: pair[0])]


def gather_leading(block):
    rows, cols = lax.axis_size("row"), lax.axis_size("col")
    row_index, col_index = lax.axis_index("row"), lax.axis_index("col")
    depth = 0
    for axis, size, index in (("row", rows, row_index), ("col", cols, col_index)):
        for bit in range(size.bit_length() - 2, -1, -1):
            block = joined(block, axis, bit, rows, cols, index, depth)
            depth += 1
    return block.reshape((rows * cols,) + block.shape[depth:])


def sum_adapters(grads, owners):
    rows, cols = lax.axis_size("row"), lax.axis_size("col")
    devices = rows * cols
    width = grads.shape[-1]
    part = width // devices
    pieces = grads.reshape(R, devices, part).transpose(1, 0, 2)
    mine = lax.all_to_all(pieces, BOTH, split_axis=0, concat_axis=0, tiled=True)
    hot = (lax.broadcasted_iota(jnp.int32, (NA, devices), 0) == owners[None, :]).astype(BF)
    summed = low(dot("ad,drp->arp", hot, mine))
    whole = gather_leading(summed)
    return whole.transpose(1, 2, 0, 3).reshape(NA, R, width).astype(F32)


def place(parts, col_index):
    cols = len(parts)
    stacked = jnp.stack(parts, axis=-2)
    index = jnp.arange(cols)
    one_hot = (index[:, None] == (index[None, :] ^ col_index)).astype(stacked.dtype)
    picked = [
        sum(stacked[..., j, :] * one_hot[i, j] for j in range(cols)) for i in range(cols)
    ]
    return jnp.concatenate(picked, axis=-1)


def attention_pair(query_heads, key_heads, value_heads, key_open):
    def scores_of():
        raw_scores = dot("qhd,khd->hqk", query_heads, key_heads) * 0.125
        return jnp.where(key_open[None, None, :], raw_scores, -1e30)

    scores = scores_of()
    top_score = jnp.max(scores, axis=-1, keepdims=True)
    exponent = jnp.exp(scores - top_score)
    row_total = jnp.sum(exponent, axis=-1, keepdims=True)
    log_total = top_score + jnp.log(row_total)
    soft_low = (exponent / row_total).astype(BF)
    attended = dot("hqk,khd->qhd", soft_low, value_heads)

    def backward(grad_heads):
        soft_again = jnp.exp(scores_of() - log_total)
        grad_values = dot("hqk,qhd->khd", soft_again.astype(BF), grad_heads)
        grad_soft = dot("qhd,khd->hqk", grad_heads, value_heads)
        grad_scores = (
            soft_again * (grad_soft - jnp.sum(grad_soft * soft_again, axis=-1, keepdims=True))
        ).astype(BF)
        grad_queries = dot("hqk,khd->qhd", grad_scores, key_heads) * 0.125
        grad_keys = dot("hqk,qhd->khd", grad_scores, query_heads) * 0.125
        return (grad_queries, grad_keys, grad_values)

    return (attended, backward)


def per_device(
    tokens_in,
    grad_out,
    keep_mask,
    adapter_index,
    ln_gain,
    ln_shift,
    w_qkv,
    bias_qv,
    w_proj,
    w_fc1,
    bias_fc1,
    w_fc2,
    bias_out,
    qkv_down,
    qkv_up,
    proj_down,
    proj_up,
    fc1_down,
    fc1_up,
    fc2_down,
    fc2_up,
):
    rows, cols = lax.axis_size("row"), lax.axis_size("col")
    column = lax.axis_index("col")
    assert adapter_index.shape[0] == cols
    hid = D // cols
    ffn = FF // cols

    x_rows = lax.all_to_all(tokens_in, "col", split_axis=0, concat_axis=1, tiled=True)
    g_rows = lax.all_to_all(grad_out, "col", split_axis=0, concat_axis=1, tiled=True)

    shard_q = jnp.concatenate([w_qkv[0], w_qkv[1], w_qkv[2], w_proj.T], axis=1)
    w_q = gather_blocks(shard_q, True)
    w_1 = gather_blocks(w_fc1, False)
    w_2 = gather_blocks(w_fc2.T, True)
    bias_all = lax.all_gather(
        jnp.concatenate([bias_qv.reshape(-1), bias_fc1]), "col", axis=0, tiled=False
    )
    owners = lax.all_gather(adapter_index, "row", axis=0, tiled=True)

    mask_row = lax.dynamic_index_in_dim(keep_mask, column, 0, keepdims=False)
    keep_full = jnp.concatenate([jnp.ones((BUF,), jnp.int32), mask_row])
    key_open = keep_full > 0
    keep_rows = keep_full.reshape(SEQ, 1).astype(F32)
    adapter = lax.dynamic_index_in_dim(adapter_index, column, 0, keepdims=False)

    def mine(table):
        return lax.dynamic_index_in_dim(table, adapter, 0, keepdims=False)

    def block(table, j, width):
        return lax.dynamic_slice_in_dim(table, (column ^ j) * width, width, table.ndim - 1)

    qkv_down, qkv_up, proj_down, proj_up = mine(qkv_down), mine(qkv_up), mine(proj_down), mine(proj_up)
    fc1_down, fc1_up, fc2_down, fc2_up = mine(fc1_down), mine(fc1_up), mine(fc2_down), mine(fc2_up)
    bias_out = bias_out.astype(F32)

    def bias_of(j):
        return lax.dynamic_index_in_dim(bias_all, column ^ j, 0, keepdims=False).astype(F32)

    hidden = x_rows.astype(F32)
    unit_one, inverse_one = norm_parts(hidden)
    normed_one = low(unit_one * ln_gain[0] + ln_shift[0])
    latent_one = low(dot("td,rd->tr", normed_one, qkv_down))
    q_parts, k_parts, v_parts = [], [], []
    for j in range(cols):
        up = block(qkv_up, j, hid).reshape(R, 3 * hid)
        made = dot("td,de->te", normed_one, w_q[j][:, : 3 * hid]) + dot("tr,re->te", latent_one, up)
        bias = bias_of(j)
        q_parts.append(low(made[:, :hid] + bias[:hid]))
        k_parts.append(low(made[:, hid : 2 * hid]))
        v_parts.append(low(made[:, 2 * hid :] + bias[hid : 2 * hid]))
    heads = (SEQ, H, HD)
    q_all, k_all, v_all = (jnp.concatenate(p, axis=1) for p in (q_parts, k_parts, v_parts))
    attended_heads, attention_back = attention_pair(
        q_all.reshape(heads), k_all.reshape(heads), v_all.reshape(heads), key_open
    )
    attended = low(attended_heads.reshape(SEQ, D))
    proj_down_rel = jnp.concatenate([block(proj_down, j, hid) for j in range(cols)], axis=1)
    latent_two = low(dot("th,rh->tr", attended, proj_down_rel))
    branch = dot("tr,rd->td", latent_two, proj_up) + bias_out[0]
    for j in range(cols):
        branch = branch + dot("th,dh->td", attended[:, j * hid : (j + 1) * hid], w_q[j][:, 3 * hid :])
    middle = hidden + branch
    unit_two, inverse_two = norm_parts(middle)
    normed_two = low(unit_two * ln_gain[1] + ln_shift[1])
    latent_three = low(dot("td,rd->tr", normed_two, fc1_down))

    grad_result = g_rows.astype(F32) * keep_rows
    grad_result_low = low(grad_result)
    grad_latent_four = low(dot("td,rd->tr", grad_result_low, fc2_up))

    result = bias_out[1]
    grad_normed_two = 0.0
    latent_four = 0.0
    grad_latent_three = 0.0
    g_fc2_down, g_fc1_up = [], []
    for j in range(cols):
        up_1, down_2 = block(fc1_up, j, ffn), block(fc2_down, j, ffn)
        pre_gelu = (
            dot("td,df->tf", normed_two, w_1[j])
            + dot("tr,rf->tf", latent_three, up_1)
            + bias_of(j)[2 * hid :]
        )
        activated = low(jax.nn.gelu(pre_gelu, approximate=False))
        grad_act = dot("td,df->tf", grad_result_low, w_2[j]) + dot(
            "tr,rf->tf", grad_latent_four, down_2
        )
        grad_pre = low(grad_act * gelu_slope(pre_gelu))
        latent_four = latent_four + dot("tf,rf->tr", activated, down_2)
        grad_latent_three = grad_latent_three + dot("tf,rf->tr", grad_pre, up_1)
        result = result + dot("tf,df->td", activated, w_2[j])
        grad_normed_two = grad_normed_two + dot("tf,df->td", grad_pre, w_1[j])
        g_fc2_down.append(low(dot("tr,tf->rf", grad_latent_four, activated)))
        g_fc1_up.append(low(dot("tr,tf->rf", latent_three, grad_pre)))
    latent_four = low(latent_four)
    grad_latent_three = low(grad_latent_three)
    result = result + dot("tr,rd->td", latent_four, fc2_up)
    out_rows = low(keep_rows * (middle + result))
    layer_out = lax.all_to_all(out_rows, "col", split_axis=1, concat_axis=0, tiled=True)
    grad_normed_two = grad_normed_two + dot("tr,rd->td", grad_latent_three, fc1_down)
    grad_middle = grad_result + norm_back(grad_normed_two, ln_gain[1], unit_two, inverse_two)
    grad_branch = low(grad_middle)
    grad_latent_two = low(dot("td,rd->tr", grad_branch, proj_up))
    g_attended = []
    for j in range(cols):
        g_attended.append(
            low(
                dot("td,dh->th", grad_branch, w_q[j][:, 3 * hid :])
                + dot("tr,rh->th", grad_latent_two, block(proj_down, j, hid))
            )
        )
    g_attended = jnp.concatenate(g_attended, axis=1)
    g_proj_down = low(dot("tr,th->rh", grad_latent_two, attended))
    early = jnp.concatenate(
        [
            place([g_proj_down[:, j * hid : (j + 1) * hid] for j in range(cols)], column),
            low(dot("tr,td->rd", latent_two, grad_branch)),
            low(dot("tr,td->rd", grad_latent_three, normed_two)),
            place(g_fc1_up, column),
            place(g_fc2_down, column),
            low(dot("tr,td->rd", latent_four, grad_result_low)),
        ],
        axis=1,
    )
    early_sum = sum_adapters(early, owners)

    g_q, g_k, g_v = (low(g.reshape(SEQ, D)) for g in attention_back(g_attended.reshape(heads)))
    grad_latent_one = 0.0
    grad_normed_one = 0.0
    g_up = []
    for j in range(cols):
        up = block(qkv_up, j, hid).reshape(R, 3 * hid)
        g_j = jnp.concatenate([g[:, j * hid : (j + 1) * hid] for g in (g_q, g_k, g_v)], axis=1)
        grad_latent_one = grad_latent_one + dot("te,re->tr", g_j, up)
        grad_normed_one = grad_normed_one + dot("te,de->td", g_j, w_q[j][:, : 3 * hid])
        g_up.append(low(dot("tr,te->re", latent_one, g_j)).reshape(R, 3, hid))
    grad_latent_one = low(grad_latent_one)
    late = jnp.concatenate(
        [
            low(dot("tr,td->rd", grad_latent_one, normed_one)),
            place(g_up, column).reshape(R, 3 * D),
        ],
        axis=1,
    )
    late_sum = sum_adapters(late, owners)
    grad_normed_one = grad_normed_one + dot("tr,rd->td", grad_latent_one, qkv_down)
    grad_rows = low(grad_middle + norm_back(grad_normed_one, ln_gain[0], unit_one, inverse_one))
    grad_in = lax.all_to_all(grad_rows, "col", split_axis=1, concat_axis=0, tiled=True)

    return (
        layer_out,
        grad_in,
        late_sum[..., :D],
        late_sum[..., D:].reshape(NA, R, 3, D),
        early_sum[..., :D],
        early_sum[..., D : 2 * D],
        early_sum[..., 2 * D : 3 * D],
        early_sum[..., 3 * D : 3 * D + FF],
        early_sum[..., 3 * D + FF : 3 * D + 2 * FF],
        early_sum[..., 3 * D + 2 * FF :],
    )


def solution(mesh):
    return jax.shard_map(
        per_device,
        mesh=mesh,
        in_specs=(
            P("row", "col"),
            P("row", "col"),
            P("row", None),
            P("row"),
            P(),
            P(),
            P(None, "row", "col"),
            P(None, "col"),
            P("col", "row"),
            P("row", "col"),
            P("col"),
            P("col", "row"),
            P(),
            P(),
            P(),
            P(),
            P(),
            P(),
            P(),
            P(),
            P(),
        ),
        out_specs=(P("row", "col"), P("row", "col"), P(), P(), P(), P(), P(), P(), P(), P()),
        check_vma=False,
    )
```

```python
import functools

import jax
import jax.numpy as jnp
from jax import lax
from jax.experimental import pallas as pl
from jax.experimental.pallas import tpu as pltpu
from jax.sharding import PartitionSpec as P

D = 1024
H = 16
HD = 64
FF = 4096
BUF = 64
R = 16
NA = 8
SEQ = 320
PAIR = 2 * HD
EXTRA = 16
EARLY = 4 * D + 2 * FF
LATE = 4 * D
BF = jnp.bfloat16
F32 = jnp.float32
BOTH = ("row", "col")
VMEM = pltpu.VMEM
NN = (((1,), (0,)), ((), ()))
NT = (((1,), (1,)), ((), ()))


def mm(left, right, dims=NN):
    return lax.dot_general(left, right, dims, preferred_element_type=F32)


def low(values):
    return values.astype(BF)


def norm_parts(values):
    row_mean = jnp.mean(values, axis=-1, keepdims=True)
    centered = values - row_mean
    variance = jnp.mean(centered * centered, axis=-1, keepdims=True)
    inverse = lax.rsqrt(variance + 1e-06)
    return (centered * inverse, inverse)


def norm_back(grad_normed, gain_row, unit_rows, inverse):
    scaled = grad_normed * gain_row
    first_mean = jnp.mean(scaled, axis=-1, keepdims=True)
    second_mean = jnp.mean(scaled * unit_rows, axis=-1, keepdims=True)
    return inverse * (scaled - first_mean - unit_rows * second_mean)


def call(kernel, outs, ins, spaces, scratch=(), flops=0, moved=0, aliases=None):
    return pl.pallas_call(
        kernel,
        out_shape=outs,
        in_specs=[pl.BlockSpec(memory_space=s) for s in spaces],
        out_specs=jax.tree.map(lambda _: pl.BlockSpec(memory_space=VMEM), outs),
        scratch_shapes=list(scratch),
        input_output_aliases=aliases or {},
        compiler_params=pltpu.CompilerParams(vmem_limit_bytes=56 << 20),
        cost_estimate=pl.CostEstimate(flops=flops, bytes_accessed=moved, transcendentals=0),
    )(*ins)


def sizes():
    return lax.axis_size("row"), lax.axis_size("col")


def swap(block, flip):
    rows, cols = sizes()
    pairs = []
    for i in range(rows * cols):
        row, col = flip(i // cols, i % cols)
        pairs.append((i, row * cols + col))
    return lax.ppermute(block, BOTH, pairs)


def bits_of(size):
    return size.bit_length() - 1


def stack_kernel(which, *refs):
    out = refs[-1]
    for m, ref in enumerate(refs[:-1]):
        out[which[0] ^ m] = ref[...]


def stacked(parts, index):
    shape = parts[0].shape
    flat = [p.reshape((-1, shape[-1])) for p in parts]
    out = jax.ShapeDtypeStruct((len(parts),) + flat[0].shape, flat[0].dtype)
    made = call(
        stack_kernel,
        out,
        [index.reshape(1).astype(jnp.int32)] + flat,
        [pltpu.SMEM] + [VMEM] * len(parts),
        moved=2 * len(parts) * flat[0].size * 2,
    )
    return made.reshape((len(parts),) + shape)


def group_join(block, axis, low_bit, width):
    parts = [block]
    for m in range(1, 1 << width):
        step = m << low_bit
        if axis == "row":
            parts.append(swap(block, lambda r, c: (r ^ step, c)))
        else:
            parts.append(swap(block, lambda r, c: (r, c ^ step)))
    index = (lax.axis_index(axis) >> low_bit) & ((1 << width) - 1)
    return stacked(parts, index)


def groups(top, bottom):
    out = []
    while top > bottom:
        width = min(2, top - bottom)
        out.append((top - width, width))
        top -= width
    return out


def early_groups(rows, cols):
    return [("row",) + g for g in groups(bits_of(rows), 1)] + [
        ("col",) + g for g in groups(bits_of(cols), 2)
    ]


def lead_table(rows, cols):
    table = [(0, 0)]
    for axis, bit, width in early_groups(rows, cols):
        shift = bit - (1 if axis == "row" else 2)
        new = []
        for value in range(1 << width):
            for high_col, high_row in table:
                if axis == "row":
                    new.append((high_col, high_row + (value << shift)))
                else:
                    new.append((high_col + (value << shift), high_row))
        table = new
    return table


def gather_pieces(shard):
    rows, cols = sizes()
    block = shard
    for axis, bit, width in early_groups(rows, cols):
        block = group_join(block, axis, bit, width)
    own = block.reshape((-1,) + shard.shape)

    def one(r, c):
        return (r, c ^ 2) if c % 2 == 0 else (r ^ 1, c)

    def two(r, c):
        return (r ^ 1, c) if c % 2 == 0 else (r, c ^ 2)

    def core(r, c):
        return (r, c ^ 1)

    first = swap(own, one)
    second = swap(own, two)
    both = swap(first, two)
    mine = [own, first, second, both]
    return mine + [swap(p, core) for p in mine]


def all_steps(rows, cols):
    return (
        [("row",) + g for g in groups(bits_of(rows), 1)]
        + [("row", 0, 1)]
        + [("col",) + g for g in groups(bits_of(cols), 1)]
        + [("col", 0, 1)]
    )


def all_table(rows, cols):
    table = [0]
    for axis, bit, width in all_steps(rows, cols):
        stride = (cols if axis == "row" else 1) << bit
        table = [old + value * stride for value in range(1 << width) for old in table]
    return table


def gather_leading(block):
    rows, cols = sizes()
    shape = block.shape
    for axis, bit, width in all_steps(rows, cols):
        block = group_join(block, axis, bit, width)
    return block.reshape((rows * cols,) + shape)


def gather_owners(adapter_index):
    rows, cols = sizes()
    index = lax.axis_index("row")
    block = adapter_index
    for low_bit, width in reversed(groups(bits_of(rows), 0)):
        parts = [block]
        for m in range(1, 1 << width):
            step = m << low_bit
            parts.append(swap(block, lambda r, c: (r ^ step, c)))
        here = (index >> low_bit) & ((1 << width) - 1)
        block = jnp.stack(parts)[jnp.arange(1 << width) ^ here]
    return block.reshape(-1)


class Weights:
    def __init__(self, sc, pieces, w, sems, lead, first_lane=0):
        core, low_row = sc[2], sc[3]
        self.copies = {}
        depth = pieces[0].shape[1]
        taken = pl.ds(first_lane, w.shape[2])
        for k, piece in enumerate(pieces):
            kind, away = k % 4, k // 4
            turn = (core + away) & 1
            x_rel = (0, 1 - turn, turn, 1)[kind]
            y_rel = (0, turn, 1 - turn, 1)[kind]
            for n, (high_col, high_row) in enumerate(lead):
                slot = high_col * 4 + x_rel * 2 + away
                row = (high_row * 2 + ((low_row + y_rel) & 1)) * depth
                copy = pltpu.make_async_copy(
                    piece.at[n, :, taken],
                    w.at[slot, pl.ds(pl.multiple_of(row, depth), depth), :],
                    sems.at[k, n],
                )
                self.copies[(k, n)] = copy

    def start(self):
        for copy in self.copies.values():
            copy.start()

    def wait(self):
        for copy in self.copies.values():
            copy.wait()


def column_of(sc, slot):
    return (slot // 4) * 4 + ((sc[1] & 3) ^ (slot & 3))


def weight_scratch(rows, cols, n):
    lead = len(lead_table(rows, cols))
    return [VMEM((cols, D, n), BF), pltpu.SemaphoreType.DMA((8, lead))]


def lanes(start, width):
    return pl.ds(pl.multiple_of(start, width), width)


def prep_kernel(wq, wp, w1, w2, out_q, out_a, out_b):
    hid = wq.shape[2]
    half = w1.shape[1] // 2
    for c in range(3):
        out_q[:, c * hid : (c + 1) * hid] = wq[c]
    out_q[:, 3 * hid :] = low(wp[...].astype(F32).T)
    out_a[:, :half] = w1[:, :half]
    out_b[:, :half] = w1[:, half:]
    out_a[:, half:] = low(w2[:half].astype(F32).T)
    out_b[:, half:] = low(w2[half:].astype(F32).T)


def tokens_of(ref, cols):
    return jnp.concatenate([ref[c, :SEQ, :] for c in range(cols)], axis=1).astype(F32)


def front_kernel(lead, cols, *refs):
    sc = refs[0]
    pieces = refs[1:9]
    (xa, closed, gain, shift, q_down, q_up, p_down, p_up, f_down, bias_out) = refs[9:19]
    (n1, lat1, q, k, v, lse, att, lat2, middle, n2, lat3) = refs[19:30]
    w, sems, hidden, branch = refs[30:]
    weights = Weights(sc, pieces, w, sems, lead)
    weights.start()
    a = sc[0]
    hid = D // cols
    x = tokens_of(xa, cols)
    hidden[...] = x
    unit, _ = norm_parts(x)
    n1[...] = low(unit * gain[0:1] + shift[0:1])
    lat1[...] = low(mm(n1[...], q_down[a], NT))
    weights.wait()

    def project(slot, _):
        block = column_of(sc, slot)
        up = jnp.concatenate([q_up[a, :, c, lanes(block * hid, hid)] for c in range(3)], axis=1)
        made = mm(n1[...], w[slot, :, : 3 * hid]) + mm(lat1[...], up)
        bias_q = xa[block, SEQ : SEQ + 1, :].astype(F32)
        bias_v = xa[block, SEQ + 1 : SEQ + 2, :].astype(F32)
        at = lanes(slot * hid, hid)
        q[:, at] = low(made[:, :hid] + bias_q) * jnp.asarray(0.125, BF)
        k[:, at] = low(made[:, hid : 2 * hid])
        v[:, at] = low(made[:, 2 * hid :] + bias_v)
        return 0

    lax.fori_loop(0, cols, project, 0)
    shut = closed[...] > 0.5
    left = lax.broadcasted_iota(jnp.int32, (1, PAIR), 1) < HD

    def attend(pair, _):
        at = lanes(pair * PAIR, PAIR)
        qp, kp, vp = q[:, at], k[:, at], v[:, at]
        v_t = low(vp.astype(F32).T)
        halves = []
        for h in range(2):
            masked = jnp.where(left == (h == 0), qp, jnp.zeros_like(qp))
            s = jnp.where(shut, -1e30, mm(kp, masked, NT))
            top = jnp.max(s, axis=0, keepdims=True)
            e = jnp.exp(s - top)
            total = jnp.sum(e, axis=0, keepdims=True)
            lse[pair, h : h + 1, :] = top + jnp.log(total)
            soft = low(e * (1.0 / total))
            halves.append(mm(v_t[h * HD : (h + 1) * HD], soft))
        att[:, at] = low(jnp.concatenate(halves, axis=0).T)
        return 0

    lax.fori_loop(0, H // 2, attend, 0)

    def down_two(slot, acc):
        block = column_of(sc, slot)
        return acc + mm(att[:, lanes(slot * hid, hid)], p_down[a, :, lanes(block * hid, hid)], NT)

    lat2[...] = low(lax.fori_loop(0, cols, down_two, jnp.zeros((SEQ, R), F32)))
    branch[...] = mm(lat2[...], p_up[a]) + bias_out[0:1].astype(F32)

    def out_proj(slot, _):
        branch[...] += mm(att[:, lanes(slot * hid, hid)], w[slot, :, 3 * hid :], NT)
        return 0

    lax.fori_loop(0, cols, out_proj, 0)
    mid = hidden[...] + branch[...]
    middle[...] = mid
    unit, _ = norm_parts(mid)
    n2[...] = low(unit * gain[1:2] + shift[1:2])
    lat3[...] = low(mm(n2[...], f_down[a], NT))


def ffn_steps(sc, part, cols, w, xa, n2, lat3, gr, glat4, up_1, down_2, acc, early):
    res, gn2, lat4, glat3 = acc
    a = sc[0]
    hid = D // cols
    ffn = FF // cols
    half = ffn // 2
    glat4_t = low(glat4.astype(F32).T)
    lat3_t = low(lat3[...].astype(F32).T)

    def step(slot, _):
        block = column_of(sc, slot)
        at = pl.ds(pl.multiple_of(block * ffn + part * half, half), half)
        bias = jnp.concatenate(
            [xa[block, SEQ + 2 + 2 * part + i : SEQ + 3 + 2 * part + i, :] for i in range(2)], axis=1
        ).astype(F32)
        up, down = up_1[a, :, at], down_2[a, :, at]
        w1, w2 = w[slot, :, :half], w[slot, :, half:]
        pre = mm(n2[...], w1) + mm(lat3[...], up) + bias
        back = mm(gr[...], w2) + mm(glat4, down)
        cumulative = 0.5 * (1.0 + lax.erf(pre * 0.7071067811865476))
        activated = low(pre * cumulative)
        slope = cumulative + pre * jnp.exp(-0.5 * pre * pre) * 0.3989422804014327
        grad_pre = low(back * slope)
        lat4[...] += mm(activated, down, NT)
        glat3[...] += mm(grad_pre, up, NT)
        res[...] += mm(activated, w2, NT)
        gn2[...] += mm(grad_pre, w1, NT)
        early[:, pl.ds(pl.multiple_of(3 * D + block * ffn + part * half, half), half)] = low(
            mm(lat3_t, grad_pre)
        )
        early[:, pl.ds(pl.multiple_of(3 * D + FF + block * ffn + part * half, half), half)] = low(
            mm(glat4_t, activated)
        )
        return 0

    lax.fori_loop(0, cols, step, 0)


def ffn_a_kernel(lead, cols, *refs):
    sc = refs[0]
    pieces = refs[1:9]
    xa, ga, keep, n2, lat3, up_1, down_2, up_2 = refs[9:17]
    res, gn2, lat4, glat3, gr, early = refs[17:23]
    w, sems = refs[23:]
    weights = Weights(sc, pieces, w, sems, lead)
    weights.start()
    gr[...] = low(
        jnp.concatenate([ga[c] for c in range(cols)], axis=1).astype(F32) * keep[...]
    )
    glat4 = low(mm(gr[...], up_2[sc[0]], NT))
    res[...] = jnp.zeros_like(res)
    gn2[...] = jnp.zeros_like(gn2)
    lat4[...] = jnp.zeros_like(lat4)
    glat3[...] = jnp.zeros_like(glat3)
    early[...] = jnp.zeros_like(early)
    weights.wait()
    ffn_steps(
        sc, 0, cols, w, xa, n2, lat3, gr, glat4, up_1, down_2, (res, gn2, lat4, glat3), early
    )


def ffn_b_kernel(lead, cols, *refs):
    sc = refs[0]
    pieces = refs[1:9]
    own_q = refs[9:17]
    (xa, keep, gain, n2, lat3, up_1, down_2, up_2, f_down, p_down, p_up, bias_out) = refs[17:29]
    (middle, att, lat2, gr, res_in, gn2_in, lat4_in, glat3_in, early_in) = refs[29:38]
    layer, gatt, gmid, early = refs[38:42]
    w, sems, wp, sems_p, res, gn2, lat4, glat3 = refs[42:]
    weights = Weights(sc, pieces, w, sems, lead)
    weights.start()
    proj = Weights(sc, own_q, wp, sems_p, lead, 3 * D // cols)
    proj.start()
    a = sc[0]
    hid = D // cols
    glat4 = low(mm(gr[...], up_2[a], NT))
    res[...] = res_in[...]
    gn2[...] = gn2_in[...]
    lat4[...] = lat4_in[...]
    glat3[...] = glat3_in[...]
    early[...] = early_in[...]
    weights.wait()
    ffn_steps(
        sc, 1, cols, w, xa, n2, lat3, gr, glat4, up_1, down_2, (res, gn2, lat4, glat3), early
    )
    mid = middle[...]
    lat4_low = low(lat4[...])
    out = low(
        keep[...] * (mid + res[...] + mm(lat4_low, up_2[a]) + bias_out[1:2].astype(F32))
    )
    for c in range(cols):
        layer[c] = out[:, c * hid : (c + 1) * hid]
    glat3_low = low(glat3[...])
    grad_normed = gn2[...] + mm(glat3_low, f_down[a])
    unit, inverse = norm_parts(mid)
    grad_middle = gr[...].astype(F32) + norm_back(grad_normed, gain[1:2], unit, inverse)
    gmid[...] = grad_middle
    gb = low(grad_middle)
    glat2 = low(mm(gb, p_up[a], NT))
    glat2_t = low(glat2.astype(F32).T)
    early[:, D : 2 * D] = low(mm(low(lat2[...].astype(F32).T), gb))
    early[:, 2 * D : 3 * D] = low(mm(low(glat3_low.astype(F32).T), n2[...]))
    early[:, 3 * D + 2 * FF :] = low(mm(low(lat4_low.astype(F32).T), gr[...]))
    proj.wait()

    def step(slot, _):
        block = column_of(sc, slot)
        here = lanes(slot * hid, hid)
        there = lanes(block * hid, hid)
        gatt[:, here] = low(mm(gb, wp[slot]) + mm(glat2, p_down[a, :, there]))
        early[:, there] = low(mm(glat2_t, att[:, here]))
        return 0

    lax.fori_loop(0, cols, step, 0)


def attention_back_kernel(cols, *refs):
    sc = refs[0]
    closed, q, k, v, lse, gatt, lat1, n1, q_up = refs[1:10]
    gq, gk, gv, glat1, late = refs[10:15]
    a = sc[0]
    hid = D // cols
    shut = closed[...] > 0.5
    left = lax.broadcasted_iota(jnp.int32, (1, PAIR), 1) < HD

    def attend(pair, _):
        at = lanes(pair * PAIR, PAIR)
        qp, kp, vp, gp = q[:, at], k[:, at], v[:, at], gatt[:, at]
        k_t = low(kp.astype(F32).T)
        by_q, by_k, by_v = [], [], []
        for h in range(2):
            mine = left == (h == 0)
            zero = jnp.zeros_like(qp)
            s = jnp.where(shut, -1e30, mm(kp, jnp.where(mine, qp, zero), NT))
            soft = jnp.exp(s - lse[pair, h : h + 1, :])
            grad_soft = mm(vp, jnp.where(mine, gp, zero), NT)
            total = jnp.sum(grad_soft * soft, axis=0, keepdims=True)
            grad_scores = low(soft * (grad_soft - total))
            by_v.append(mm(low(soft), gp))
            by_k.append(mm(grad_scores, qp))
            by_q.append(mm(k_t[h * HD : (h + 1) * HD], grad_scores))
        gq[:, at] = low(jnp.concatenate(by_q, axis=0).T * 0.125)
        gk[:, at] = low(jnp.where(left, by_k[0], by_k[1]))
        gv[:, at] = low(jnp.where(left, by_v[0], by_v[1]))
        return 0

    lax.fori_loop(0, H // 2, attend, 0)
    lat1_t = low(lat1[...].astype(F32).T)

    def step(slot, acc):
        block = column_of(sc, slot)
        here = lanes(slot * hid, hid)
        there = lanes(block * hid, hid)
        for c, g in enumerate((gq, gk, gv)):
            grad = g[:, here]
            acc = acc + mm(grad, q_up[a, :, c, there], NT)
            late[:, pl.ds(pl.multiple_of((c + 1) * D + block * hid, hid), hid)] = low(
                mm(lat1_t, grad)
            )
        return acc

    made = low(lax.fori_loop(0, cols, step, jnp.zeros((SEQ, R), F32)))
    glat1[...] = made
    late[:, :D] = low(mm(low(made.astype(F32).T), n1[...]))


def back_kernel(lead, cols, *refs):
    sc = refs[0]
    pieces = refs[1:9]
    xa, gain, gq, gk, gv, glat1, q_down, gmid = refs[9:17]
    out = refs[17]
    w, sems, acc = refs[18:]
    weights = Weights(sc, pieces, w, sems, lead)
    weights.start()
    hid = D // cols
    acc[...] = mm(glat1[...], q_down[sc[0]])
    x = tokens_of(xa, cols)
    unit, inverse = norm_parts(x)
    weights.wait()

    def step(slot, _):
        here = lanes(slot * hid, hid)
        grad = jnp.concatenate([gq[:, here], gk[:, here], gv[:, here]], axis=1)
        acc[...] += mm(grad, w[slot, :, : 3 * hid], NT)
        return 0

    lax.fori_loop(0, cols, step, 0)
    made = low(gmid[...] + norm_back(acc[...], gain[0:1], unit, inverse))
    for c in range(cols):
        out[c] = made[:, c * hid : (c + 1) * hid]


def sum_kernel(owners, mine, out, acc):
    acc[...] = jnp.zeros_like(acc)
    for d in range(mine.shape[0]):
        acc[owners[d]] += mine[d].astype(F32)
    out[...] = low(acc[...])


def spread_kernel(spans, part, table, whole, *outs):
    for b in range(whole.shape[0] * part // 128):
        lane = b * 128
        block = whole[table.index(lane // part), :, lane % part : lane % part + 128].astype(F32)
        for out, (start, width) in zip(outs, spans):
            if start <= lane < start + width:
                out[:, lane - start : lane - start + 128] = block


def sum_adapters(grads, owners, spans):
    rows, cols = sizes()
    devices = rows * cols
    width = grads.shape[-1]
    part = width // devices
    pieces = grads.reshape(R, devices, part).transpose(1, 0, 2)
    mine = lax.all_to_all(pieces, BOTH, split_axis=0, concat_axis=0, tiled=True)
    summed = call(
        sum_kernel,
        jax.ShapeDtypeStruct((NA, R, part), BF),
        [owners, mine],
        [pltpu.SMEM, VMEM],
        [VMEM((NA, R, part), F32)],
        moved=4 * mine.size,
    )
    whole = gather_leading(summed.reshape(NA * R, part))
    if part % 128 == 0:
        return call(
            functools.partial(spread_kernel, spans, part, all_table(rows, cols)),
            [jax.ShapeDtypeStruct((NA * R, n), F32) for _, n in spans],
            [whole],
            [VMEM],
            moved=6 * whole.size,
        )
    table = all_table(rows, cols)
    whole = whole[jnp.array([table.index(d) for d in range(devices)])]
    flat = jnp.swapaxes(whole, 0, 1).reshape(NA * R, width).astype(F32)
    return [flat[:, s : s + n] for s, n in spans]


def per_device(
    tokens_in,
    grad_out,
    keep_mask,
    adapter_index,
    ln_gain,
    ln_shift,
    w_qkv,
    bias_qv,
    w_proj,
    w_fc1,
    bias_fc1,
    w_fc2,
    bias_out,
    qkv_down,
    qkv_up,
    proj_down,
    proj_up,
    fc1_down,
    fc1_up,
    fc2_down,
    fc2_up,
):
    rows, cols = sizes()
    row, column = lax.axis_index("row"), lax.axis_index("col")
    assert adapter_index.shape[0] == cols and cols >= 4 and rows >= 2
    hid = D // cols
    n = 4 * hid
    blk = D // rows
    lead = lead_table(rows, cols)

    biases = jnp.concatenate(
        [bias_qv, bias_fc1.reshape(4, hid), jnp.zeros((EXTRA - 6, hid), BF)], axis=0
    )
    tokens = jnp.concatenate(
        [tokens_in.reshape(cols, SEQ, hid), jnp.broadcast_to(biases, (cols, EXTRA, hid))], axis=1
    )
    xa = lax.all_to_all(tokens, "col", split_axis=0, concat_axis=0, tiled=True)
    ga = lax.all_to_all(
        grad_out.reshape(cols, SEQ, hid), "col", split_axis=0, concat_axis=0, tiled=True
    )
    shard = jax.ShapeDtypeStruct((blk, n), BF)
    shard_q, shard_a, shard_b = call(
        prep_kernel, [shard] * 3, [w_qkv, w_proj, w_fc1, w_fc2], [VMEM] * 4, moved=12 * blk * n
    )
    pieces_q = gather_pieces(shard_q)
    pieces_a = gather_pieces(shard_a)
    pieces_b = gather_pieces(shard_b)
    owners = gather_owners(adapter_index)

    mask_row = lax.dynamic_index_in_dim(keep_mask, column, 0, keepdims=False)
    keep = jnp.concatenate([jnp.ones((BUF,), F32), mask_row.astype(F32)]).reshape(SEQ, 1)
    closed = 1.0 - keep
    adapter = lax.dynamic_index_in_dim(adapter_index, column, 0, keepdims=False)
    sc = jnp.stack([adapter, column, column % 2, row % 2]).astype(jnp.int32)

    def shaped(width, dtype, height=SEQ):
        return jax.ShapeDtypeStruct((height, width), dtype)

    big, small = shaped(D, BF), shaped(R, BF)
    scratch = weight_scratch(rows, cols, n)
    flops = 2 * SEQ * D * D
    any_space = [pl.ANY] * 8
    n1, lat1, q, k, v, lse, att, lat2, middle, n2, lat3 = call(
        functools.partial(front_kernel, lead, cols),
        [
            big,
            small,
            big,
            big,
            big,
            jax.ShapeDtypeStruct((H // 2, 2, SEQ), F32),
            big,
            small,
            shaped(D, F32),
            big,
            small,
        ],
        [sc, *pieces_q, xa, closed, ln_gain, ln_shift, qkv_down, qkv_up, proj_down, proj_up]
        + [fc1_down, bias_out],
        [pltpu.SMEM] + any_space + [VMEM] * 10,
        scratch + [VMEM((SEQ, D), F32), VMEM((SEQ, D), F32)],
        flops=5 * flops,
        moved=8 * D * D + 16 * SEQ * D,
    )
    wide = shaped(D, F32)
    thin = shaped(R, F32)
    res, gn2, lat4, glat3, gr, early = call(
        functools.partial(ffn_a_kernel, lead, cols),
        [wide, wide, thin, thin, big, shaped(EARLY, BF, R)],
        [sc, *pieces_a, xa, ga, keep, n2, lat3, fc1_up, fc2_down, fc2_up],
        [pltpu.SMEM] + any_space + [VMEM] * 8,
        scratch,
        flops=8 * flops,
        moved=8 * D * D + 16 * SEQ * D,
    )
    layer, gatt, gmid, early = call(
        functools.partial(ffn_b_kernel, lead, cols),
        [jax.ShapeDtypeStruct((cols, SEQ, hid), BF), big, wide, shaped(EARLY, BF, R)],
        [sc, *pieces_b, *pieces_q, xa, keep, ln_gain, n2, lat3, fc1_up, fc2_down, fc2_up]
        + [fc1_down, proj_down, proj_up, bias_out]
        + [middle, att, lat2, gr, res, gn2, lat4, glat3, early],
        [pltpu.SMEM] + any_space * 2 + [VMEM] * 21,
        scratch
        + [VMEM((cols, D, hid), BF), scratch[1]]
        + [VMEM((SEQ, D), F32), VMEM((SEQ, D), F32), VMEM((SEQ, R), F32), VMEM((SEQ, R), F32)],
        flops=10 * flops,
        moved=10 * D * D + 24 * SEQ * D,
    )
    layer = lax.all_to_all(layer, "col", split_axis=0, concat_axis=0, tiled=True)
    early_sum = sum_adapters(
        early,
        owners,
        ((0, D), (D, D), (2 * D, D), (3 * D, FF), (3 * D + FF, FF), (3 * D + 2 * FF, D)),
    )
    gq, gk, gv, glat1, late = call(
        functools.partial(attention_back_kernel, cols),
        [big, big, big, small, shaped(LATE, BF, R)],
        [sc, closed, q, k, v, lse, gatt, lat1, n1, qkv_up],
        [pltpu.SMEM] + [VMEM] * 9,
        flops=5 * flops,
        moved=16 * SEQ * D,
    )
    late_sum = sum_adapters(late, owners, ((0, D), (D, D), (2 * D, D), (3 * D, D)))
    grad_in = call(
        functools.partial(back_kernel, lead, cols),
        jax.ShapeDtypeStruct((cols, SEQ, hid), BF),
        [sc, *pieces_q, xa, ln_gain, gq, gk, gv, glat1, qkv_down, gmid],
        [pltpu.SMEM] + any_space + [VMEM] * 8,
        scratch + [VMEM((SEQ, D), F32)],
        flops=3 * flops,
        moved=8 * D * D + 8 * SEQ * D,
    )
    grad_in = lax.all_to_all(grad_in, "col", split_axis=0, concat_axis=0, tiled=True)

    def split(table, last=()):
        return table.reshape((NA, R) + last + (-1,))

    g_qkv_up = jnp.stack([split(t) for t in late_sum[1:]], axis=2)
    return (
        layer.reshape(cols * SEQ, hid),
        grad_in.reshape(cols * SEQ, hid),
        split(late_sum[0]),
        g_qkv_up,
        split(early_sum[0]),
        split(early_sum[1]),
        split(early_sum[2]),
        split(early_sum[3]),
        split(early_sum[4]),
        split(early_sum[5]),
    )


def solution(mesh):
    return jax.shard_map(
        per_device,
        mesh=mesh,
        in_specs=(
            P("row", "col"),
            P("row", "col"),
            P("row", None),
            P("row"),
            P(),
            P(),
            P(None, "row", "col"),
            P(None, "col"),
            P("col", "row"),
            P("row", "col"),
            P("col"),
            P("col", "row"),
            P(),
            P(),
            P(),
            P(),
            P(),
            P(),
            P(),
            P(),
            P(),
        ),
        out_specs=(P("row", "col"), P("row", "col"), P(), P(), P(), P(), P(), P(), P(), P()),
        check_vma=False,
    )
```

```python
import functools

import jax
import jax.numpy as jnp
from jax import lax
from jax.experimental import pallas as pl
from jax.experimental.pallas import tpu as pltpu
from jax.sharding import PartitionSpec as P

D = 1024
H = 16
HD = 64
FF = 4096
BUF = 64
R = 16
NA = 8
SEQ = 320
PAIR = 2 * HD
EXTRA = 16
BF = jnp.bfloat16
F32 = jnp.float32
BOTH = ("row", "col")
VMEM = pltpu.VMEM
NN = (((1,), (0,)), ((), ()))
NT = (((1,), (1,)), ((), ()))


def mm(left, right, dims=NN):
    return lax.dot_general(left, right, dims, preferred_element_type=F32)


def low(values):
    return values.astype(BF)


def norm_parts(values):
    row_mean = jnp.mean(values, axis=-1, keepdims=True)
    centered = values - row_mean
    variance = jnp.mean(centered * centered, axis=-1, keepdims=True)
    inverse = lax.rsqrt(variance + 1e-06)
    return (centered * inverse, inverse)


def norm_back(grad_normed, gain_row, unit_rows, inverse):
    scaled = grad_normed * gain_row
    first_mean = jnp.mean(scaled, axis=-1, keepdims=True)
    second_mean = jnp.mean(scaled * unit_rows, axis=-1, keepdims=True)
    return inverse * (scaled - first_mean - unit_rows * second_mean)


def call(kernel, outs, ins, spaces, scratch=()):
    return pl.pallas_call(
        kernel,
        out_shape=outs,
        in_specs=[pl.BlockSpec(memory_space=s) for s in spaces],
        out_specs=jax.tree.map(lambda _: pl.BlockSpec(memory_space=VMEM), outs),
        scratch_shapes=list(scratch),
        compiler_params=pltpu.CompilerParams(vmem_limit_bytes=56 << 20),
        cost_estimate=pl.CostEstimate(flops=0, bytes_accessed=0, transcendentals=0),
    )(*ins)


def sizes():
    return lax.axis_size("row"), lax.axis_size("col")


def swap(block, flip):
    rows, cols = sizes()
    pairs = []
    for i in range(rows * cols):
        row, col = flip(i // cols, i % cols)
        pairs.append((i, row * cols + col))
    return lax.ppermute(block, BOTH, pairs)


def bits_of(size):
    return size.bit_length() - 1


def stack_kernel(which, *refs):
    out = refs[-1]
    for m, ref in enumerate(refs[:-1]):
        out[which[0] ^ m] = ref[...]


def stacked(parts, index):
    shape = parts[0].shape
    flat = [p.reshape((-1, shape[-1])) for p in parts]
    out = jax.ShapeDtypeStruct((len(parts),) + flat[0].shape, flat[0].dtype)
    made = call(
        stack_kernel,
        out,
        [index.reshape(1).astype(jnp.int32)] + flat,
        [pltpu.SMEM] + [VMEM] * len(parts),
    )
    return made.reshape((len(parts),) + shape)


def group_join(block, axis, low_bit, width):
    parts = [block]
    for m in range(1, 1 << width):
        step = m << low_bit
        if axis == "row":
            parts.append(swap(block, lambda r, c: (r ^ step, c)))
        else:
            parts.append(swap(block, lambda r, c: (r, c ^ step)))
    index = (lax.axis_index(axis) >> low_bit) & ((1 << width) - 1)
    return stacked(parts, index)


def groups(top, bottom):
    out = []
    while top > bottom:
        width = min(2, top - bottom)
        out.append((top - width, width))
        top -= width
    return out


def early_groups(rows, cols):
    return [("row",) + g for g in groups(bits_of(rows), 1)] + [
        ("col",) + g for g in groups(bits_of(cols), 2)
    ]


def lead_table(rows, cols):
    table = [(0, 0)]
    for axis, bit, width in early_groups(rows, cols):
        shift = bit - (1 if axis == "row" else 2)
        new = []
        for value in range(1 << width):
            for high_col, high_row in table:
                if axis == "row":
                    new.append((high_col, high_row + (value << shift)))
                else:
                    new.append((high_col + (value << shift), high_row))
        table = new
    return table


def after(value, *others):
    return lax.optimization_barrier((value,) + others)[0]


def gather_high(shard):
    rows, cols = sizes()
    block = shard
    for axis, bit, width in early_groups(rows, cols):
        block = group_join(block, axis, bit, width)
    return block.reshape((-1,) + shard.shape)


def flip_one(r, c):
    return (r, c ^ 2) if c % 2 == 0 else (r ^ 1, c)


def flip_two(r, c):
    return (r ^ 1, c) if c % 2 == 0 else (r, c ^ 2)


def flip_core(r, c):
    return (r, c ^ 1)


def all_steps(rows, cols):
    return (
        [("row",) + g for g in groups(bits_of(rows), 1)]
        + [("row", 0, 1)]
        + [("col",) + g for g in groups(bits_of(cols), 1)]
        + [("col", 0, 1)]
    )


def all_table(rows, cols):
    table = [0]
    for axis, bit, width in all_steps(rows, cols):
        stride = (cols if axis == "row" else 1) << bit
        table = [old + value * stride for value in range(1 << width) for old in table]
    return table


def gather_leading(block, waits):
    rows, cols = sizes()
    shape = block.shape
    for i, (axis, bit, width) in enumerate(all_steps(rows, cols)):
        if i in waits:
            block = after(block, *waits[i])
        block = group_join(block, axis, bit, width)
    return block.reshape((rows * cols,) + shape)


def gather_owners(adapter_index):
    rows, cols = sizes()
    index = lax.axis_index("row")
    block = adapter_index
    for low_bit, width in reversed(groups(bits_of(rows), 0)):
        parts = [block]
        for m in range(1, 1 << width):
            step = m << low_bit
            parts.append(swap(block, lambda r, c: (r ^ step, c)))
        here = (index >> low_bit) & ((1 << width) - 1)
        block = jnp.stack(parts)[jnp.arange(1 << width) ^ here]
    return block.reshape(-1)


class Weights:
    def __init__(self, sc, pieces, w, sems, lead, first_lane=0):
        core, low_row = sc[2], sc[3]
        self.copies = {}
        depth = pieces[0].shape[1]
        taken = pl.ds(first_lane, w.shape[2])
        for k, piece in enumerate(pieces):
            kind, away = k % 4, k // 4
            turn = (core + away) & 1
            x_rel = (0, 1 - turn, turn, 1)[kind]
            y_rel = (0, turn, 1 - turn, 1)[kind]
            for n, (high_col, high_row) in enumerate(lead):
                slot = high_col * 4 + x_rel * 2 + away
                row = (high_row * 2 + ((low_row + y_rel) & 1)) * depth
                copy = pltpu.make_async_copy(
                    piece.at[n, :, taken],
                    w.at[slot, pl.ds(pl.multiple_of(row, depth), depth), :],
                    sems.at[k, n],
                )
                self.copies[(k, n)] = copy

    def start(self):
        for copy in self.copies.values():
            copy.start()

    def wait(self):
        for copy in self.copies.values():
            copy.wait()


def column_of(sc, slot):
    return (slot // 4) * 4 + ((sc[1] & 3) ^ (slot & 3))


def weight_scratch(rows, cols, n):
    lead = len(lead_table(rows, cols))
    return [VMEM((cols, D, n), BF), pltpu.SemaphoreType.DMA((8, lead))]


def lanes(start, width):
    return pl.ds(pl.multiple_of(start, width), width)


def prep_q_kernel(wq, wp, out):
    hid = wq.shape[2]
    for c in range(3):
        out[:, c * hid : (c + 1) * hid] = wq[c]
    out[:, 3 * hid :] = low(wp[...].astype(F32).T)


def prep_f_kernel(w1, w2, out_a, out_b):
    half = w1.shape[1] // 2
    out_a[:, :half] = w1[:, :half]
    out_b[:, :half] = w1[:, half:]
    out_a[:, half:] = low(w2[:half].astype(F32).T)
    out_b[:, half:] = low(w2[half:].astype(F32).T)


def tokens_of(ref, cols):
    return jnp.concatenate([ref[c, :SEQ, :] for c in range(cols)], axis=1).astype(F32)


def front_kernel(lead, cols, *refs):
    sc = refs[0]
    pieces = refs[1:9]
    (xa, closed, gain, shift, q_down, q_up, p_down, p_up, f_down, bias_out) = refs[9:19]
    (n1, lat1, q, k, v, lse, att, lat2, middle, n2, lat3) = refs[19:30]
    w, sems, hidden, branch = refs[30:]
    weights = Weights(sc, pieces, w, sems, lead)
    weights.start()
    a = sc[0]
    hid = D // cols
    x = tokens_of(xa, cols)
    hidden[...] = x
    unit, _ = norm_parts(x)
    n1[...] = low(unit * gain[0:1] + shift[0:1])
    lat1[...] = low(mm(n1[...], q_down[a], NT))
    weights.wait()

    def project(slot, _):
        block = column_of(sc, slot)
        up = jnp.concatenate([q_up[a, :, c, lanes(block * hid, hid)] for c in range(3)], axis=1)
        made = mm(n1[...], w[slot, :, : 3 * hid]) + mm(lat1[...], up)
        bias_q = xa[block, SEQ : SEQ + 1, :].astype(F32)
        bias_v = xa[block, SEQ + 1 : SEQ + 2, :].astype(F32)
        at = lanes(slot * hid, hid)
        q[:, at] = low(made[:, :hid] + bias_q) * jnp.asarray(0.125, BF)
        k[:, at] = low(made[:, hid : 2 * hid])
        v[:, at] = low(made[:, 2 * hid :] + bias_v)
        return 0

    lax.fori_loop(0, cols, project, 0)
    shut = closed[...] > 0.5
    left = lax.broadcasted_iota(jnp.int32, (1, PAIR), 1) < HD

    def attend(pair, _):
        at = lanes(pair * PAIR, PAIR)
        qp, kp, vp = q[:, at], k[:, at], v[:, at]
        v_t = low(vp.astype(F32).T)
        halves = []
        for h in range(2):
            masked = jnp.where(left == (h == 0), qp, jnp.zeros_like(qp))
            s = jnp.where(shut, -1e30, mm(kp, masked, NT))
            top = jnp.max(s, axis=0, keepdims=True)
            e = jnp.exp(s - top)
            total = jnp.sum(e, axis=0, keepdims=True)
            lse[pair, h : h + 1, :] = top + jnp.log(total)
            soft = low(e * (1.0 / total))
            halves.append(mm(v_t[h * HD : (h + 1) * HD], soft))
        att[:, at] = low(jnp.concatenate(halves, axis=0).T)
        return 0

    lax.fori_loop(0, H // 2, attend, 0)

    def down_two(slot, acc):
        block = column_of(sc, slot)
        return acc + mm(att[:, lanes(slot * hid, hid)], p_down[a, :, lanes(block * hid, hid)], NT)

    lat2[...] = low(lax.fori_loop(0, cols, down_two, jnp.zeros((SEQ, R), F32)))
    branch[...] = mm(lat2[...], p_up[a]) + bias_out[0:1].astype(F32)

    def out_proj(slot, _):
        branch[...] += mm(att[:, lanes(slot * hid, hid)], w[slot, :, 3 * hid :], NT)
        return 0

    lax.fori_loop(0, cols, out_proj, 0)
    mid = hidden[...] + branch[...]
    middle[...] = mid
    unit, _ = norm_parts(mid)
    n2[...] = low(unit * gain[1:2] + shift[1:2])
    lat3[...] = low(mm(n2[...], f_down[a], NT))


def ffn_steps(sc, part, cols, w, xa, n2, lat3, gr, glat4, up_1, down_2, acc, early):
    res, gn2, lat4, glat3 = acc
    a = sc[0]
    hid = D // cols
    ffn = FF // cols
    half = ffn // 2
    glat4_t = low(glat4.astype(F32).T)
    lat3_t = low(lat3[...].astype(F32).T)

    def step(slot, _):
        block = column_of(sc, slot)
        at = pl.ds(pl.multiple_of(block * ffn + part * half, half), half)
        bias = jnp.concatenate(
            [xa[block, SEQ + 2 + 2 * part + i : SEQ + 3 + 2 * part + i, :] for i in range(2)], axis=1
        ).astype(F32)
        up, down = up_1[a, :, at], down_2[a, :, at]
        w1, w2 = w[slot, :, :half], w[slot, :, half:]
        pre = mm(n2[...], w1) + mm(lat3[...], up) + bias
        back = mm(gr[...], w2) + mm(glat4, down)
        cumulative = 0.5 * (1.0 + lax.erf(pre * 0.7071067811865476))
        activated = low(pre * cumulative)
        slope = cumulative + pre * jnp.exp(-0.5 * pre * pre) * 0.3989422804014327
        grad_pre = low(back * slope)
        lat4[...] += mm(activated, down, NT)
        glat3[...] += mm(grad_pre, up, NT)
        res[...] += mm(activated, w2, NT)
        gn2[...] += mm(grad_pre, w1, NT)
        early[:, lanes(block * half, half)] = low(mm(lat3_t, grad_pre))
        early[:, lanes(FF // 2 + block * half, half)] = low(mm(glat4_t, activated))
        return 0

    lax.fori_loop(0, cols, step, 0)


def ffn_a_kernel(lead, cols, *refs):
    sc = refs[0]
    pieces = refs[1:9]
    xa, ga, keep, n2, lat3, up_1, down_2, up_2 = refs[9:17]
    res, gn2, lat4, glat3, gr, early = refs[17:23]
    w, sems = refs[23:]
    weights = Weights(sc, pieces, w, sems, lead)
    weights.start()
    gr[...] = low(
        jnp.concatenate([ga[c] for c in range(cols)], axis=1).astype(F32) * keep[...]
    )
    glat4 = low(mm(gr[...], up_2[sc[0]], NT))
    res[...] = jnp.zeros_like(res)
    gn2[...] = jnp.zeros_like(gn2)
    lat4[...] = jnp.zeros_like(lat4)
    glat3[...] = jnp.zeros_like(glat3)
    weights.wait()
    ffn_steps(
        sc, 0, cols, w, xa, n2, lat3, gr, glat4, up_1, down_2, (res, gn2, lat4, glat3), early
    )


def ffn_b_kernel(lead, cols, *refs):
    sc = refs[0]
    pieces = refs[1:9]
    own_q = refs[9:17]
    (xa, keep, gain, n2, lat3, up_1, down_2, up_2, f_down, p_down, p_up, bias_out) = refs[17:29]
    (middle, att, lat2, gr, res_in, gn2_in, lat4_in, glat3_in) = refs[29:37]
    layer, gatt, gmid, early = refs[37:41]
    w, sems, wp, sems_p, res, gn2, lat4, glat3 = refs[41:]
    weights = Weights(sc, pieces, w, sems, lead)
    weights.start()
    proj = Weights(sc, own_q, wp, sems_p, lead, 3 * D // cols)
    proj.start()
    a = sc[0]
    hid = D // cols
    glat4 = low(mm(gr[...], up_2[a], NT))
    res[...] = res_in[...]
    gn2[...] = gn2_in[...]
    lat4[...] = lat4_in[...]
    glat3[...] = glat3_in[...]
    weights.wait()
    ffn_steps(
        sc, 1, cols, w, xa, n2, lat3, gr, glat4, up_1, down_2, (res, gn2, lat4, glat3), early
    )
    mid = middle[...]
    lat4_low = low(lat4[...])
    out = low(
        keep[...] * (mid + res[...] + mm(lat4_low, up_2[a]) + bias_out[1:2].astype(F32))
    )
    for c in range(cols):
        layer[c] = out[:, c * hid : (c + 1) * hid]
    glat3_low = low(glat3[...])
    grad_normed = gn2[...] + mm(glat3_low, f_down[a])
    unit, inverse = norm_parts(mid)
    grad_middle = gr[...].astype(F32) + norm_back(grad_normed, gain[1:2], unit, inverse)
    gmid[...] = grad_middle
    gb = low(grad_middle)
    glat2 = low(mm(gb, p_up[a], NT))
    glat2_t = low(glat2.astype(F32).T)
    early[:, FF + D : FF + 2 * D] = low(mm(low(lat2[...].astype(F32).T), gb))
    early[:, FF + 2 * D : FF + 3 * D] = low(mm(low(glat3_low.astype(F32).T), n2[...]))
    early[:, FF + 3 * D :] = low(mm(low(lat4_low.astype(F32).T), gr[...]))
    proj.wait()

    def step(slot, _):
        block = column_of(sc, slot)
        here = lanes(slot * hid, hid)
        there = lanes(block * hid, hid)
        gatt[:, here] = low(mm(gb, wp[slot]) + mm(glat2, p_down[a, :, there]))
        early[:, lanes(FF + block * hid, hid)] = low(mm(glat2_t, att[:, here]))
        return 0

    lax.fori_loop(0, cols, step, 0)


def attention_back_kernel(cols, *refs):
    sc = refs[0]
    closed, q, k, v, lse, gatt, lat1, n1, q_up = refs[1:10]
    gq, gk, gv, glat1, late = refs[10:15]
    a = sc[0]
    hid = D // cols
    shut = closed[...] > 0.5
    left = lax.broadcasted_iota(jnp.int32, (1, PAIR), 1) < HD

    def attend(pair, _):
        at = lanes(pair * PAIR, PAIR)
        qp, kp, vp, gp = q[:, at], k[:, at], v[:, at], gatt[:, at]
        k_t = low(kp.astype(F32).T)
        by_q, by_k, by_v = [], [], []
        for h in range(2):
            mine = left == (h == 0)
            zero = jnp.zeros_like(qp)
            s = jnp.where(shut, -1e30, mm(kp, jnp.where(mine, qp, zero), NT))
            soft = jnp.exp(s - lse[pair, h : h + 1, :])
            grad_soft = mm(vp, jnp.where(mine, gp, zero), NT)
            total = jnp.sum(grad_soft * soft, axis=0, keepdims=True)
            grad_scores = low(soft * (grad_soft - total))
            by_v.append(mm(low(soft), gp))
            by_k.append(mm(grad_scores, qp))
            by_q.append(mm(k_t[h * HD : (h + 1) * HD], grad_scores))
        gq[:, at] = low(jnp.concatenate(by_q, axis=0).T * 0.125)
        gk[:, at] = low(jnp.where(left, by_k[0], by_k[1]))
        gv[:, at] = low(jnp.where(left, by_v[0], by_v[1]))
        return 0

    lax.fori_loop(0, H // 2, attend, 0)
    lat1_t = low(lat1[...].astype(F32).T)

    def step(slot, acc):
        block = column_of(sc, slot)
        here = lanes(slot * hid, hid)
        there = lanes(block * hid, hid)
        for c, g in enumerate((gq, gk, gv)):
            grad = g[:, here]
            acc = acc + mm(grad, q_up[a, :, c, there], NT)
            late[:, pl.ds(pl.multiple_of((c + 1) * D + block * hid, hid), hid)] = low(
                mm(lat1_t, grad)
            )
        return acc

    made = low(lax.fori_loop(0, cols, step, jnp.zeros((SEQ, R), F32)))
    glat1[...] = made
    late[:, :D] = low(mm(low(made.astype(F32).T), n1[...]))


def back_kernel(lead, cols, *refs):
    sc = refs[0]
    pieces = refs[1:9]
    xa, gain, gq, gk, gv, glat1, q_down, gmid, layer = refs[9:18]
    out = refs[18]
    w, sems, acc = refs[19:]
    weights = Weights(sc, pieces, w, sems, lead)
    weights.start()
    hid = D // cols
    acc[...] = mm(glat1[...], q_down[sc[0]])
    x = tokens_of(xa, cols)
    unit, inverse = norm_parts(x)
    weights.wait()

    def step(slot, _):
        here = lanes(slot * hid, hid)
        grad = jnp.concatenate([gq[:, here], gk[:, here], gv[:, here]], axis=1)
        acc[...] += mm(grad, w[slot, :, : 3 * hid], NT)
        return 0

    lax.fori_loop(0, cols, step, 0)
    made = low(gmid[...] + norm_back(acc[...], gain[0:1], unit, inverse))
    for c in range(cols):
        out[c, :SEQ] = layer[c]
        out[c, SEQ:] = made[:, c * hid : (c + 1) * hid]


def sum_kernel(owners, *refs):
    mines, out, acc = refs[:-2], refs[-2], refs[-1]
    acc[...] = jnp.zeros_like(acc)
    lane = 0
    for mine in mines:
        part = mine.shape[-1]
        for d in range(mine.shape[0]):
            acc[owners[d], :, lane : lane + part] += mine[d].astype(F32)
        lane += part
    out[...] = low(acc[...])


def spread_kernel(maps, parts, table, whole, *outs):
    base = 0
    for part, spans in zip(parts, maps):
        for out, put, start, width in spans:
            for lane in range(0, width, 128):
                at = start + lane
                here = base + at % part
                block = whole[table.index(at // part), :, here : here + 128]
                outs[out][:, put + lane : put + lane + 128] = block.astype(F32)
        base += part


def send_grads(grads):
    rows, cols = sizes()
    devices = rows * cols
    part = grads.shape[-1] // devices
    pieces = grads.reshape(R, devices, part).transpose(1, 0, 2)
    return lax.all_to_all(pieces, BOTH, split_axis=0, concat_axis=0, tiled=True)


def sum_grads(mines, owners):
    part = sum(m.shape[-1] for m in mines)
    summed = call(
        sum_kernel,
        jax.ShapeDtypeStruct((NA, R, part), BF),
        [owners, *mines],
        [pltpu.SMEM] + [VMEM] * len(mines),
        [VMEM((NA, R, part), F32)],
    )
    return summed.reshape(NA * R, part)


def spread(whole, parts, maps, widths):
    rows, cols = sizes()
    devices = rows * cols
    table = all_table(rows, cols)
    if all(p % 128 == 0 for p in parts):
        return call(
            functools.partial(spread_kernel, maps, parts, table),
            [jax.ShapeDtypeStruct((NA * R, n), F32) for n in widths],
            [whole],
            [VMEM],
        )
    whole = whole[jnp.array([table.index(d) for d in range(devices)])].astype(F32)
    found = [[] for _ in widths]
    base = 0
    for part, spans in zip(parts, maps):
        flat = jnp.swapaxes(whole[:, :, base : base + part], 0, 1).reshape(NA * R, devices * part)
        for out, put, start, width in spans:
            found[out].append((put, flat[:, start : start + width]))
        base += part
    return [jnp.concatenate([x for _, x in sorted(f, key=lambda e: e[0])], axis=1) for f in found]


def per_device(
    tokens_in,
    grad_out,
    keep_mask,
    adapter_index,
    ln_gain,
    ln_shift,
    w_qkv,
    bias_qv,
    w_proj,
    w_fc1,
    bias_fc1,
    w_fc2,
    bias_out,
    qkv_down,
    qkv_up,
    proj_down,
    proj_up,
    fc1_down,
    fc1_up,
    fc2_down,
    fc2_up,
):
    rows, cols = sizes()
    row, column = lax.axis_index("row"), lax.axis_index("col")
    assert adapter_index.shape[0] == cols and cols >= 4 and rows >= 2
    hid = D // cols
    n = 4 * hid
    blk = D // rows
    lead = lead_table(rows, cols)

    biases = jnp.concatenate(
        [bias_qv, bias_fc1.reshape(4, hid), jnp.zeros((EXTRA - 6, hid), BF)], axis=0
    )
    tokens = jnp.concatenate(
        [tokens_in.reshape(cols, SEQ, hid), jnp.broadcast_to(biases, (cols, EXTRA, hid))], axis=1
    )
    xa = lax.all_to_all(tokens, "col", split_axis=0, concat_axis=0, tiled=True)
    ga = lax.all_to_all(
        grad_out.reshape(cols, SEQ, hid), "col", split_axis=0, concat_axis=0, tiled=True
    )
    shard = jax.ShapeDtypeStruct((blk, n), BF)
    shard_q = call(prep_q_kernel, shard, [w_qkv, w_proj], [VMEM] * 2)
    shard_a, shard_b = call(prep_f_kernel, [shard] * 2, [w_fc1, w_fc2], [VMEM] * 2)
    owners = gather_owners(adapter_index)
    with jax.named_scope("q_high"):
        own_q = gather_high(shard_q)
    with jax.named_scope("fa_high"):
        own_a = gather_high(after(shard_a, own_q))
    with jax.named_scope("fb_high"):
        own_b = gather_high(after(shard_b, own_a))
    own_q = after(own_q, xa, owners)
    with jax.named_scope("q_one"):
        one_q = swap(own_q, flip_one)
    with jax.named_scope("q_two"):
        two_q = swap(own_q, flip_two)
    own_a = after(own_a, one_q, two_q, ga)
    with jax.named_scope("q_both"):
        both_q = swap(one_q, flip_two)
    with jax.named_scope("q_core"):
        pieces_q = [own_q, one_q, two_q, both_q]
        pieces_q = pieces_q + [swap(p, flip_core) for p in pieces_q]
    with jax.named_scope("fa_one"):
        one_a = swap(own_a, flip_one)
    with jax.named_scope("fa_two"):
        two_a = swap(own_a, flip_two)

    mask_row = lax.dynamic_index_in_dim(keep_mask, column, 0, keepdims=False)
    keep = jnp.concatenate([jnp.ones((BUF,), F32), mask_row.astype(F32)]).reshape(SEQ, 1)
    closed = 1.0 - keep
    adapter = lax.dynamic_index_in_dim(adapter_index, column, 0, keepdims=False)
    sc = jnp.stack([adapter, column, column % 2, row % 2]).astype(jnp.int32)

    def shaped(width, dtype, height=SEQ):
        return jax.ShapeDtypeStruct((height, width), dtype)

    big, small = shaped(D, BF), shaped(R, BF)
    scratch = weight_scratch(rows, cols, n)
    any_space = [pl.ANY] * 8
    n1, lat1, q, k, v, lse, att, lat2, middle, n2, lat3 = call(
        functools.partial(front_kernel, lead, cols),
        [
            big,
            small,
            big,
            big,
            big,
            jax.ShapeDtypeStruct((H // 2, 2, SEQ), F32),
            big,
            small,
            shaped(D, F32),
            big,
            small,
        ],
        [sc, *pieces_q, xa, closed, ln_gain, ln_shift, qkv_down, qkv_up, proj_down, proj_up]
        + [fc1_down, bias_out],
        [pltpu.SMEM] + any_space + [VMEM] * 10,
        scratch + [VMEM((SEQ, D), F32), VMEM((SEQ, D), F32)],
    )
    with jax.named_scope("fa_both"):
        both_a = swap(after(one_a, n1), flip_two)
    with jax.named_scope("fa_core"):
        pieces_a = [own_a, one_a, two_a, both_a]
        pieces_a = pieces_a + [swap(p, flip_core) for p in pieces_a]
    own_b = after(own_b, n1, one_a, two_a)
    with jax.named_scope("fb_one"):
        one_b = swap(own_b, flip_one)
    with jax.named_scope("fb_two"):
        two_b = swap(own_b, flip_two)
    wide = shaped(D, F32)
    thin = shaped(R, F32)
    res, gn2, lat4, glat3, gr, early_a = call(
        functools.partial(ffn_a_kernel, lead, cols),
        [wide, wide, thin, thin, big, shaped(FF, BF, R)],
        [sc, *pieces_a, xa, ga, keep, n2, lat3, fc1_up, fc2_down, fc2_up],
        [pltpu.SMEM] + any_space + [VMEM] * 8,
        scratch,
    )
    with jax.named_scope("fb_both"):
        both_b = swap(after(one_b, res), flip_two)
    with jax.named_scope("grads_a_send"):
        mine_a = send_grads(early_a)
    with jax.named_scope("fb_core"):
        pieces_b = [own_b, one_b, two_b, after(both_b, mine_a)]
        pieces_b = pieces_b + [swap(p, flip_core) for p in pieces_b]
    layer, gatt, gmid, early_b = call(
        functools.partial(ffn_b_kernel, lead, cols),
        [jax.ShapeDtypeStruct((cols, SEQ, hid), BF), big, wide, shaped(FF + 4 * D, BF, R)],
        [sc, *pieces_b, *pieces_q, xa, keep, ln_gain, n2, lat3, fc1_up, fc2_down, fc2_up]
        + [fc1_down, proj_down, proj_up, bias_out]
        + [middle, att, lat2, gr, res, gn2, lat4, glat3],
        [pltpu.SMEM] + any_space * 2 + [VMEM] * 20,
        scratch
        + [VMEM((cols, D, hid), BF), scratch[1]]
        + [VMEM((SEQ, D), F32), VMEM((SEQ, D), F32), VMEM((SEQ, R), F32), VMEM((SEQ, R), F32)],
    )
    with jax.named_scope("grads_b_send"):
        mine_b = send_grads(early_b)
    gq, gk, gv, glat1, late = call(
        functools.partial(attention_back_kernel, cols),
        [big, big, big, small, shaped(4 * D, BF, R)],
        [sc, closed, q, k, v, lse, gatt, lat1, n1, qkv_up],
        [pltpu.SMEM] + [VMEM] * 9,
    )
    with jax.named_scope("grads_c_send"):
        mine_c = send_grads(late)
    with jax.named_scope("grads_b"):
        part_b = sum_grads([mine_a, after(mine_b, late)], owners)
    gmid = after(gmid, part_b)
    sent = call(
        functools.partial(back_kernel, lead, cols),
        jax.ShapeDtypeStruct((cols, 2 * SEQ, hid), BF),
        [sc, *pieces_q, xa, ln_gain, gq, gk, gv, glat1, qkv_down, gmid, layer],
        [pltpu.SMEM] + any_space + [VMEM] * 9,
        scratch + [VMEM((SEQ, D), F32)],
    )
    with jax.named_scope("rows_out"):
        rows_out = lax.all_to_all(sent, "col", split_axis=0, concat_axis=0, tiled=True)
    layer, grad_in = rows_out[:, :SEQ], rows_out[:, SEQ:]
    with jax.named_scope("grads_b"):
        whole_b = gather_leading(part_b, {1: [sent, mine_c]})
    with jax.named_scope("grads_c"):
        whole_c = gather_leading(sum_grads([mine_c], owners), {})
    half = FF // cols // 2
    map_a, map_b = (
        tuple(
            (out, (2 * block + part) * half, base + block * half, half)
            for out, base in ((0, 0), (1, FF // 2))
            for block in range(cols)
        )
        for part in (0, 1)
    )
    map_b = map_b + tuple((2 + i, 0, FF + i * D, D) for i in range(4))
    parts = [mine_a.shape[-1], mine_b.shape[-1]]
    early_sum = spread(whole_b, parts, [map_a, map_b], [FF, FF, D, D, D, D])
    map_c = tuple((i, 0, i * D, D) for i in range(4))
    late_sum = spread(whole_c, [mine_c.shape[-1]], [map_c], [D] * 4)

    def split(table, last=()):
        return table.reshape((NA, R) + last + (-1,))

    g_qkv_up = jnp.stack([split(t) for t in late_sum[1:]], axis=2)
    g_fc1_up, g_fc2_down, g_proj_down, g_proj_up, g_fc1_down, g_fc2_up = map(split, early_sum)
    return (
        layer.reshape(cols * SEQ, hid),
        grad_in.reshape(cols * SEQ, hid),
        split(late_sum[0]),
        g_qkv_up,
        g_proj_down,
        g_proj_up,
        g_fc1_down,
        g_fc1_up,
        g_fc2_down,
        g_fc2_up,
    )


def solution(mesh):
    return jax.shard_map(
        per_device,
        mesh=mesh,
        in_specs=(
            P("row", "col"),
            P("row", "col"),
            P("row", None),
            P("row"),
            P(),
            P(),
            P(None, "row", "col"),
            P(None, "col"),
            P("col", "row"),
            P("row", "col"),
            P("col"),
            P("col", "row"),
            P(),
            P(),
            P(),
            P(),
            P(),
            P(),
            P(),
            P(),
            P(),
        ),
        out_specs=(P("row", "col"), P("row", "col"), P(), P(), P(), P(), P(), P(), P(), P()),
        check_vma=False,
    )
```

```python
import functools

import jax
import jax.numpy as jnp
from jax import lax
from jax.experimental import pallas as pl
from jax.experimental.pallas import tpu as pltpu
from jax.sharding import PartitionSpec as P

D = 1024
H = 16
HD = 64
FF = 4096
BUF = 64
R = 16
NA = 8
SEQ = 320
PAIR = 2 * HD
EXTRA = 16
FRONT, FFN_A, FFN_B, ATT, BACK = 56, 56, 56, 56, 56
BF = jnp.bfloat16
F32 = jnp.float32
BOTH = ("row", "col")
VMEM = pltpu.VMEM
NN = (((1,), (0,)), ((), ()))
NT = (((1,), (1,)), ((), ()))


def mm(left, right, dims=NN):
    return lax.dot_general(left, right, dims, preferred_element_type=F32)


def low(values):
    return values.astype(BF)


def norm_parts(values):
    row_mean = jnp.mean(values, axis=-1, keepdims=True)
    centered = values - row_mean
    variance = jnp.mean(centered * centered, axis=-1, keepdims=True)
    inverse = lax.rsqrt(variance + 1e-06)
    return (centered * inverse, inverse)


def norm_back(grad_normed, gain_row, unit_rows, inverse):
    scaled = grad_normed * gain_row
    first_mean = jnp.mean(scaled, axis=-1, keepdims=True)
    second_mean = jnp.mean(scaled * unit_rows, axis=-1, keepdims=True)
    return inverse * (scaled - first_mean - unit_rows * second_mean)


def call(kernel, outs, ins, spaces, scratch=(), out_space=VMEM, mib=4):
    return pl.pallas_call(
        kernel,
        out_shape=outs,
        in_specs=[pl.BlockSpec(memory_space=s) for s in spaces],
        out_specs=jax.tree.map(lambda _: pl.BlockSpec(memory_space=out_space), outs),
        scratch_shapes=list(scratch),
        compiler_params=pltpu.CompilerParams(vmem_limit_bytes=mib << 20),
        cost_estimate=pl.CostEstimate(flops=0, bytes_accessed=0, transcendentals=0),
    )(*ins)


def sizes():
    return lax.axis_size("row"), lax.axis_size("col")


def swap(block, flip):
    rows, cols = sizes()
    pairs = []
    for i in range(rows * cols):
        row, col = flip(i // cols, i % cols)
        pairs.append((i, row * cols + col))
    return lax.ppermute(block, BOTH, pairs)


def bits_of(size):
    return size.bit_length() - 1


def stack_kernel(which, *refs):
    parts, out, sems = refs[:-2], refs[-2], refs[-1]
    copies = [
        pltpu.make_async_copy(ref, out.at[which[0] ^ m], sems.at[m]) for m, ref in enumerate(parts)
    ]
    for copy in copies:
        copy.start()
    for copy in copies:
        copy.wait()


def stacked(parts, index):
    shape = parts[0].shape
    flat = [p.reshape((-1, shape[-1])) for p in parts]
    out = jax.ShapeDtypeStruct((len(parts),) + flat[0].shape, flat[0].dtype)
    made = call(
        stack_kernel,
        out,
        [index.reshape(1).astype(jnp.int32)] + flat,
        [pltpu.SMEM] + [pl.ANY] * len(parts),
        [pltpu.SemaphoreType.DMA((len(parts),))],
    )
    return made.reshape((len(parts),) + shape)


def group_join(block, axis, low_bit, width):
    parts = [block]
    for m in range(1, 1 << width):
        step = m << low_bit
        if axis == "row":
            parts.append(swap(block, lambda r, c: (r ^ step, c)))
        else:
            parts.append(swap(block, lambda r, c: (r, c ^ step)))
    index = (lax.axis_index(axis) >> low_bit) & ((1 << width) - 1)
    return stacked(parts, index), parts


def groups(top, bottom):
    out = []
    while top > bottom:
        width = min(2, top - bottom)
        out.append((top - width, width))
        top -= width
    return out


def early_groups(rows, cols):
    return [("row",) + g for g in groups(bits_of(rows), 1)] + [
        ("col",) + g for g in groups(bits_of(cols), 2)
    ]


def lead_table(rows, cols):
    table = [(0, 0)]
    for axis, bit, width in early_groups(rows, cols):
        shift = bit - (1 if axis == "row" else 2)
        new = []
        for value in range(1 << width):
            for high_col, high_row in table:
                if axis == "row":
                    new.append((high_col, high_row + (value << shift)))
                else:
                    new.append((high_col + (value << shift), high_row))
        table = new
    return table


def after(value, *others):
    return lax.optimization_barrier((value,) + others)[0]


def after_all(values, *others):
    return lax.optimization_barrier(tuple(values) + others)[: len(values)]


def gather_high(shard):
    rows, cols = sizes()
    block, parts = shard, []
    for axis, bit, width in early_groups(rows, cols):
        block, parts = group_join(block, axis, bit, width)
    return block.reshape((-1,) + shard.shape), parts[1:]


def lane_join_kernel(*refs):
    parts, out, sems = refs[:-2], refs[-2], refs[-1]
    copies, lane = [], 0
    for i, part in enumerate(parts):
        width = part.shape[-1]
        copies.append(pltpu.make_async_copy(part, out.at[:, :, lane : lane + width], sems.at[i]))
        lane += width
    for copy in copies:
        copy.start()
    for copy in copies:
        copy.wait()


def lane_join(*parts):
    if any(p.shape[-1] % 128 for p in parts):
        return jnp.concatenate(parts, axis=-1)
    shape = parts[0].shape[:-1] + (sum(p.shape[-1] for p in parts),)
    return call(
        lane_join_kernel,
        jax.ShapeDtypeStruct(shape, parts[0].dtype),
        parts,
        [pl.ANY] * len(parts),
        [pltpu.SemaphoreType.DMA((len(parts),))],
    )


def flip_one(r, c):
    return (r, c ^ 2) if c % 2 == 0 else (r ^ 1, c)


def flip_two(r, c):
    return (r ^ 1, c) if c % 2 == 0 else (r, c ^ 2)


def flip_core(r, c):
    return (r, c ^ 1)


def with_cores(pieces):
    return pieces + [swap(p, flip_core) for p in pieces]


def piece_place(sc, k):
    kind, away = k % 4, k // 4
    turn = (sc[2] + away) & 1
    return (0, 1 - turn, turn, 1)[kind], (0, turn, 1 - turn, 1)[kind], away


class Weights:
    def __init__(self, sc, pieces, w, sems, lead, first_lane=0):
        self.copies = []
        depth = pieces[0].shape[1]
        taken = pl.ds(first_lane, w.shape[2])
        for k, piece in enumerate(pieces):
            x_rel, y_rel, away = piece_place(sc, k)
            for n, (high_col, high_row) in enumerate(lead):
                slot = high_col * 4 + x_rel * 2 + away
                row = (high_row * 2 + ((sc[3] + y_rel) & 1)) * depth
                self.copies.append(
                    pltpu.make_async_copy(
                        piece.at[n, :, taken],
                        w.at[slot, pl.ds(pl.multiple_of(row, depth), depth), :],
                        sems.at[k, n],
                    )
                )

    def start(self):
        for copy in self.copies:
            copy.start()

    def wait(self):
        for copy in self.copies:
            copy.wait()


def column_of(sc, slot):
    return (slot // 4) * 4 + ((sc[1] & 3) ^ (slot & 3))


def weight_scratch(rows, cols, n):
    lead = len(lead_table(rows, cols))
    return [VMEM((cols, D, n), BF), pltpu.SemaphoreType.DMA((8, lead))]


def put(ref, start, value, lane=0):
    part = ref.shape[-1] - lane
    for i in range(value.shape[-1] // part):
        ref[start // part + i, :R, lane:] = value[:, i * part : (i + 1) * part]


def lanes(start, width):
    return pl.ds(pl.multiple_of(start, width), width)


def prep_q_kernel(wq, wp, out):
    hid = wq.shape[2]
    for c in range(3):
        out[:, c * hid : (c + 1) * hid] = wq[c]
    out[:, 3 * hid :] = low(wp[...].astype(F32).T)


def prep_rows_kernel(tokens, grads, bias_qv, bias_f, out):
    cols, seq = out.shape[0], tokens.shape[1]
    for c in range(cols):
        out[c, :seq] = tokens[c]
        out[c, seq : 2 * seq] = grads[c]
        out[c, 2 * seq : 2 * seq + 2] = bias_qv[...]
        out[c, 2 * seq + 2 : 2 * seq + 6] = bias_f[...]


def prep_f_kernel(sc, mask, w1, w2, out_a, out_b, keep, closed):
    row = mask[pl.ds(sc[1], 1), :].astype(F32)
    row = jnp.concatenate([jnp.ones((1, BUF), F32), row], axis=1)
    column = jnp.broadcast_to(row, (8, SEQ)).T[:, :1]
    keep[...] = column
    closed[...] = 1.0 - column
    half = w1.shape[1] // 2
    out_a[:, :half] = w1[:, :half]
    out_b[:, :half] = w1[:, half:]
    out_a[:, half:] = low(w2[:half].astype(F32).T)
    out_b[:, half:] = low(w2[half:].astype(F32).T)


def tokens_of(ref, cols):
    return jnp.concatenate([ref[c, :SEQ, :] for c in range(cols)], axis=1).astype(F32)


def front_kernel(lead, cols, *refs):
    sc = refs[0]
    pieces = refs[1:9]
    (xa, closed, gain, shift, q_down, q_up, p_down, p_up, f_down, bias_out) = refs[9:19]
    (n1, lat1, q, k, v, lse, att, lat2, middle, n2, lat3) = refs[19:30]
    w, sems, hidden, branch = refs[30:]
    weights = Weights(sc, pieces, w, sems, lead)
    weights.start()
    a = sc[0]
    hid = D // cols
    x = tokens_of(xa, cols)
    hidden[...] = x
    unit, _ = norm_parts(x)
    n1[...] = low(unit * gain[0:1] + shift[0:1])
    lat1[...] = low(mm(n1[...], q_down[a], NT))
    weights.wait()

    def project(slot, _):
        block = column_of(sc, slot)
        up = jnp.concatenate([q_up[c, :, lanes(block * hid, hid)] for c in range(3)], axis=1)
        made = mm(n1[...], w[slot, :, : 3 * hid]) + mm(lat1[...], up)
        bias_q = xa[block, 2 * SEQ : 2 * SEQ + 1, :].astype(F32)
        bias_v = xa[block, 2 * SEQ + 1 : 2 * SEQ + 2, :].astype(F32)
        at = lanes(slot * hid, hid)
        q[:, at] = low(made[:, :hid] + bias_q) * jnp.asarray(0.125, BF)
        k[:, at] = low(made[:, hid : 2 * hid])
        v[:, at] = low(made[:, 2 * hid :] + bias_v)
        return 0

    lax.fori_loop(0, cols, project, 0)
    shut = closed[...] > 0.5
    left = lax.broadcasted_iota(jnp.int32, (1, PAIR), 1) < HD

    def attend(pair, _):
        at = lanes(pair * PAIR, PAIR)
        qp, kp, vp = q[:, at], k[:, at], v[:, at]
        v_t = low(vp.astype(F32).T)
        halves = []
        for h in range(2):
            masked = jnp.where(left == (h == 0), qp, jnp.zeros_like(qp))
            s = jnp.where(shut, -1e30, mm(kp, masked, NT))
            top = jnp.max(s, axis=0, keepdims=True)
            e = jnp.exp(s - top)
            total = jnp.sum(e, axis=0, keepdims=True)
            lse[pair, h : h + 1, :] = top + jnp.log(total)
            soft = low(e * (1.0 / total))
            halves.append(mm(v_t[h * HD : (h + 1) * HD], soft))
        att[:, at] = low(jnp.concatenate(halves, axis=0).T)
        return 0

    lax.fori_loop(0, H // 2, attend, 0)

    def down_two(slot, acc):
        block = column_of(sc, slot)
        return acc + mm(att[:, lanes(slot * hid, hid)], p_down[a, :, lanes(block * hid, hid)], NT)

    lat2[...] = low(lax.fori_loop(0, cols, down_two, jnp.zeros((SEQ, R), F32)))
    branch[...] = mm(lat2[...], p_up[a]) + bias_out[0:1].astype(F32)

    def out_proj(slot, _):
        branch[...] += mm(att[:, lanes(slot * hid, hid)], w[slot, :, 3 * hid :], NT)
        return 0

    lax.fori_loop(0, cols, out_proj, 0)
    mid = hidden[...] + branch[...]
    middle[...] = mid
    unit, _ = norm_parts(mid)
    n2[...] = low(unit * gain[1:2] + shift[1:2])
    lat3[...] = low(mm(n2[...], f_down[a], NT))


def ffn_steps(sc, part, cols, w, xa, n2, lat3, gr, glat4, up_1, down_2, acc, early, lane=0):
    res, gn2, lat4, glat3 = acc
    a = sc[0]
    hid = D // cols
    ffn = FF // cols
    half = ffn // 2
    glat4_t = low(glat4.astype(F32).T)
    lat3_t = low(lat3[...].astype(F32).T)

    def step(slot, _):
        block = column_of(sc, slot)
        at = pl.ds(pl.multiple_of(block * ffn + part * half, half), half)
        bias = jnp.concatenate(
            [xa[block, 2 * SEQ + 2 + 2 * part + i : 2 * SEQ + 3 + 2 * part + i, :] for i in range(2)],
            axis=1,
        ).astype(F32)
        up, down = up_1[a, :, at], down_2[a, :, at]
        w1, w2 = w[slot, :, :half], w[slot, :, half:]
        pre = mm(n2[...], w1) + mm(lat3[...], up) + bias
        back = mm(gr[...], w2) + mm(glat4, down)
        cumulative = 0.5 * (1.0 + lax.erf(pre * 0.7071067811865476))
        activated = low(pre * cumulative)
        slope = cumulative + pre * jnp.exp(-0.5 * pre * pre) * 0.3989422804014327
        grad_pre = low(back * slope)
        lat4[...] += mm(activated, down, NT)
        glat3[...] += mm(grad_pre, up, NT)
        res[...] += mm(activated, w2, NT)
        gn2[...] += mm(grad_pre, w1, NT)
        put(early, block * half, low(mm(lat3_t, grad_pre)), lane)
        put(early, FF // 2 + block * half, low(mm(glat4_t, activated)), lane)
        return 0

    lax.fori_loop(0, cols, step, 0)


def ffn_a_kernel(lead, cols, *refs):
    sc = refs[0]
    pieces = refs[1:9]
    xa, keep, n2, lat3, up_1, down_2, up_2 = refs[9:16]
    res, gn2, lat4, glat3, gr, early = refs[16:22]
    w, sems = refs[22:]
    weights = Weights(sc, pieces, w, sems, lead)
    weights.start()
    gr[...] = low(
        jnp.concatenate([xa[c, SEQ : 2 * SEQ] for c in range(cols)], axis=1).astype(F32) * keep[...]
    )
    glat4 = low(mm(gr[...], up_2[sc[0]], NT))
    res[...] = jnp.zeros_like(res)
    gn2[...] = jnp.zeros_like(gn2)
    lat4[...] = jnp.zeros_like(lat4)
    glat3[...] = jnp.zeros_like(glat3)
    weights.wait()
    ffn_steps(
        sc, 0, cols, w, xa, n2, lat3, gr, glat4, up_1, down_2, (res, gn2, lat4, glat3), early
    )


def ffn_b_kernel(lead, cols, *refs):
    sc = refs[0]
    pieces = refs[1:9]
    own_q = refs[9:17]
    (xa, keep, gain, n2, lat3, up_1, down_2, up_2, f_down, p_down, p_up, bias_out) = refs[17:29]
    (middle, att, lat2, gr, res_in, gn2_in, lat4_in, glat3_in, early_in) = refs[29:38]
    layer, gatt, gmid, early = refs[38:42]
    w, sems, wp, sems_p, res, gn2, lat4, glat3 = refs[42:]
    lane = early_in.shape[-1]
    early[:, :R, :lane] = early_in[...]
    early[:, R:] = low(jnp.full((early.shape[0], R, early.shape[2]), sc[0], F32))
    weights = Weights(sc, pieces, w, sems, lead)
    weights.start()
    proj = Weights(sc, own_q, wp, sems_p, lead, 3 * D // cols)
    proj.start()
    a = sc[0]
    hid = D // cols
    glat4 = low(mm(gr[...], up_2[a], NT))
    res[...] = res_in[...]
    gn2[...] = gn2_in[...]
    lat4[...] = lat4_in[...]
    glat3[...] = glat3_in[...]
    weights.wait()
    ffn_steps(
        sc, 1, cols, w, xa, n2, lat3, gr, glat4, up_1, down_2, (res, gn2, lat4, glat3), early, lane
    )
    mid = middle[...]
    lat4_low = low(lat4[...])
    out = low(
        keep[...] * (mid + res[...] + mm(lat4_low, up_2[a]) + bias_out[1:2].astype(F32))
    )
    for c in range(cols):
        layer[c] = out[:, c * hid : (c + 1) * hid]
    glat3_low = low(glat3[...])
    grad_normed = gn2[...] + mm(glat3_low, f_down[a])
    unit, inverse = norm_parts(mid)
    grad_middle = gr[...].astype(F32) + norm_back(grad_normed, gain[1:2], unit, inverse)
    gmid[...] = grad_middle
    gb = low(grad_middle)
    glat2 = low(mm(gb, p_up[a], NT))
    glat2_t = low(glat2.astype(F32).T)
    put(early, FF + D, low(mm(low(lat2[...].astype(F32).T), gb)), lane)
    put(early, FF + 2 * D, low(mm(low(glat3_low.astype(F32).T), n2[...])), lane)
    put(early, FF + 3 * D, low(mm(low(lat4_low.astype(F32).T), gr[...])), lane)
    proj.wait()

    def step(slot, _):
        block = column_of(sc, slot)
        here = lanes(slot * hid, hid)
        there = lanes(block * hid, hid)
        gatt[:, here] = low(mm(gb, wp[slot]) + mm(glat2, p_down[a, :, there]))
        put(early, FF + block * hid, low(mm(glat2_t, att[:, here])), lane)
        return 0

    lax.fori_loop(0, cols, step, 0)


def attention_back_kernel(cols, *refs):
    sc = refs[0]
    closed, q, k, v, lse, gatt, lat1, n1, q_up = refs[1:10]
    gq, gk, gv, glat1, late = refs[10:15]
    a = sc[0]
    hid = D // cols
    shut = closed[...] > 0.5
    left = lax.broadcasted_iota(jnp.int32, (1, PAIR), 1) < HD

    def attend(pair, _):
        at = lanes(pair * PAIR, PAIR)
        qp, kp, vp, gp = q[:, at], k[:, at], v[:, at], gatt[:, at]
        k_t = low(kp.astype(F32).T)
        by_q, by_k, by_v = [], [], []
        for h in range(2):
            mine = left == (h == 0)
            zero = jnp.zeros_like(qp)
            s = jnp.where(shut, -1e30, mm(kp, jnp.where(mine, qp, zero), NT))
            soft = jnp.exp(s - lse[pair, h : h + 1, :])
            grad_soft = mm(vp, jnp.where(mine, gp, zero), NT)
            total = jnp.sum(grad_soft * soft, axis=0, keepdims=True)
            grad_scores = low(soft * (grad_soft - total))
            by_v.append(mm(low(soft), gp))
            by_k.append(mm(grad_scores, qp))
            by_q.append(mm(k_t[h * HD : (h + 1) * HD], grad_scores))
        gq[:, at] = low(jnp.concatenate(by_q, axis=0).T * 0.125)
        gk[:, at] = low(jnp.where(left, by_k[0], by_k[1]))
        gv[:, at] = low(jnp.where(left, by_v[0], by_v[1]))
        return 0

    lax.fori_loop(0, H // 2, attend, 0)
    lat1_t = low(lat1[...].astype(F32).T)

    def step(slot, acc):
        block = column_of(sc, slot)
        here = lanes(slot * hid, hid)
        there = lanes(block * hid, hid)
        for c, g in enumerate((gq, gk, gv)):
            grad = g[:, here]
            acc = acc + mm(grad, q_up[c, :, there], NT)
            put(late, (c + 1) * D + block * hid, low(mm(lat1_t, grad)))
        return acc

    made = low(lax.fori_loop(0, cols, step, jnp.zeros((SEQ, R), F32)))
    glat1[...] = made
    put(late, 0, low(mm(low(made.astype(F32).T), n1[...])))


def back_kernel(lead, cols, *refs):
    sc = refs[0]
    pieces = refs[1:9]
    xa, gain, gq, gk, gv, glat1, q_down, gmid, layer = refs[9:18]
    out = refs[18]
    w, sems, acc = refs[19:]
    weights = Weights(sc, pieces, w, sems, lead)
    weights.start()
    hid = D // cols
    acc[...] = mm(glat1[...], q_down[sc[0]])
    x = tokens_of(xa, cols)
    unit, inverse = norm_parts(x)
    weights.wait()

    def step(slot, _):
        here = lanes(slot * hid, hid)
        grad = jnp.concatenate([gq[:, here], gk[:, here], gv[:, here]], axis=1)
        acc[...] += mm(grad, w[slot, :, : 3 * hid], NT)
        return 0

    lax.fori_loop(0, cols, step, 0)
    made = low(gmid[...] + norm_back(acc[...], gain[0:1], unit, inverse))
    for c in range(cols):
        out[c, :SEQ] = layer[c]
        out[c, SEQ:] = made[:, c * hid : (c + 1) * hid]


def sum_kernel(owners, *refs):
    mines, out, acc = refs[:-2], refs[-2], refs[-1]
    acc[...] = jnp.zeros_like(acc)
    lane = 0
    for mine in mines:
        part = mine.shape[-1]
        for d in range(mine.shape[0]):
            acc[owners[d], :, lane : lane + part] += mine[d, :R].astype(F32)
        lane += part
    out[...] = low(acc[...])


def spread_kernel(lead, cols, parts, maps, *refs):
    sc, pieces = refs[0], refs[1:9]
    count = (len(refs) - 11) // 2
    outs, whole, made = refs[9 : 9 + count], refs[9 + count], refs[10 + count : 10 + 2 * count]
    sems_in, sems_out = refs[10 + 2 * count :]
    copies = []
    for k, piece in enumerate(pieces):
        x_rel, y_rel, away = piece_place(sc, k)
        for n, (high_col, high_row) in enumerate(lead):
            row = high_row * 2 + ((sc[3] + y_rel) & 1)
            col = high_col * 4 + ((sc[1] & 3) ^ (x_rel * 2 + away))
            copies.append(
                pltpu.make_async_copy(piece.at[n], whole.at[row * cols + col], sems_in.at[k, n])
            )
    for copy in copies:
        copy.start()
    for copy in copies:
        copy.wait()
    found = [[] for _ in outs]
    base = 0
    for part, spans in zip(parts, maps):
        for out, section, there, start, width in spans:
            for lane in range(0, width, 128):
                at = start + lane
                found[out].append((section, there + lane, at // part, base + at % part))
        base += part
    leaving = []
    for i, (out, buffer) in enumerate(zip(outs, made)):
        for section, there, device, here in found[i]:
            block = whole[device, :, here : here + 128].astype(F32)
            if section is None:
                buffer[:, there : there + 128] = block
            else:
                buffer[:, section, :, there : there + 128] = block.reshape(NA, R, 128)
        leaving.append(pltpu.make_async_copy(buffer, out, sems_out.at[i]))
        leaving[-1].start()
    for copy in leaving:
        copy.wait()


def place_kernel(lead, cols, *refs):
    sc, pieces, out, sems = refs[0], refs[1:9], refs[9], refs[10]
    copies = []
    for k, piece in enumerate(pieces):
        x_rel, y_rel, away = piece_place(sc, k)
        for n, (high_col, high_row) in enumerate(lead):
            row = high_row * 2 + ((sc[3] + y_rel) & 1)
            col = high_col * 4 + ((sc[1] & 3) ^ (x_rel * 2 + away))
            copies.append(pltpu.make_async_copy(piece.at[n], out.at[row * cols + col], sems.at[k, n]))
    for copy in copies:
        copy.start()
    for copy in copies:
        copy.wait()


def send_grads(grads):
    return lax.all_to_all(grads, BOTH, split_axis=0, concat_axis=0, tiled=True)


def sum_grads(mines, owners):
    part = sum(m.shape[-1] for m in mines)
    summed = call(
        sum_kernel,
        jax.ShapeDtypeStruct((NA, R, part), BF),
        [owners, *mines],
        [pltpu.SMEM] + [VMEM] * len(mines),
        [VMEM((NA, R, part), F32)],
    )
    return summed.reshape(NA * R, part)


def spread(sc, pieces, parts, maps, shapes):
    rows, cols = sizes()
    devices = rows * cols
    lead = lead_table(rows, cols)
    arrivals = pltpu.SemaphoreType.DMA((8, len(lead)))
    whole = (devices, NA * R, sum(parts))
    ins, spaces = [sc, *pieces], [pltpu.SMEM] + [pl.ANY] * 8
    if all(p % 128 == 0 for p in parts):
        return call(
            functools.partial(spread_kernel, lead, cols, parts, maps),
            [jax.ShapeDtypeStruct(x, F32) for x in shapes],
            ins,
            spaces,
            [VMEM(whole, BF)]
            + [VMEM(x, F32) for x in shapes]
            + [arrivals, pltpu.SemaphoreType.DMA((len(shapes),))],
            pl.ANY,
            56,
        )
    whole = call(
        functools.partial(place_kernel, lead, cols),
        jax.ShapeDtypeStruct(whole, BF),
        ins,
        spaces,
        [arrivals],
    )
    found = [[] for _ in shapes]
    base = 0
    for part, spans in zip(parts, maps):
        flat = jnp.swapaxes(whole[:, :, base : base + part], 0, 1).reshape(NA * R, devices * part)
        for out, section, there, start, width in spans:
            found[out].append((section or 0, there, flat[:, start : start + width].astype(F32)))
        base += part
    return [
        (
            jnp.concatenate([x for _, _, x in sorted(f, key=lambda e: e[:2])], axis=1)
            if len(shape) == 2
            else jnp.stack([x.reshape(NA, R, -1) for _, _, x in sorted(f, key=lambda e: e[:2])], 1)
        )
        for f, shape in zip(found, shapes)
    ]


def per_device(
    tokens_in,
    grad_out,
    keep_mask,
    adapter_index,
    ln_gain,
    ln_shift,
    w_qkv,
    bias_qv,
    w_proj,
    w_fc1,
    bias_fc1,
    w_fc2,
    bias_out,
    qkv_down,
    qkv_up,
    proj_down,
    proj_up,
    fc1_down,
    fc1_up,
    fc2_down,
    fc2_up,
):
    rows, cols = sizes()
    row, column = lax.axis_index("row"), lax.axis_index("col")
    assert adapter_index.shape[0] == cols and cols >= 4 and rows >= 2
    hid = D // cols
    n = 4 * hid
    blk = D // rows
    lead = lead_table(rows, cols)

    shard = jax.ShapeDtypeStruct((blk, n), BF)
    shard_q = call(prep_q_kernel, shard, [w_qkv, w_proj], [VMEM] * 2)
    with jax.named_scope("q_high"):
        own_q, came_q = gather_high(shard_q)
    rows_in = call(
        prep_rows_kernel,
        jax.ShapeDtypeStruct((cols, 2 * SEQ + EXTRA, hid), BF),
        [after(tokens_in, shard_q).reshape(cols, SEQ, hid), grad_out.reshape(cols, SEQ, hid), bias_qv]
        + [bias_fc1.reshape(4, hid)],
        [VMEM] * 4,
    )
    xa = lax.all_to_all(rows_in, "col", split_axis=0, concat_axis=0, tiled=True)
    adapter = lax.dynamic_index_in_dim(adapter_index, column, 0, keepdims=False)
    sc = jnp.stack([adapter, column, column % 2, row % 2]).astype(jnp.int32)
    up_qkv = jnp.swapaxes(lax.dynamic_index_in_dim(qkv_up, adapter, 0, keepdims=False), 0, 1)
    shard_a, shard_b, keep, closed = call(
        prep_f_kernel,
        [shard] * 2 + [jax.ShapeDtypeStruct((SEQ, 1), F32)] * 2,
        [sc, keep_mask, w_fc1, w_fc2],
        [pltpu.SMEM] + [VMEM] * 3,
    )

    own_q, shard_a, shard_b = after_all(
        (own_q, shard_a, shard_b), xa, keep, closed, sc, up_qkv, *came_q
    )
    with jax.named_scope("q_one"):
        one_q = swap(own_q, flip_one)
    with jax.named_scope("q_two"):
        two_q = swap(own_q, flip_two)
    with jax.named_scope("fa_high"):
        own_a, came_a = gather_high(shard_a)
    own_q, one_q, two_q = after_all((own_q, one_q, two_q), *came_a)
    with jax.named_scope("q_both"):
        both_q = swap(one_q, flip_two)
    with jax.named_scope("q_core"):
        away_q = [swap(p, flip_core) for p in (own_q, one_q, two_q)]
    both_q, own_a, shard_b = after_all((both_q, own_a, shard_b), *away_q)
    with jax.named_scope("q_core"):
        pieces_q = [own_q, one_q, two_q, both_q] + away_q + [swap(both_q, flip_core)]
    with jax.named_scope("fa_one"):
        one_a = swap(own_a, flip_one)
    with jax.named_scope("fa_two"):
        two_a = swap(own_a, flip_two)
    with jax.named_scope("fb_high"):
        own_b, came_b = gather_high(shard_b)

    def shaped(width, dtype, height=SEQ):
        return jax.ShapeDtypeStruct((height, width), dtype)

    big, small = shaped(D, BF), shaped(R, BF)
    scratch = weight_scratch(rows, cols, n)
    any_space = [pl.ANY] * 8
    n1, lat1, q, k, v, lse, att, lat2, middle, n2, lat3 = call(
        functools.partial(front_kernel, lead, cols),
        [
            big,
            small,
            big,
            big,
            big,
            jax.ShapeDtypeStruct((H // 2, 2, SEQ), F32),
            big,
            small,
            shaped(D, F32),
            big,
            small,
        ],
        [sc, *pieces_q, xa, closed, ln_gain, ln_shift, qkv_down, up_qkv, proj_down]
        + [proj_up]
        + [fc1_down, bias_out],
        [pltpu.SMEM] + any_space + [VMEM] * 10,
        scratch + [VMEM((SEQ, D), F32), VMEM((SEQ, D), F32)],
        mib=FRONT,
    )
    own_a, one_a, two_a = after_all((own_a, one_a, two_a), n1, *came_b)
    with jax.named_scope("fa_both"):
        both_a = swap(one_a, flip_two)
    with jax.named_scope("fa_core"):
        away_a = [swap(p, flip_core) for p in (own_a, one_a, two_a)]
    both_a, own_b = after_all((both_a, own_b), *away_a)
    with jax.named_scope("fa_core"):
        pieces_a = [own_a, one_a, two_a, both_a] + away_a + [swap(both_a, flip_core)]
    with jax.named_scope("fb_one"):
        one_b = swap(own_b, flip_one)
    with jax.named_scope("fb_two"):
        two_b = swap(own_b, flip_two)
    wide = shaped(D, F32)
    thin = shaped(R, F32)
    res, gn2, lat4, glat3, gr, early_a = call(
        functools.partial(ffn_a_kernel, lead, cols),
        [wide, wide, thin, thin, big, jax.ShapeDtypeStruct((rows * cols, R, FF // (rows * cols)), BF)],
        [sc, *pieces_a, xa, keep, n2, lat3, fc1_up, fc2_down, fc2_up],
        [pltpu.SMEM] + any_space + [VMEM] * 7,
        scratch,
        mib=FFN_A,
    )
    own_b, one_b, two_b = after_all((own_b, one_b, two_b), res)
    with jax.named_scope("fb_both"):
        both_b = swap(one_b, flip_two)
    with jax.named_scope("fb_core"):
        away_b = [swap(p, flip_core) for p in (own_b, one_b, two_b)]
        pieces_b = [own_b, one_b, two_b, both_b] + away_b + [swap(both_b, flip_core)]
    layer, gatt, gmid, grads_b = call(
        functools.partial(ffn_b_kernel, lead, cols),
        [jax.ShapeDtypeStruct((cols, SEQ, hid), BF), big, wide]
        + [jax.ShapeDtypeStruct((rows * cols, 2 * R, 12 * D // (rows * cols)), BF)],
        [sc, *pieces_b, *pieces_q, xa, keep, ln_gain, n2, lat3, fc1_up, fc2_down, fc2_up]
        + [fc1_down, proj_down, proj_up, bias_out]
        + [middle, att, lat2, gr, res, gn2, lat4, glat3, early_a],
        [pltpu.SMEM] + any_space * 2 + [VMEM] * 21,
        scratch
        + [VMEM((cols, D, hid), BF), scratch[1]]
        + [VMEM((SEQ, D), F32), VMEM((SEQ, D), F32), VMEM((SEQ, R), F32), VMEM((SEQ, R), F32)],
        mib=FFN_B,
    )
    with jax.named_scope("grads_b_send"):
        mine_b = send_grads(grads_b)
        owners = mine_b[:, R, 0].astype(jnp.int32)
    gq, gk, gv, glat1, late = call(
        functools.partial(attention_back_kernel, cols),
        [big, big, big, small, jax.ShapeDtypeStruct((rows * cols, R, 4 * D // (rows * cols)), BF)],
        [sc, closed, q, k, v, lse, gatt, lat1, n1, up_qkv],
        [pltpu.SMEM] + [VMEM] * 9,
        mib=ATT,
    )
    with jax.named_scope("grads_c_send"):
        mine_c = send_grads(late)
    with jax.named_scope("grads_b"):
        part_b = sum_grads([after(mine_b, late)], owners)
    gmid = after(gmid, part_b)
    sent = call(
        functools.partial(back_kernel, lead, cols),
        jax.ShapeDtypeStruct((cols, 2 * SEQ, hid), BF),
        [sc, *pieces_q, xa, ln_gain, gq, gk, gv, glat1, qkv_down, gmid, layer],
        [pltpu.SMEM] + any_space + [VMEM] * 9,
        scratch + [VMEM((SEQ, D), F32)],
        mib=BACK,
    )
    with jax.named_scope("grads"):
        own_b, _ = gather_high(part_b)
        own_c, _ = gather_high(after(sum_grads([mine_c], owners), sent))
        own = lane_join(own_b, own_c)
        one, two = swap(own, flip_one), swap(own, flip_two)
        both = swap(after(one, two), flip_two)
        pieces = with_cores([own, one, two, both])
        half = FF // cols // 2
        map_a, map_b = (
            tuple(
                (out, None, (2 * block + part) * half, base + block * half, half)
                for out, base in ((0, 0), (1, FF // 2))
                for block in range(cols)
            )
            for part in (0, 1)
        )
        map_b = map_b + tuple((2 + i, None, 0, FF + i * D, D) for i in range(4))
        map_c = ((6, None, 0, 0, D),) + tuple((7, c, 0, (c + 1) * D, D) for c in range(3))
        parts = [early_a.shape[-1], mine_b.shape[-1] - early_a.shape[-1], mine_c.shape[-1]]
        shapes = [(NA * R, FF)] * 2 + [(NA * R, D)] * 5 + [(NA, 3, R, D)]
        sums = spread(sc, pieces, parts, [map_a, map_b, map_c], shapes)

    with jax.named_scope("rows_out"):
        sent = after(sent, both)
        rows_out = lax.all_to_all(sent, "col", split_axis=0, concat_axis=0, tiled=True)
    layer, grad_in = rows_out[:, :SEQ], rows_out[:, SEQ:]

    def split(table):
        return table.reshape((NA, R) + table.shape[1:])

    g_fc1_up, g_fc2_down, g_proj_down, g_proj_up, g_fc1_down, g_fc2_up = map(split, sums[:6])
    return (
        layer.reshape(cols * SEQ, hid),
        grad_in.reshape(cols * SEQ, hid),
        split(sums[6]),
        jnp.swapaxes(sums[7], 1, 2),
        g_proj_down,
        g_proj_up,
        g_fc1_down,
        g_fc1_up,
        g_fc2_down,
        g_fc2_up,
    )


def solution(mesh):
    return jax.shard_map(
        per_device,
        mesh=mesh,
        in_specs=(
            P("row", "col"),
            P("row", "col"),
            P("row", None),
            P("row"),
            P(),
            P(),
            P(None, "row", "col"),
            P(None, "col"),
            P("col", "row"),
            P("row", "col"),
            P("col"),
            P("col", "row"),
            P(),
            P(),
            P(),
            P(),
            P(),
            P(),
            P(),
            P(),
            P(),
        ),
        out_specs=(P("row", "col"), P("row", "col"), P(), P(), P(), P(), P(), P(), P(), P()),
        check_vma=False,
    )
```

```python
import functools

import jax
import jax.numpy as jnp
from jax import lax
from jax.experimental import pallas as pl
from jax.experimental.pallas import tpu as pltpu
from jax.sharding import PartitionSpec as P

D = 1024
H = 16
HD = 64
FF = 4096
BUF = 64
R = 16
NA = 8
SEQ = 320
PAIR = 2 * HD
EXTRA = 16
OWNER = 128
FRONT, FFN_A, FFN_B, ATT, BACK = 56, 56, 56, 56, 56
BF = jnp.bfloat16
F32 = jnp.float32
BOTH = ("row", "col")
VMEM = pltpu.VMEM
NN = (((1,), (0,)), ((), ()))
NT = (((1,), (1,)), ((), ()))


def mm(left, right, dims=NN):
    return lax.dot_general(left, right, dims, preferred_element_type=F32)


def low(values):
    return values.astype(BF)


def norm_parts(values):
    row_mean = jnp.mean(values, axis=-1, keepdims=True)
    centered = values - row_mean
    variance = jnp.mean(centered * centered, axis=-1, keepdims=True)
    inverse = lax.rsqrt(variance + 1e-06)
    return (centered * inverse, inverse)


def norm_back(grad_normed, gain_row, unit_rows, inverse):
    scaled = grad_normed * gain_row
    first_mean = jnp.mean(scaled, axis=-1, keepdims=True)
    second_mean = jnp.mean(scaled * unit_rows, axis=-1, keepdims=True)
    return inverse * (scaled - first_mean - unit_rows * second_mean)


def call(kernel, outs, ins, spaces, scratch=(), out_space=VMEM, mib=4):
    return pl.pallas_call(
        kernel,
        out_shape=outs,
        in_specs=[pl.BlockSpec(memory_space=s) for s in spaces],
        out_specs=jax.tree.map(lambda _: pl.BlockSpec(memory_space=out_space), outs),
        scratch_shapes=list(scratch),
        compiler_params=pltpu.CompilerParams(vmem_limit_bytes=mib << 20),
        cost_estimate=pl.CostEstimate(flops=0, bytes_accessed=0, transcendentals=0),
    )(*ins)


def sizes():
    return lax.axis_size("row"), lax.axis_size("col")


def swap(block, flip):
    rows, cols = sizes()
    pairs = []
    for i in range(rows * cols):
        row, col = flip(i // cols, i % cols)
        pairs.append((i, row * cols + col))
    return lax.ppermute(block, BOTH, pairs)


def bits_of(size):
    return size.bit_length() - 1


def stack_kernel(which, *refs):
    parts, out, sems = refs[:-2], refs[-2], refs[-1]
    copies = [
        pltpu.make_async_copy(ref, out.at[which[0] ^ m], sems.at[m]) for m, ref in enumerate(parts)
    ]
    for copy in copies:
        copy.start()
    for copy in copies:
        copy.wait()


def stacked(parts, index):
    shape = parts[0].shape
    flat = [p.reshape((-1, shape[-1])) for p in parts]
    out = jax.ShapeDtypeStruct((len(parts),) + flat[0].shape, flat[0].dtype)
    made = call(
        stack_kernel,
        out,
        [index.reshape(1).astype(jnp.int32)] + flat,
        [pltpu.SMEM] + [pl.ANY] * len(parts),
        [pltpu.SemaphoreType.DMA((len(parts),))],
    )
    return made.reshape((len(parts),) + shape)


def group_join(block, axis, low_bit, width):
    parts = [block]
    for m in range(1, 1 << width):
        step = m << low_bit
        if axis == "row":
            parts.append(swap(block, lambda r, c: (r ^ step, c)))
        else:
            parts.append(swap(block, lambda r, c: (r, c ^ step)))
    index = (lax.axis_index(axis) >> low_bit) & ((1 << width) - 1)
    return stacked(parts, index), parts


def groups(top, bottom):
    out = []
    while top > bottom:
        width = min(2, top - bottom)
        out.append((top - width, width))
        top -= width
    return out


def early_groups(rows, cols):
    return [("row",) + g for g in groups(bits_of(rows), 1)] + [
        ("col",) + g for g in groups(bits_of(cols), 2)
    ]


def lead_table(rows, cols):
    table = [(0, 0)]
    for axis, bit, width in early_groups(rows, cols):
        shift = bit - (1 if axis == "row" else 2)
        new = []
        for value in range(1 << width):
            for high_col, high_row in table:
                if axis == "row":
                    new.append((high_col, high_row + (value << shift)))
                else:
                    new.append((high_col + (value << shift), high_row))
        table = new
    return table


def after(value, *others):
    return lax.optimization_barrier((value,) + others)[0]


def after_all(values, *others):
    return lax.optimization_barrier(tuple(values) + others)[: len(values)]


def gather_high(shard):
    rows, cols = sizes()
    block, parts = shard, []
    for axis, bit, width in early_groups(rows, cols):
        block, parts = group_join(block, axis, bit, width)
    return block.reshape((-1,) + shard.shape), parts[1:]


def lane_join_kernel(*refs):
    parts, out, sems = refs[:-2], refs[-2], refs[-1]
    copies, lane = [], 0
    for i, part in enumerate(parts):
        width = part.shape[-1]
        copies.append(pltpu.make_async_copy(part, out.at[:, :, lane : lane + width], sems.at[i]))
        lane += width
    for copy in copies:
        copy.start()
    for copy in copies:
        copy.wait()


def lane_join(*parts):
    if any(p.shape[-1] % 128 for p in parts):
        return jnp.concatenate(parts, axis=-1)
    shape = parts[0].shape[:-1] + (sum(p.shape[-1] for p in parts),)
    return call(
        lane_join_kernel,
        jax.ShapeDtypeStruct(shape, parts[0].dtype),
        parts,
        [pl.ANY] * len(parts),
        [pltpu.SemaphoreType.DMA((len(parts),))],
    )


def flip_one(r, c):
    return (r, c ^ 2) if c % 2 == 0 else (r ^ 1, c)


def flip_two(r, c):
    return (r ^ 1, c) if c % 2 == 0 else (r, c ^ 2)


def flip_core(r, c):
    return (r, c ^ 1)


def with_cores(pieces):
    return pieces + [swap(p, flip_core) for p in pieces]


def piece_place(sc, k):
    kind, away = k % 4, k // 4
    turn = (sc[2] + away) & 1
    return (0, 1 - turn, turn, 1)[kind], (0, turn, 1 - turn, 1)[kind], away


class Weights:
    def __init__(self, sc, pieces, w, sems, lead, first_lane=0):
        self.copies = []
        depth = pieces[0].shape[1]
        taken = pl.ds(first_lane, w.shape[2])
        for k, piece in enumerate(pieces):
            x_rel, y_rel, away = piece_place(sc, k)
            for n, (high_col, high_row) in enumerate(lead):
                slot = high_col * 4 + x_rel * 2 + away
                row = (high_row * 2 + ((sc[3] + y_rel) & 1)) * depth
                self.copies.append(
                    pltpu.make_async_copy(
                        piece.at[n, :, taken],
                        w.at[slot, pl.ds(pl.multiple_of(row, depth), depth), :],
                        sems.at[k, n],
                    )
                )

    def start(self):
        for copy in self.copies:
            copy.start()

    def wait(self):
        for copy in self.copies:
            copy.wait()


def column_of(sc, slot):
    return (slot // 4) * 4 + ((sc[1] & 3) ^ (slot & 3))


def weight_scratch(rows, cols, n):
    lead = len(lead_table(rows, cols))
    return [VMEM((cols, D, n), BF), pltpu.SemaphoreType.DMA((8, lead))]


def put(ref, start, value, lane=0, spare=0):
    end = ref.shape[-1] - spare
    part = end - lane
    for i in range(value.shape[-1] // part):
        ref[start // part + i, :, lane:end] = value[:, i * part : (i + 1) * part]


def lanes(start, width):
    return pl.ds(pl.multiple_of(start, width), width)


def prep_q_kernel(wq, wp, out):
    hid = wq.shape[2]
    for c in range(3):
        out[:, c * hid : (c + 1) * hid] = wq[c]
    out[:, 3 * hid :] = low(wp[...].astype(F32).T)


def prep_rows_kernel(tokens, grads, bias_qv, bias_f, out):
    cols, seq = out.shape[0], tokens.shape[1]
    for c in range(cols):
        out[c, :seq] = tokens[c]
        out[c, seq : 2 * seq] = grads[c]
        out[c, 2 * seq : 2 * seq + 2] = bias_qv[...]
        out[c, 2 * seq + 2 : 2 * seq + 6] = bias_f[...]


def prep_f_kernel(sc, mask, w1, w2, out_a, out_b, keep, closed):
    row = mask[pl.ds(sc[1], 1), :].astype(F32)
    row = jnp.concatenate([jnp.ones((1, BUF), F32), row], axis=1)
    column = jnp.broadcast_to(row, (8, SEQ)).T[:, :1]
    keep[...] = column
    closed[...] = 1.0 - column
    half = w1.shape[1] // 2
    out_a[:, :half] = w1[:, :half]
    out_b[:, :half] = w1[:, half:]
    out_a[:, half:] = low(w2[:half].astype(F32).T)
    out_b[:, half:] = low(w2[half:].astype(F32).T)


def tokens_of(ref, cols):
    return jnp.concatenate([ref[c, :SEQ, :] for c in range(cols)], axis=1).astype(F32)


def front_kernel(lead, cols, *refs):
    sc = refs[0]
    pieces = refs[1:9]
    (xa, closed, gain, shift, q_down, q_up, p_down, p_up, f_down, bias_out) = refs[9:19]
    (n1, lat1, q, k, v, lse, att, lat2, middle, n2, lat3) = refs[19:30]
    w, sems, hidden, branch = refs[30:]
    weights = Weights(sc, pieces, w, sems, lead)
    weights.start()
    a = sc[0]
    hid = D // cols
    x = tokens_of(xa, cols)
    hidden[...] = x
    unit, _ = norm_parts(x)
    n1[...] = low(unit * gain[0:1] + shift[0:1])
    lat1[...] = low(mm(n1[...], q_down[a], NT))
    weights.wait()

    def project(slot, _):
        block = column_of(sc, slot)
        up = jnp.concatenate([q_up[c, :, lanes(block * hid, hid)] for c in range(3)], axis=1)
        made = mm(n1[...], w[slot, :, : 3 * hid]) + mm(lat1[...], up)
        bias_q = xa[block, 2 * SEQ : 2 * SEQ + 1, :].astype(F32)
        bias_v = xa[block, 2 * SEQ + 1 : 2 * SEQ + 2, :].astype(F32)
        at = lanes(slot * hid, hid)
        q[:, at] = low(made[:, :hid] + bias_q) * jnp.asarray(0.125, BF)
        k[:, at] = low(made[:, hid : 2 * hid])
        v[:, at] = low(made[:, 2 * hid :] + bias_v)
        return 0

    lax.fori_loop(0, cols, project, 0)
    shut = closed[...] > 0.5
    left = lax.broadcasted_iota(jnp.int32, (1, PAIR), 1) < HD

    def attend(pair, _):
        at = lanes(pair * PAIR, PAIR)
        qp, kp, vp = q[:, at], k[:, at], v[:, at]
        v_t = low(vp.astype(F32).T)
        halves = []
        for h in range(2):
            masked = jnp.where(left == (h == 0), qp, jnp.zeros_like(qp))
            s = jnp.where(shut, -1e30, mm(kp, masked, NT))
            top = jnp.max(s, axis=0, keepdims=True)
            e = jnp.exp(s - top)
            total = jnp.sum(e, axis=0, keepdims=True)
            lse[pair, h : h + 1, :] = top + jnp.log(total)
            soft = low(e * (1.0 / total))
            halves.append(mm(v_t[h * HD : (h + 1) * HD], soft))
        att[:, at] = low(jnp.concatenate(halves, axis=0).T)
        return 0

    lax.fori_loop(0, H // 2, attend, 0)

    def down_two(slot, acc):
        block = column_of(sc, slot)
        return acc + mm(att[:, lanes(slot * hid, hid)], p_down[a, :, lanes(block * hid, hid)], NT)

    lat2[...] = low(lax.fori_loop(0, cols, down_two, jnp.zeros((SEQ, R), F32)))
    branch[...] = mm(lat2[...], p_up[a]) + bias_out[0:1].astype(F32)

    def out_proj(slot, _):
        branch[...] += mm(att[:, lanes(slot * hid, hid)], w[slot, :, 3 * hid :], NT)
        return 0

    lax.fori_loop(0, cols, out_proj, 0)
    mid = hidden[...] + branch[...]
    middle[...] = mid
    unit, _ = norm_parts(mid)
    n2[...] = low(unit * gain[1:2] + shift[1:2])
    lat3[...] = low(mm(n2[...], f_down[a], NT))


def ffn_steps(sc, part, cols, w, xa, n2, lat3, gr, glat4, up_1, down_2, acc, early, lane=0, spare=0):
    res, gn2, lat4, glat3 = acc
    a = sc[0]
    hid = D // cols
    ffn = FF // cols
    half = ffn // 2
    glat4_t = low(glat4.astype(F32).T)
    lat3_t = low(lat3[...].astype(F32).T)

    def step(slot, _):
        block = column_of(sc, slot)
        at = pl.ds(pl.multiple_of(block * ffn + part * half, half), half)
        bias = jnp.concatenate(
            [xa[block, 2 * SEQ + 2 + 2 * part + i : 2 * SEQ + 3 + 2 * part + i, :] for i in range(2)],
            axis=1,
        ).astype(F32)
        up, down = up_1[a, :, at], down_2[a, :, at]
        w1, w2 = w[slot, :, :half], w[slot, :, half:]
        pre = mm(n2[...], w1) + mm(lat3[...], up) + bias
        back = mm(gr[...], w2) + mm(glat4, down)
        cumulative = 0.5 * (1.0 + lax.erf(pre * 0.7071067811865476))
        activated = low(pre * cumulative)
        slope = cumulative + pre * jnp.exp(-0.5 * pre * pre) * 0.3989422804014327
        grad_pre = low(back * slope)
        lat4[...] += mm(activated, down, NT)
        glat3[...] += mm(grad_pre, up, NT)
        res[...] += mm(activated, w2, NT)
        gn2[...] += mm(grad_pre, w1, NT)
        put(early, block * half, low(mm(lat3_t, grad_pre)), lane, spare)
        put(early, FF // 2 + block * half, low(mm(glat4_t, activated)), lane, spare)
        return 0

    lax.fori_loop(0, cols, step, 0)


def ffn_a_kernel(lead, cols, *refs):
    sc = refs[0]
    pieces = refs[1:9]
    xa, keep, n2, lat3, up_1, down_2, up_2 = refs[9:16]
    res, gn2, lat4, glat3, gr, early = refs[16:22]
    w, sems = refs[22:]
    weights = Weights(sc, pieces, w, sems, lead)
    weights.start()
    gr[...] = low(
        jnp.concatenate([xa[c, SEQ : 2 * SEQ] for c in range(cols)], axis=1).astype(F32) * keep[...]
    )
    glat4 = low(mm(gr[...], up_2[sc[0]], NT))
    res[...] = jnp.zeros_like(res)
    gn2[...] = jnp.zeros_like(gn2)
    lat4[...] = jnp.zeros_like(lat4)
    glat3[...] = jnp.zeros_like(glat3)
    weights.wait()
    ffn_steps(
        sc, 0, cols, w, xa, n2, lat3, gr, glat4, up_1, down_2, (res, gn2, lat4, glat3), early
    )


def ffn_b_kernel(lead, cols, *refs):
    sc = refs[0]
    pieces = refs[1:9]
    own_q = refs[9:17]
    (xa, keep, gain, n2, lat3, up_1, down_2, up_2, f_down, p_down, p_up, bias_out) = refs[17:29]
    (middle, att, lat2, gr, res_in, gn2_in, lat4_in, glat3_in, early_in) = refs[29:38]
    layer, gatt, gmid, early = refs[38:42]
    w, sems, wp, sems_p, res, gn2, lat4, glat3 = refs[42:]
    lane = early_in.shape[-1]
    early[:, :, :lane] = early_in[...]
    early[:, :, early.shape[2] - OWNER :] = low(jnp.full((early.shape[0], R, OWNER), sc[0], F32))
    weights = Weights(sc, pieces, w, sems, lead)
    weights.start()
    proj = Weights(sc, own_q, wp, sems_p, lead, 3 * D // cols)
    proj.start()
    a = sc[0]
    hid = D // cols
    glat4 = low(mm(gr[...], up_2[a], NT))
    res[...] = res_in[...]
    gn2[...] = gn2_in[...]
    lat4[...] = lat4_in[...]
    glat3[...] = glat3_in[...]
    weights.wait()
    ffn_steps(
        sc, 1, cols, w, xa, n2, lat3, gr, glat4, up_1, down_2, (res, gn2, lat4, glat3), early, lane, OWNER
    )
    mid = middle[...]
    lat4_low = low(lat4[...])
    out = low(
        keep[...] * (mid + res[...] + mm(lat4_low, up_2[a]) + bias_out[1:2].astype(F32))
    )
    for c in range(cols):
        layer[c] = out[:, c * hid : (c + 1) * hid]
    glat3_low = low(glat3[...])
    grad_normed = gn2[...] + mm(glat3_low, f_down[a])
    unit, inverse = norm_parts(mid)
    grad_middle = gr[...].astype(F32) + norm_back(grad_normed, gain[1:2], unit, inverse)
    gmid[...] = grad_middle
    gb = low(grad_middle)
    glat2 = low(mm(gb, p_up[a], NT))
    glat2_t = low(glat2.astype(F32).T)
    put(early, FF + D, low(mm(low(lat2[...].astype(F32).T), gb)), lane, OWNER)
    put(early, FF + 2 * D, low(mm(low(glat3_low.astype(F32).T), n2[...])), lane, OWNER)
    put(early, FF + 3 * D, low(mm(low(lat4_low.astype(F32).T), gr[...])), lane, OWNER)
    proj.wait()

    def step(slot, _):
        block = column_of(sc, slot)
        here = lanes(slot * hid, hid)
        there = lanes(block * hid, hid)
        gatt[:, here] = low(mm(gb, wp[slot]) + mm(glat2, p_down[a, :, there]))
        put(early, FF + block * hid, low(mm(glat2_t, att[:, here])), lane, OWNER)
        return 0

    lax.fori_loop(0, cols, step, 0)


def attention_back_kernel(cols, *refs):
    sc = refs[0]
    closed, q, k, v, lse, gatt, lat1, n1, q_up = refs[1:10]
    gq, gk, gv, glat1, late = refs[10:15]
    a = sc[0]
    hid = D // cols
    shut = closed[...] > 0.5
    left = lax.broadcasted_iota(jnp.int32, (1, PAIR), 1) < HD

    def attend(pair, _):
        at = lanes(pair * PAIR, PAIR)
        qp, kp, vp, gp = q[:, at], k[:, at], v[:, at], gatt[:, at]
        k_t = low(kp.astype(F32).T)
        by_q, by_k, by_v = [], [], []
        for h in range(2):
            mine = left == (h == 0)
            zero = jnp.zeros_like(qp)
            s = jnp.where(shut, -1e30, mm(kp, jnp.where(mine, qp, zero), NT))
            soft = jnp.exp(s - lse[pair, h : h + 1, :])
            grad_soft = mm(vp, jnp.where(mine, gp, zero), NT)
            total = jnp.sum(grad_soft * soft, axis=0, keepdims=True)
            grad_scores = low(soft * (grad_soft - total))
            by_v.append(mm(low(soft), gp))
            by_k.append(mm(grad_scores, qp))
            by_q.append(mm(k_t[h * HD : (h + 1) * HD], grad_scores))
        gq[:, at] = low(jnp.concatenate(by_q, axis=0).T * 0.125)
        gk[:, at] = low(jnp.where(left, by_k[0], by_k[1]))
        gv[:, at] = low(jnp.where(left, by_v[0], by_v[1]))
        return 0

    lax.fori_loop(0, H // 2, attend, 0)
    lat1_t = low(lat1[...].astype(F32).T)

    def step(slot, acc):
        block = column_of(sc, slot)
        here = lanes(slot * hid, hid)
        there = lanes(block * hid, hid)
        for c, g in enumerate((gq, gk, gv)):
            grad = g[:, here]
            acc = acc + mm(grad, q_up[c, :, there], NT)
            put(late, (c + 1) * D + block * hid, low(mm(lat1_t, grad)))
        return acc

    made = low(lax.fori_loop(0, cols, step, jnp.zeros((SEQ, R), F32)))
    glat1[...] = made
    put(late, 0, low(mm(low(made.astype(F32).T), n1[...])))


def back_kernel(lead, cols, *refs):
    sc = refs[0]
    pieces = refs[1:9]
    xa, gain, gq, gk, gv, glat1, q_down, gmid, layer = refs[9:18]
    out = refs[18]
    w, sems, acc = refs[19:]
    weights = Weights(sc, pieces, w, sems, lead)
    weights.start()
    hid = D // cols
    acc[...] = mm(glat1[...], q_down[sc[0]])
    x = tokens_of(xa, cols)
    unit, inverse = norm_parts(x)
    weights.wait()

    def step(slot, _):
        here = lanes(slot * hid, hid)
        grad = jnp.concatenate([gq[:, here], gk[:, here], gv[:, here]], axis=1)
        acc[...] += mm(grad, w[slot, :, : 3 * hid], NT)
        return 0

    lax.fori_loop(0, cols, step, 0)
    made = low(gmid[...] + norm_back(acc[...], gain[0:1], unit, inverse))
    for c in range(cols):
        out[c, :SEQ] = layer[c]
        out[c, SEQ:] = made[:, c * hid : (c + 1) * hid]


def sum_kernel(owners, mine, out, acc):
    acc[...] = jnp.zeros_like(acc)
    for d in range(mine.shape[0]):
        acc[owners[d]] += mine[d, :, : acc.shape[2]].astype(F32)
    out[...] = low(acc[...])


def spread_kernel(lead, cols, parts, maps, *refs):
    sc, pieces = refs[0], refs[1:9]
    count = (len(refs) - 11) // 2
    outs, whole, made = refs[9 : 9 + count], refs[9 + count], refs[10 + count : 10 + 2 * count]
    sems_in, sems_out = refs[10 + 2 * count :]
    copies = []
    for k, piece in enumerate(pieces):
        x_rel, y_rel, away = piece_place(sc, k)
        for n, (high_col, high_row) in enumerate(lead):
            row = high_row * 2 + ((sc[3] + y_rel) & 1)
            col = high_col * 4 + ((sc[1] & 3) ^ (x_rel * 2 + away))
            copies.append(
                pltpu.make_async_copy(piece.at[n], whole.at[row * cols + col], sems_in.at[k, n])
            )
    for copy in copies:
        copy.start()
    for copy in copies:
        copy.wait()
    found = [[] for _ in outs]
    base = 0
    for part, spans in zip(parts, maps):
        for out, section, there, start, width in spans:
            for lane in range(0, width, 128):
                at = start + lane
                found[out].append((section, there + lane, at // part, base + at % part))
        base += part
    leaving = []
    for i, (out, buffer) in enumerate(zip(outs, made)):
        for section, there, device, here in found[i]:
            block = whole[device, :, here : here + 128].astype(F32)
            if section is None:
                buffer[:, there : there + 128] = block
            else:
                buffer[:, section, :, there : there + 128] = block.reshape(NA, R, 128)
        leaving.append(pltpu.make_async_copy(buffer, out, sems_out.at[i]))
        leaving[-1].start()
    for copy in leaving:
        copy.wait()


def place_kernel(lead, cols, *refs):
    sc, pieces, out, sems = refs[0], refs[1:9], refs[9], refs[10]
    copies = []
    for k, piece in enumerate(pieces):
        x_rel, y_rel, away = piece_place(sc, k)
        for n, (high_col, high_row) in enumerate(lead):
            row = high_row * 2 + ((sc[3] + y_rel) & 1)
            col = high_col * 4 + ((sc[1] & 3) ^ (x_rel * 2 + away))
            copies.append(pltpu.make_async_copy(piece.at[n], out.at[row * cols + col], sems.at[k, n]))
    for copy in copies:
        copy.start()
    for copy in copies:
        copy.wait()


def send_grads(grads):
    return lax.all_to_all(grads, BOTH, split_axis=0, concat_axis=0, tiled=True)


def sum_grads(mine, owners, part):
    summed = call(
        sum_kernel,
        jax.ShapeDtypeStruct((NA, R, part), BF),
        [owners, mine],
        [pltpu.SMEM, VMEM],
        [VMEM((NA, R, part), F32)],
    )
    return summed.reshape(NA * R, part)


def spread(sc, pieces, parts, maps, shapes):
    rows, cols = sizes()
    devices = rows * cols
    lead = lead_table(rows, cols)
    arrivals = pltpu.SemaphoreType.DMA((8, len(lead)))
    whole = (devices, NA * R, sum(parts))
    ins, spaces = [sc, *pieces], [pltpu.SMEM] + [pl.ANY] * 8
    if all(p % 128 == 0 for p in parts):
        return call(
            functools.partial(spread_kernel, lead, cols, parts, maps),
            [jax.ShapeDtypeStruct(x, F32) for x in shapes],
            ins,
            spaces,
            [VMEM(whole, BF)]
            + [VMEM(x, F32) for x in shapes]
            + [arrivals, pltpu.SemaphoreType.DMA((len(shapes),))],
            pl.ANY,
            56,
        )
    whole = call(
        functools.partial(place_kernel, lead, cols),
        jax.ShapeDtypeStruct(whole, BF),
        ins,
        spaces,
        [arrivals],
    )
    found = [[] for _ in shapes]
    base = 0
    for part, spans in zip(parts, maps):
        flat = jnp.swapaxes(whole[:, :, base : base + part], 0, 1).reshape(NA * R, devices * part)
        for out, section, there, start, width in spans:
            found[out].append((section or 0, there, flat[:, start : start + width].astype(F32)))
        base += part
    return [
        (
            jnp.concatenate([x for _, _, x in sorted(f, key=lambda e: e[:2])], axis=1)
            if len(shape) == 2
            else jnp.stack([x.reshape(NA, R, -1) for _, _, x in sorted(f, key=lambda e: e[:2])], 1)
        )
        for f, shape in zip(found, shapes)
    ]


def per_device(
    tokens_in,
    grad_out,
    keep_mask,
    adapter_index,
    ln_gain,
    ln_shift,
    w_qkv,
    bias_qv,
    w_proj,
    w_fc1,
    bias_fc1,
    w_fc2,
    bias_out,
    qkv_down,
    qkv_up,
    proj_down,
    proj_up,
    fc1_down,
    fc1_up,
    fc2_down,
    fc2_up,
):
    rows, cols = sizes()
    row, column = lax.axis_index("row"), lax.axis_index("col")
    assert adapter_index.shape[0] == cols and cols >= 4 and rows >= 2
    hid = D // cols
    n = 4 * hid
    blk = D // rows
    lead = lead_table(rows, cols)

    shard = jax.ShapeDtypeStruct((blk, n), BF)
    shard_q = call(prep_q_kernel, shard, [w_qkv, w_proj], [VMEM] * 2, mib=56)
    with jax.named_scope("q_high"):
        own_q, came_q = gather_high(shard_q)
    rows_in = call(
        prep_rows_kernel,
        jax.ShapeDtypeStruct((cols, 2 * SEQ + EXTRA, hid), BF),
        [after(tokens_in, shard_q).reshape(cols, SEQ, hid), grad_out.reshape(cols, SEQ, hid), bias_qv]
        + [bias_fc1.reshape(4, hid)],
        [VMEM] * 4,
        mib=56,
    )
    xa = lax.all_to_all(rows_in, "col", split_axis=0, concat_axis=0, tiled=True)
    adapter = lax.dynamic_index_in_dim(adapter_index, column, 0, keepdims=False)
    sc = jnp.stack([adapter, column, column % 2, row % 2]).astype(jnp.int32)
    up_qkv = jnp.swapaxes(lax.dynamic_index_in_dim(qkv_up, adapter, 0, keepdims=False), 0, 1)
    shard_a, shard_b, keep, closed = call(
        prep_f_kernel,
        [shard] * 2 + [jax.ShapeDtypeStruct((SEQ, 1), F32)] * 2,
        [sc, keep_mask, w_fc1, w_fc2],
        [pltpu.SMEM] + [VMEM] * 3,
    )

    own_q, shard_a, shard_b = after_all(
        (own_q, shard_a, shard_b), xa, keep, closed, sc, up_qkv, *came_q
    )
    with jax.named_scope("q_one"):
        one_q = swap(own_q, flip_one)
    with jax.named_scope("q_two"):
        two_q = swap(own_q, flip_two)
    with jax.named_scope("fa_high"):
        own_a, came_a = gather_high(shard_a)
    own_q, one_q, two_q = after_all((own_q, one_q, two_q), *came_a)
    with jax.named_scope("q_both"):
        both_q = swap(one_q, flip_two)
    with jax.named_scope("q_core"):
        away_q = [swap(p, flip_core) for p in (own_q, one_q, two_q)]
    both_q, own_a, shard_b = after_all((both_q, own_a, shard_b), *away_q)
    with jax.named_scope("q_core"):
        pieces_q = [own_q, one_q, two_q, both_q] + away_q + [swap(both_q, flip_core)]
    with jax.named_scope("fa_one"):
        one_a = swap(own_a, flip_one)
    with jax.named_scope("fa_two"):
        two_a = swap(own_a, flip_two)
    with jax.named_scope("fb_high"):
        own_b, came_b = gather_high(shard_b)

    def shaped(width, dtype, height=SEQ):
        return jax.ShapeDtypeStruct((height, width), dtype)

    big, small = shaped(D, BF), shaped(R, BF)
    scratch = weight_scratch(rows, cols, n)
    any_space = [pl.ANY] * 8
    n1, lat1, q, k, v, lse, att, lat2, middle, n2, lat3 = call(
        functools.partial(front_kernel, lead, cols),
        [
            big,
            small,
            big,
            big,
            big,
            jax.ShapeDtypeStruct((H // 2, 2, SEQ), F32),
            big,
            small,
            shaped(D, F32),
            big,
            small,
        ],
        [sc, *pieces_q, xa, closed, ln_gain, ln_shift, qkv_down, up_qkv, proj_down]
        + [proj_up]
        + [fc1_down, bias_out],
        [pltpu.SMEM] + any_space + [VMEM] * 10,
        scratch + [VMEM((SEQ, D), F32), VMEM((SEQ, D), F32)],
        mib=FRONT,
    )
    own_a, one_a, two_a = after_all((own_a, one_a, two_a), n1, *came_b)
    with jax.named_scope("fa_both"):
        both_a = swap(one_a, flip_two)
    with jax.named_scope("fa_core"):
        away_a = [swap(p, flip_core) for p in (own_a, one_a, two_a)]
    both_a, own_b = after_all((both_a, own_b), *away_a)
    with jax.named_scope("fa_core"):
        pieces_a = [own_a, one_a, two_a, both_a] + away_a + [swap(both_a, flip_core)]
    with jax.named_scope("fb_one"):
        one_b = swap(own_b, flip_one)
    with jax.named_scope("fb_two"):
        two_b = swap(own_b, flip_two)
    wide = shaped(D, F32)
    thin = shaped(R, F32)
    res, gn2, lat4, glat3, gr, early_a = call(
        functools.partial(ffn_a_kernel, lead, cols),
        [wide, wide, thin, thin, big, jax.ShapeDtypeStruct((rows * cols, R, FF // (rows * cols)), BF)],
        [sc, *pieces_a, xa, keep, n2, lat3, fc1_up, fc2_down, fc2_up],
        [pltpu.SMEM] + any_space + [VMEM] * 7,
        scratch,
        mib=FFN_A,
    )
    own_b, one_b, two_b = after_all((own_b, one_b, two_b), res)
    with jax.named_scope("fb_both"):
        both_b = swap(one_b, flip_two)
    with jax.named_scope("fb_core"):
        away_b = [swap(p, flip_core) for p in (own_b, one_b, two_b)]
        pieces_b = [own_b, one_b, two_b, both_b] + away_b + [swap(both_b, flip_core)]
    layer, gatt, gmid, grads_b = call(
        functools.partial(ffn_b_kernel, lead, cols),
        [jax.ShapeDtypeStruct((cols, SEQ, hid), BF), big, wide]
        + [jax.ShapeDtypeStruct((rows * cols, R, 12 * D // (rows * cols) + OWNER), BF)],
        [sc, *pieces_b, *pieces_q, xa, keep, ln_gain, n2, lat3, fc1_up, fc2_down, fc2_up]
        + [fc1_down, proj_down, proj_up, bias_out]
        + [middle, att, lat2, gr, res, gn2, lat4, glat3, early_a],
        [pltpu.SMEM] + any_space * 2 + [VMEM] * 21,
        scratch
        + [VMEM((cols, D, hid), BF), scratch[1]]
        + [VMEM((SEQ, D), F32), VMEM((SEQ, D), F32), VMEM((SEQ, R), F32), VMEM((SEQ, R), F32)],
        mib=FFN_B,
    )
    with jax.named_scope("grads_b_send"):
        mine_b = send_grads(grads_b)
        owners = mine_b[:, 0, mine_b.shape[2] - 1].astype(jnp.int32)
    gq, gk, gv, glat1, late = call(
        functools.partial(attention_back_kernel, cols),
        [big, big, big, small, jax.ShapeDtypeStruct((rows * cols, R, 4 * D // (rows * cols)), BF)],
        [sc, closed, q, k, v, lse, gatt, lat1, n1, up_qkv],
        [pltpu.SMEM] + [VMEM] * 9,
        mib=ATT,
    )
    with jax.named_scope("grads_c_send"):
        mine_c = send_grads(late)
    with jax.named_scope("grads_b"):
        own_b, _ = gather_high(sum_grads(after(mine_b, late), owners, mine_b.shape[2] - OWNER))
        own_c, _ = gather_high(sum_grads(mine_c, owners, mine_c.shape[2]))
        own = lane_join(own_b, own_c)
    gmid = after(gmid, own)
    sent = call(
        functools.partial(back_kernel, lead, cols),
        jax.ShapeDtypeStruct((cols, 2 * SEQ, hid), BF),
        [sc, *pieces_q, xa, ln_gain, gq, gk, gv, glat1, qkv_down, gmid, layer],
        [pltpu.SMEM] + any_space + [VMEM] * 9,
        scratch + [VMEM((SEQ, D), F32)],
        mib=BACK,
    )
    with jax.named_scope("grads"):
        one, two = swap(own, flip_one), swap(own, flip_two)
        both = swap(after(one, two, sent), flip_two)
        pieces = with_cores([own, one, two, both])
        half = FF // cols // 2
        map_a, map_b = (
            tuple(
                (out, None, (2 * block + part) * half, base + block * half, half)
                for out, base in ((0, 0), (1, FF // 2))
                for block in range(cols)
            )
            for part in (0, 1)
        )
        map_b = map_b + tuple((2 + i, None, 0, FF + i * D, D) for i in range(4))
        map_c = ((6, None, 0, 0, D),) + tuple((7, c, 0, (c + 1) * D, D) for c in range(3))
        parts = [early_a.shape[-1], mine_b.shape[-1] - early_a.shape[-1] - OWNER, mine_c.shape[-1]]
        shapes = [(NA * R, FF)] * 2 + [(NA * R, D)] * 5 + [(NA, 3, R, D)]
        sums = spread(sc, pieces, parts, [map_a, map_b, map_c], shapes)

    with jax.named_scope("rows_out"):
        sent = after(sent, both)
        rows_out = lax.all_to_all(sent, "col", split_axis=0, concat_axis=0, tiled=True)
    layer, grad_in = rows_out[:, :SEQ], rows_out[:, SEQ:]

    def split(table):
        return table.reshape((NA, R) + table.shape[1:])

    g_fc1_up, g_fc2_down, g_proj_down, g_proj_up, g_fc1_down, g_fc2_up = map(split, sums[:6])
    return (
        layer.reshape(cols * SEQ, hid),
        grad_in.reshape(cols * SEQ, hid),
        split(sums[6]),
        jnp.swapaxes(sums[7], 1, 2),
        g_proj_down,
        g_proj_up,
        g_fc1_down,
        g_fc1_up,
        g_fc2_down,
        g_fc2_up,
    )


def solution(mesh):
    return jax.shard_map(
        per_device,
        mesh=mesh,
        in_specs=(
            P("row", "col"),
            P("row", "col"),
            P("row", None),
            P("row"),
            P(),
            P(),
            P(None, "row", "col"),
            P(None, "col"),
            P("col", "row"),
            P("row", "col"),
            P("col"),
            P("col", "row"),
            P(),
            P(),
            P(),
            P(),
            P(),
            P(),
            P(),
            P(),
            P(),
        ),
        out_specs=(P("row", "col"), P("row", "col"), P(), P(), P(), P(), P(), P(), P(), P()),
        check_vma=False,
    )
```

```python
import functools

import jax
import jax.numpy as jnp
from jax import lax
from jax.experimental import pallas as pl
from jax.experimental.pallas import tpu as pltpu
from jax.sharding import PartitionSpec as P

D = 1024
H = 16
HD = 64
FF = 4096
BUF = 64
R = 16
NA = 8
SEQ = 320
PAIR = 2 * HD
EXTRA = 16
OWNER = 128
SPREAD = 56
FRONT, FFN_A, FFN_B, ATT, BACK = 56, 56, 56, 56, 56
BF = jnp.bfloat16
F32 = jnp.float32
BOTH = ("row", "col")
VMEM = pltpu.VMEM
NN = (((1,), (0,)), ((), ()))
NT = (((1,), (1,)), ((), ()))


def mm(left, right, dims=NN):
    return lax.dot_general(left, right, dims, preferred_element_type=F32)


def low(values):
    return values.astype(BF)


def norm_parts(values):
    row_mean = jnp.mean(values, axis=-1, keepdims=True)
    centered = values - row_mean
    variance = jnp.mean(centered * centered, axis=-1, keepdims=True)
    inverse = lax.rsqrt(variance + 1e-06)
    return (centered * inverse, inverse)


def norm_back(grad_normed, gain_row, unit_rows, inverse):
    scaled = grad_normed * gain_row
    first_mean = jnp.mean(scaled, axis=-1, keepdims=True)
    second_mean = jnp.mean(scaled * unit_rows, axis=-1, keepdims=True)
    return inverse * (scaled - first_mean - unit_rows * second_mean)


def call(kernel, outs, ins, spaces, scratch=(), out_space=VMEM, mib=4):
    return pl.pallas_call(
        kernel,
        out_shape=outs,
        in_specs=[pl.BlockSpec(memory_space=s) for s in spaces],
        out_specs=jax.tree.map(lambda _: pl.BlockSpec(memory_space=out_space), outs),
        scratch_shapes=list(scratch),
        compiler_params=pltpu.CompilerParams(vmem_limit_bytes=mib << 20),
        cost_estimate=pl.CostEstimate(flops=0, bytes_accessed=0, transcendentals=0),
    )(*ins)


def sizes():
    return lax.axis_size("row"), lax.axis_size("col")


def swap(block, flip):
    rows, cols = sizes()
    pairs = []
    for i in range(rows * cols):
        row, col = flip(i // cols, i % cols)
        pairs.append((i, row * cols + col))
    return lax.ppermute(block, BOTH, pairs)


def bits_of(size):
    return size.bit_length() - 1


def stack_kernel(which, *refs):
    parts, out, sems = refs[:-2], refs[-2], refs[-1]
    copies = [
        pltpu.make_async_copy(ref, out.at[which[0] ^ m], sems.at[m]) for m, ref in enumerate(parts)
    ]
    for copy in copies:
        copy.start()
    for copy in copies:
        copy.wait()


def stacked(parts, index):
    shape = parts[0].shape
    flat = [p.reshape((-1, shape[-1])) for p in parts]
    out = jax.ShapeDtypeStruct((len(parts),) + flat[0].shape, flat[0].dtype)
    made = call(
        stack_kernel,
        out,
        [index.reshape(1).astype(jnp.int32)] + flat,
        [pltpu.SMEM] + [pl.ANY] * len(parts),
        [pltpu.SemaphoreType.DMA((len(parts),))],
    )
    return made.reshape((len(parts),) + shape)


def group_join(block, axis, low_bit, width):
    parts = [block]
    for m in range(1, 1 << width):
        step = m << low_bit
        if axis == "row":
            parts.append(swap(block, lambda r, c: (r ^ step, c)))
        else:
            parts.append(swap(block, lambda r, c: (r, c ^ step)))
    index = (lax.axis_index(axis) >> low_bit) & ((1 << width) - 1)
    return stacked(parts, index), parts


def groups(top, bottom):
    out = []
    while top > bottom:
        width = min(2, top - bottom)
        out.append((top - width, width))
        top -= width
    return out


def early_groups(rows, cols):
    return [("row",) + g for g in groups(bits_of(rows), 1)] + [
        ("col",) + g for g in groups(bits_of(cols), 2)
    ]


def lead_table(rows, cols):
    table = [(0, 0)]
    for axis, bit, width in early_groups(rows, cols):
        shift = bit - (1 if axis == "row" else 2)
        new = []
        for value in range(1 << width):
            for high_col, high_row in table:
                if axis == "row":
                    new.append((high_col, high_row + (value << shift)))
                else:
                    new.append((high_col + (value << shift), high_row))
        table = new
    return table


def after(value, *others):
    return lax.optimization_barrier((value,) + others)[0]


def after_all(values, *others):
    return lax.optimization_barrier(tuple(values) + others)[: len(values)]


def gather_high(shard):
    rows, cols = sizes()
    block, parts = shard, []
    for axis, bit, width in early_groups(rows, cols):
        block, parts = group_join(block, axis, bit, width)
    return block.reshape((-1,) + shard.shape), parts[1:]


def lane_join_kernel(*refs):
    parts, out, sems = refs[:-2], refs[-2], refs[-1]
    copies, lane = [], 0
    for i, part in enumerate(parts):
        width = part.shape[-1]
        copies.append(pltpu.make_async_copy(part, out.at[:, :, lane : lane + width], sems.at[i]))
        lane += width
    for copy in copies:
        copy.start()
    for copy in copies:
        copy.wait()


def lane_join(*parts):
    if any(p.shape[-1] % 128 for p in parts):
        return jnp.concatenate(parts, axis=-1)
    shape = parts[0].shape[:-1] + (sum(p.shape[-1] for p in parts),)
    return call(
        lane_join_kernel,
        jax.ShapeDtypeStruct(shape, parts[0].dtype),
        parts,
        [pl.ANY] * len(parts),
        [pltpu.SemaphoreType.DMA((len(parts),))],
    )


def flip_one(r, c):
    return (r, c ^ 2) if c % 2 == 0 else (r ^ 1, c)


def flip_two(r, c):
    return (r ^ 1, c) if c % 2 == 0 else (r, c ^ 2)


def flip_core(r, c):
    return (r, c ^ 1)


def with_cores(pieces):
    return pieces + [swap(p, flip_core) for p in pieces]


def piece_place(sc, k):
    kind, away = k % 4, k // 4
    turn = (sc[2] + away) & 1
    return (0, 1 - turn, turn, 1)[kind], (0, turn, 1 - turn, 1)[kind], away


class Weights:
    def __init__(self, sc, pieces, w, sems, lead, first_lane=0):
        self.copies = []
        depth = pieces[0].shape[1]
        taken = pl.ds(first_lane, w.shape[2])
        for k, piece in enumerate(pieces):
            x_rel, y_rel, away = piece_place(sc, k)
            for n, (high_col, high_row) in enumerate(lead):
                slot = high_col * 4 + x_rel * 2 + away
                row = (high_row * 2 + ((sc[3] + y_rel) & 1)) * depth
                self.copies.append(
                    pltpu.make_async_copy(
                        piece.at[n, :, taken],
                        w.at[slot, pl.ds(pl.multiple_of(row, depth), depth), :],
                        sems.at[k, n],
                    )
                )

    def start(self):
        for copy in self.copies:
            copy.start()

    def wait(self, away=None):
        half = len(self.copies) // 2
        for copy in self.copies if away is None else self.copies[away * half : (away + 1) * half]:
            copy.wait()

    def slot(self, i, cols):
        half = cols // 2

        @pl.when(i == 0)
        def _():
            self.wait(0)

        @pl.when(i == half)
        def _():
            self.wait(1)

        return lax.rem(i, half) * 2 + i // half


def column_of(sc, slot):
    return (slot // 4) * 4 + ((sc[1] & 3) ^ (slot & 3))


def weight_scratch(rows, cols, n):
    lead = len(lead_table(rows, cols))
    return [VMEM((cols, D, n), BF), pltpu.SemaphoreType.DMA((8, lead))]


def put(ref, start, value, lane=0, spare=0):
    end = ref.shape[-1] - spare
    part = end - lane
    for i in range(value.shape[-1] // part):
        ref[start // part + i, :, lane:end] = value[:, i * part : (i + 1) * part]


def lanes(start, width):
    return pl.ds(pl.multiple_of(start, width), width)


def prep_q_kernel(tokens, grads, bias_qv, bias_f, wq, wp, rows, out):
    hid = wq.shape[2]
    seq = tokens.shape[1]
    for c in range(tokens.shape[0]):
        rows[c, :seq] = tokens[c]
        rows[c, seq : 2 * seq] = grads[c]
        rows[c, 2 * seq : 2 * seq + 2] = bias_qv[...]
        for i in range(4):
            rows[c, 2 * seq + 2 + i : 2 * seq + 3 + i] = bias_f[:, i * hid : (i + 1) * hid]
    for c in range(3):
        out[:, c * hid : (c + 1) * hid] = wq[c]
    out[:, 3 * hid :] = low(wp[...].astype(F32).T)


def prep_f_kernel(sc, mask, w1, w2, out_a, out_b, keep, closed):
    row = mask[pl.ds(sc[1], 1), :].astype(F32)
    row = jnp.concatenate([jnp.ones((1, BUF), F32), row], axis=1)
    column = jnp.broadcast_to(row, (8, SEQ)).T[:, :1]
    keep[...] = column
    closed[...] = 1.0 - column
    half = w1.shape[1] // 2
    out_a[:, :half] = w1[:, :half]
    out_b[:, :half] = w1[:, half:]
    out_a[:, half:] = low(w2[:half].astype(F32).T)
    out_b[:, half:] = low(w2[half:].astype(F32).T)


def fetch(sems, *pairs):
    copies = [pltpu.make_async_copy(src, dst, sems.at[i]) for i, (src, dst) in enumerate(pairs)]
    for copy in copies:
        copy.start()
    return copies


def rows_at(xa, start, height):
    return xa.at[:, pl.ds(start, height), :]


def across(ref, cols):
    return jnp.concatenate([ref[c] for c in range(cols)], axis=1).astype(F32)


def both_heads(pair):
    left = lax.broadcasted_iota(jnp.int32, (1, PAIR), 1) < HD
    zero = jnp.zeros_like(pair)
    return jnp.concatenate([jnp.where(left, pair, zero), jnp.where(left, zero, pair)], axis=0)


def own_heads(made, scale=1.0):
    both = jnp.concatenate([made[:HD, :SEQ], made[HD:, SEQ:]], axis=0)
    return low(both.T * scale)


def front_kernel(lead, cols, *refs):
    sc = refs[0]
    pieces = refs[1:9]
    (xa, closed, gain, shift, q_down, q_up, p_down, p_up, f_down, bias_out) = refs[9:19]
    (n1, lat1, q, k, v, lse, att, lat2, middle, n2, lat3) = refs[19:30]
    w, sems, hidden, branch, xs, bs, row_qd, row_pd, row_pu, row_fd, sems_f = refs[30:]
    a = sc[0]
    hid = D // cols
    first = fetch(
        sems_f,
        (rows_at(xa, 0, SEQ), xs),
        (q_down.at[a], row_qd),
        (rows_at(xa, 2 * SEQ, EXTRA), bs),
        (p_down.at[a], row_pd),
        (p_up.at[a], row_pu),
        (f_down.at[a], row_fd),
    )
    weights = Weights(sc, pieces, w, sems, lead)
    weights.start()
    first[0].wait()
    x = across(xs, cols)
    hidden[...] = x
    unit, _ = norm_parts(x)
    n1[...] = low(unit * gain[0:1] + shift[0:1])
    for copy in first[1:]:
        copy.wait()
    lat1[...] = low(mm(n1[...], row_qd[...], NT))

    def project(i, _):
        slot = weights.slot(i, cols)
        block = column_of(sc, slot)
        up = jnp.concatenate([q_up[c, :, lanes(block * hid, hid)] for c in range(3)], axis=1)
        made = mm(n1[...], w[slot, :, : 3 * hid]) + mm(lat1[...], up)
        bias_q = bs[block, 0:1, :].astype(F32)
        bias_v = bs[block, 1:2, :].astype(F32)
        at = lanes(slot * hid, hid)
        q[:, at] = low(made[:, :hid] + bias_q) * jnp.asarray(0.125, BF)
        k[:, at] = low(made[:, hid : 2 * hid])
        v[:, at] = low(made[:, 2 * hid :] + bias_v)
        return 0

    lax.fori_loop(0, cols, project, 0)
    shut = closed[...] > 0.5

    def attend(pair, _):
        at = lanes(pair * PAIR, PAIR)
        v_t = low(v[:, at].astype(F32).T)
        s = jnp.where(shut, -1e30, mm(k[:, at], both_heads(q[:, at]), NT))
        top = jnp.max(s, axis=0, keepdims=True)
        e = jnp.exp(s - top)
        total = jnp.sum(e, axis=0, keepdims=True)
        lse[pair] = top + jnp.log(total)
        att[:, at] = own_heads(mm(v_t, low(e * (1.0 / total))))
        return 0

    lax.fori_loop(0, H // 2, attend, 0, unroll=4)

    def down_two(slot, acc):
        block = column_of(sc, slot)
        return acc + mm(att[:, lanes(slot * hid, hid)], row_pd[:, lanes(block * hid, hid)], NT)

    lat2[...] = low(lax.fori_loop(0, cols, down_two, jnp.zeros((SEQ, R), F32)))
    branch[...] = mm(lat2[...], row_pu[...]) + bias_out[0:1].astype(F32)

    def out_proj(slot, _):
        branch[...] += mm(att[:, lanes(slot * hid, hid)], w[slot, :, 3 * hid :], NT)
        return 0

    lax.fori_loop(0, cols, out_proj, 0)
    mid = hidden[...] + branch[...]
    middle[...] = mid
    unit, _ = norm_parts(mid)
    n2[...] = low(unit * gain[1:2] + shift[1:2])
    lat3[...] = low(mm(n2[...], row_fd[...], NT))


def ffn_steps(weights, sc, part, cols, w, bs, n2, lat3, gr, glat4, up_1, down_2, acc, early, lane=0, spare=0):
    res, gn2, lat4, glat3 = acc
    hid = D // cols
    ffn = FF // cols
    half = ffn // 2
    glat4_t = low(glat4.astype(F32).T)
    lat3_t = low(lat3[...].astype(F32).T)

    def step(i, _):
        slot = weights.slot(i, cols)
        block = column_of(sc, slot)
        at = pl.ds(pl.multiple_of(block * ffn + part * half, half), half)
        bias = jnp.concatenate(
            [bs[block, 2 + 2 * part + i : 3 + 2 * part + i, :] for i in range(2)], axis=1
        ).astype(F32)
        up, down = up_1[:, at], down_2[:, at]
        w1, w2 = w[slot, :, :half], w[slot, :, half:]
        pre = mm(n2[...], w1) + mm(lat3[...], up) + bias
        back = mm(gr[...], w2) + mm(glat4, down)
        cumulative = 0.5 * (1.0 + lax.erf(pre * 0.7071067811865476))
        activated = low(pre * cumulative)
        slope = cumulative + pre * jnp.exp(-0.5 * pre * pre) * 0.3989422804014327
        grad_pre = low(back * slope)
        lat4[...] += mm(activated, down, NT)
        glat3[...] += mm(grad_pre, up, NT)
        res[...] += mm(activated, w2, NT)
        gn2[...] += mm(grad_pre, w1, NT)
        put(early, block * half, low(mm(lat3_t, grad_pre)), lane, spare)
        put(early, FF // 2 + block * half, low(mm(glat4_t, activated)), lane, spare)
        return 0

    lax.fori_loop(0, cols, step, 0)


def ffn_a_kernel(lead, cols, *refs):
    sc = refs[0]
    pieces = refs[1:9]
    xa, keep, n2, lat3, up_1, down_2, up_2 = refs[9:16]
    res, gn2, lat4, glat3, gr, early = refs[16:22]
    w, sems, gs, bs, row_u1, row_d2, row_u2, sems_f = refs[22:]
    a = sc[0]
    first = fetch(
        sems_f,
        (rows_at(xa, SEQ, SEQ), gs),
        (up_2.at[a], row_u2),
        (rows_at(xa, 2 * SEQ, EXTRA), bs),
        (up_1.at[a], row_u1),
        (down_2.at[a], row_d2),
    )
    weights = Weights(sc, pieces, w, sems, lead)
    weights.start()
    first[0].wait()
    gr[...] = low(across(gs, cols) * keep[...])
    for copy in first[1:]:
        copy.wait()
    glat4 = low(mm(gr[...], row_u2[...], NT))
    res[...] = jnp.zeros_like(res)
    gn2[...] = jnp.zeros_like(gn2)
    lat4[...] = jnp.zeros_like(lat4)
    glat3[...] = jnp.zeros_like(glat3)
    ffn_steps(
        weights, sc, 0, cols, w, bs, n2, lat3, gr, glat4, row_u1, row_d2, (res, gn2, lat4, glat3), early
    )


def ffn_b_kernel(lead, cols, *refs):
    sc = refs[0]
    pieces = refs[1:9]
    own_q = refs[9:17]
    (xa, keep, gain, n2, lat3, up_1, down_2, up_2, f_down, p_down, p_up, bias_out) = refs[17:29]
    (middle, att, lat2, gr, res_in, gn2_in, lat4_in, glat3_in, early_in) = refs[29:38]
    layer, gatt, gmid, early = refs[38:42]
    w, sems, wp, sems_p, res, gn2, lat4, glat3 = refs[42:50]
    bs, row_u1, row_d2, row_u2, row_fd, row_pd, row_pu, mid_s, att_s, res_s, gn2_s, early_s = refs[50:62]
    sems_f = refs[62]
    lane = early_in.shape[-1]
    a = sc[0]
    first = fetch(
        sems_f,
        (up_2.at[a], row_u2),
        (rows_at(xa, 2 * SEQ, EXTRA), bs),
        (up_1.at[a], row_u1),
        (down_2.at[a], row_d2),
    )
    early[:, :, early.shape[2] - OWNER :] = low(jnp.full((early.shape[0], R, OWNER), sc[0], F32))
    weights = Weights(sc, pieces, w, sems, lead)
    weights.start()
    proj = Weights(sc, own_q, wp, sems_p, lead, 3 * D // cols)
    last = fetch(
        sems_f.at[pl.ds(4, 8)],
        (res_in, res_s),
        (middle, mid_s),
        (gn2_in, gn2_s),
        (f_down.at[a], row_fd),
        (p_up.at[a], row_pu),
        (p_down.at[a], row_pd),
        (att, att_s),
        (early_in, early_s),
    )
    proj.start()
    hid = D // cols
    for copy in first:
        copy.wait()
    glat4 = low(mm(gr[...], row_u2[...], NT))
    res[...] = jnp.zeros_like(res)
    gn2[...] = jnp.zeros_like(gn2)
    lat4[...] = lat4_in[...]
    glat3[...] = glat3_in[...]
    ffn_steps(
        weights, sc, 1, cols, w, bs, n2, lat3, gr, glat4, row_u1, row_d2, (res, gn2, lat4, glat3), early, lane, OWNER
    )
    for copy in last:
        copy.wait()
    early[:, :, :lane] = early_s[...]
    mid = mid_s[...]
    lat4_low = low(lat4[...])
    out = low(
        keep[...]
        * (mid + (res_s[...] + res[...]) + mm(lat4_low, row_u2[...]) + bias_out[1:2].astype(F32))
    )
    for c in range(cols):
        layer[c] = out[:, c * hid : (c + 1) * hid]
    glat3_low = low(glat3[...])
    grad_normed = gn2_s[...] + gn2[...] + mm(glat3_low, row_fd[...])
    unit, inverse = norm_parts(mid)
    grad_middle = gr[...].astype(F32) + norm_back(grad_normed, gain[1:2], unit, inverse)
    gmid[...] = grad_middle
    gb = low(grad_middle)
    glat2 = low(mm(gb, row_pu[...], NT))
    glat2_t = low(glat2.astype(F32).T)
    put(early, FF + D, low(mm(low(lat2[...].astype(F32).T), gb)), lane, OWNER)
    put(early, FF + 2 * D, low(mm(low(glat3_low.astype(F32).T), n2[...])), lane, OWNER)
    put(early, FF + 3 * D, low(mm(low(lat4_low.astype(F32).T), gr[...])), lane, OWNER)
    proj.wait()

    def step(slot, _):
        block = column_of(sc, slot)
        here = lanes(slot * hid, hid)
        there = lanes(block * hid, hid)
        gatt[:, here] = low(mm(gb, wp[slot]) + mm(glat2, row_pd[:, there]))
        put(early, FF + block * hid, low(mm(glat2_t, att_s[:, here])), lane, OWNER)
        return 0

    lax.fori_loop(0, cols, step, 0)


def attention_back_kernel(cols, *refs):
    sc = refs[0]
    closed, q, k, v, lse, gatt, lat1, n1, q_up = refs[1:10]
    gq, gk, gv, glat1, late = refs[10:15]
    a = sc[0]
    hid = D // cols
    shut = closed[...] > 0.5

    def attend(pair, _):
        at = lanes(pair * PAIR, PAIR)
        kp = k[:, at]
        k_t = low(kp.astype(F32).T)
        q_both, g_both = both_heads(q[:, at]), both_heads(gatt[:, at])
        s = jnp.where(shut, -1e30, mm(kp, q_both, NT))
        soft = jnp.exp(s - lse[pair])
        grad_soft = mm(v[:, at], g_both, NT)
        total = jnp.sum(grad_soft * soft, axis=0, keepdims=True)
        grad_scores = low(soft * (grad_soft - total))
        gq[:, at] = own_heads(mm(k_t, grad_scores), 0.125)
        gk[:, at] = low(mm(grad_scores, q_both))
        gv[:, at] = low(mm(low(soft), g_both))
        return 0

    lax.fori_loop(0, H // 2, attend, 0, unroll=4)
    lat1_t = low(lat1[...].astype(F32).T)

    def step(slot, acc):
        block = column_of(sc, slot)
        here = lanes(slot * hid, hid)
        there = lanes(block * hid, hid)
        for c, g in enumerate((gq, gk, gv)):
            grad = g[:, here]
            acc = acc + mm(grad, q_up[c, :, there], NT)
            put(late, (c + 1) * D + block * hid, low(mm(lat1_t, grad)))
        return acc

    made = low(lax.fori_loop(0, cols, step, jnp.zeros((SEQ, R), F32)))
    glat1[...] = made
    put(late, 0, low(mm(low(made.astype(F32).T), n1[...])))


def back_kernel(lead, cols, *refs):
    sc = refs[0]
    pieces = refs[1:9]
    xa, gain, gq, gk, gv, glat1, q_down, gmid, layer = refs[9:18]
    out = refs[18]
    w, sems, acc, xs, row_qd, gmid_s, sems_f = refs[19:]
    first = fetch(
        sems_f,
        (rows_at(xa, 0, SEQ), xs),
        (q_down.at[sc[0]], row_qd),
        (gmid, gmid_s),
        (layer, rows_at(out, 0, SEQ)),
    )
    weights = Weights(sc, pieces, w, sems, lead)
    weights.start()
    hid = D // cols
    for copy in first:
        copy.wait()
    acc[...] = mm(glat1[...], row_qd[...])
    x = across(xs, cols)
    unit, inverse = norm_parts(x)

    def step(i, _):
        slot = weights.slot(i, cols)
        here = lanes(slot * hid, hid)
        grad = jnp.concatenate([gq[:, here], gk[:, here], gv[:, here]], axis=1)
        acc[...] += mm(grad, w[slot, :, : 3 * hid], NT)
        return 0

    lax.fori_loop(0, cols, step, 0)
    made = low(gmid_s[...] + norm_back(acc[...], gain[0:1], unit, inverse))
    for c in range(cols):
        out[c, SEQ:] = made[:, c * hid : (c + 1) * hid]


def sum_kernel(owners, mine, out, acc):
    acc[...] = jnp.zeros_like(acc)
    for d in range(mine.shape[0]):
        acc[owners[d]] += mine[d, :, : acc.shape[2]].astype(F32)
    out[...] = low(acc[...])


def spread_kernel(lead, cols, parts, maps, *refs):
    sc, pieces = refs[0], refs[1:9]
    count = (len(refs) - 11) // 2
    outs, whole, made = refs[9 : 9 + count], refs[9 + count], refs[10 + count : 10 + 2 * count]
    sems_in, sems_out = refs[10 + 2 * count :]
    copies = []
    for k, piece in enumerate(pieces):
        x_rel, y_rel, away = piece_place(sc, k)
        for n, (high_col, high_row) in enumerate(lead):
            row = high_row * 2 + ((sc[3] + y_rel) & 1)
            col = high_col * 4 + ((sc[1] & 3) ^ (x_rel * 2 + away))
            copies.append(
                pltpu.make_async_copy(piece.at[n], whole.at[row * cols + col], sems_in.at[k, n])
            )
    for copy in copies:
        copy.start()
    for copy in copies:
        copy.wait()
    found = [[] for _ in outs]
    base = 0
    for part, spans in zip(parts, maps):
        for out, section, there, start, width in spans:
            for lane in range(0, width, 128):
                at = start + lane
                found[out].append((section, there + lane, at // part, base + at % part))
        base += part
    leaving = []
    for i, (out, buffer) in enumerate(zip(outs, made)):
        for section, there, device, here in found[i]:
            block = whole[device, :, here : here + 128].astype(F32)
            if section is None:
                buffer[:, there : there + 128] = block
            else:
                buffer[:, section, :, there : there + 128] = block.reshape(NA, R, 128)
        leaving.append(pltpu.make_async_copy(buffer, out, sems_out.at[i]))
        leaving[-1].start()
    for copy in leaving:
        copy.wait()


def place_kernel(lead, cols, *refs):
    sc, pieces, out, sems = refs[0], refs[1:9], refs[9], refs[10]
    copies = []
    for k, piece in enumerate(pieces):
        x_rel, y_rel, away = piece_place(sc, k)
        for n, (high_col, high_row) in enumerate(lead):
            row = high_row * 2 + ((sc[3] + y_rel) & 1)
            col = high_col * 4 + ((sc[1] & 3) ^ (x_rel * 2 + away))
            copies.append(pltpu.make_async_copy(piece.at[n], out.at[row * cols + col], sems.at[k, n]))
    for copy in copies:
        copy.start()
    for copy in copies:
        copy.wait()


def send_grads(grads):
    return lax.all_to_all(grads, BOTH, split_axis=0, concat_axis=0, tiled=True)


def sum_grads(mine, owners, part):
    summed = call(
        sum_kernel,
        jax.ShapeDtypeStruct((NA, R, part), BF),
        [owners, mine],
        [pltpu.SMEM, VMEM],
        [VMEM((NA, R, part), F32)],
    )
    return summed.reshape(NA * R, part)


def spread(sc, pieces, parts, maps, shapes):
    rows, cols = sizes()
    devices = rows * cols
    lead = lead_table(rows, cols)
    arrivals = pltpu.SemaphoreType.DMA((8, len(lead)))
    whole = (devices, NA * R, sum(parts))
    ins, spaces = [sc, *pieces], [pltpu.SMEM] + [pl.ANY] * 8
    if all(p % 128 == 0 for p in parts):
        return call(
            functools.partial(spread_kernel, lead, cols, parts, maps),
            [jax.ShapeDtypeStruct(x, F32) for x in shapes],
            ins,
            spaces,
            [VMEM(whole, BF)]
            + [VMEM(x, F32) for x in shapes]
            + [arrivals, pltpu.SemaphoreType.DMA((len(shapes),))],
            pl.ANY,
            SPREAD,
        )
    whole = call(
        functools.partial(place_kernel, lead, cols),
        jax.ShapeDtypeStruct(whole, BF),
        ins,
        spaces,
        [arrivals],
    )
    found = [[] for _ in shapes]
    base = 0
    for part, spans in zip(parts, maps):
        flat = jnp.swapaxes(whole[:, :, base : base + part], 0, 1).reshape(NA * R, devices * part)
        for out, section, there, start, width in spans:
            found[out].append((section or 0, there, flat[:, start : start + width].astype(F32)))
        base += part
    return [
        (
            jnp.concatenate([x for _, _, x in sorted(f, key=lambda e: e[:2])], axis=1)
            if len(shape) == 2
            else jnp.stack([x.reshape(NA, R, -1) for _, _, x in sorted(f, key=lambda e: e[:2])], 1)
        )
        for f, shape in zip(found, shapes)
    ]


def per_device(
    tokens_in,
    grad_out,
    keep_mask,
    adapter_index,
    ln_gain,
    ln_shift,
    w_qkv,
    bias_qv,
    w_proj,
    w_fc1,
    bias_fc1,
    w_fc2,
    bias_out,
    qkv_down,
    qkv_up,
    proj_down,
    proj_up,
    fc1_down,
    fc1_up,
    fc2_down,
    fc2_up,
):
    rows, cols = sizes()
    row, column = lax.axis_index("row"), lax.axis_index("col")
    assert adapter_index.shape[0] == cols and cols >= 4 and rows >= 2
    hid = D // cols
    n = 4 * hid
    blk = D // rows
    lead = lead_table(rows, cols)

    shard = jax.ShapeDtypeStruct((blk, n), BF)
    rows_in, shard_q = call(
        prep_q_kernel,
        [jax.ShapeDtypeStruct((cols, 2 * SEQ + EXTRA, hid), BF), shard],
        [tokens_in.reshape(cols, SEQ, hid), grad_out.reshape(cols, SEQ, hid), bias_qv]
        + [bias_fc1.reshape(1, n), w_qkv, w_proj],
        [VMEM] * 6,
        mib=56,
    )
    with jax.named_scope("q_high"):
        own_q, came_q = gather_high(shard_q)
    xa = lax.all_to_all(rows_in, "col", split_axis=0, concat_axis=0, tiled=True)
    adapter = lax.dynamic_index_in_dim(adapter_index, column, 0, keepdims=False)
    sc = jnp.stack([adapter, column, column % 2, row % 2]).astype(jnp.int32)
    up_qkv = jnp.swapaxes(lax.dynamic_index_in_dim(qkv_up, adapter, 0, keepdims=False), 0, 1)
    shard_a, shard_b, keep, closed = call(
        prep_f_kernel,
        [shard] * 2 + [jax.ShapeDtypeStruct((SEQ, 1), F32)] * 2,
        [sc, keep_mask, w_fc1, w_fc2],
        [pltpu.SMEM] + [VMEM] * 3,
    )

    own_q, shard_a, shard_b = after_all(
        (own_q, shard_a, shard_b), xa, keep, closed, sc, up_qkv, *came_q
    )
    with jax.named_scope("q_one"):
        one_q = swap(own_q, flip_one)
    with jax.named_scope("q_two"):
        two_q = swap(own_q, flip_two)
    with jax.named_scope("fa_high"):
        own_a, came_a = gather_high(shard_a)
    own_q, one_q, two_q = after_all((own_q, one_q, two_q), *came_a)
    with jax.named_scope("q_both"):
        both_q = swap(one_q, flip_two)
    with jax.named_scope("q_core"):
        away_q = [swap(p, flip_core) for p in (own_q, one_q, two_q)]
    own_a, shard_b = after_all((own_a, shard_b), *away_q)
    with jax.named_scope("q_core"):
        pieces_q = [own_q, one_q, two_q, both_q] + away_q + [swap(both_q, flip_core)]
    with jax.named_scope("fa_one"):
        one_a = swap(own_a, flip_one)
    with jax.named_scope("fa_two"):
        two_a = swap(own_a, flip_two)
    with jax.named_scope("fb_high"):
        own_b, came_b = gather_high(shard_b)

    def shaped(width, dtype, height=SEQ):
        return jax.ShapeDtypeStruct((height, width), dtype)

    big, small = shaped(D, BF), shaped(R, BF)
    scratch = weight_scratch(rows, cols, n)
    rows_space, bias_space = VMEM((cols, SEQ, hid), BF), VMEM((cols, EXTRA, hid), BF)
    any_space = [pl.ANY] * 8
    n1, lat1, q, k, v, lse, att, lat2, middle, n2, lat3 = call(
        functools.partial(front_kernel, lead, cols),
        [
            big,
            small,
            big,
            big,
            big,
            jax.ShapeDtypeStruct((H // 2, 1, 2 * SEQ), F32),
            big,
            small,
            shaped(D, F32),
            big,
            small,
        ],
        [sc, *pieces_q, xa, closed, ln_gain, ln_shift, qkv_down, up_qkv, proj_down]
        + [proj_up]
        + [fc1_down, bias_out],
        [pltpu.SMEM] + any_space + [pl.ANY] + [VMEM] * 3 + [pl.ANY, VMEM] + [pl.ANY] * 3 + [VMEM],
        scratch
        + [VMEM((SEQ, D), F32), VMEM((SEQ, D), F32), rows_space, bias_space]
        + [VMEM((R, D), BF)] * 4
        + [pltpu.SemaphoreType.DMA((6,))],
        mib=FRONT,
    )
    own_a, one_a, two_a = after_all((own_a, one_a, two_a), n1, *came_b)
    with jax.named_scope("fa_both"):
        both_a = swap(one_a, flip_two)
    with jax.named_scope("fa_core"):
        away_a = [swap(p, flip_core) for p in (own_a, one_a, two_a)]
    own_b = after(own_b, *away_a)
    with jax.named_scope("fa_core"):
        pieces_a = [own_a, one_a, two_a, both_a] + away_a + [swap(both_a, flip_core)]
    with jax.named_scope("fb_one"):
        one_b = swap(own_b, flip_one)
    with jax.named_scope("fb_two"):
        two_b = swap(own_b, flip_two)
    wide = shaped(D, F32)
    thin = shaped(R, F32)
    res, gn2, lat4, glat3, gr, early_a = call(
        functools.partial(ffn_a_kernel, lead, cols),
        [wide, wide, thin, thin, big, jax.ShapeDtypeStruct((rows * cols, R, FF // (rows * cols)), BF)],
        [sc, *pieces_a, xa, keep, n2, lat3, fc1_up, fc2_down, fc2_up],
        [pltpu.SMEM] + any_space + [pl.ANY] + [VMEM] * 3 + [pl.ANY] * 3,
        scratch
        + [rows_space, bias_space, VMEM((R, FF), BF), VMEM((R, FF), BF), VMEM((R, D), BF)]
        + [pltpu.SemaphoreType.DMA((5,))],
        mib=FFN_A,
    )
    own_b, one_b, two_b = after_all((own_b, one_b, two_b), res)
    with jax.named_scope("fb_both"):
        both_b = swap(one_b, flip_two)
    with jax.named_scope("fb_core"):
        away_b = [swap(p, flip_core) for p in (own_b, one_b, two_b)]
        pieces_b = [own_b, one_b, two_b, both_b] + away_b + [swap(both_b, flip_core)]
    layer, gatt, gmid, grads_b = call(
        functools.partial(ffn_b_kernel, lead, cols),
        [jax.ShapeDtypeStruct((cols, SEQ, hid), BF), big, wide]
        + [jax.ShapeDtypeStruct((rows * cols, R, 12 * D // (rows * cols) + OWNER), BF)],
        [sc, *pieces_b, *pieces_q, xa, keep, ln_gain, n2, lat3, fc1_up, fc2_down, fc2_up]
        + [fc1_down, proj_down, proj_up, bias_out]
        + [middle, att, lat2, gr, res, gn2, lat4, glat3, early_a],
        [pltpu.SMEM]
        + any_space * 2
        + [pl.ANY, VMEM, VMEM, VMEM, VMEM]
        + [pl.ANY] * 6
        + [VMEM, pl.ANY, pl.ANY, VMEM, VMEM, pl.ANY, pl.ANY, VMEM, VMEM, pl.ANY],
        scratch
        + [VMEM((cols, D, hid), BF), scratch[1]]
        + [VMEM((SEQ, D), F32), VMEM((SEQ, D), F32), VMEM((SEQ, R), F32), VMEM((SEQ, R), F32)]
        + [bias_space, VMEM((R, FF), BF), VMEM((R, FF), BF)]
        + [VMEM((R, D), BF)] * 4
        + [VMEM((SEQ, D), F32), VMEM((SEQ, D), BF), VMEM((SEQ, D), F32), VMEM((SEQ, D), F32)]
        + [VMEM(early_a.shape, BF), pltpu.SemaphoreType.DMA((12,))],
        mib=FFN_B,
    )
    with jax.named_scope("grads_b_send"):
        mine_b = send_grads(grads_b)
        owners = mine_b[:, 0, mine_b.shape[2] - 1].astype(jnp.int32)
    gq, gk, gv, glat1, late = call(
        functools.partial(attention_back_kernel, cols),
        [big, big, big, small, jax.ShapeDtypeStruct((rows * cols, R, 4 * D // (rows * cols)), BF)],
        [sc, closed, q, k, v, lse, gatt, lat1, n1, up_qkv],
        [pltpu.SMEM] + [VMEM] * 9,
        mib=ATT,
    )
    with jax.named_scope("grads_c_send"):
        mine_c = send_grads(late)
    with jax.named_scope("grads_b"):
        own_b, _ = gather_high(sum_grads(after(mine_b, late), owners, mine_b.shape[2] - OWNER))
        own_c, _ = gather_high(sum_grads(mine_c, owners, mine_c.shape[2]))
        own = lane_join(own_b, own_c)
    gmid = after(gmid, own)
    sent = call(
        functools.partial(back_kernel, lead, cols),
        jax.ShapeDtypeStruct((cols, 2 * SEQ, hid), BF),
        [sc, *pieces_q, xa, ln_gain, gq, gk, gv, glat1, qkv_down, gmid, layer],
        [pltpu.SMEM] + any_space + [pl.ANY] + [VMEM] * 5 + [pl.ANY] * 3,
        scratch
        + [VMEM((SEQ, D), F32), rows_space, VMEM((R, D), BF), VMEM((SEQ, D), F32)]
        + [pltpu.SemaphoreType.DMA((4,))],
        mib=BACK,
    )
    with jax.named_scope("grads"):
        one, two = swap(own, flip_one), swap(own, flip_two)
        own, one, two = after_all((own, one, two), sent)
        both = swap(one, flip_two)
        pieces = with_cores([own, one, two, both])
        half = FF // cols // 2
        map_a, map_b = (
            tuple(
                (out, None, (2 * block + part) * half, base + block * half, half)
                for out, base in ((0, 0), (1, FF // 2))
                for block in range(cols)
            )
            for part in (0, 1)
        )
        map_b = map_b + tuple((2 + i, None, 0, FF + i * D, D) for i in range(4))
        map_c = ((6, None, 0, 0, D),) + tuple((7, c, 0, (c + 1) * D, D) for c in range(3))
        parts = [early_a.shape[-1], mine_b.shape[-1] - early_a.shape[-1] - OWNER, mine_c.shape[-1]]
        shapes = [(NA * R, FF)] * 2 + [(NA * R, D)] * 5 + [(NA, 3, R, D)]
        sums = spread(sc, pieces, parts, [map_a, map_b, map_c], shapes)

    with jax.named_scope("rows_out"):
        sent = after(sent, pieces[4])
        rows_out = lax.all_to_all(sent, "col", split_axis=0, concat_axis=0, tiled=True)
    layer, grad_in = rows_out[:, :SEQ], rows_out[:, SEQ:]

    def split(table):
        return table.reshape((NA, R) + table.shape[1:])

    g_fc1_up, g_fc2_down, g_proj_down, g_proj_up, g_fc1_down, g_fc2_up = map(split, sums[:6])
    return (
        layer.reshape(cols * SEQ, hid),
        grad_in.reshape(cols * SEQ, hid),
        split(sums[6]),
        jnp.swapaxes(sums[7], 1, 2),
        g_proj_down,
        g_proj_up,
        g_fc1_down,
        g_fc1_up,
        g_fc2_down,
        g_fc2_up,
    )


def solution(mesh):
    return jax.shard_map(
        per_device,
        mesh=mesh,
        in_specs=(
            P("row", "col"),
            P("row", "col"),
            P("row", None),
            P("row"),
            P(),
            P(),
            P(None, "row", "col"),
            P(None, "col"),
            P("col", "row"),
            P("row", "col"),
            P("col"),
            P("col", "row"),
            P(),
            P(),
            P(),
            P(),
            P(),
            P(),
            P(),
            P(),
            P(),
        ),
        out_specs=(P("row", "col"), P("row", "col"), P(), P(), P(), P(), P(), P(), P(), P()),
        check_vma=False,
    )
```

```python
import functools

import jax
import jax.numpy as jnp
from jax import lax
from jax.experimental import pallas as pl
from jax.experimental.pallas import tpu as pltpu
from jax.sharding import PartitionSpec as P

D = 1024
H = 16
HD = 64
FF = 4096
BUF = 64
R = 16
NA = 8
SEQ = 320
PAIR = 2 * HD
EXTRA = 16
SPREAD = 56
FRONT, FFN_A, FFN_B, ATT, BACK = 56, 56, 56, 56, 56
BF = jnp.bfloat16
F32 = jnp.float32
BOTH = ("row", "col")
VMEM = pltpu.VMEM
NN = (((1,), (0,)), ((), ()))
NT = (((1,), (1,)), ((), ()))


def mm(left, right, dims=NN):
    return lax.dot_general(left, right, dims, preferred_element_type=F32)


def low(values):
    return values.astype(BF)


def norm_parts(values):
    row_mean = jnp.mean(values, axis=-1, keepdims=True)
    centered = values - row_mean
    variance = jnp.mean(centered * centered, axis=-1, keepdims=True)
    inverse = lax.rsqrt(variance + 1e-06)
    return (centered * inverse, inverse)


def norm_back(grad_normed, gain_row, unit_rows, inverse):
    scaled = grad_normed * gain_row
    first_mean = jnp.mean(scaled, axis=-1, keepdims=True)
    second_mean = jnp.mean(scaled * unit_rows, axis=-1, keepdims=True)
    return inverse * (scaled - first_mean - unit_rows * second_mean)


def call(kernel, outs, ins, spaces, scratch=(), out_space=VMEM, mib=4):
    return pl.pallas_call(
        kernel,
        out_shape=outs,
        in_specs=[pl.BlockSpec(memory_space=s) for s in spaces],
        out_specs=jax.tree.map(lambda _: pl.BlockSpec(memory_space=out_space), outs),
        scratch_shapes=list(scratch),
        compiler_params=pltpu.CompilerParams(vmem_limit_bytes=mib << 20),
        cost_estimate=pl.CostEstimate(flops=0, bytes_accessed=0, transcendentals=0),
    )(*ins)


def sizes():
    return lax.axis_size("row"), lax.axis_size("col")


def swap(block, flip):
    rows, cols = sizes()
    pairs = []
    for i in range(rows * cols):
        row, col = flip(i // cols, i % cols)
        pairs.append((i, row * cols + col))
    return lax.ppermute(block, BOTH, pairs)


def bits_of(size):
    return size.bit_length() - 1


def stack_kernel(which, *refs):
    parts, out, sems = refs[:-2], refs[-2], refs[-1]
    copies = [
        pltpu.make_async_copy(ref, out.at[which[0] ^ m], sems.at[m]) for m, ref in enumerate(parts)
    ]
    for copy in copies:
        copy.start()
    for copy in copies:
        copy.wait()


def stacked(parts, index):
    shape = parts[0].shape
    flat = [p.reshape((-1, shape[-1])) for p in parts]
    out = jax.ShapeDtypeStruct((len(parts),) + flat[0].shape, flat[0].dtype)
    made = call(
        stack_kernel,
        out,
        [index.reshape(1).astype(jnp.int32)] + flat,
        [pltpu.SMEM] + [pl.ANY] * len(parts),
        [pltpu.SemaphoreType.DMA((len(parts),))],
    )
    return made.reshape((len(parts),) + shape)


def group_join(block, axis, low_bit, width):
    parts = [block]
    for m in range(1, 1 << width):
        step = m << low_bit
        if axis == "row":
            parts.append(swap(block, lambda r, c: (r ^ step, c)))
        else:
            parts.append(swap(block, lambda r, c: (r, c ^ step)))
    index = (lax.axis_index(axis) >> low_bit) & ((1 << width) - 1)
    return stacked(parts, index), parts


def groups(top, bottom, most):
    out = []
    while top > bottom:
        width = min(most, top - bottom)
        out.append((top - width, width))
        top -= width
    return out


def early_groups(rows, cols, most):
    return [("row",) + g for g in groups(bits_of(rows), 1, most)] + [
        ("col",) + g for g in groups(bits_of(cols), 2, most)
    ]


def lead_table(rows, cols, most=2):
    table = [(0, 0)]
    for axis, bit, width in early_groups(rows, cols, most):
        shift = bit - (1 if axis == "row" else 2)
        new = []
        for value in range(1 << width):
            for high_col, high_row in table:
                if axis == "row":
                    new.append((high_col, high_row + (value << shift)))
                else:
                    new.append((high_col + (value << shift), high_row))
        table = new
    return table


def after(value, *others):
    return lax.optimization_barrier((value,) + others)[0]


def after_all(values, *others):
    return lax.optimization_barrier(tuple(values) + others)[: len(values)]


def gather_high(shard, most=2):
    rows, cols = sizes()
    block, parts = shard, []
    for axis, bit, width in early_groups(rows, cols, most):
        block, parts = group_join(block, axis, bit, width)
    return block.reshape((-1,) + shard.shape), parts[1:]


def lane_join_kernel(orders, *refs):
    parts, out, sems = refs[:-2], refs[-2], refs[-1]
    copies, lane = [], 0
    for i, (part, order) in enumerate(zip(parts, orders)):
        width = part.shape[-1]
        for n, put_at in enumerate(order):
            target = out.at[put_at, :, lane : lane + width]
            copies.append(pltpu.make_async_copy(part.at[n], target, sems.at[i, n]))
        lane += width
    for copy in copies:
        copy.start()
    for copy in copies:
        copy.wait()


def lane_join(parts, orders):
    if any(p.shape[-1] % 128 for p in parts):
        placed = [p[jnp.array(sorted(range(len(o)), key=o.index))] for p, o in zip(parts, orders)]
        return jnp.concatenate(placed, axis=-1)
    shape = parts[0].shape[:-1] + (sum(p.shape[-1] for p in parts),)
    return call(
        functools.partial(lane_join_kernel, orders),
        jax.ShapeDtypeStruct(shape, parts[0].dtype),
        parts,
        [pl.ANY] * len(parts),
        [pltpu.SemaphoreType.DMA((len(parts), shape[0]))],
    )


def flip_one(r, c):
    return (r, c ^ 2) if c % 2 == 0 else (r ^ 1, c)


def flip_two(r, c):
    return (r ^ 1, c) if c % 2 == 0 else (r, c ^ 2)


def flip_core(r, c):
    return (r, c ^ 1)


def with_cores(pieces):
    return pieces + [swap(p, flip_core) for p in pieces]


def owner_parts(block, bit):
    step = 1 << bit
    return [block, swap(block, lambda r, c: (r ^ step, c))]


def owner_stack(parts, bit):
    return jnp.stack(parts)[jnp.arange(2) ^ ((lax.axis_index("row") >> bit) & 1)]


def piece_place(sc, k):
    kind, away = k % 4, k // 4
    turn = (sc[2] + away) & 1
    return (0, 1 - turn, turn, 1)[kind], (0, turn, 1 - turn, 1)[kind], away


class Weights:
    def __init__(self, sc, pieces, w, sems, lead, first_lane=0):
        self.copies = []
        depth = pieces[0].shape[1]
        taken = pl.ds(first_lane, w.shape[2])
        for k, piece in enumerate(pieces):
            x_rel, y_rel, away = piece_place(sc, k)
            for n, (high_col, high_row) in enumerate(lead):
                slot = high_col * 4 + x_rel * 2 + away
                row = (high_row * 2 + ((sc[3] + y_rel) & 1)) * depth
                self.copies.append(
                    pltpu.make_async_copy(
                        piece.at[n, :, taken],
                        w.at[slot, pl.ds(pl.multiple_of(row, depth), depth), :],
                        sems.at[k, n],
                    )
                )

    def start(self):
        for copy in self.copies:
            copy.start()

    def wait(self, away=None):
        half = len(self.copies) // 2
        for copy in self.copies if away is None else self.copies[away * half : (away + 1) * half]:
            copy.wait()

    def slot(self, i, cols):
        half = cols // 2

        @pl.when(i == 0)
        def _():
            self.wait(0)

        @pl.when(i == half)
        def _():
            self.wait(1)

        return lax.rem(i, half) * 2 + i // half


def column_of(sc, slot):
    return (slot // 4) * 4 + ((sc[1] & 3) ^ (slot & 3))


def weight_scratch(rows, cols, n):
    lead = len(lead_table(rows, cols))
    return [VMEM((cols, D, n), BF), pltpu.SemaphoreType.DMA((8, lead))]


def put(ref, start, value, lane=0):
    part = ref.shape[-1] - lane
    for i in range(value.shape[-1] // part):
        ref[start // part + i, :, lane:] = value[:, i * part : (i + 1) * part]


def lanes(start, width):
    return pl.ds(pl.multiple_of(start, width), width)


def prep_q_kernel(tokens, grads, bias_qv, bias_f, wq, wp, rows, out):
    hid = wq.shape[2]
    seq = tokens.shape[1]
    for c in range(tokens.shape[0]):
        rows[c, :seq] = tokens[c]
        rows[c, seq : 2 * seq] = grads[c]
        rows[c, 2 * seq : 2 * seq + 2] = bias_qv[...]
        for i in range(4):
            rows[c, 2 * seq + 2 + i : 2 * seq + 3 + i] = bias_f[:, i * hid : (i + 1) * hid]
    for c in range(3):
        out[:, c * hid : (c + 1) * hid] = wq[c]
    out[:, 3 * hid :] = low(wp[...].astype(F32).T)


def prep_f_kernel(sc, mask, w1, w2, out_a, out_b, keep, closed):
    row = mask[pl.ds(sc[1], 1), :].astype(F32)
    row = jnp.concatenate([jnp.ones((1, BUF), F32), row], axis=1)
    column = jnp.broadcast_to(row, (8, SEQ)).T[:, :1]
    keep[...] = column
    closed[...] = 1.0 - column
    half = w1.shape[1] // 2
    out_a[:, :half] = w1[:, :half]
    out_b[:, :half] = w1[:, half:]
    out_a[:, half:] = low(w2[:half].astype(F32).T)
    out_b[:, half:] = low(w2[half:].astype(F32).T)


def fetch(sems, *pairs):
    copies = [pltpu.make_async_copy(src, dst, sems.at[i]) for i, (src, dst) in enumerate(pairs)]
    for copy in copies:
        copy.start()
    return copies


def rows_at(xa, start, height):
    return xa.at[:, pl.ds(start, height), :]


def across(ref, cols):
    return jnp.concatenate([ref[c] for c in range(cols)], axis=1).astype(F32)


def both_heads(pair):
    left = lax.broadcasted_iota(jnp.int32, (1, PAIR), 1) < HD
    zero = jnp.zeros_like(pair)
    return jnp.concatenate([jnp.where(left, pair, zero), jnp.where(left, zero, pair)], axis=0)


def own_heads(made, scale=1.0):
    both = jnp.concatenate([made[:HD, :SEQ], made[HD:, SEQ:]], axis=0)
    return low(both.T * scale)


def front_kernel(lead, cols, *refs):
    sc = refs[0]
    pieces = refs[1:9]
    (xa, closed, gain, shift, q_down, q_up, p_down, p_up, f_down, bias_out) = refs[9:19]
    (n1, lat1, q, k, v, lse, att, lat2, middle, n2, lat3) = refs[19:30]
    w, sems, hidden, branch, xs, bs, row_qd, row_pd, row_pu, row_fd, sems_f = refs[30:]
    a = sc[0]
    hid = D // cols
    first = fetch(
        sems_f,
        (rows_at(xa, 0, SEQ), xs),
        (q_down.at[a], row_qd),
        (rows_at(xa, 2 * SEQ, EXTRA), bs),
        (p_down.at[a], row_pd),
        (p_up.at[a], row_pu),
        (f_down.at[a], row_fd),
    )
    weights = Weights(sc, pieces, w, sems, lead)
    weights.start()
    first[0].wait()
    x = across(xs, cols)
    hidden[...] = x
    unit, _ = norm_parts(x)
    n1[...] = low(unit * gain[0:1] + shift[0:1])
    for copy in first[1:]:
        copy.wait()
    lat1[...] = low(mm(n1[...], row_qd[...], NT))

    def project(i, _):
        slot = weights.slot(i, cols)
        block = column_of(sc, slot)
        up = jnp.concatenate([q_up[c, :, lanes(block * hid, hid)] for c in range(3)], axis=1)
        made = mm(n1[...], w[slot, :, : 3 * hid]) + mm(lat1[...], up)
        bias_q = bs[block, 0:1, :].astype(F32)
        bias_v = bs[block, 1:2, :].astype(F32)
        at = lanes(slot * hid, hid)
        q[:, at] = low(made[:, :hid] + bias_q) * jnp.asarray(0.125, BF)
        k[:, at] = low(made[:, hid : 2 * hid])
        v[:, at] = low(made[:, 2 * hid :] + bias_v)
        return 0

    lax.fori_loop(0, cols, project, 0)
    shut = closed[...] > 0.5

    def attend(pair, _):
        at = lanes(pair * PAIR, PAIR)
        v_t = low(v[:, at].astype(F32).T)
        s = jnp.where(shut, -1e30, mm(k[:, at], both_heads(q[:, at]), NT))
        top = jnp.max(s, axis=0, keepdims=True)
        e = jnp.exp(s - top)
        total = jnp.sum(e, axis=0, keepdims=True)
        lse[pair] = top + jnp.log(total)
        att[:, at] = own_heads(mm(v_t, low(e * (1.0 / total))))
        return 0

    lax.fori_loop(0, H // 2, attend, 0, unroll=4)

    def down_two(slot, acc):
        block = column_of(sc, slot)
        return acc + mm(att[:, lanes(slot * hid, hid)], row_pd[:, lanes(block * hid, hid)], NT)

    lat2[...] = low(lax.fori_loop(0, cols, down_two, jnp.zeros((SEQ, R), F32)))
    branch[...] = mm(lat2[...], row_pu[...]) + bias_out[0:1].astype(F32)

    def out_proj(slot, _):
        branch[...] += mm(att[:, lanes(slot * hid, hid)], w[slot, :, 3 * hid :], NT)
        return 0

    lax.fori_loop(0, cols, out_proj, 0)
    mid = hidden[...] + branch[...]
    middle[...] = mid
    unit, _ = norm_parts(mid)
    n2[...] = low(unit * gain[1:2] + shift[1:2])
    lat3[...] = low(mm(n2[...], row_fd[...], NT))


def ffn_steps(weights, sc, part, cols, w, bs, n2, lat3, gr, glat4, up_1, down_2, acc, early, lane=0):
    res, gn2, lat4, glat3 = acc
    hid = D // cols
    ffn = FF // cols
    half = ffn // 2
    glat4_t = low(glat4.astype(F32).T)
    lat3_t = low(lat3[...].astype(F32).T)

    def step(i, _):
        slot = weights.slot(i, cols)
        block = column_of(sc, slot)
        at = pl.ds(pl.multiple_of(block * ffn + part * half, half), half)
        bias = jnp.concatenate(
            [bs[block, 2 + 2 * part + i : 3 + 2 * part + i, :] for i in range(2)], axis=1
        ).astype(F32)
        up, down = up_1[:, at], down_2[:, at]
        w1, w2 = w[slot, :, :half], w[slot, :, half:]
        pre = mm(n2[...], w1) + mm(lat3[...], up) + bias
        back = mm(gr[...], w2) + mm(glat4, down)
        cumulative = 0.5 * (1.0 + lax.erf(pre * 0.7071067811865476))
        activated = low(pre * cumulative)
        slope = cumulative + pre * jnp.exp(-0.5 * pre * pre) * 0.3989422804014327
        grad_pre = low(back * slope)
        lat4[...] += mm(activated, down, NT)
        glat3[...] += mm(grad_pre, up, NT)
        res[...] += mm(activated, w2, NT)
        gn2[...] += mm(grad_pre, w1, NT)
        put(early, block * half, low(mm(lat3_t, grad_pre)), lane)
        put(early, FF // 2 + block * half, low(mm(glat4_t, activated)), lane)
        return 0

    lax.fori_loop(0, cols, step, 0)


def ffn_a_kernel(lead, cols, *refs):
    sc = refs[0]
    pieces = refs[1:9]
    xa, keep, n2, lat3, up_1, down_2, up_2 = refs[9:16]
    res, gn2, lat4, glat3, gr, early = refs[16:22]
    w, sems, gs, bs, row_u1, row_d2, row_u2, sems_f = refs[22:]
    a = sc[0]
    first = fetch(
        sems_f,
        (rows_at(xa, SEQ, SEQ), gs),
        (up_2.at[a], row_u2),
        (rows_at(xa, 2 * SEQ, EXTRA), bs),
        (up_1.at[a], row_u1),
        (down_2.at[a], row_d2),
    )
    weights = Weights(sc, pieces, w, sems, lead)
    weights.start()
    first[0].wait()
    gr[...] = low(across(gs, cols) * keep[...])
    for copy in first[1:]:
        copy.wait()
    glat4 = low(mm(gr[...], row_u2[...], NT))
    res[...] = jnp.zeros_like(res)
    gn2[...] = jnp.zeros_like(gn2)
    lat4[...] = jnp.zeros_like(lat4)
    glat3[...] = jnp.zeros_like(glat3)
    ffn_steps(
        weights, sc, 0, cols, w, bs, n2, lat3, gr, glat4, row_u1, row_d2, (res, gn2, lat4, glat3), early
    )


def ffn_b_kernel(lead, cols, *refs):
    sc = refs[0]
    pieces = refs[1:9]
    own_q = refs[9:17]
    (xa, keep, gain, n2, lat3, up_1, down_2, up_2, f_down, p_down, p_up, bias_out) = refs[17:29]
    (middle, att, lat2, gr, res_in, gn2_in, lat4_in, glat3_in, early_in) = refs[29:38]
    layer, gatt, gmid, early = refs[38:42]
    w, sems, wp, sems_p, res, gn2, lat4, glat3 = refs[42:50]
    bs, row_u1, row_d2, row_u2, row_fd, row_pd, row_pu, mid_s, att_s, res_s, gn2_s, early_s = refs[50:62]
    sems_f = refs[62]
    lane = early_in.shape[-1]
    a = sc[0]
    first = fetch(
        sems_f,
        (up_2.at[a], row_u2),
        (rows_at(xa, 2 * SEQ, EXTRA), bs),
        (up_1.at[a], row_u1),
        (down_2.at[a], row_d2),
    )
    weights = Weights(sc, pieces, w, sems, lead)
    weights.start()
    proj = Weights(sc, own_q, wp, sems_p, lead, 3 * D // cols)
    last = fetch(
        sems_f.at[pl.ds(4, 8)],
        (res_in, res_s),
        (middle, mid_s),
        (gn2_in, gn2_s),
        (f_down.at[a], row_fd),
        (p_up.at[a], row_pu),
        (p_down.at[a], row_pd),
        (att, att_s),
        (early_in, early_s),
    )
    proj.start()
    hid = D // cols
    for copy in first:
        copy.wait()
    glat4 = low(mm(gr[...], row_u2[...], NT))
    res[...] = jnp.zeros_like(res)
    gn2[...] = jnp.zeros_like(gn2)
    lat4[...] = lat4_in[...]
    glat3[...] = glat3_in[...]
    ffn_steps(
        weights, sc, 1, cols, w, bs, n2, lat3, gr, glat4, row_u1, row_d2, (res, gn2, lat4, glat3), early, lane
    )
    for copy in last:
        copy.wait()
    early[:, :, :lane] = early_s[...]
    mid = mid_s[...]
    lat4_low = low(lat4[...])
    out = low(
        keep[...]
        * (mid + (res_s[...] + res[...]) + mm(lat4_low, row_u2[...]) + bias_out[1:2].astype(F32))
    )
    for c in range(cols):
        layer[c] = out[:, c * hid : (c + 1) * hid]
    glat3_low = low(glat3[...])
    grad_normed = gn2_s[...] + gn2[...] + mm(glat3_low, row_fd[...])
    unit, inverse = norm_parts(mid)
    grad_middle = gr[...].astype(F32) + norm_back(grad_normed, gain[1:2], unit, inverse)
    gmid[...] = grad_middle
    gb = low(grad_middle)
    glat2 = low(mm(gb, row_pu[...], NT))
    glat2_t = low(glat2.astype(F32).T)
    put(early, FF + D, low(mm(low(lat2[...].astype(F32).T), gb)), lane)
    put(early, FF + 2 * D, low(mm(low(glat3_low.astype(F32).T), n2[...])), lane)
    put(early, FF + 3 * D, low(mm(low(lat4_low.astype(F32).T), gr[...])), lane)
    proj.wait()

    def step(slot, _):
        block = column_of(sc, slot)
        here = lanes(slot * hid, hid)
        there = lanes(block * hid, hid)
        gatt[:, here] = low(mm(gb, wp[slot]) + mm(glat2, row_pd[:, there]))
        put(early, FF + block * hid, low(mm(glat2_t, att_s[:, here])), lane)
        return 0

    lax.fori_loop(0, cols, step, 0)


def attention_back_kernel(cols, *refs):
    sc = refs[0]
    closed, q, k, v, lse, gatt, lat1, n1, q_up = refs[1:10]
    gq, gk, gv, glat1, late = refs[10:15]
    a = sc[0]
    hid = D // cols
    shut = closed[...] > 0.5

    def attend(pair, _):
        at = lanes(pair * PAIR, PAIR)
        kp = k[:, at]
        k_t = low(kp.astype(F32).T)
        q_both, g_both = both_heads(q[:, at]), both_heads(gatt[:, at])
        s = jnp.where(shut, -1e30, mm(kp, q_both, NT))
        soft = jnp.exp(s - lse[pair])
        grad_soft = mm(v[:, at], g_both, NT)
        total = jnp.sum(grad_soft * soft, axis=0, keepdims=True)
        grad_scores = low(soft * (grad_soft - total))
        gq[:, at] = own_heads(mm(k_t, grad_scores), 0.125)
        gk[:, at] = low(mm(grad_scores, q_both))
        gv[:, at] = low(mm(low(soft), g_both))
        return 0

    lax.fori_loop(0, H // 2, attend, 0, unroll=4)
    lat1_t = low(lat1[...].astype(F32).T)

    def step(slot, acc):
        block = column_of(sc, slot)
        here = lanes(slot * hid, hid)
        there = lanes(block * hid, hid)
        for c, g in enumerate((gq, gk, gv)):
            grad = g[:, here]
            acc = acc + mm(grad, q_up[c, :, there], NT)
            put(late, (c + 1) * D + block * hid, low(mm(lat1_t, grad)))
        return acc

    made = low(lax.fori_loop(0, cols, step, jnp.zeros((SEQ, R), F32)))
    glat1[...] = made
    put(late, 0, low(mm(low(made.astype(F32).T), n1[...])))


def back_kernel(lead, cols, *refs):
    sc = refs[0]
    pieces = refs[1:9]
    xa, gain, gq, gk, gv, glat1, q_down, gmid, layer = refs[9:18]
    out = refs[18]
    w, sems, acc, xs, row_qd, gmid_s, sems_f = refs[19:]
    first = fetch(
        sems_f,
        (rows_at(xa, 0, SEQ), xs),
        (q_down.at[sc[0]], row_qd),
        (gmid, gmid_s),
        (layer, rows_at(out, 0, SEQ)),
    )
    weights = Weights(sc, pieces, w, sems, lead)
    weights.start()
    hid = D // cols
    for copy in first:
        copy.wait()
    acc[...] = mm(glat1[...], row_qd[...])
    x = across(xs, cols)
    unit, inverse = norm_parts(x)

    def step(i, _):
        slot = weights.slot(i, cols)
        here = lanes(slot * hid, hid)
        grad = jnp.concatenate([gq[:, here], gk[:, here], gv[:, here]], axis=1)
        acc[...] += mm(grad, w[slot, :, : 3 * hid], NT)
        return 0

    lax.fori_loop(0, cols, step, 0)
    made = low(gmid_s[...] + norm_back(acc[...], gain[0:1], unit, inverse))
    for c in range(cols):
        out[c, SEQ:] = made[:, c * hid : (c + 1) * hid]


def sum_kernel(owners, mine, out, acc):
    acc[...] = jnp.zeros_like(acc)
    for d in range(mine.shape[0]):
        acc[owners[d]] += mine[d, :, : acc.shape[2]].astype(F32)
    out[...] = low(acc[...])


def spread_kernel(lead, cols, parts, maps, *refs):
    sc, pieces = refs[0], refs[1:9]
    count = (len(refs) - 11) // 2
    outs, whole, made = refs[9 : 9 + count], refs[9 + count], refs[10 + count : 10 + 2 * count]
    sems_in, sems_out = refs[10 + 2 * count :]
    copies = []
    for k, piece in enumerate(pieces):
        x_rel, y_rel, away = piece_place(sc, k)
        for n, (high_col, high_row) in enumerate(lead):
            row = high_row * 2 + ((sc[3] + y_rel) & 1)
            col = high_col * 4 + ((sc[1] & 3) ^ (x_rel * 2 + away))
            copies.append(
                pltpu.make_async_copy(piece.at[n], whole.at[row * cols + col], sems_in.at[k, n])
            )
    for copy in copies:
        copy.start()
    for copy in copies:
        copy.wait()
    found = [[] for _ in outs]
    base = 0
    for part, spans in zip(parts, maps):
        for out, section, there, start, width in spans:
            for lane in range(0, width, 128):
                at = start + lane
                found[out].append((section, there + lane, at // part, base + at % part))
        base += part
    leaving = []
    for i, (out, buffer) in enumerate(zip(outs, made)):
        for section, there, device, here in found[i]:
            block = whole[device, :, here : here + 128].astype(F32)
            if section is None:
                buffer[:, there : there + 128] = block
            else:
                buffer[:, section, :, there : there + 128] = block.reshape(NA, R, 128)
        leaving.append(pltpu.make_async_copy(buffer, out, sems_out.at[i]))
        leaving[-1].start()
    for copy in leaving:
        copy.wait()


def place_kernel(lead, cols, *refs):
    sc, pieces, out, sems = refs[0], refs[1:9], refs[9], refs[10]
    copies = []
    for k, piece in enumerate(pieces):
        x_rel, y_rel, away = piece_place(sc, k)
        for n, (high_col, high_row) in enumerate(lead):
            row = high_row * 2 + ((sc[3] + y_rel) & 1)
            col = high_col * 4 + ((sc[1] & 3) ^ (x_rel * 2 + away))
            copies.append(pltpu.make_async_copy(piece.at[n], out.at[row * cols + col], sems.at[k, n]))
    for copy in copies:
        copy.start()
    for copy in copies:
        copy.wait()


def send_grads(grads):
    return lax.all_to_all(grads, BOTH, split_axis=0, concat_axis=0, tiled=True)


def sum_grads(mine, owners, part):
    summed = call(
        sum_kernel,
        jax.ShapeDtypeStruct((NA, R, part), BF),
        [owners, mine],
        [pltpu.SMEM, VMEM],
        [VMEM((NA, R, part), F32)],
    )
    return summed.reshape(NA * R, part)


def spread(sc, pieces, parts, maps, shapes):
    rows, cols = sizes()
    devices = rows * cols
    lead = lead_table(rows, cols)
    arrivals = pltpu.SemaphoreType.DMA((8, len(lead)))
    whole = (devices, NA * R, sum(parts))
    ins, spaces = [sc, *pieces], [pltpu.SMEM] + [pl.ANY] * 8
    if all(p % 128 == 0 for p in parts):
        return call(
            functools.partial(spread_kernel, lead, cols, parts, maps),
            [jax.ShapeDtypeStruct(x, F32) for x in shapes],
            ins,
            spaces,
            [VMEM(whole, BF)]
            + [VMEM(x, F32) for x in shapes]
            + [arrivals, pltpu.SemaphoreType.DMA((len(shapes),))],
            pl.ANY,
            SPREAD,
        )
    whole = call(
        functools.partial(place_kernel, lead, cols),
        jax.ShapeDtypeStruct(whole, BF),
        ins,
        spaces,
        [arrivals],
    )
    found = [[] for _ in shapes]
    base = 0
    for part, spans in zip(parts, maps):
        flat = jnp.swapaxes(whole[:, :, base : base + part], 0, 1).reshape(NA * R, devices * part)
        for out, section, there, start, width in spans:
            found[out].append((section or 0, there, flat[:, start : start + width].astype(F32)))
        base += part
    return [
        (
            jnp.concatenate([x for _, _, x in sorted(f, key=lambda e: e[:2])], axis=1)
            if len(shape) == 2
            else jnp.stack([x.reshape(NA, R, -1) for _, _, x in sorted(f, key=lambda e: e[:2])], 1)
        )
        for f, shape in zip(found, shapes)
    ]


def per_device(
    tokens_in,
    grad_out,
    keep_mask,
    adapter_index,
    ln_gain,
    ln_shift,
    w_qkv,
    bias_qv,
    w_proj,
    w_fc1,
    bias_fc1,
    w_fc2,
    bias_out,
    qkv_down,
    qkv_up,
    proj_down,
    proj_up,
    fc1_down,
    fc1_up,
    fc2_down,
    fc2_up,
):
    rows, cols = sizes()
    row, column = lax.axis_index("row"), lax.axis_index("col")
    assert adapter_index.shape[0] == cols and cols >= 4 and rows >= 2
    hid = D // cols
    n = 4 * hid
    blk = D // rows
    lead = lead_table(rows, cols)

    shard = jax.ShapeDtypeStruct((blk, n), BF)
    rows_in, shard_q = call(
        prep_q_kernel,
        [jax.ShapeDtypeStruct((cols, 2 * SEQ + EXTRA, hid), BF), shard],
        [tokens_in.reshape(cols, SEQ, hid), grad_out.reshape(cols, SEQ, hid), bias_qv]
        + [bias_fc1.reshape(1, n), w_qkv, w_proj],
        [VMEM] * 6,
        mib=56,
    )
    with jax.named_scope("q_high"):
        own_q, came_q = gather_high(shard_q)
    xa = lax.all_to_all(rows_in, "col", split_axis=0, concat_axis=0, tiled=True)
    adapter = lax.dynamic_index_in_dim(adapter_index, column, 0, keepdims=False)
    sc = jnp.stack([adapter, column, column % 2, row % 2]).astype(jnp.int32)
    up_qkv = jnp.swapaxes(lax.dynamic_index_in_dim(qkv_up, adapter, 0, keepdims=False), 0, 1)
    shard_a, shard_b, keep, closed = call(
        prep_f_kernel,
        [shard] * 2 + [jax.ShapeDtypeStruct((SEQ, 1), F32)] * 2,
        [sc, keep_mask, w_fc1, w_fc2],
        [pltpu.SMEM] + [VMEM] * 3,
    )

    own_q, shard_a, shard_b = after_all(
        (own_q, shard_a, shard_b), xa, keep, closed, sc, up_qkv, *came_q
    )
    with jax.named_scope("q_one"):
        one_q = swap(own_q, flip_one)
    with jax.named_scope("q_two"):
        two_q = swap(own_q, flip_two)
    with jax.named_scope("fa_high"):
        own_a, came_a = gather_high(shard_a)
    own_q, one_q, two_q = after_all((own_q, one_q, two_q), *came_a)
    with jax.named_scope("q_both"):
        both_q = swap(one_q, flip_two)
    with jax.named_scope("q_core"):
        away_q = [swap(p, flip_core) for p in (own_q, one_q, two_q)]
    own_a, shard_b = after_all((own_a, shard_b), *away_q)
    with jax.named_scope("q_core"):
        pieces_q = [own_q, one_q, two_q, both_q] + away_q + [swap(both_q, flip_core)]
    with jax.named_scope("fa_one"):
        one_a = swap(own_a, flip_one)
    with jax.named_scope("fa_two"):
        two_a = swap(own_a, flip_two)
    with jax.named_scope("fb_high"):
        own_b, came_b = gather_high(shard_b)

    def shaped(width, dtype, height=SEQ):
        return jax.ShapeDtypeStruct((height, width), dtype)

    big, small = shaped(D, BF), shaped(R, BF)
    scratch = weight_scratch(rows, cols, n)
    rows_space, bias_space = VMEM((cols, SEQ, hid), BF), VMEM((cols, EXTRA, hid), BF)
    any_space = [pl.ANY] * 8
    n1, lat1, q, k, v, lse, att, lat2, middle, n2, lat3 = call(
        functools.partial(front_kernel, lead, cols),
        [
            big,
            small,
            big,
            big,
            big,
            jax.ShapeDtypeStruct((H // 2, 1, 2 * SEQ), F32),
            big,
            small,
            shaped(D, F32),
            big,
            small,
        ],
        [sc, *pieces_q, xa, closed, ln_gain, ln_shift, qkv_down, up_qkv, proj_down]
        + [proj_up]
        + [fc1_down, bias_out],
        [pltpu.SMEM] + any_space + [pl.ANY] + [VMEM] * 3 + [pl.ANY, VMEM] + [pl.ANY] * 3 + [VMEM],
        scratch
        + [VMEM((SEQ, D), F32), VMEM((SEQ, D), F32), rows_space, bias_space]
        + [VMEM((R, D), BF)] * 4
        + [pltpu.SemaphoreType.DMA((6,))],
        mib=FRONT,
    )
    own_a, one_a, two_a = after_all((own_a, one_a, two_a), n1, *came_b)
    bits = list(reversed(range(bits_of(rows))))
    owners = after(adapter_index, n1)
    for bit in bits[:-1]:
        owners = owner_stack(owner_parts(owners, bit), bit)
    with jax.named_scope("fa_both"):
        both_a = swap(one_a, flip_two)
    with jax.named_scope("fa_core"):
        away_a = [swap(p, flip_core) for p in (own_a, one_a, two_a)]
    own_b, owners = after_all((own_b, owners), *away_a)
    owners = owner_parts(owners, 0)
    with jax.named_scope("fa_core"):
        pieces_a = [own_a, one_a, two_a, both_a] + away_a + [swap(both_a, flip_core)]
    with jax.named_scope("fb_one"):
        one_b = swap(own_b, flip_one)
    with jax.named_scope("fb_two"):
        two_b = swap(own_b, flip_two)
    wide = shaped(D, F32)
    thin = shaped(R, F32)
    res, gn2, lat4, glat3, gr, early_a = call(
        functools.partial(ffn_a_kernel, lead, cols),
        [wide, wide, thin, thin, big, jax.ShapeDtypeStruct((rows * cols, R, FF // (rows * cols)), BF)],
        [sc, *pieces_a, xa, keep, n2, lat3, fc1_up, fc2_down, fc2_up],
        [pltpu.SMEM] + any_space + [pl.ANY] + [VMEM] * 3 + [pl.ANY] * 3,
        scratch
        + [rows_space, bias_space, VMEM((R, FF), BF), VMEM((R, FF), BF), VMEM((R, D), BF)]
        + [pltpu.SemaphoreType.DMA((5,))],
        mib=FFN_A,
    )
    own_b, one_b, two_b, *owners = after_all((own_b, one_b, two_b, *owners), res)
    owners = owner_stack(owners, 0).transpose(tuple(bits) + (len(bits),)).reshape(-1)
    with jax.named_scope("fb_both"):
        both_b = swap(one_b, flip_two)
    with jax.named_scope("fb_core"):
        away_b = [swap(p, flip_core) for p in (own_b, one_b, two_b)]
        pieces_b = [own_b, one_b, two_b, both_b] + away_b + [swap(both_b, flip_core)]
    layer, gatt, gmid, grads_b = call(
        functools.partial(ffn_b_kernel, lead, cols),
        [jax.ShapeDtypeStruct((cols, SEQ, hid), BF), big, wide]
        + [jax.ShapeDtypeStruct((rows * cols, R, 12 * D // (rows * cols)), BF)],
        [sc, *pieces_b, *pieces_q, xa, keep, ln_gain, n2, lat3, fc1_up, fc2_down, fc2_up]
        + [fc1_down, proj_down, proj_up, bias_out]
        + [middle, att, lat2, gr, res, gn2, lat4, glat3, early_a],
        [pltpu.SMEM]
        + any_space * 2
        + [pl.ANY, VMEM, VMEM, VMEM, VMEM]
        + [pl.ANY] * 6
        + [VMEM, pl.ANY, pl.ANY, VMEM, VMEM, pl.ANY, pl.ANY, VMEM, VMEM, pl.ANY],
        scratch
        + [VMEM((cols, D, hid), BF), scratch[1]]
        + [VMEM((SEQ, D), F32), VMEM((SEQ, D), F32), VMEM((SEQ, R), F32), VMEM((SEQ, R), F32)]
        + [bias_space, VMEM((R, FF), BF), VMEM((R, FF), BF)]
        + [VMEM((R, D), BF)] * 4
        + [VMEM((SEQ, D), F32), VMEM((SEQ, D), BF), VMEM((SEQ, D), F32), VMEM((SEQ, D), F32)]
        + [VMEM(early_a.shape, BF), pltpu.SemaphoreType.DMA((12,))],
        mib=FFN_B,
    )
    with jax.named_scope("grads_b_send"):
        mine_b = send_grads(grads_b)
    gq, gk, gv, glat1, late = call(
        functools.partial(attention_back_kernel, cols),
        [big, big, big, small, jax.ShapeDtypeStruct((rows * cols, R, 4 * D // (rows * cols)), BF)],
        [sc, closed, q, k, v, lse, gatt, lat1, n1, up_qkv],
        [pltpu.SMEM] + [VMEM] * 9,
        mib=ATT,
    )
    with jax.named_scope("grads_c_send"):
        mine_c = send_grads(late)
    with jax.named_scope("grads_b"):
        own_b, _ = gather_high(
            sum_grads(after(mine_b, late), owners, mine_b.shape[2]), 1
        )
        own_c, _ = gather_high(sum_grads(mine_c, owners, mine_c.shape[2]))
        order_b = tuple(lead.index(place) for place in lead_table(rows, cols, 1))
        own = lane_join([own_b, own_c], [order_b, tuple(range(len(lead)))])
    gmid = after(gmid, own)
    sent = call(
        functools.partial(back_kernel, lead, cols),
        jax.ShapeDtypeStruct((cols, 2 * SEQ, hid), BF),
        [sc, *pieces_q, xa, ln_gain, gq, gk, gv, glat1, qkv_down, gmid, layer],
        [pltpu.SMEM] + any_space + [pl.ANY] + [VMEM] * 5 + [pl.ANY] * 3,
        scratch
        + [VMEM((SEQ, D), F32), rows_space, VMEM((R, D), BF), VMEM((SEQ, D), F32)]
        + [pltpu.SemaphoreType.DMA((4,))],
        mib=BACK,
    )
    with jax.named_scope("grads"):
        one, two = swap(own, flip_one), swap(own, flip_two)
        own, one, two = after_all((own, one, two), sent)
        both = swap(one, flip_two)
        pieces = with_cores([own, one, two, both])
        half = FF // cols // 2
        map_a, map_b = (
            tuple(
                (out, None, (2 * block + part) * half, base + block * half, half)
                for out, base in ((0, 0), (1, FF // 2))
                for block in range(cols)
            )
            for part in (0, 1)
        )
        map_b = map_b + tuple((2 + i, None, 0, FF + i * D, D) for i in range(4))
        map_c = ((6, None, 0, 0, D),) + tuple((7, c, 0, (c + 1) * D, D) for c in range(3))
        parts = [early_a.shape[-1], mine_b.shape[-1] - early_a.shape[-1], mine_c.shape[-1]]
        shapes = [(NA * R, FF)] * 2 + [(NA * R, D)] * 5 + [(NA, 3, R, D)]
        sums = spread(sc, pieces, parts, [map_a, map_b, map_c], shapes)

    with jax.named_scope("rows_out"):
        sent = after(sent, pieces[4])
        rows_out = lax.all_to_all(sent, "col", split_axis=0, concat_axis=0, tiled=True)
    layer, grad_in = rows_out[:, :SEQ], rows_out[:, SEQ:]

    def split(table):
        return table.reshape((NA, R) + table.shape[1:])

    g_fc1_up, g_fc2_down, g_proj_down, g_proj_up, g_fc1_down, g_fc2_up = map(split, sums[:6])
    return (
        layer.reshape(cols * SEQ, hid),
        grad_in.reshape(cols * SEQ, hid),
        split(sums[6]),
        jnp.swapaxes(sums[7], 1, 2),
        g_proj_down,
        g_proj_up,
        g_fc1_down,
        g_fc1_up,
        g_fc2_down,
        g_fc2_up,
    )


def solution(mesh):
    return jax.shard_map(
        per_device,
        mesh=mesh,
        in_specs=(
            P("row", "col"),
            P("row", "col"),
            P("row", None),
            P("row"),
            P(),
            P(),
            P(None, "row", "col"),
            P(None, "col"),
            P("col", "row"),
            P("row", "col"),
            P("col"),
            P("col", "row"),
            P(),
            P(),
            P(),
            P(),
            P(),
            P(),
            P(),
            P(),
            P(),
        ),
        out_specs=(P("row", "col"), P("row", "col"), P(), P(), P(), P(), P(), P(), P(), P()),
        check_vma=False,
    )
```

```python
import functools

import jax
import jax.numpy as jnp
from jax import lax
from jax.experimental import pallas as pl
from jax.experimental.pallas import tpu as pltpu
from jax.sharding import PartitionSpec as P

D = 1024
H = 16
HD = 64
FF = 4096
BUF = 64
R = 16
NA = 8
SEQ = 320
PAIR = 2 * HD
EXTRA = 16
SPREAD = 56
FRONT, FFN_A, FFN_B, ATT, BACK = 56, 56, 56, 56, 56
BF = jnp.bfloat16
F32 = jnp.float32
BOTH = ("row", "col")
VMEM = pltpu.VMEM
NN = (((1,), (0,)), ((), ()))
NT = (((1,), (1,)), ((), ()))


def mm(left, right, dims=NN):
    return lax.dot_general(left, right, dims, preferred_element_type=F32)


def low(values):
    return values.astype(BF)


def norm_parts(values):
    row_mean = jnp.mean(values, axis=-1, keepdims=True)
    centered = values - row_mean
    variance = jnp.mean(centered * centered, axis=-1, keepdims=True)
    inverse = lax.rsqrt(variance + 1e-06)
    return (centered * inverse, inverse)


def norm_back(grad_normed, gain_row, unit_rows, inverse):
    scaled = grad_normed * gain_row
    first_mean = jnp.mean(scaled, axis=-1, keepdims=True)
    second_mean = jnp.mean(scaled * unit_rows, axis=-1, keepdims=True)
    return inverse * (scaled - first_mean - unit_rows * second_mean)


def call(kernel, outs, ins, spaces, scratch=(), out_space=VMEM, mib=4):
    return pl.pallas_call(
        kernel,
        out_shape=outs,
        in_specs=[pl.BlockSpec(memory_space=s) for s in spaces],
        out_specs=jax.tree.map(lambda _: pl.BlockSpec(memory_space=out_space), outs),
        scratch_shapes=list(scratch),
        compiler_params=pltpu.CompilerParams(vmem_limit_bytes=mib << 20),
        cost_estimate=pl.CostEstimate(flops=0, bytes_accessed=0, transcendentals=0),
    )(*ins)


def sizes():
    return lax.axis_size("row"), lax.axis_size("col")


def swap(block, flip):
    rows, cols = sizes()
    pairs = []
    for i in range(rows * cols):
        row, col = flip(i // cols, i % cols)
        pairs.append((i, row * cols + col))
    return lax.ppermute(block, BOTH, pairs)


def bits_of(size):
    return size.bit_length() - 1


def stack_kernel(which, *refs):
    parts, out, sems = refs[:-2], refs[-2], refs[-1]
    copies = [
        pltpu.make_async_copy(ref, out.at[which[0] ^ m], sems.at[m]) for m, ref in enumerate(parts)
    ]
    for copy in copies:
        copy.start()
    for copy in copies:
        copy.wait()


def stacked(parts, index):
    shape = parts[0].shape
    flat = [p.reshape((-1, shape[-1])) for p in parts]
    out = jax.ShapeDtypeStruct((len(parts),) + flat[0].shape, flat[0].dtype)
    made = call(
        stack_kernel,
        out,
        [index.reshape(1).astype(jnp.int32)] + flat,
        [pltpu.SMEM] + [pl.ANY] * len(parts),
        [pltpu.SemaphoreType.DMA((len(parts),))],
    )
    return made.reshape((len(parts),) + shape)


def group_join(block, axis, low_bit, width):
    parts = [block]
    for m in range(1, 1 << width):
        step = m << low_bit
        if axis == "row":
            parts.append(swap(block, lambda r, c: (r ^ step, c)))
        else:
            parts.append(swap(block, lambda r, c: (r, c ^ step)))
    index = (lax.axis_index(axis) >> low_bit) & ((1 << width) - 1)
    return stacked(parts, index), parts


def groups(top, bottom, most):
    out = []
    while top > bottom:
        width = min(most, top - bottom)
        out.append((top - width, width))
        top -= width
    return out


def early_groups(rows, cols, most):
    return [("row",) + g for g in groups(bits_of(rows), 1, most)] + [
        ("col",) + g for g in groups(bits_of(cols), 2, most)
    ]


def lead_table(rows, cols, most=2):
    table = [(0, 0)]
    for axis, bit, width in early_groups(rows, cols, most):
        shift = bit - (1 if axis == "row" else 2)
        new = []
        for value in range(1 << width):
            for high_col, high_row in table:
                if axis == "row":
                    new.append((high_col, high_row + (value << shift)))
                else:
                    new.append((high_col + (value << shift), high_row))
        table = new
    return table


def after(value, *others):
    return lax.optimization_barrier((value,) + others)[0]


def after_all(values, *others):
    return lax.optimization_barrier(tuple(values) + others)[: len(values)]


def gather_high(shard, most=2):
    rows, cols = sizes()
    block, parts = shard, []
    for axis, bit, width in early_groups(rows, cols, most):
        block, parts = group_join(block, axis, bit, width)
    return block.reshape((-1,) + shard.shape), parts[1:]


def lane_join_kernel(orders, *refs):
    parts, out, sems = refs[:-2], refs[-2], refs[-1]
    copies, lane = [], 0
    for i, (part, order) in enumerate(zip(parts, orders)):
        width = part.shape[-1]
        for n, put_at in enumerate(order):
            target = out.at[put_at, :, lane : lane + width]
            copies.append(pltpu.make_async_copy(part.at[n], target, sems.at[i, n]))
        lane += width
    for copy in copies:
        copy.start()
    for copy in copies:
        copy.wait()


def lane_join(parts, orders):
    if any(p.shape[-1] % 128 for p in parts):
        placed = [p[jnp.array(sorted(range(len(o)), key=o.index))] for p, o in zip(parts, orders)]
        return jnp.concatenate(placed, axis=-1)
    shape = parts[0].shape[:-1] + (sum(p.shape[-1] for p in parts),)
    return call(
        functools.partial(lane_join_kernel, orders),
        jax.ShapeDtypeStruct(shape, parts[0].dtype),
        parts,
        [pl.ANY] * len(parts),
        [pltpu.SemaphoreType.DMA((len(parts), shape[0]))],
    )


def flip_one(r, c):
    return (r, c ^ 2) if c % 2 == 0 else (r ^ 1, c)


def flip_two(r, c):
    return (r ^ 1, c) if c % 2 == 0 else (r, c ^ 2)


def flip_core(r, c):
    return (r, c ^ 1)


def with_cores(pieces):
    return pieces + [swap(p, flip_core) for p in pieces]


def owner_parts(block, bit):
    step = 1 << bit
    return [block, swap(block, lambda r, c: (r ^ step, c))]


def owner_stack(parts, bit):
    return jnp.stack(parts)[jnp.arange(2) ^ ((lax.axis_index("row") >> bit) & 1)]


def piece_place(sc, k):
    kind, away = k % 4, k // 4
    turn = (sc[2] + away) & 1
    return (0, 1 - turn, turn, 1)[kind], (0, turn, 1 - turn, 1)[kind], away


class Weights:
    def __init__(self, sc, pieces, w, sems, lead, first_lane=0):
        self.copies = []
        depth = pieces[0].shape[1]
        taken = pl.ds(first_lane, w.shape[2])
        for k, piece in enumerate(pieces):
            x_rel, y_rel, away = piece_place(sc, k)
            for n, (high_col, high_row) in enumerate(lead):
                slot = high_col * 4 + x_rel * 2 + away
                row = (high_row * 2 + ((sc[3] + y_rel) & 1)) * depth
                self.copies.append(
                    pltpu.make_async_copy(
                        piece.at[n, :, taken],
                        w.at[slot, pl.ds(pl.multiple_of(row, depth), depth), :],
                        sems.at[k, n],
                    )
                )

    def start(self):
        for copy in self.copies:
            copy.start()

    def wait(self, away=None):
        half = len(self.copies) // 2
        for copy in self.copies if away is None else self.copies[away * half : (away + 1) * half]:
            copy.wait()

    def slot(self, i, cols):
        half = cols // 2

        @pl.when(i == 0)
        def _():
            self.wait(0)

        @pl.when(i == half)
        def _():
            self.wait(1)

        return lax.rem(i, half) * 2 + i // half


def column_of(sc, slot):
    return (slot // 4) * 4 + ((sc[1] & 3) ^ (slot & 3))


def weight_scratch(rows, cols, n):
    lead = len(lead_table(rows, cols))
    return [VMEM((cols, D, n), BF), pltpu.SemaphoreType.DMA((8, lead))]


def put(ref, start, value, lane=0):
    part = ref.shape[-1] - lane
    for i in range(value.shape[-1] // part):
        ref[start // part + i, :, lane:] = value[:, i * part : (i + 1) * part]


def lanes(start, width):
    return pl.ds(pl.multiple_of(start, width), width)


def prep_q_kernel(tokens, grads, bias_qv, bias_f, wq, wp, rows, out):
    hid = wq.shape[2]
    seq = tokens.shape[1]
    for c in range(tokens.shape[0]):
        rows[c, :seq] = tokens[c]
        rows[c, seq : 2 * seq] = grads[c]
        rows[c, 2 * seq : 2 * seq + 2] = bias_qv[...]
        for i in range(4):
            rows[c, 2 * seq + 2 + i, :] = bias_f[pl.ds(i * hid, hid)]
    for c in range(3):
        out[:, c * hid : (c + 1) * hid] = wq[c]
    out[:, 3 * hid :] = low(wp[...].astype(F32).T)


def prep_f_kernel(sc, mask, w1, w2, out_a, out_b, keep, closed):
    row = mask[pl.ds(sc[1], 1), :].astype(F32)
    row = jnp.concatenate([jnp.ones((1, BUF), F32), row], axis=1)
    column = jnp.broadcast_to(row, (8, SEQ)).T[:, :1]
    keep[...] = column
    closed[...] = 1.0 - column
    half = w1.shape[1] // 2
    out_a[:, :half] = w1[:, :half]
    out_b[:, :half] = w1[:, half:]
    out_a[:, half:] = low(w2[:half].astype(F32).T)
    out_b[:, half:] = low(w2[half:].astype(F32).T)


def fetch(sems, *pairs):
    copies = [pltpu.make_async_copy(src, dst, sems.at[i]) for i, (src, dst) in enumerate(pairs)]
    for copy in copies:
        copy.start()
    return copies


def rows_at(xa, start, height):
    return xa.at[:, pl.ds(start, height), :]


def across(ref, cols):
    return jnp.concatenate([ref[c] for c in range(cols)], axis=1).astype(F32)


def both_heads(pair):
    left = lax.broadcasted_iota(jnp.int32, (1, PAIR), 1) < HD
    zero = jnp.zeros_like(pair)
    return jnp.concatenate([jnp.where(left, pair, zero), jnp.where(left, zero, pair)], axis=0)


def own_heads(made, scale=1.0):
    both = jnp.concatenate([made[:HD, :SEQ], made[HD:, SEQ:]], axis=0)
    return low(both.T * scale)


def front_kernel(lead, cols, *refs):
    sc = refs[0]
    pieces = refs[1:9]
    (xa, closed, gain, shift, q_down, q_up, p_down, p_up, f_down, bias_out) = refs[9:19]
    (n1, lat1, q, k, v, lse, att, lat2, middle, n2, lat3) = refs[19:30]
    w, sems, hidden, branch, xs, bs, row_qd, row_pd, row_pu, row_fd, sems_f = refs[30:]
    a = sc[0]
    hid = D // cols
    first = fetch(
        sems_f,
        (rows_at(xa, 0, SEQ), xs),
        (q_down.at[a], row_qd),
        (rows_at(xa, 2 * SEQ, EXTRA), bs),
        (p_down.at[a], row_pd),
        (p_up.at[a], row_pu),
        (f_down.at[a], row_fd),
    )
    weights = Weights(sc, pieces, w, sems, lead)
    weights.start()
    first[0].wait()
    x = across(xs, cols)
    hidden[...] = x
    unit, _ = norm_parts(x)
    n1[...] = low(unit * gain[0:1] + shift[0:1])
    for copy in first[1:]:
        copy.wait()
    lat1[...] = low(mm(n1[...], row_qd[...], NT))

    def project(i, _):
        slot = weights.slot(i, cols)
        block = column_of(sc, slot)
        up = jnp.concatenate([q_up[c, :, lanes(block * hid, hid)] for c in range(3)], axis=1)
        made = mm(n1[...], w[slot, :, : 3 * hid]) + mm(lat1[...], up)
        bias_q = bs[block, 0:1, :].astype(F32)
        bias_v = bs[block, 1:2, :].astype(F32)
        at = lanes(slot * hid, hid)
        q[:, at] = low(made[:, :hid] + bias_q) * jnp.asarray(0.125, BF)
        k[:, at] = low(made[:, hid : 2 * hid])
        v[:, at] = low(made[:, 2 * hid :] + bias_v)
        return 0

    lax.fori_loop(0, cols, project, 0)
    shut = closed[...] > 0.5

    def attend(pair, _):
        at = lanes(pair * PAIR, PAIR)
        v_t = low(v[:, at].astype(F32).T)
        s = jnp.where(shut, -1e30, mm(k[:, at], both_heads(q[:, at]), NT))
        top = jnp.max(s, axis=0, keepdims=True)
        e = jnp.exp(s - top)
        total = jnp.sum(e, axis=0, keepdims=True)
        lse[pair] = top + jnp.log(total)
        att[:, at] = own_heads(mm(v_t, low(e * (1.0 / total))))
        return 0

    lax.fori_loop(0, H // 2, attend, 0, unroll=4)

    def down_two(slot, acc):
        block = column_of(sc, slot)
        return acc + mm(att[:, lanes(slot * hid, hid)], row_pd[:, lanes(block * hid, hid)], NT)

    lat2[...] = low(lax.fori_loop(0, cols, down_two, jnp.zeros((SEQ, R), F32)))
    branch[...] = mm(lat2[...], row_pu[...]) + bias_out[0:1].astype(F32)

    def out_proj(slot, _):
        branch[...] += mm(att[:, lanes(slot * hid, hid)], w[slot, :, 3 * hid :], NT)
        return 0

    lax.fori_loop(0, cols, out_proj, 0)
    mid = hidden[...] + branch[...]
    middle[...] = mid
    unit, _ = norm_parts(mid)
    n2[...] = low(unit * gain[1:2] + shift[1:2])
    lat3[...] = low(mm(n2[...], row_fd[...], NT))


def ffn_steps(weights, sc, part, cols, w, bs, n2, lat3, gr, glat4, up_1, down_2, acc, early, lane=0):
    res, gn2, lat4, glat3 = acc
    hid = D // cols
    ffn = FF // cols
    half = ffn // 2
    glat4_t = low(glat4.astype(F32).T)
    lat3_t = low(lat3[...].astype(F32).T)

    def step(i, _):
        slot = weights.slot(i, cols)
        block = column_of(sc, slot)
        at = pl.ds(pl.multiple_of(block * ffn + part * half, half), half)
        bias = jnp.concatenate(
            [bs[block, 2 + 2 * part + i : 3 + 2 * part + i, :] for i in range(2)], axis=1
        ).astype(F32)
        up, down = up_1[:, at], down_2[:, at]
        w1, w2 = w[slot, :, :half], w[slot, :, half:]
        pre = mm(n2[...], w1) + mm(lat3[...], up) + bias
        back = mm(gr[...], w2) + mm(glat4, down)
        cumulative = 0.5 * (1.0 + lax.erf(pre * 0.7071067811865476))
        activated = low(pre * cumulative)
        slope = cumulative + pre * jnp.exp(-0.5 * pre * pre) * 0.3989422804014327
        grad_pre = low(back * slope)
        lat4[...] += mm(activated, down, NT)
        glat3[...] += mm(grad_pre, up, NT)
        res[...] += mm(activated, w2, NT)
        gn2[...] += mm(grad_pre, w1, NT)
        put(early, block * half, low(mm(lat3_t, grad_pre)), lane)
        put(early, FF // 2 + block * half, low(mm(glat4_t, activated)), lane)
        return 0

    lax.fori_loop(0, cols, step, 0)


def ffn_a_kernel(lead, cols, *refs):
    sc = refs[0]
    pieces = refs[1:9]
    xa, keep, n2, lat3, up_1, down_2, up_2 = refs[9:16]
    res, gn2, lat4, glat3, gr, early = refs[16:22]
    w, sems, gs, bs, row_u1, row_d2, row_u2, sems_f = refs[22:]
    a = sc[0]
    first = fetch(
        sems_f,
        (rows_at(xa, SEQ, SEQ), gs),
        (up_2.at[a], row_u2),
        (rows_at(xa, 2 * SEQ, EXTRA), bs),
        (up_1.at[a], row_u1),
        (down_2.at[a], row_d2),
    )
    weights = Weights(sc, pieces, w, sems, lead)
    weights.start()
    first[0].wait()
    gr[...] = low(across(gs, cols) * keep[...])
    for copy in first[1:]:
        copy.wait()
    glat4 = low(mm(gr[...], row_u2[...], NT))
    res[...] = jnp.zeros_like(res)
    gn2[...] = jnp.zeros_like(gn2)
    lat4[...] = jnp.zeros_like(lat4)
    glat3[...] = jnp.zeros_like(glat3)
    ffn_steps(
        weights, sc, 0, cols, w, bs, n2, lat3, gr, glat4, row_u1, row_d2, (res, gn2, lat4, glat3), early
    )


def ffn_b_kernel(lead, cols, *refs):
    sc = refs[0]
    pieces = refs[1:9]
    own_q = refs[9:17]
    (xa, keep, gain, n2, lat3, up_1, down_2, up_2, f_down, p_down, p_up, bias_out) = refs[17:29]
    (middle, att, lat2, gr, res_in, gn2_in, lat4_in, glat3_in, early_in) = refs[29:38]
    layer, gatt, gmid, early = refs[38:42]
    w, sems, wp, sems_p, res, gn2, lat4, glat3 = refs[42:50]
    bs, row_u1, row_d2, row_u2, row_fd, row_pd, row_pu, mid_s, att_s, res_s, gn2_s, early_s = refs[50:62]
    sems_f = refs[62]
    lane = early_in.shape[-1]
    a = sc[0]
    first = fetch(
        sems_f,
        (up_2.at[a], row_u2),
        (rows_at(xa, 2 * SEQ, EXTRA), bs),
        (up_1.at[a], row_u1),
        (down_2.at[a], row_d2),
    )
    weights = Weights(sc, pieces, w, sems, lead)
    weights.start()
    proj = Weights(sc, own_q, wp, sems_p, lead, 3 * D // cols)
    last = fetch(
        sems_f.at[pl.ds(4, 8)],
        (res_in, res_s),
        (middle, mid_s),
        (gn2_in, gn2_s),
        (f_down.at[a], row_fd),
        (p_up.at[a], row_pu),
        (p_down.at[a], row_pd),
        (att, att_s),
        (early_in, early_s),
    )
    proj.start()
    hid = D // cols
    for copy in first:
        copy.wait()
    glat4 = low(mm(gr[...], row_u2[...], NT))
    res[...] = jnp.zeros_like(res)
    gn2[...] = jnp.zeros_like(gn2)
    lat4[...] = lat4_in[...]
    glat3[...] = glat3_in[...]
    ffn_steps(
        weights, sc, 1, cols, w, bs, n2, lat3, gr, glat4, row_u1, row_d2, (res, gn2, lat4, glat3), early, lane
    )
    for copy in last:
        copy.wait()
    early[:, :, :lane] = early_s[...]
    mid = mid_s[...]
    lat4_low = low(lat4[...])
    out = low(
        keep[...]
        * (mid + (res_s[...] + res[...]) + mm(lat4_low, row_u2[...]) + bias_out[1:2].astype(F32))
    )
    for c in range(cols):
        layer[c] = out[:, c * hid : (c + 1) * hid]
    glat3_low = low(glat3[...])
    grad_normed = gn2_s[...] + gn2[...] + mm(glat3_low, row_fd[...])
    unit, inverse = norm_parts(mid)
    grad_middle = gr[...].astype(F32) + norm_back(grad_normed, gain[1:2], unit, inverse)
    gmid[...] = grad_middle
    gb = low(grad_middle)
    glat2 = low(mm(gb, row_pu[...], NT))
    glat2_t = low(glat2.astype(F32).T)
    put(early, FF + D, low(mm(low(lat2[...].astype(F32).T), gb)), lane)
    put(early, FF + 2 * D, low(mm(low(glat3_low.astype(F32).T), n2[...])), lane)
    put(early, FF + 3 * D, low(mm(low(lat4_low.astype(F32).T), gr[...])), lane)
    proj.wait()

    def step(slot, _):
        block = column_of(sc, slot)
        here = lanes(slot * hid, hid)
        there = lanes(block * hid, hid)
        gatt[:, here] = low(mm(gb, wp[slot]) + mm(glat2, row_pd[:, there]))
        put(early, FF + block * hid, low(mm(glat2_t, att_s[:, here])), lane)
        return 0

    lax.fori_loop(0, cols, step, 0)


def attention_back_kernel(cols, *refs):
    sc = refs[0]
    closed, q, k, v, lse, gatt, lat1, n1, q_up = refs[1:10]
    gq, gk, gv, glat1, late = refs[10:15]
    a = sc[0]
    hid = D // cols
    shut = closed[...] > 0.5

    def attend(pair, _):
        at = lanes(pair * PAIR, PAIR)
        kp = k[:, at]
        k_t = low(kp.astype(F32).T)
        q_both, g_both = both_heads(q[:, at]), both_heads(gatt[:, at])
        s = jnp.where(shut, -1e30, mm(kp, q_both, NT))
        soft = jnp.exp(s - lse[pair])
        grad_soft = mm(v[:, at], g_both, NT)
        total = jnp.sum(grad_soft * soft, axis=0, keepdims=True)
        grad_scores = low(soft * (grad_soft - total))
        gq[:, at] = own_heads(mm(k_t, grad_scores), 0.125)
        gk[:, at] = low(mm(grad_scores, q_both))
        gv[:, at] = low(mm(low(soft), g_both))
        return 0

    lax.fori_loop(0, H // 2, attend, 0, unroll=4)
    lat1_t = low(lat1[...].astype(F32).T)

    def step(slot, acc):
        block = column_of(sc, slot)
        here = lanes(slot * hid, hid)
        there = lanes(block * hid, hid)
        for c, g in enumerate((gq, gk, gv)):
            grad = g[:, here]
            acc = acc + mm(grad, q_up[c, :, there], NT)
            put(late, (c + 1) * D + block * hid, low(mm(lat1_t, grad)))
        return acc

    made = low(lax.fori_loop(0, cols, step, jnp.zeros((SEQ, R), F32)))
    glat1[...] = made
    put(late, 0, low(mm(low(made.astype(F32).T), n1[...])))


def back_kernel(lead, cols, *refs):
    sc = refs[0]
    pieces = refs[1:9]
    xa, gain, gq, gk, gv, glat1, q_down, gmid, layer = refs[9:18]
    out = refs[18]
    w, sems, acc, xs, row_qd, gmid_s, sems_f = refs[19:]
    first = fetch(
        sems_f,
        (rows_at(xa, 0, SEQ), xs),
        (q_down.at[sc[0]], row_qd),
        (gmid, gmid_s),
        (layer, rows_at(out, 0, SEQ)),
    )
    weights = Weights(sc, pieces, w, sems, lead)
    weights.start()
    hid = D // cols
    for copy in first:
        copy.wait()
    acc[...] = mm(glat1[...], row_qd[...])
    x = across(xs, cols)
    unit, inverse = norm_parts(x)

    def step(i, _):
        slot = weights.slot(i, cols)
        here = lanes(slot * hid, hid)
        grad = jnp.concatenate([gq[:, here], gk[:, here], gv[:, here]], axis=1)
        acc[...] += mm(grad, w[slot, :, : 3 * hid], NT)
        return 0

    lax.fori_loop(0, cols, step, 0)
    made = low(gmid_s[...] + norm_back(acc[...], gain[0:1], unit, inverse))
    for c in range(cols):
        out[c, SEQ:] = made[:, c * hid : (c + 1) * hid]


def sum_kernel(owners, mine, out, acc):
    acc[...] = jnp.zeros_like(acc)
    for d in range(mine.shape[0]):
        acc[owners[d]] += mine[d, :, : acc.shape[2]].astype(F32)
    out[...] = low(acc[...])


def spread_kernel(lead, cols, parts, maps, *refs):
    sc, pieces = refs[0], refs[1:9]
    count = (len(refs) - 11) // 2
    outs, whole, made = refs[9 : 9 + count], refs[9 + count], refs[10 + count : 10 + 2 * count]
    sems_in, sems_out = refs[10 + 2 * count :]
    copies = []
    for k, piece in enumerate(pieces):
        x_rel, y_rel, away = piece_place(sc, k)
        for n, (high_col, high_row) in enumerate(lead):
            row = high_row * 2 + ((sc[3] + y_rel) & 1)
            col = high_col * 4 + ((sc[1] & 3) ^ (x_rel * 2 + away))
            copies.append(
                pltpu.make_async_copy(piece.at[n], whole.at[row * cols + col], sems_in.at[k, n])
            )
    for copy in copies:
        copy.start()
    for copy in copies:
        copy.wait()
    found = [[] for _ in outs]
    base = 0
    for part, spans in zip(parts, maps):
        for out, section, there, start, width in spans:
            for lane in range(0, width, 128):
                at = start + lane
                found[out].append((section, there + lane, at // part, base + at % part))
        base += part
    leaving = []
    for i, (out, buffer) in enumerate(zip(outs, made)):
        for section, there, device, here in found[i]:
            block = whole[device, :, here : here + 128].astype(F32)
            if section is None:
                buffer[:, there : there + 128] = block
            else:
                buffer[:, section, :, there : there + 128] = block.reshape(NA, R, 128)
        leaving.append(pltpu.make_async_copy(buffer, out, sems_out.at[i]))
        leaving[-1].start()
    for copy in leaving:
        copy.wait()


def place_kernel(lead, cols, *refs):
    sc, pieces, out, sems = refs[0], refs[1:9], refs[9], refs[10]
    copies = []
    for k, piece in enumerate(pieces):
        x_rel, y_rel, away = piece_place(sc, k)
        for n, (high_col, high_row) in enumerate(lead):
            row = high_row * 2 + ((sc[3] + y_rel) & 1)
            col = high_col * 4 + ((sc[1] & 3) ^ (x_rel * 2 + away))
            copies.append(pltpu.make_async_copy(piece.at[n], out.at[row * cols + col], sems.at[k, n]))
    for copy in copies:
        copy.start()
    for copy in copies:
        copy.wait()


def send_grads(grads):
    return lax.all_to_all(grads, BOTH, split_axis=0, concat_axis=0, tiled=True)


def sum_grads(mine, owners, part):
    summed = call(
        sum_kernel,
        jax.ShapeDtypeStruct((NA, R, part), BF),
        [owners, mine],
        [pltpu.SMEM, VMEM],
        [VMEM((NA, R, part), F32)],
    )
    return summed.reshape(NA * R, part)


def spread(sc, pieces, parts, maps, shapes):
    rows, cols = sizes()
    devices = rows * cols
    lead = lead_table(rows, cols)
    arrivals = pltpu.SemaphoreType.DMA((8, len(lead)))
    whole = (devices, NA * R, sum(parts))
    ins, spaces = [sc, *pieces], [pltpu.SMEM] + [pl.ANY] * 8
    if all(p % 128 == 0 for p in parts):
        return call(
            functools.partial(spread_kernel, lead, cols, parts, maps),
            [jax.ShapeDtypeStruct(x, F32) for x in shapes],
            ins,
            spaces,
            [VMEM(whole, BF)]
            + [VMEM(x, F32) for x in shapes]
            + [arrivals, pltpu.SemaphoreType.DMA((len(shapes),))],
            pl.ANY,
            SPREAD,
        )
    whole = call(
        functools.partial(place_kernel, lead, cols),
        jax.ShapeDtypeStruct(whole, BF),
        ins,
        spaces,
        [arrivals],
    )
    found = [[] for _ in shapes]
    base = 0
    for part, spans in zip(parts, maps):
        flat = jnp.swapaxes(whole[:, :, base : base + part], 0, 1).reshape(NA * R, devices * part)
        for out, section, there, start, width in spans:
            found[out].append((section or 0, there, flat[:, start : start + width].astype(F32)))
        base += part
    return [
        (
            jnp.concatenate([x for _, _, x in sorted(f, key=lambda e: e[:2])], axis=1)
            if len(shape) == 2
            else jnp.stack([x.reshape(NA, R, -1) for _, _, x in sorted(f, key=lambda e: e[:2])], 1)
        )
        for f, shape in zip(found, shapes)
    ]


def per_device(
    tokens_in,
    grad_out,
    keep_mask,
    adapter_index,
    ln_gain,
    ln_shift,
    w_qkv,
    bias_qv,
    w_proj,
    w_fc1,
    bias_fc1,
    w_fc2,
    bias_out,
    qkv_down,
    qkv_up,
    proj_down,
    proj_up,
    fc1_down,
    fc1_up,
    fc2_down,
    fc2_up,
):
    rows, cols = sizes()
    row, column = lax.axis_index("row"), lax.axis_index("col")
    assert adapter_index.shape[0] == cols and cols >= 4 and rows >= 2
    hid = D // cols
    n = 4 * hid
    blk = D // rows
    lead = lead_table(rows, cols)

    shard = jax.ShapeDtypeStruct((blk, n), BF)
    rows_in, shard_q = call(
        prep_q_kernel,
        [jax.ShapeDtypeStruct((cols, 2 * SEQ + EXTRA, hid), BF), shard],
        [tokens_in.reshape(cols, SEQ, hid), grad_out.reshape(cols, SEQ, hid), bias_qv]
        + [bias_fc1, w_qkv, w_proj],
        [VMEM] * 6,
        mib=56,
    )
    with jax.named_scope("q_high"):
        own_q, came_q = gather_high(shard_q)
    xa = lax.all_to_all(rows_in, "col", split_axis=0, concat_axis=0, tiled=True)
    adapter = lax.dynamic_index_in_dim(adapter_index, column, 0, keepdims=False)
    sc = jnp.stack([adapter, column, column % 2, row % 2]).astype(jnp.int32)
    up_qkv = jnp.swapaxes(lax.dynamic_index_in_dim(qkv_up, adapter, 0, keepdims=False), 0, 1)
    shard_a, shard_b, keep, closed = call(
        prep_f_kernel,
        [shard] * 2 + [jax.ShapeDtypeStruct((SEQ, 1), F32)] * 2,
        [sc, keep_mask, w_fc1, w_fc2],
        [pltpu.SMEM] + [VMEM] * 3,
    )

    own_q, shard_a, shard_b = after_all(
        (own_q, shard_a, shard_b), xa, keep, closed, sc, up_qkv, *came_q
    )
    with jax.named_scope("q_one"):
        one_q = swap(own_q, flip_one)
    with jax.named_scope("q_two"):
        two_q = swap(own_q, flip_two)
    with jax.named_scope("fa_high"):
        own_a, came_a = gather_high(shard_a)
    own_q, one_q, two_q = after_all((own_q, one_q, two_q), *came_a)
    with jax.named_scope("q_both"):
        both_q = swap(one_q, flip_two)
    with jax.named_scope("q_core"):
        away_q = [swap(p, flip_core) for p in (own_q, one_q, two_q)]
    own_a, shard_b = after_all((own_a, shard_b), *away_q)
    with jax.named_scope("q_core"):
        pieces_q = [own_q, one_q, two_q, both_q] + away_q + [swap(both_q, flip_core)]
    with jax.named_scope("fa_one"):
        one_a = swap(own_a, flip_one)
    with jax.named_scope("fa_two"):
        two_a = swap(own_a, flip_two)
    with jax.named_scope("fb_high"):
        own_b, came_b = gather_high(shard_b)

    def shaped(width, dtype, height=SEQ):
        return jax.ShapeDtypeStruct((height, width), dtype)

    big, small = shaped(D, BF), shaped(R, BF)
    scratch = weight_scratch(rows, cols, n)
    rows_space, bias_space = VMEM((cols, SEQ, hid), BF), VMEM((cols, EXTRA, hid), BF)
    any_space = [pl.ANY] * 8
    n1, lat1, q, k, v, lse, att, lat2, middle, n2, lat3 = call(
        functools.partial(front_kernel, lead, cols),
        [
            big,
            small,
            big,
            big,
            big,
            jax.ShapeDtypeStruct((H // 2, 1, 2 * SEQ), F32),
            big,
            small,
            shaped(D, F32),
            big,
            small,
        ],
        [sc, *pieces_q, xa, closed, ln_gain, ln_shift, qkv_down, up_qkv, proj_down]
        + [proj_up]
        + [fc1_down, bias_out],
        [pltpu.SMEM] + any_space + [pl.ANY] + [VMEM] * 3 + [pl.ANY, VMEM] + [pl.ANY] * 3 + [VMEM],
        scratch
        + [VMEM((SEQ, D), F32), VMEM((SEQ, D), F32), rows_space, bias_space]
        + [VMEM((R, D), BF)] * 4
        + [pltpu.SemaphoreType.DMA((6,))],
        mib=FRONT,
    )
    own_a, one_a, two_a = after_all((own_a, one_a, two_a), n1, *came_b)
    bits = list(reversed(range(bits_of(rows))))
    owners = after(adapter_index, n1)
    for bit in bits[:-1]:
        owners = owner_stack(owner_parts(owners, bit), bit)
    with jax.named_scope("fa_both"):
        both_a = swap(one_a, flip_two)
    with jax.named_scope("fa_core"):
        away_a = [swap(p, flip_core) for p in (own_a, one_a, two_a)]
    own_b, owners = after_all((own_b, owners), *away_a)
    owners = owner_parts(owners, 0)
    with jax.named_scope("fa_core"):
        pieces_a = [own_a, one_a, two_a, both_a] + away_a + [swap(both_a, flip_core)]
    with jax.named_scope("fb_one"):
        one_b = swap(own_b, flip_one)
    with jax.named_scope("fb_two"):
        two_b = swap(own_b, flip_two)
    wide = shaped(D, F32)
    thin = shaped(R, F32)
    res, gn2, lat4, glat3, gr, early_a = call(
        functools.partial(ffn_a_kernel, lead, cols),
        [wide, wide, thin, thin, big, jax.ShapeDtypeStruct((rows * cols, R, FF // (rows * cols)), BF)],
        [sc, *pieces_a, xa, keep, n2, lat3, fc1_up, fc2_down, fc2_up],
        [pltpu.SMEM] + any_space + [pl.ANY] + [VMEM] * 3 + [pl.ANY] * 3,
        scratch
        + [rows_space, bias_space, VMEM((R, FF), BF), VMEM((R, FF), BF), VMEM((R, D), BF)]
        + [pltpu.SemaphoreType.DMA((5,))],
        mib=FFN_A,
    )
    own_b, one_b, two_b, *owners = after_all((own_b, one_b, two_b, *owners), res)
    owners = owner_stack(owners, 0).transpose(tuple(bits) + (len(bits),)).reshape(-1)
    with jax.named_scope("fb_both"):
        both_b = swap(one_b, flip_two)
    with jax.named_scope("fb_core"):
        away_b = [swap(p, flip_core) for p in (own_b, one_b, two_b)]
        pieces_b = [own_b, one_b, two_b, both_b] + away_b + [swap(both_b, flip_core)]
    layer, gatt, gmid, grads_b = call(
        functools.partial(ffn_b_kernel, lead, cols),
        [jax.ShapeDtypeStruct((cols, SEQ, hid), BF), big, wide]
        + [jax.ShapeDtypeStruct((rows * cols, R, 12 * D // (rows * cols)), BF)],
        [sc, *pieces_b, *pieces_q, xa, keep, ln_gain, n2, lat3, fc1_up, fc2_down, fc2_up]
        + [fc1_down, proj_down, proj_up, bias_out]
        + [middle, att, lat2, gr, res, gn2, lat4, glat3, early_a],
        [pltpu.SMEM]
        + any_space * 2
        + [pl.ANY, VMEM, VMEM, VMEM, VMEM]
        + [pl.ANY] * 6
        + [VMEM, pl.ANY, pl.ANY, VMEM, VMEM, pl.ANY, pl.ANY, VMEM, VMEM, pl.ANY],
        scratch
        + [VMEM((cols, D, hid), BF), scratch[1]]
        + [VMEM((SEQ, D), F32), VMEM((SEQ, D), F32), VMEM((SEQ, R), F32), VMEM((SEQ, R), F32)]
        + [bias_space, VMEM((R, FF), BF), VMEM((R, FF), BF)]
        + [VMEM((R, D), BF)] * 4
        + [VMEM((SEQ, D), F32), VMEM((SEQ, D), BF), VMEM((SEQ, D), F32), VMEM((SEQ, D), F32)]
        + [VMEM(early_a.shape, BF), pltpu.SemaphoreType.DMA((12,))],
        mib=FFN_B,
    )
    with jax.named_scope("grads_b_send"):
        mine_b = send_grads(grads_b)
    gq, gk, gv, glat1, late = call(
        functools.partial(attention_back_kernel, cols),
        [big, big, big, small, jax.ShapeDtypeStruct((rows * cols, R, 4 * D // (rows * cols)), BF)],
        [sc, closed, q, k, v, lse, gatt, lat1, n1, up_qkv],
        [pltpu.SMEM] + [VMEM] * 9,
        mib=ATT,
    )
    with jax.named_scope("grads_c_send"):
        mine_c = send_grads(late)
    with jax.named_scope("grads_b"):
        own_b, _ = gather_high(
            sum_grads(after(mine_b, late), owners, mine_b.shape[2]), 1
        )
        own_c, _ = gather_high(sum_grads(mine_c, owners, mine_c.shape[2]))
        order_b = tuple(lead.index(place) for place in lead_table(rows, cols, 1))
        own = lane_join([own_b, own_c], [order_b, tuple(range(len(lead)))])
    gmid = after(gmid, own)
    sent = call(
        functools.partial(back_kernel, lead, cols),
        jax.ShapeDtypeStruct((cols, 2 * SEQ, hid), BF),
        [sc, *pieces_q, xa, ln_gain, gq, gk, gv, glat1, qkv_down, gmid, layer],
        [pltpu.SMEM] + any_space + [pl.ANY] + [VMEM] * 5 + [pl.ANY] * 3,
        scratch
        + [VMEM((SEQ, D), F32), rows_space, VMEM((R, D), BF), VMEM((SEQ, D), F32)]
        + [pltpu.SemaphoreType.DMA((4,))],
        mib=BACK,
    )
    with jax.named_scope("grads"):
        one, two = swap(own, flip_one), swap(own, flip_two)
        own, one, two = after_all((own, one, two), sent)
        both = swap(one, flip_two)
        pieces = with_cores([own, one, two, both])
        half = FF // cols // 2
        map_a, map_b = (
            tuple(
                (out, None, (2 * block + part) * half, base + block * half, half)
                for out, base in ((0, 0), (1, FF // 2))
                for block in range(cols)
            )
            for part in (0, 1)
        )
        map_b = map_b + tuple((2 + i, None, 0, FF + i * D, D) for i in range(4))
        map_c = ((6, None, 0, 0, D),) + tuple((7, c, 0, (c + 1) * D, D) for c in range(3))
        parts = [early_a.shape[-1], mine_b.shape[-1] - early_a.shape[-1], mine_c.shape[-1]]
        shapes = [(NA * R, FF)] * 2 + [(NA * R, D)] * 5 + [(NA, 3, R, D)]
        sums = spread(sc, pieces, parts, [map_a, map_b, map_c], shapes)

    with jax.named_scope("rows_out"):
        sent = after(sent, pieces[4])
        rows_out = lax.all_to_all(sent, "col", split_axis=0, concat_axis=0, tiled=True)
    layer, grad_in = rows_out[:, :SEQ], rows_out[:, SEQ:]

    def split(table):
        return table.reshape((NA, R) + table.shape[1:])

    g_fc1_up, g_fc2_down, g_proj_down, g_proj_up, g_fc1_down, g_fc2_up = map(split, sums[:6])
    return (
        layer.reshape(cols * SEQ, hid),
        grad_in.reshape(cols * SEQ, hid),
        split(sums[6]),
        jnp.swapaxes(sums[7], 1, 2),
        g_proj_down,
        g_proj_up,
        g_fc1_down,
        g_fc1_up,
        g_fc2_down,
        g_fc2_up,
    )


def solution(mesh):
    return jax.shard_map(
        per_device,
        mesh=mesh,
        in_specs=(
            P("row", "col"),
            P("row", "col"),
            P("row", None),
            P("row"),
            P(),
            P(),
            P(None, "row", "col"),
            P(None, "col"),
            P("col", "row"),
            P("row", "col"),
            P("col"),
            P("col", "row"),
            P(),
            P(),
            P(),
            P(),
            P(),
            P(),
            P(),
            P(),
            P(),
        ),
        out_specs=(P("row", "col"), P("row", "col"), P(), P(), P(), P(), P(), P(), P(), P()),
        check_vma=False,
    )
```

```python
import functools

import jax
import jax.numpy as jnp
from jax import lax
from jax.experimental import pallas as pl
from jax.experimental.pallas import tpu as pltpu
from jax.sharding import PartitionSpec as P

D = 1024
H = 16
HD = 64
FF = 4096
BUF = 64
R = 16
NA = 8
SEQ = 320
PAIR = 2 * HD
EXTRA = 16
SPREAD = 56
FRONT, FFN_A, FFN_B, ATT, BACK = 56, 56, 56, 56, 56
BF = jnp.bfloat16
F32 = jnp.float32
BOTH = ("row", "col")
VMEM = pltpu.VMEM
NN = (((1,), (0,)), ((), ()))
NT = (((1,), (1,)), ((), ()))


def mm(left, right, dims=NN):
    return lax.dot_general(left, right, dims, preferred_element_type=F32)


def low(values):
    return values.astype(BF)


def norm_parts(values):
    row_mean = jnp.mean(values, axis=-1, keepdims=True)
    centered = values - row_mean
    variance = jnp.mean(centered * centered, axis=-1, keepdims=True)
    inverse = lax.rsqrt(variance + 1e-06)
    return (centered * inverse, inverse)


def norm_back(grad_normed, gain_row, unit_rows, inverse):
    scaled = grad_normed * gain_row
    first_mean = jnp.mean(scaled, axis=-1, keepdims=True)
    second_mean = jnp.mean(scaled * unit_rows, axis=-1, keepdims=True)
    return inverse * (scaled - first_mean - unit_rows * second_mean)


def call(kernel, outs, ins, spaces, scratch=(), out_space=VMEM, mib=4):
    return pl.pallas_call(
        kernel,
        out_shape=outs,
        in_specs=[pl.BlockSpec(memory_space=s) for s in spaces],
        out_specs=jax.tree.map(lambda _: pl.BlockSpec(memory_space=out_space), outs),
        scratch_shapes=list(scratch),
        compiler_params=pltpu.CompilerParams(vmem_limit_bytes=mib << 20),
        cost_estimate=pl.CostEstimate(flops=0, bytes_accessed=0, transcendentals=0),
    )(*ins)


def sizes():
    return lax.axis_size("row"), lax.axis_size("col")


def swap(block, flip):
    rows, cols = sizes()
    pairs = []
    for i in range(rows * cols):
        row, col = flip(i // cols, i % cols)
        pairs.append((i, row * cols + col))
    return lax.ppermute(block, BOTH, pairs)


def bits_of(size):
    return size.bit_length() - 1


def stack_kernel(which, *refs):
    parts, out, sems = refs[:-2], refs[-2], refs[-1]
    copies = [
        pltpu.make_async_copy(ref, out.at[which[0] ^ m], sems.at[m]) for m, ref in enumerate(parts)
    ]
    for copy in copies:
        copy.start()
    for copy in copies:
        copy.wait()


def stacked(parts, index, out_space=VMEM):
    shape = parts[0].shape
    flat = [p.reshape((-1, shape[-1])) for p in parts]
    out = jax.ShapeDtypeStruct((len(parts),) + flat[0].shape, flat[0].dtype)
    made = call(
        stack_kernel,
        out,
        [index.reshape(1).astype(jnp.int32)] + flat,
        [pltpu.SMEM] + [pl.ANY] * len(parts),
        [pltpu.SemaphoreType.DMA((len(parts),))],
        out_space,
    )
    return made.reshape((len(parts),) + shape)


def group_join(block, axis, low_bit, width):
    parts = [block]
    for m in range(1, 1 << width):
        step = m << low_bit
        if axis == "row":
            parts.append(swap(block, lambda r, c: (r ^ step, c)))
        else:
            parts.append(swap(block, lambda r, c: (r, c ^ step)))
    index = (lax.axis_index(axis) >> low_bit) & ((1 << width) - 1)
    return stacked(parts, index), parts


def groups(top, bottom, most):
    out = []
    while top > bottom:
        width = min(most, top - bottom)
        out.append((top - width, width))
        top -= width
    return out


def early_groups(rows, cols, most):
    return [("row",) + g for g in groups(bits_of(rows), 1, most)] + [
        ("col",) + g for g in groups(bits_of(cols), 2, most)
    ]


def lead_table(rows, cols, most=2):
    table = [(0, 0)]
    for axis, bit, width in early_groups(rows, cols, most):
        shift = bit - (1 if axis == "row" else 2)
        new = []
        for value in range(1 << width):
            for high_col, high_row in table:
                if axis == "row":
                    new.append((high_col, high_row + (value << shift)))
                else:
                    new.append((high_col + (value << shift), high_row))
        table = new
    return table


def after(value, *others):
    return lax.optimization_barrier((value,) + others)[0]


def after_all(values, *others):
    return lax.optimization_barrier(tuple(values) + others)[: len(values)]


def exchange_rows(parts):
    came = [parts[0]]
    for j in range(1, len(parts)):
        came.append(swap(parts[j], lambda r, c: (r, c ^ j)))
    return came


def gather_high(shard, most=2):
    rows, cols = sizes()
    block, parts = shard, []
    for axis, bit, width in early_groups(rows, cols, most):
        block, parts = group_join(block, axis, bit, width)
    return block.reshape((-1,) + shard.shape), parts[1:]


def lane_join_kernel(orders, *refs):
    parts, out, sems = refs[:-2], refs[-2], refs[-1]
    copies, lane = [], 0
    for i, (part, order) in enumerate(zip(parts, orders)):
        width = part.shape[-1]
        for n, put_at in enumerate(order):
            target = out.at[put_at, :, lane : lane + width]
            copies.append(pltpu.make_async_copy(part.at[n], target, sems.at[i, n]))
        lane += width
    for copy in copies:
        copy.start()
    for copy in copies:
        copy.wait()


def lane_join(parts, orders):
    if any(p.shape[-1] % 128 for p in parts):
        placed = [p[jnp.array(sorted(range(len(o)), key=o.index))] for p, o in zip(parts, orders)]
        return jnp.concatenate(placed, axis=-1)
    shape = parts[0].shape[:-1] + (sum(p.shape[-1] for p in parts),)
    return call(
        functools.partial(lane_join_kernel, orders),
        jax.ShapeDtypeStruct(shape, parts[0].dtype),
        parts,
        [pl.ANY] * len(parts),
        [pltpu.SemaphoreType.DMA((len(parts), shape[0]))],
    )


def flip_one(r, c):
    return (r, c ^ 2) if c % 2 == 0 else (r ^ 1, c)


def flip_two(r, c):
    return (r ^ 1, c) if c % 2 == 0 else (r, c ^ 2)


def flip_core(r, c):
    return (r, c ^ 1)


def with_cores(pieces):
    return pieces + [swap(p, flip_core) for p in pieces]


def owner_parts(block, bit):
    step = 1 << bit
    return [block, swap(block, lambda r, c: (r ^ step, c))]


def owner_stack(parts, bit):
    return jnp.stack(parts)[jnp.arange(2) ^ ((lax.axis_index("row") >> bit) & 1)]


def piece_place(sc, k):
    kind, away = k % 4, k // 4
    turn = (sc[2] + away) & 1
    return (0, 1 - turn, turn, 1)[kind], (0, turn, 1 - turn, 1)[kind], away


class Weights:
    def __init__(self, sc, pieces, w, sems, lead, first_lane=0):
        self.copies = []
        depth = pieces[0].shape[1]
        taken = pl.ds(first_lane, w.shape[2])
        for k, piece in enumerate(pieces):
            x_rel, y_rel, away = piece_place(sc, k)
            for n, (high_col, high_row) in enumerate(lead):
                slot = high_col * 4 + x_rel * 2 + away
                row = (high_row * 2 + ((sc[3] + y_rel) & 1)) * depth
                self.copies.append(
                    pltpu.make_async_copy(
                        piece.at[n, :, taken],
                        w.at[slot, pl.ds(pl.multiple_of(row, depth), depth), :],
                        sems.at[k, n],
                    )
                )

    def start(self):
        for copy in self.copies:
            copy.start()

    def wait(self, away=None):
        half = len(self.copies) // 2
        for copy in self.copies if away is None else self.copies[away * half : (away + 1) * half]:
            copy.wait()

    def slot(self, i, cols):
        half = cols // 2

        @pl.when(i == 0)
        def _():
            self.wait(0)

        @pl.when(i == half)
        def _():
            self.wait(1)

        return lax.rem(i, half) * 2 + i // half


def column_of(sc, slot):
    return (slot // 4) * 4 + ((sc[1] & 3) ^ (slot & 3))


def weight_scratch(rows, cols, n):
    lead = len(lead_table(rows, cols))
    return [VMEM((cols, D, n), BF), pltpu.SemaphoreType.DMA((8, lead))]


def put(ref, start, value, lane=0):
    part = ref.shape[-1] - lane
    for i in range(value.shape[-1] // part):
        ref[start // part + i, :, lane:] = value[:, i * part : (i + 1) * part]


def lanes(start, width):
    return pl.ds(pl.multiple_of(start, width), width)


def prep_q_kernel(tokens, grads, bias_qv, bias_f, wq, wp, rows, out):
    hid = wq.shape[2]
    seq = tokens.shape[1]
    for c in range(tokens.shape[0]):
        rows[c, :seq] = tokens[c]
        rows[c, seq : 2 * seq] = grads[c]
        rows[c, 2 * seq : 2 * seq + 2] = bias_qv[...]
        for i in range(4):
            rows[c, 2 * seq + 2 + i, :] = bias_f[pl.ds(i * hid, hid)]
    for c in range(3):
        out[:, c * hid : (c + 1) * hid] = wq[c]
    out[:, 3 * hid :] = low(wp[...].astype(F32).T)


def prep_f_kernel(sc, mask, w1, w2, out_a, out_b, keep, closed):
    row = mask[pl.ds(sc[1], 1), :].astype(F32)
    row = jnp.concatenate([jnp.ones((1, BUF), F32), row], axis=1)
    column = jnp.broadcast_to(row, (8, SEQ)).T[:, :1]
    keep[...] = column
    closed[...] = 1.0 - column
    half = w1.shape[1] // 2
    out_a[:, :half] = w1[:, :half]
    out_b[:, :half] = w1[:, half:]
    out_a[:, half:] = low(w2[:half].astype(F32).T)
    out_b[:, half:] = low(w2[half:].astype(F32).T)


def fetch(sems, *pairs):
    copies = [pltpu.make_async_copy(src, dst, sems.at[i]) for i, (src, dst) in enumerate(pairs)]
    for copy in copies:
        copy.start()
    return copies


def to_columns(sc, made, buffer, outs):
    hid = outs[0].shape[-1]
    buffer[...] = made
    for j, out in enumerate(outs):
        out[...] = buffer[:, lanes((sc[1] ^ j) * hid, hid)]


def rows_at(xa, start, height):
    return xa.at[:, pl.ds(start, height), :]


def across(ref, cols):
    return jnp.concatenate([ref[c] for c in range(cols)], axis=1).astype(F32)


def both_heads(pair):
    left = lax.broadcasted_iota(jnp.int32, (1, PAIR), 1) < HD
    zero = jnp.zeros_like(pair)
    return jnp.concatenate([jnp.where(left, pair, zero), jnp.where(left, zero, pair)], axis=0)


def own_heads(made, scale=1.0):
    both = jnp.concatenate([made[:HD, :SEQ], made[HD:, SEQ:]], axis=0)
    return low(both.T * scale)


def front_kernel(lead, cols, *refs):
    sc = refs[0]
    pieces = refs[1:9]
    (xa, closed, gain, shift, q_down, q_up, p_down, p_up, f_down, bias_out) = refs[9:19]
    (n1, lat1, q, k, v, lse, att, lat2, middle, n2, lat3) = refs[19:30]
    w, sems, hidden, branch, xs, bs, row_qd, row_pd, row_pu, row_fd, sems_f = refs[30:]
    a = sc[0]
    hid = D // cols
    first = fetch(
        sems_f,
        (rows_at(xa, 0, SEQ), xs),
        (q_down.at[a], row_qd),
        (rows_at(xa, 2 * SEQ, EXTRA), bs),
        (p_down.at[a], row_pd),
        (p_up.at[a], row_pu),
        (f_down.at[a], row_fd),
    )
    weights = Weights(sc, pieces, w, sems, lead)
    weights.start()
    first[0].wait()
    x = across(xs, cols)
    hidden[...] = x
    unit, _ = norm_parts(x)
    n1[...] = low(unit * gain[0:1] + shift[0:1])
    for copy in first[1:]:
        copy.wait()
    lat1[...] = low(mm(n1[...], row_qd[...], NT))

    def project(i, _):
        slot = weights.slot(i, cols)
        block = column_of(sc, slot)
        up = jnp.concatenate([q_up[c, :, lanes(block * hid, hid)] for c in range(3)], axis=1)
        made = mm(n1[...], w[slot, :, : 3 * hid]) + mm(lat1[...], up)
        bias_q = bs[block, 0:1, :].astype(F32)
        bias_v = bs[block, 1:2, :].astype(F32)
        at = lanes(slot * hid, hid)
        q[:, at] = low(made[:, :hid] + bias_q) * jnp.asarray(0.125, BF)
        k[:, at] = low(made[:, hid : 2 * hid])
        v[:, at] = low(made[:, 2 * hid :] + bias_v)
        return 0

    lax.fori_loop(0, cols, project, 0)
    shut = closed[...] > 0.5

    def attend(pair, _):
        at = lanes(pair * PAIR, PAIR)
        v_t = low(v[:, at].astype(F32).T)
        s = jnp.where(shut, -1e30, mm(k[:, at], both_heads(q[:, at]), NT))
        top = jnp.max(s, axis=0, keepdims=True)
        e = jnp.exp(s - top)
        total = jnp.sum(e, axis=0, keepdims=True)
        lse[pair] = top + jnp.log(total)
        att[:, at] = own_heads(mm(v_t, low(e * (1.0 / total))))
        return 0

    lax.fori_loop(0, H // 2, attend, 0, unroll=4)

    def down_two(slot, acc):
        block = column_of(sc, slot)
        return acc + mm(att[:, lanes(slot * hid, hid)], row_pd[:, lanes(block * hid, hid)], NT)

    lat2[...] = low(lax.fori_loop(0, cols, down_two, jnp.zeros((SEQ, R), F32)))
    branch[...] = mm(lat2[...], row_pu[...]) + bias_out[0:1].astype(F32)

    def out_proj(slot, _):
        branch[...] += mm(att[:, lanes(slot * hid, hid)], w[slot, :, 3 * hid :], NT)
        return 0

    lax.fori_loop(0, cols, out_proj, 0)
    mid = hidden[...] + branch[...]
    middle[...] = mid
    unit, _ = norm_parts(mid)
    n2[...] = low(unit * gain[1:2] + shift[1:2])
    lat3[...] = low(mm(n2[...], row_fd[...], NT))


def ffn_steps(weights, sc, part, cols, w, bs, n2, lat3, gr, glat4, up_1, down_2, acc, early, lane=0):
    res, gn2, lat4, glat3 = acc
    hid = D // cols
    ffn = FF // cols
    half = ffn // 2
    glat4_t = low(glat4.astype(F32).T)
    lat3_t = low(lat3[...].astype(F32).T)

    def step(i, _):
        slot = weights.slot(i, cols)
        block = column_of(sc, slot)
        at = pl.ds(pl.multiple_of(block * ffn + part * half, half), half)
        bias = jnp.concatenate(
            [bs[block, 2 + 2 * part + i : 3 + 2 * part + i, :] for i in range(2)], axis=1
        ).astype(F32)
        up, down = up_1[:, at], down_2[:, at]
        w1, w2 = w[slot, :, :half], w[slot, :, half:]
        pre = mm(n2[...], w1) + mm(lat3[...], up) + bias
        back = mm(gr[...], w2) + mm(glat4, down)
        cumulative = 0.5 * (1.0 + lax.erf(pre * 0.7071067811865476))
        activated = low(pre * cumulative)
        slope = cumulative + pre * jnp.exp(-0.5 * pre * pre) * 0.3989422804014327
        grad_pre = low(back * slope)
        lat4[...] += mm(activated, down, NT)
        glat3[...] += mm(grad_pre, up, NT)
        res[...] += mm(activated, w2, NT)
        gn2[...] += mm(grad_pre, w1, NT)
        put(early, block * half, low(mm(lat3_t, grad_pre)), lane)
        put(early, FF // 2 + block * half, low(mm(glat4_t, activated)), lane)
        return 0

    lax.fori_loop(0, cols, step, 0)


def ffn_a_kernel(lead, cols, *refs):
    sc = refs[0]
    pieces = refs[1:9]
    xa, keep, n2, lat3, up_1, down_2, up_2 = refs[9:16]
    res, gn2, lat4, glat3, gr, early = refs[16:22]
    w, sems, gs, bs, row_u1, row_d2, row_u2, sems_f = refs[22:]
    a = sc[0]
    first = fetch(
        sems_f,
        (rows_at(xa, SEQ, SEQ), gs),
        (up_2.at[a], row_u2),
        (rows_at(xa, 2 * SEQ, EXTRA), bs),
        (up_1.at[a], row_u1),
        (down_2.at[a], row_d2),
    )
    weights = Weights(sc, pieces, w, sems, lead)
    weights.start()
    first[0].wait()
    gr[...] = low(across(gs, cols) * keep[...])
    for copy in first[1:]:
        copy.wait()
    glat4 = low(mm(gr[...], row_u2[...], NT))
    res[...] = jnp.zeros_like(res)
    gn2[...] = jnp.zeros_like(gn2)
    lat4[...] = jnp.zeros_like(lat4)
    glat3[...] = jnp.zeros_like(glat3)
    ffn_steps(
        weights, sc, 0, cols, w, bs, n2, lat3, gr, glat4, row_u1, row_d2, (res, gn2, lat4, glat3), early
    )


def ffn_b_kernel(lead, cols, *refs):
    sc = refs[0]
    pieces = refs[1:9]
    own_q = refs[9:17]
    (xa, keep, gain, n2, lat3, up_1, down_2, up_2, f_down, p_down, p_up, bias_out) = refs[17:29]
    (middle, att, lat2, gr, res_in, gn2_in, lat4_in, glat3_in, early_in) = refs[29:38]
    layer, refs = refs[38 : 38 + cols], refs[:38] + refs[38 + cols :]
    gatt, gmid, early = refs[38:41]
    refs = refs[:41] + (None,) + refs[41:]
    w, sems, wp, sems_p, res, gn2, lat4, glat3 = refs[42:50]
    bs, row_u1, row_d2, row_u2, row_fd, row_pd, row_pu, mid_s, att_s, res_s, gn2_s, early_s = refs[50:62]
    sems_f, out_s = refs[62:]
    lane = early_in.shape[-1]
    a = sc[0]
    first = fetch(
        sems_f,
        (up_2.at[a], row_u2),
        (rows_at(xa, 2 * SEQ, EXTRA), bs),
        (up_1.at[a], row_u1),
        (down_2.at[a], row_d2),
    )
    weights = Weights(sc, pieces, w, sems, lead)
    weights.start()
    proj = Weights(sc, own_q, wp, sems_p, lead, 3 * D // cols)
    last = fetch(
        sems_f.at[pl.ds(4, 8)],
        (res_in, res_s),
        (middle, mid_s),
        (gn2_in, gn2_s),
        (f_down.at[a], row_fd),
        (p_up.at[a], row_pu),
        (p_down.at[a], row_pd),
        (att, att_s),
        (early_in, early_s),
    )
    proj.start()
    hid = D // cols
    for copy in first:
        copy.wait()
    glat4 = low(mm(gr[...], row_u2[...], NT))
    res[...] = jnp.zeros_like(res)
    gn2[...] = jnp.zeros_like(gn2)
    lat4[...] = lat4_in[...]
    glat3[...] = glat3_in[...]
    ffn_steps(
        weights, sc, 1, cols, w, bs, n2, lat3, gr, glat4, row_u1, row_d2, (res, gn2, lat4, glat3), early, lane
    )
    for copy in last:
        copy.wait()
    early[:, :, :lane] = early_s[...]
    mid = mid_s[...]
    lat4_low = low(lat4[...])
    out = low(
        keep[...]
        * (mid + (res_s[...] + res[...]) + mm(lat4_low, row_u2[...]) + bias_out[1:2].astype(F32))
    )
    to_columns(sc, out, out_s, layer)
    glat3_low = low(glat3[...])
    grad_normed = gn2_s[...] + gn2[...] + mm(glat3_low, row_fd[...])
    unit, inverse = norm_parts(mid)
    grad_middle = gr[...].astype(F32) + norm_back(grad_normed, gain[1:2], unit, inverse)
    gmid[...] = grad_middle
    gb = low(grad_middle)
    glat2 = low(mm(gb, row_pu[...], NT))
    glat2_t = low(glat2.astype(F32).T)
    put(early, FF + D, low(mm(low(lat2[...].astype(F32).T), gb)), lane)
    put(early, FF + 2 * D, low(mm(low(glat3_low.astype(F32).T), n2[...])), lane)
    put(early, FF + 3 * D, low(mm(low(lat4_low.astype(F32).T), gr[...])), lane)
    proj.wait()

    def step(slot, _):
        block = column_of(sc, slot)
        here = lanes(slot * hid, hid)
        there = lanes(block * hid, hid)
        gatt[:, here] = low(mm(gb, wp[slot]) + mm(glat2, row_pd[:, there]))
        put(early, FF + block * hid, low(mm(glat2_t, att_s[:, here])), lane)
        return 0

    lax.fori_loop(0, cols, step, 0)


def attention_back_kernel(cols, *refs):
    sc = refs[0]
    closed, q, k, v, lse, gatt, lat1, n1, q_up = refs[1:10]
    gq, gk, gv, glat1, late = refs[10:15]
    a = sc[0]
    hid = D // cols
    shut = closed[...] > 0.5

    def attend(pair, _):
        at = lanes(pair * PAIR, PAIR)
        kp = k[:, at]
        k_t = low(kp.astype(F32).T)
        q_both, g_both = both_heads(q[:, at]), both_heads(gatt[:, at])
        s = jnp.where(shut, -1e30, mm(kp, q_both, NT))
        soft = jnp.exp(s - lse[pair])
        grad_soft = mm(v[:, at], g_both, NT)
        total = jnp.sum(grad_soft * soft, axis=0, keepdims=True)
        grad_scores = low(soft * (grad_soft - total))
        gq[:, at] = own_heads(mm(k_t, grad_scores), 0.125)
        gk[:, at] = low(mm(grad_scores, q_both))
        gv[:, at] = low(mm(low(soft), g_both))
        return 0

    lax.fori_loop(0, H // 2, attend, 0, unroll=4)
    lat1_t = low(lat1[...].astype(F32).T)

    def step(slot, acc):
        block = column_of(sc, slot)
        here = lanes(slot * hid, hid)
        there = lanes(block * hid, hid)
        for c, g in enumerate((gq, gk, gv)):
            grad = g[:, here]
            acc = acc + mm(grad, q_up[c, :, there], NT)
            put(late, (c + 1) * D + block * hid, low(mm(lat1_t, grad)))
        return acc

    made = low(lax.fori_loop(0, cols, step, jnp.zeros((SEQ, R), F32)))
    glat1[...] = made
    put(late, 0, low(mm(low(made.astype(F32).T), n1[...])))


def back_kernel(lead, cols, *refs):
    sc = refs[0]
    pieces = refs[1:9]
    xa, gain, gq, gk, gv, glat1, q_down, gmid = refs[9:17]
    outs = refs[17 : 17 + cols]
    w, sems, acc, xs, row_qd, gmid_s, sems_f, out_s = refs[17 + cols :]
    first = fetch(
        sems_f,
        (rows_at(xa, 0, SEQ), xs),
        (q_down.at[sc[0]], row_qd),
        (gmid, gmid_s),
    )
    weights = Weights(sc, pieces, w, sems, lead)
    weights.start()
    hid = D // cols
    for copy in first:
        copy.wait()
    acc[...] = mm(glat1[...], row_qd[...])
    x = across(xs, cols)
    unit, inverse = norm_parts(x)

    def step(i, _):
        slot = weights.slot(i, cols)
        here = lanes(slot * hid, hid)
        grad = jnp.concatenate([gq[:, here], gk[:, here], gv[:, here]], axis=1)
        acc[...] += mm(grad, w[slot, :, : 3 * hid], NT)
        return 0

    lax.fori_loop(0, cols, step, 0)
    made = low(gmid_s[...] + norm_back(acc[...], gain[0:1], unit, inverse))
    to_columns(sc, made, out_s, outs)


def sum_kernel(owners, mine, out, acc):
    acc[...] = jnp.zeros_like(acc)
    for d in range(mine.shape[0]):
        acc[owners[d]] += mine[d, :, : acc.shape[2]].astype(F32)
    out[...] = low(acc[...])


def spread_kernel(lead, cols, parts, maps, *refs):
    sc, pieces = refs[0], refs[1:9]
    count = (len(refs) - 11) // 2
    outs, whole, made = refs[9 : 9 + count], refs[9 + count], refs[10 + count : 10 + 2 * count]
    sems_in, sems_out = refs[10 + 2 * count :]
    copies = []
    for k, piece in enumerate(pieces):
        x_rel, y_rel, away = piece_place(sc, k)
        for n, (high_col, high_row) in enumerate(lead):
            row = high_row * 2 + ((sc[3] + y_rel) & 1)
            col = high_col * 4 + ((sc[1] & 3) ^ (x_rel * 2 + away))
            copies.append(
                pltpu.make_async_copy(piece.at[n], whole.at[row * cols + col], sems_in.at[k, n])
            )
    for copy in copies:
        copy.start()
    for copy in copies:
        copy.wait()
    found = [[] for _ in outs]
    base = 0
    for part, spans in zip(parts, maps):
        for out, section, there, start, width in spans:
            for lane in range(0, width, 128):
                at = start + lane
                found[out].append((section, there + lane, at // part, base + at % part))
        base += part
    leaving = []
    for i, (out, buffer) in enumerate(zip(outs, made)):
        for section, there, device, here in found[i]:
            block = whole[device, :, here : here + 128].astype(F32)
            if section is None:
                buffer[:, there : there + 128] = block
            else:
                buffer[:, section, :, there : there + 128] = block.reshape(NA, R, 128)
        leaving.append(pltpu.make_async_copy(buffer, out, sems_out.at[i]))
        leaving[-1].start()
    for copy in leaving:
        copy.wait()


def place_kernel(lead, cols, *refs):
    sc, pieces, out, sems = refs[0], refs[1:9], refs[9], refs[10]
    copies = []
    for k, piece in enumerate(pieces):
        x_rel, y_rel, away = piece_place(sc, k)
        for n, (high_col, high_row) in enumerate(lead):
            row = high_row * 2 + ((sc[3] + y_rel) & 1)
            col = high_col * 4 + ((sc[1] & 3) ^ (x_rel * 2 + away))
            copies.append(pltpu.make_async_copy(piece.at[n], out.at[row * cols + col], sems.at[k, n]))
    for copy in copies:
        copy.start()
    for copy in copies:
        copy.wait()


def send_grads(grads):
    return lax.all_to_all(grads, BOTH, split_axis=0, concat_axis=0, tiled=True)


def sum_grads(mine, owners, part):
    summed = call(
        sum_kernel,
        jax.ShapeDtypeStruct((NA, R, part), BF),
        [owners, mine],
        [pltpu.SMEM, VMEM],
        [VMEM((NA, R, part), F32)],
    )
    return summed.reshape(NA * R, part)


def spread(sc, pieces, parts, maps, shapes):
    rows, cols = sizes()
    devices = rows * cols
    lead = lead_table(rows, cols)
    arrivals = pltpu.SemaphoreType.DMA((8, len(lead)))
    whole = (devices, NA * R, sum(parts))
    ins, spaces = [sc, *pieces], [pltpu.SMEM] + [pl.ANY] * 8
    if all(p % 128 == 0 for p in parts):
        return call(
            functools.partial(spread_kernel, lead, cols, parts, maps),
            [jax.ShapeDtypeStruct(x, F32) for x in shapes],
            ins,
            spaces,
            [VMEM(whole, BF)]
            + [VMEM(x, F32) for x in shapes]
            + [arrivals, pltpu.SemaphoreType.DMA((len(shapes),))],
            pl.ANY,
            SPREAD,
        )
    whole = call(
        functools.partial(place_kernel, lead, cols),
        jax.ShapeDtypeStruct(whole, BF),
        ins,
        spaces,
        [arrivals],
    )
    found = [[] for _ in shapes]
    base = 0
    for part, spans in zip(parts, maps):
        flat = jnp.swapaxes(whole[:, :, base : base + part], 0, 1).reshape(NA * R, devices * part)
        for out, section, there, start, width in spans:
            found[out].append((section or 0, there, flat[:, start : start + width].astype(F32)))
        base += part
    return [
        (
            jnp.concatenate([x for _, _, x in sorted(f, key=lambda e: e[:2])], axis=1)
            if len(shape) == 2
            else jnp.stack([x.reshape(NA, R, -1) for _, _, x in sorted(f, key=lambda e: e[:2])], 1)
        )
        for f, shape in zip(found, shapes)
    ]


def per_device(
    tokens_in,
    grad_out,
    keep_mask,
    adapter_index,
    ln_gain,
    ln_shift,
    w_qkv,
    bias_qv,
    w_proj,
    w_fc1,
    bias_fc1,
    w_fc2,
    bias_out,
    qkv_down,
    qkv_up,
    proj_down,
    proj_up,
    fc1_down,
    fc1_up,
    fc2_down,
    fc2_up,
):
    rows, cols = sizes()
    row, column = lax.axis_index("row"), lax.axis_index("col")
    assert adapter_index.shape[0] == cols and cols >= 4 and rows >= 2
    hid = D // cols
    n = 4 * hid
    blk = D // rows
    lead = lead_table(rows, cols)

    shard = jax.ShapeDtypeStruct((blk, n), BF)
    rows_in, shard_q = call(
        prep_q_kernel,
        [jax.ShapeDtypeStruct((cols, 2 * SEQ + EXTRA, hid), BF), shard],
        [tokens_in.reshape(cols, SEQ, hid), grad_out.reshape(cols, SEQ, hid), bias_qv]
        + [bias_fc1, w_qkv, w_proj],
        [VMEM] * 6,
        mib=56,
    )
    with jax.named_scope("q_high"):
        own_q, came_q = gather_high(shard_q)
    xa = lax.all_to_all(rows_in, "col", split_axis=0, concat_axis=0, tiled=True)
    adapter = lax.dynamic_index_in_dim(adapter_index, column, 0, keepdims=False)
    sc = jnp.stack([adapter, column, column % 2, row % 2]).astype(jnp.int32)
    up_qkv = jnp.swapaxes(lax.dynamic_index_in_dim(qkv_up, adapter, 0, keepdims=False), 0, 1)
    shard_a, shard_b, keep, closed = call(
        prep_f_kernel,
        [shard] * 2 + [jax.ShapeDtypeStruct((SEQ, 1), F32)] * 2,
        [sc, keep_mask, w_fc1, w_fc2],
        [pltpu.SMEM] + [VMEM] * 3,
    )

    own_q, shard_a, shard_b = after_all(
        (own_q, shard_a, shard_b), xa, keep, closed, sc, up_qkv, *came_q
    )
    with jax.named_scope("q_one"):
        one_q = swap(own_q, flip_one)
    with jax.named_scope("q_two"):
        two_q = swap(own_q, flip_two)
    with jax.named_scope("fa_high"):
        own_a, came_a = gather_high(shard_a)
    own_q, one_q, two_q = after_all((own_q, one_q, two_q), *came_a)
    with jax.named_scope("q_both"):
        both_q = swap(one_q, flip_two)
    with jax.named_scope("q_core"):
        away_q = [swap(p, flip_core) for p in (own_q, one_q, two_q)]
    own_a, shard_b = after_all((own_a, shard_b), *away_q)
    with jax.named_scope("q_core"):
        pieces_q = [own_q, one_q, two_q, both_q] + away_q + [swap(both_q, flip_core)]
    with jax.named_scope("fa_one"):
        one_a = swap(own_a, flip_one)
    with jax.named_scope("fa_two"):
        two_a = swap(own_a, flip_two)
    with jax.named_scope("fb_high"):
        own_b, came_b = gather_high(shard_b)

    def shaped(width, dtype, height=SEQ):
        return jax.ShapeDtypeStruct((height, width), dtype)

    big, small = shaped(D, BF), shaped(R, BF)
    scratch = weight_scratch(rows, cols, n)
    rows_space, bias_space = VMEM((cols, SEQ, hid), BF), VMEM((cols, EXTRA, hid), BF)
    any_space = [pl.ANY] * 8
    n1, lat1, q, k, v, lse, att, lat2, middle, n2, lat3 = call(
        functools.partial(front_kernel, lead, cols),
        [
            big,
            small,
            big,
            big,
            big,
            jax.ShapeDtypeStruct((H // 2, 1, 2 * SEQ), F32),
            big,
            small,
            shaped(D, F32),
            big,
            small,
        ],
        [sc, *pieces_q, xa, closed, ln_gain, ln_shift, qkv_down, up_qkv, proj_down]
        + [proj_up]
        + [fc1_down, bias_out],
        [pltpu.SMEM] + any_space + [pl.ANY] + [VMEM] * 3 + [pl.ANY, VMEM] + [pl.ANY] * 3 + [VMEM],
        scratch
        + [VMEM((SEQ, D), F32), VMEM((SEQ, D), F32), rows_space, bias_space]
        + [VMEM((R, D), BF)] * 4
        + [pltpu.SemaphoreType.DMA((6,))],
        mib=FRONT,
    )
    own_a, one_a, two_a = after_all((own_a, one_a, two_a), n1, *came_b)
    bits = list(reversed(range(bits_of(rows))))
    owners = after(adapter_index, n1)
    for bit in bits[:-1]:
        owners = owner_stack(owner_parts(owners, bit), bit)
    with jax.named_scope("fa_both"):
        both_a = swap(one_a, flip_two)
    with jax.named_scope("fa_core"):
        away_a = [swap(p, flip_core) for p in (own_a, one_a, two_a)]
    own_b, owners = after_all((own_b, owners), *away_a)
    owners = owner_parts(owners, 0)
    with jax.named_scope("fa_core"):
        pieces_a = [own_a, one_a, two_a, both_a] + away_a + [swap(both_a, flip_core)]
    with jax.named_scope("fb_one"):
        one_b = swap(own_b, flip_one)
    with jax.named_scope("fb_two"):
        two_b = swap(own_b, flip_two)
    wide = shaped(D, F32)
    thin = shaped(R, F32)
    res, gn2, lat4, glat3, gr, early_a = call(
        functools.partial(ffn_a_kernel, lead, cols),
        [wide, wide, thin, thin, big, jax.ShapeDtypeStruct((rows * cols, R, FF // (rows * cols)), BF)],
        [sc, *pieces_a, xa, keep, n2, lat3, fc1_up, fc2_down, fc2_up],
        [pltpu.SMEM] + any_space + [pl.ANY] + [VMEM] * 3 + [pl.ANY] * 3,
        scratch
        + [rows_space, bias_space, VMEM((R, FF), BF), VMEM((R, FF), BF), VMEM((R, D), BF)]
        + [pltpu.SemaphoreType.DMA((5,))],
        mib=FFN_A,
    )
    own_b, one_b, two_b, *owners = after_all((own_b, one_b, two_b, *owners), res)
    owners = owner_stack(owners, 0).transpose(tuple(bits) + (len(bits),)).reshape(-1)
    with jax.named_scope("fb_both"):
        both_b = swap(one_b, flip_two)
    with jax.named_scope("fb_core"):
        away_b = [swap(p, flip_core) for p in (own_b, one_b, two_b)]
        pieces_b = [own_b, one_b, two_b, both_b] + away_b + [swap(both_b, flip_core)]
    *layer, gatt, gmid, grads_b = call(
        functools.partial(ffn_b_kernel, lead, cols),
        [shaped(hid, BF)] * cols + [big, wide]
        + [jax.ShapeDtypeStruct((rows * cols, R, 12 * D // (rows * cols)), BF)],
        [sc, *pieces_b, *pieces_q, xa, keep, ln_gain, n2, lat3, fc1_up, fc2_down, fc2_up]
        + [fc1_down, proj_down, proj_up, bias_out]
        + [middle, att, lat2, gr, res, gn2, lat4, glat3, early_a],
        [pltpu.SMEM]
        + any_space * 2
        + [pl.ANY, VMEM, VMEM, VMEM, VMEM]
        + [pl.ANY] * 6
        + [VMEM, pl.ANY, pl.ANY, VMEM, VMEM, pl.ANY, pl.ANY, VMEM, VMEM, pl.ANY],
        scratch
        + [VMEM((cols, D, hid), BF), scratch[1]]
        + [VMEM((SEQ, D), F32), VMEM((SEQ, D), F32), VMEM((SEQ, R), F32), VMEM((SEQ, R), F32)]
        + [bias_space, VMEM((R, FF), BF), VMEM((R, FF), BF)]
        + [VMEM((R, D), BF)] * 4
        + [VMEM((SEQ, D), F32), VMEM((SEQ, D), BF), VMEM((SEQ, D), F32), VMEM((SEQ, D), F32)]
        + [VMEM(early_a.shape, BF), pltpu.SemaphoreType.DMA((12,)), VMEM((SEQ, D), BF)],
        mib=FFN_B,
    )
    with jax.named_scope("grads_b_send"):
        mine_b = send_grads(grads_b)
    with jax.named_scope("layer_out"):
        layer = exchange_rows(layer)
    gq, gk, gv, glat1, late = call(
        functools.partial(attention_back_kernel, cols),
        [big, big, big, small, jax.ShapeDtypeStruct((rows * cols, R, 4 * D // (rows * cols)), BF)],
        [sc, closed, q, k, v, lse, gatt, lat1, n1, up_qkv],
        [pltpu.SMEM] + [VMEM] * 9,
        mib=ATT,
    )
    with jax.named_scope("grads_c_send"):
        mine_c = send_grads(late)
    with jax.named_scope("grads_b"):
        own_b, _ = gather_high(
            sum_grads(after(mine_b, late, *layer), owners, mine_b.shape[2]), 1
        )
        own_c, _ = gather_high(sum_grads(mine_c, owners, mine_c.shape[2]))
        order_b = tuple(lead.index(place) for place in lead_table(rows, cols, 1))
        own = lane_join([own_b, own_c], [order_b, tuple(range(len(lead)))])
    gmid = after(gmid, own)
    sent = call(
        functools.partial(back_kernel, lead, cols),
        [shaped(hid, BF)] * cols,
        [sc, *pieces_q, xa, ln_gain, gq, gk, gv, glat1, qkv_down, gmid],
        [pltpu.SMEM] + any_space + [pl.ANY] + [VMEM] * 5 + [pl.ANY] * 2,
        scratch
        + [VMEM((SEQ, D), F32), rows_space, VMEM((R, D), BF), VMEM((SEQ, D), F32)]
        + [pltpu.SemaphoreType.DMA((3,)), VMEM((SEQ, D), BF)],
        mib=BACK,
    )
    with jax.named_scope("grads"):
        one, two = swap(own, flip_one), swap(own, flip_two)
        own, one, two = after_all((own, one, two), *sent)
        layer_out = stacked(after_all(layer, one, two), column, pl.ANY)
        both = swap(one, flip_two)
        away = [swap(p, flip_core) for p in (own, one, two)]
        both = after(both, layer_out)
        pieces = [own, one, two, both] + away + [swap(both, flip_core)]
        half = FF // cols // 2
        map_a, map_b = (
            tuple(
                (out, None, (2 * block + part) * half, base + block * half, half)
                for out, base in ((0, 0), (1, FF // 2))
                for block in range(cols)
            )
            for part in (0, 1)
        )
        map_b = map_b + tuple((2 + i, None, 0, FF + i * D, D) for i in range(4))
        map_c = ((6, None, 0, 0, D),) + tuple((7, c, 0, (c + 1) * D, D) for c in range(3))
        parts = [early_a.shape[-1], mine_b.shape[-1] - early_a.shape[-1], mine_c.shape[-1]]
        shapes = [(NA * R, FF)] * 2 + [(NA * R, D)] * 5 + [(NA, 3, R, D)]
        sums = spread(sc, pieces, parts, [map_a, map_b, map_c], shapes)

    with jax.named_scope("rows_out"):
        grad_rows = exchange_rows(after_all(sent, *away))
        grad_in = stacked(after_all(grad_rows, sums[0]), column, pl.ANY)

    def split(table):
        return table.reshape((NA, R) + table.shape[1:])

    g_fc1_up, g_fc2_down, g_proj_down, g_proj_up, g_fc1_down, g_fc2_up = map(split, sums[:6])
    return (
        layer_out.reshape(cols * SEQ, hid),
        grad_in.reshape(cols * SEQ, hid),
        split(sums[6]),
        jnp.swapaxes(sums[7], 1, 2),
        g_proj_down,
        g_proj_up,
        g_fc1_down,
        g_fc1_up,
        g_fc2_down,
        g_fc2_up,
    )


def solution(mesh):
    return jax.shard_map(
        per_device,
        mesh=mesh,
        in_specs=(
            P("row", "col"),
            P("row", "col"),
            P("row", None),
            P("row"),
            P(),
            P(),
            P(None, "row", "col"),
            P(None, "col"),
            P("col", "row"),
            P("row", "col"),
            P("col"),
            P("col", "row"),
            P(),
            P(),
            P(),
            P(),
            P(),
            P(),
            P(),
            P(),
            P(),
        ),
        out_specs=(P("row", "col"), P("row", "col"), P(), P(), P(), P(), P(), P(), P(), P()),
        check_vma=False,
    )
```

```python
import functools

import jax
import jax.numpy as jnp
from jax import lax
from jax.experimental import pallas as pl
from jax.experimental.pallas import tpu as pltpu
from jax.sharding import PartitionSpec as P

D = 1024
H = 16
HD = 64
FF = 4096
BUF = 64
R = 16
NA = 8
SEQ = 320
PAIR = 2 * HD
EXTRA = 16
SPREAD = 56
FRONT, FFN_A, FFN_B, ATT, BACK = 56, 56, 56, 56, 56
BF = jnp.bfloat16
F32 = jnp.float32
BOTH = ("row", "col")
VMEM = pltpu.VMEM
NN = (((1,), (0,)), ((), ()))
NT = (((1,), (1,)), ((), ()))


def mm(left, right, dims=NN):
    return lax.dot_general(left, right, dims, preferred_element_type=F32)


def low(values):
    return values.astype(BF)


def norm_parts(values):
    row_mean = jnp.mean(values, axis=-1, keepdims=True)
    centered = values - row_mean
    variance = jnp.mean(centered * centered, axis=-1, keepdims=True)
    inverse = lax.rsqrt(variance + 1e-06)
    return (centered * inverse, inverse)


def norm_back(grad_normed, gain_row, unit_rows, inverse):
    scaled = grad_normed * gain_row
    first_mean = jnp.mean(scaled, axis=-1, keepdims=True)
    second_mean = jnp.mean(scaled * unit_rows, axis=-1, keepdims=True)
    return inverse * (scaled - first_mean - unit_rows * second_mean)


def call(kernel, outs, ins, spaces, scratch=(), out_space=VMEM, mib=4):
    return pl.pallas_call(
        kernel,
        out_shape=outs,
        in_specs=[pl.BlockSpec(memory_space=s) for s in spaces],
        out_specs=jax.tree.map(lambda _: pl.BlockSpec(memory_space=out_space), outs),
        scratch_shapes=list(scratch),
        compiler_params=pltpu.CompilerParams(vmem_limit_bytes=mib << 20),
        cost_estimate=pl.CostEstimate(flops=0, bytes_accessed=0, transcendentals=0),
    )(*ins)


def sizes():
    return lax.axis_size("row"), lax.axis_size("col")


def swap(block, flip):
    rows, cols = sizes()
    pairs = []
    for i in range(rows * cols):
        row, col = flip(i // cols, i % cols)
        pairs.append((i, row * cols + col))
    return lax.ppermute(block, BOTH, pairs)


def bits_of(size):
    return size.bit_length() - 1


def stack_kernel(which, *refs):
    parts, out, sems = refs[:-2], refs[-2], refs[-1]
    copies = [
        pltpu.make_async_copy(ref, out.at[which[0] ^ m], sems.at[m]) for m, ref in enumerate(parts)
    ]
    for copy in copies:
        copy.start()
    for copy in copies:
        copy.wait()


def stacked(parts, index, out_space=VMEM):
    shape = parts[0].shape
    flat = [p.reshape((-1, shape[-1])) for p in parts]
    out = jax.ShapeDtypeStruct((len(parts),) + flat[0].shape, flat[0].dtype)
    made = call(
        stack_kernel,
        out,
        [index.reshape(1).astype(jnp.int32)] + flat,
        [pltpu.SMEM] + [pl.ANY] * len(parts),
        [pltpu.SemaphoreType.DMA((len(parts),))],
        out_space,
    )
    return made.reshape((len(parts),) + shape)


def group_join(block, axis, low_bit, width):
    parts = [block]
    for m in range(1, 1 << width):
        step = m << low_bit
        if axis == "row":
            parts.append(swap(block, lambda r, c: (r ^ step, c)))
        else:
            parts.append(swap(block, lambda r, c: (r, c ^ step)))
    index = (lax.axis_index(axis) >> low_bit) & ((1 << width) - 1)
    return stacked(parts, index), parts


def groups(top, bottom, most):
    out = []
    while top > bottom:
        width = min(most, top - bottom)
        out.append((top - width, width))
        top -= width
    return out


def early_groups(rows, cols, most):
    return [("row",) + g for g in groups(bits_of(rows), 1, most)] + [
        ("col",) + g for g in groups(bits_of(cols), 2, most)
    ]


def lead_table(rows, cols, most=2):
    table = [(0, 0)]
    for axis, bit, width in early_groups(rows, cols, most):
        shift = bit - (1 if axis == "row" else 2)
        new = []
        for value in range(1 << width):
            for high_col, high_row in table:
                if axis == "row":
                    new.append((high_col, high_row + (value << shift)))
                else:
                    new.append((high_col + (value << shift), high_row))
        table = new
    return table


def after(value, *others):
    return lax.optimization_barrier((value,) + others)[0]


def after_all(values, *others):
    return lax.optimization_barrier(tuple(values) + others)[: len(values)]


def exchange_rows(parts):
    came = [parts[0]]
    for j in range(1, len(parts)):
        came.append(swap(parts[j], lambda r, c: (r, c ^ j)))
    return came


def gather_high(shard, most=2):
    rows, cols = sizes()
    block, parts = shard, []
    for axis, bit, width in early_groups(rows, cols, most):
        block, parts = group_join(block, axis, bit, width)
    return block.reshape((-1,) + shard.shape), parts[1:]


def lane_join_kernel(orders, *refs):
    parts, out, sems = refs[:-2], refs[-2], refs[-1]
    copies, lane = [], 0
    for i, (part, order) in enumerate(zip(parts, orders)):
        width = part.shape[-1]
        for n, put_at in enumerate(order):
            target = out.at[put_at, :, lane : lane + width]
            copies.append(pltpu.make_async_copy(part.at[n], target, sems.at[i, n]))
        lane += width
    for copy in copies:
        copy.start()
    for copy in copies:
        copy.wait()


def lane_join(parts, orders):
    if any(p.shape[-1] % 128 for p in parts):
        placed = [p[jnp.array(sorted(range(len(o)), key=o.index))] for p, o in zip(parts, orders)]
        return jnp.concatenate(placed, axis=-1)
    shape = parts[0].shape[:-1] + (sum(p.shape[-1] for p in parts),)
    return call(
        functools.partial(lane_join_kernel, orders),
        jax.ShapeDtypeStruct(shape, parts[0].dtype),
        parts,
        [pl.ANY] * len(parts),
        [pltpu.SemaphoreType.DMA((len(parts), shape[0]))],
    )


def flip_one(r, c):
    return (r, c ^ 2) if c % 2 == 0 else (r ^ 1, c)


def flip_two(r, c):
    return (r ^ 1, c) if c % 2 == 0 else (r, c ^ 2)


def flip_core(r, c):
    return (r, c ^ 1)


def with_cores(pieces):
    return pieces + [swap(p, flip_core) for p in pieces]


def owner_parts(block, bit):
    step = 1 << bit
    return [block, swap(block, lambda r, c: (r ^ step, c))]


def owner_stack(parts, bit):
    return jnp.stack(parts)[jnp.arange(2) ^ ((lax.axis_index("row") >> bit) & 1)]


def piece_place(sc, k):
    kind, away = k % 4, k // 4
    turn = (sc[2] + away) & 1
    return (0, 1 - turn, turn, 1)[kind], (0, turn, 1 - turn, 1)[kind], away


class Weights:
    def __init__(self, sc, pieces, w, sems, lead, first_lane=0):
        self.copies = []
        depth = pieces[0].shape[1]
        taken = pl.ds(first_lane, w.shape[2])
        for k, piece in enumerate(pieces):
            x_rel, y_rel, away = piece_place(sc, k)
            for n, (high_col, high_row) in enumerate(lead):
                slot = high_col * 4 + x_rel * 2 + away
                row = (high_row * 2 + ((sc[3] + y_rel) & 1)) * depth
                self.copies.append(
                    pltpu.make_async_copy(
                        piece.at[n, :, taken],
                        w.at[slot, pl.ds(pl.multiple_of(row, depth), depth), :],
                        sems.at[k, n],
                    )
                )

    def start(self):
        for copy in self.copies:
            copy.start()

    def wait(self, away=None):
        half = len(self.copies) // 2
        for copy in self.copies if away is None else self.copies[away * half : (away + 1) * half]:
            copy.wait()

    def slot(self, i, cols):
        half = cols // 2

        @pl.when(i == 0)
        def _():
            self.wait(0)

        @pl.when(i == half)
        def _():
            self.wait(1)

        return lax.rem(i, half) * 2 + i // half


def column_of(sc, slot):
    return (slot // 4) * 4 + ((sc[1] & 3) ^ (slot & 3))


def weight_scratch(rows, cols, n):
    lead = len(lead_table(rows, cols))
    return [VMEM((cols, D, n), BF), pltpu.SemaphoreType.DMA((8, lead))]


def put(ref, start, value, lane=0):
    part = ref.shape[-1] - lane
    for i in range(value.shape[-1] // part):
        ref[start // part + i, :, lane:] = value[:, i * part : (i + 1) * part]


def lanes(start, width):
    return pl.ds(pl.multiple_of(start, width), width)


def prep_q_kernel(tokens, grads, bias_qv, bias_f, wq, wp, rows, out):
    hid = wq.shape[2]
    seq = tokens.shape[1]
    for c in range(tokens.shape[0]):
        rows[c, :seq] = tokens[c]
        rows[c, seq : 2 * seq] = grads[c]
        rows[c, 2 * seq : 2 * seq + 2] = bias_qv[...]
        for i in range(4):
            rows[c, 2 * seq + 2 + i, :] = bias_f[pl.ds(i * hid, hid)]
    for c in range(3):
        out[:, c * hid : (c + 1) * hid] = wq[c]
    out[:, 3 * hid :] = low(wp[...].astype(F32).T)


def prep_f_kernel(sc, mask, w1, w2, out_a, out_b, keep, closed):
    row = mask[pl.ds(sc[1], 1), :].astype(F32)
    row = jnp.concatenate([jnp.ones((1, BUF), F32), row], axis=1)
    column = jnp.broadcast_to(row, (8, SEQ)).T[:, :1]
    keep[...] = column
    closed[...] = 1.0 - column
    half = w1.shape[1] // 2
    out_a[:, :half] = w1[:, :half]
    out_b[:, :half] = w1[:, half:]
    out_a[:, half:] = low(w2[:half].astype(F32).T)
    out_b[:, half:] = low(w2[half:].astype(F32).T)


def fetch(sems, *pairs):
    copies = [pltpu.make_async_copy(src, dst, sems.at[i]) for i, (src, dst) in enumerate(pairs)]
    for copy in copies:
        copy.start()
    return copies


def to_columns(sc, made, buffer, outs):
    hid = outs[0].shape[-1]
    buffer[...] = made
    for j, out in enumerate(outs):
        out[...] = buffer[:, lanes((sc[1] ^ j) * hid, hid)]


def rows_at(xa, start, height):
    return xa.at[:, pl.ds(start, height), :]


def across(ref, cols):
    return jnp.concatenate([ref[c] for c in range(cols)], axis=1).astype(F32)


def both_heads(pair):
    left = lax.broadcasted_iota(jnp.int32, (1, PAIR), 1) < HD
    zero = jnp.zeros_like(pair)
    return jnp.concatenate([jnp.where(left, pair, zero), jnp.where(left, zero, pair)], axis=0)


def own_heads(made, scale=1.0):
    both = jnp.concatenate([made[:HD, :SEQ], made[HD:, SEQ:]], axis=0)
    return low(both.T * scale)


def front_kernel(lead, cols, *refs):
    sc = refs[0]
    pieces = refs[1:9]
    (xa, closed, gain, shift, q_down, q_up, p_down, p_up, f_down, bias_out) = refs[9:19]
    (n1, lat1, q, k, v, lse, att, lat2, middle, n2, lat3) = refs[19:30]
    w, sems, hidden, branch, xs, bs, row_qd, row_pd, row_pu, row_fd, sems_f = refs[30:]
    a = sc[0]
    hid = D // cols
    first = fetch(
        sems_f,
        (rows_at(xa, 0, SEQ), xs),
        (q_down.at[a], row_qd),
        (rows_at(xa, 2 * SEQ, EXTRA), bs),
        (p_down.at[a], row_pd),
        (p_up.at[a], row_pu),
        (f_down.at[a], row_fd),
    )
    weights = Weights(sc, pieces, w, sems, lead)
    weights.start()
    first[0].wait()
    x = across(xs, cols)
    hidden[...] = x
    unit, _ = norm_parts(x)
    n1[...] = low(unit * gain[0:1] + shift[0:1])
    for copy in first[1:]:
        copy.wait()
    lat1[...] = low(mm(n1[...], row_qd[...], NT))

    def project(i, _):
        slot = weights.slot(i, cols)
        block = column_of(sc, slot)
        up = jnp.concatenate([q_up[c, :, lanes(block * hid, hid)] for c in range(3)], axis=1)
        made = mm(n1[...], w[slot, :, : 3 * hid]) + mm(lat1[...], up)
        bias_q = bs[block, 0:1, :].astype(F32)
        bias_v = bs[block, 1:2, :].astype(F32)
        at = lanes(slot * hid, hid)
        q[:, at] = low(made[:, :hid] + bias_q) * jnp.asarray(0.125, BF)
        k[:, at] = low(made[:, hid : 2 * hid])
        v[:, at] = low(made[:, 2 * hid :] + bias_v)
        return 0

    lax.fori_loop(0, cols, project, 0)
    shut = closed[...] > 0.5

    def attend(pair, _):
        at = lanes(pair * PAIR, PAIR)
        v_t = low(v[:, at].astype(F32).T)
        s = jnp.where(shut, -1e30, mm(k[:, at], both_heads(q[:, at]), NT))
        top = jnp.max(s, axis=0, keepdims=True)
        e = jnp.exp(s - top)
        total = jnp.sum(e, axis=0, keepdims=True)
        lse[pair] = top + jnp.log(total)
        att[:, at] = own_heads(mm(v_t, low(e * (1.0 / total))))
        return 0

    lax.fori_loop(0, H // 2, attend, 0, unroll=4)

    def down_two(slot, acc):
        block = column_of(sc, slot)
        return acc + mm(att[:, lanes(slot * hid, hid)], row_pd[:, lanes(block * hid, hid)], NT)

    lat2[...] = low(lax.fori_loop(0, cols, down_two, jnp.zeros((SEQ, R), F32)))
    branch[...] = mm(lat2[...], row_pu[...]) + bias_out[0:1].astype(F32)

    def out_proj(slot, _):
        branch[...] += mm(att[:, lanes(slot * hid, hid)], w[slot, :, 3 * hid :], NT)
        return 0

    lax.fori_loop(0, cols, out_proj, 0)
    mid = hidden[...] + branch[...]
    middle[...] = mid
    unit, _ = norm_parts(mid)
    n2[...] = low(unit * gain[1:2] + shift[1:2])
    lat3[...] = low(mm(n2[...], row_fd[...], NT))


def ffn_steps(weights, sc, part, cols, w, bs, n2, lat3, gr, glat4, up_1, down_2, acc, early, lane=0):
    res, gn2, lat4, glat3 = acc
    hid = D // cols
    ffn = FF // cols
    half = ffn // 2
    glat4_t = low(glat4.astype(F32).T)
    lat3_t = low(lat3[...].astype(F32).T)

    def step(i, _):
        slot = weights.slot(i, cols)
        block = column_of(sc, slot)
        at = pl.ds(pl.multiple_of(block * ffn + part * half, half), half)
        bias = jnp.concatenate(
            [bs[block, 2 + 2 * part + i : 3 + 2 * part + i, :] for i in range(2)], axis=1
        ).astype(F32)
        up, down = up_1[:, at], down_2[:, at]
        w1, w2 = w[slot, :, :half], w[slot, :, half:]
        pre = mm(n2[...], w1) + mm(lat3[...], up) + bias
        back = mm(gr[...], w2) + mm(glat4, down)
        cumulative = 0.5 * (1.0 + lax.erf(pre * 0.7071067811865476))
        activated = low(pre * cumulative)
        slope = cumulative + pre * jnp.exp(-0.5 * pre * pre) * 0.3989422804014327
        grad_pre = low(back * slope)
        lat4[...] += mm(activated, down, NT)
        glat3[...] += mm(grad_pre, up, NT)
        res[...] += mm(activated, w2, NT)
        gn2[...] += mm(grad_pre, w1, NT)
        put(early, block * half, low(mm(lat3_t, grad_pre)), lane)
        put(early, FF // 2 + block * half, low(mm(glat4_t, activated)), lane)
        return 0

    lax.fori_loop(0, cols, step, 0)


def ffn_a_kernel(lead, cols, *refs):
    sc = refs[0]
    pieces = refs[1:9]
    xa, keep, n2, lat3, up_1, down_2, up_2 = refs[9:16]
    res, gn2, lat4, glat3, gr, early = refs[16:22]
    w, sems, gs, bs, row_u1, row_d2, row_u2, sems_f = refs[22:]
    a = sc[0]
    first = fetch(
        sems_f,
        (rows_at(xa, SEQ, SEQ), gs),
        (up_2.at[a], row_u2),
        (rows_at(xa, 2 * SEQ, EXTRA), bs),
        (up_1.at[a], row_u1),
        (down_2.at[a], row_d2),
    )
    weights = Weights(sc, pieces, w, sems, lead)
    weights.start()
    first[0].wait()
    gr[...] = low(across(gs, cols) * keep[...])
    for copy in first[1:]:
        copy.wait()
    glat4 = low(mm(gr[...], row_u2[...], NT))
    res[...] = jnp.zeros_like(res)
    gn2[...] = jnp.zeros_like(gn2)
    lat4[...] = jnp.zeros_like(lat4)
    glat3[...] = jnp.zeros_like(glat3)
    ffn_steps(
        weights, sc, 0, cols, w, bs, n2, lat3, gr, glat4, row_u1, row_d2, (res, gn2, lat4, glat3), early
    )


def ffn_b_kernel(lead, cols, *refs):
    sc = refs[0]
    pieces = refs[1:9]
    own_q = refs[9:17]
    (xa, keep, gain, n2, lat3, up_1, down_2, up_2, f_down, p_down, p_up, bias_out) = refs[17:29]
    (middle, att, lat2, gr, res_in, gn2_in, lat4_in, glat3_in, early_in) = refs[29:38]
    layer, refs = refs[38 : 38 + cols], refs[:38] + refs[38 + cols :]
    gatt, gmid, early = refs[38:41]
    refs = refs[:41] + (None,) + refs[41:]
    w, sems, wp, sems_p, res, gn2, lat4, glat3 = refs[42:50]
    bs, row_u1, row_d2, row_u2, row_fd, row_pd, row_pu, mid_s, att_s, res_s, gn2_s, early_s = refs[50:62]
    sems_f, out_s = refs[62:]
    lane = early_in.shape[-1]
    a = sc[0]
    first = fetch(
        sems_f,
        (up_2.at[a], row_u2),
        (rows_at(xa, 2 * SEQ, EXTRA), bs),
        (up_1.at[a], row_u1),
        (down_2.at[a], row_d2),
    )
    weights = Weights(sc, pieces, w, sems, lead)
    weights.start()
    proj = Weights(sc, own_q, wp, sems_p, lead, 3 * D // cols)
    last = fetch(
        sems_f.at[pl.ds(4, 8)],
        (res_in, res_s),
        (middle, mid_s),
        (gn2_in, gn2_s),
        (f_down.at[a], row_fd),
        (p_up.at[a], row_pu),
        (p_down.at[a], row_pd),
        (att, att_s),
        (early_in, early_s),
    )
    proj.start()
    hid = D // cols
    for copy in first:
        copy.wait()
    glat4 = low(mm(gr[...], row_u2[...], NT))
    res[...] = jnp.zeros_like(res)
    gn2[...] = jnp.zeros_like(gn2)
    lat4[...] = lat4_in[...]
    glat3[...] = glat3_in[...]
    ffn_steps(
        weights, sc, 1, cols, w, bs, n2, lat3, gr, glat4, row_u1, row_d2, (res, gn2, lat4, glat3), early, lane
    )
    for copy in last:
        copy.wait()
    early[:, :, :lane] = early_s[...]
    mid = mid_s[...]
    lat4_low = low(lat4[...])
    out = low(
        keep[...]
        * (mid + (res_s[...] + res[...]) + mm(lat4_low, row_u2[...]) + bias_out[1:2].astype(F32))
    )
    to_columns(sc, out, out_s, layer)
    glat3_low = low(glat3[...])
    grad_normed = gn2_s[...] + gn2[...] + mm(glat3_low, row_fd[...])
    unit, inverse = norm_parts(mid)
    grad_middle = gr[...].astype(F32) + norm_back(grad_normed, gain[1:2], unit, inverse)
    gmid[...] = grad_middle
    gb = low(grad_middle)
    glat2 = low(mm(gb, row_pu[...], NT))
    glat2_t = low(glat2.astype(F32).T)
    put(early, FF + D, low(mm(low(lat2[...].astype(F32).T), gb)), lane)
    put(early, FF + 2 * D, low(mm(low(glat3_low.astype(F32).T), n2[...])), lane)
    put(early, FF + 3 * D, low(mm(low(lat4_low.astype(F32).T), gr[...])), lane)
    proj.wait()

    def step(slot, _):
        block = column_of(sc, slot)
        here = lanes(slot * hid, hid)
        there = lanes(block * hid, hid)
        gatt[:, here] = low(mm(gb, wp[slot]) + mm(glat2, row_pd[:, there]))
        put(early, FF + block * hid, low(mm(glat2_t, att_s[:, here])), lane)
        return 0

    lax.fori_loop(0, cols, step, 0)


def attention_back_kernel(cols, *refs):
    sc = refs[0]
    closed, q, k, v, lse, gatt, lat1, n1, q_up = refs[1:10]
    gq, gk, gv, glat1, late = refs[10:15]
    a = sc[0]
    hid = D // cols
    shut = closed[...] > 0.5

    def attend(pair, _):
        at = lanes(pair * PAIR, PAIR)
        kp = k[:, at]
        k_t = low(kp.astype(F32).T)
        q_both, g_both = both_heads(q[:, at]), both_heads(gatt[:, at])
        s = jnp.where(shut, -1e30, mm(kp, q_both, NT))
        soft = jnp.exp(s - lse[pair])
        grad_soft = mm(v[:, at], g_both, NT)
        total = jnp.sum(grad_soft * soft, axis=0, keepdims=True)
        grad_scores = low(soft * (grad_soft - total))
        gq[:, at] = own_heads(mm(k_t, grad_scores), 0.125)
        gk[:, at] = low(mm(grad_scores, q_both))
        gv[:, at] = low(mm(low(soft), g_both))
        return 0

    lax.fori_loop(0, H // 2, attend, 0, unroll=4)
    lat1_t = low(lat1[...].astype(F32).T)

    def step(slot, acc):
        block = column_of(sc, slot)
        here = lanes(slot * hid, hid)
        there = lanes(block * hid, hid)
        for c, g in enumerate((gq, gk, gv)):
            grad = g[:, here]
            acc = acc + mm(grad, q_up[c, :, there], NT)
            put(late, (c + 1) * D + block * hid, low(mm(lat1_t, grad)))
        return acc

    made = low(lax.fori_loop(0, cols, step, jnp.zeros((SEQ, R), F32)))
    glat1[...] = made
    put(late, 0, low(mm(low(made.astype(F32).T), n1[...])))


def back_kernel(lead, cols, *refs):
    sc = refs[0]
    pieces = refs[1:9]
    xa, gain, gq, gk, gv, glat1, q_down, gmid = refs[9:17]
    outs = refs[17 : 17 + cols]
    w, sems, acc, xs, row_qd, gmid_s, sems_f, out_s = refs[17 + cols :]
    first = fetch(
        sems_f,
        (rows_at(xa, 0, SEQ), xs),
        (q_down.at[sc[0]], row_qd),
        (gmid, gmid_s),
    )
    weights = Weights(sc, pieces, w, sems, lead)
    weights.start()
    hid = D // cols
    for copy in first:
        copy.wait()
    acc[...] = mm(glat1[...], row_qd[...])
    x = across(xs, cols)
    unit, inverse = norm_parts(x)

    def step(i, _):
        slot = weights.slot(i, cols)
        here = lanes(slot * hid, hid)
        grad = jnp.concatenate([gq[:, here], gk[:, here], gv[:, here]], axis=1)
        acc[...] += mm(grad, w[slot, :, : 3 * hid], NT)
        return 0

    lax.fori_loop(0, cols, step, 0)
    made = low(gmid_s[...] + norm_back(acc[...], gain[0:1], unit, inverse))
    to_columns(sc, made, out_s, outs)


def sum_kernel(owners, mine, out, acc):
    acc[...] = jnp.zeros_like(acc)
    for d in range(mine.shape[0]):
        acc[owners[d]] += mine[d, :, : acc.shape[2]].astype(F32)
    out[...] = low(acc[...])


def spread_kernel(lead, cols, parts, maps, *refs):
    sc, pieces = refs[0], refs[1:9]
    count = (len(refs) - 11) // 2
    outs, whole, made = refs[9 : 9 + count], refs[9 + count], refs[10 + count : 10 + 2 * count]
    sems_in, sems_out = refs[10 + 2 * count :]
    copies = []
    for k, piece in enumerate(pieces):
        x_rel, y_rel, away = piece_place(sc, k)
        for n, (high_col, high_row) in enumerate(lead):
            row = high_row * 2 + ((sc[3] + y_rel) & 1)
            col = high_col * 4 + ((sc[1] & 3) ^ (x_rel * 2 + away))
            copies.append(
                pltpu.make_async_copy(piece.at[n], whole.at[row * cols + col], sems_in.at[k, n])
            )
    for copy in copies:
        copy.start()
    for copy in copies:
        copy.wait()
    found = [[] for _ in outs]
    base = 0
    for part, spans in zip(parts, maps):
        for out, section, there, start, width in spans:
            for lane in range(0, width, 128):
                at = start + lane
                found[out].append((section, there + lane, at // part, base + at % part))
        base += part
    leaving = []
    for i, (out, buffer) in enumerate(zip(outs, made)):
        for section, there, device, here in found[i]:
            block = whole[device, :, here : here + 128].astype(F32)
            if section is None:
                buffer[:, there : there + 128] = block
            else:
                buffer[:, section, :, there : there + 128] = block.reshape(NA, R, 128)
        leaving.append(pltpu.make_async_copy(buffer, out, sems_out.at[i]))
        leaving[-1].start()
    for copy in leaving:
        copy.wait()


def place_kernel(lead, cols, *refs):
    sc, pieces, out, sems = refs[0], refs[1:9], refs[9], refs[10]
    copies = []
    for k, piece in enumerate(pieces):
        x_rel, y_rel, away = piece_place(sc, k)
        for n, (high_col, high_row) in enumerate(lead):
            row = high_row * 2 + ((sc[3] + y_rel) & 1)
            col = high_col * 4 + ((sc[1] & 3) ^ (x_rel * 2 + away))
            copies.append(pltpu.make_async_copy(piece.at[n], out.at[row * cols + col], sems.at[k, n]))
    for copy in copies:
        copy.start()
    for copy in copies:
        copy.wait()


def send_grads(grads):
    return lax.all_to_all(grads, BOTH, split_axis=0, concat_axis=0, tiled=True)


def sum_grads(mine, owners, part):
    summed = call(
        sum_kernel,
        jax.ShapeDtypeStruct((NA, R, part), BF),
        [owners, mine],
        [pltpu.SMEM, VMEM],
        [VMEM((NA, R, part), F32)],
    )
    return summed.reshape(NA * R, part)


def spread(sc, pieces, parts, maps, shapes):
    rows, cols = sizes()
    devices = rows * cols
    lead = lead_table(rows, cols)
    arrivals = pltpu.SemaphoreType.DMA((8, len(lead)))
    whole = (devices, NA * R, sum(parts))
    ins, spaces = [sc, *pieces], [pltpu.SMEM] + [pl.ANY] * 8
    if all(p % 128 == 0 for p in parts):
        return call(
            functools.partial(spread_kernel, lead, cols, parts, maps),
            [jax.ShapeDtypeStruct(x, F32) for x in shapes],
            ins,
            spaces,
            [VMEM(whole, BF)]
            + [VMEM(x, F32) for x in shapes]
            + [arrivals, pltpu.SemaphoreType.DMA((len(shapes),))],
            pl.ANY,
            SPREAD,
        )
    whole = call(
        functools.partial(place_kernel, lead, cols),
        jax.ShapeDtypeStruct(whole, BF),
        ins,
        spaces,
        [arrivals],
    )
    found = [[] for _ in shapes]
    base = 0
    for part, spans in zip(parts, maps):
        flat = jnp.swapaxes(whole[:, :, base : base + part], 0, 1).reshape(NA * R, devices * part)
        for out, section, there, start, width in spans:
            found[out].append((section or 0, there, flat[:, start : start + width].astype(F32)))
        base += part
    return [
        (
            jnp.concatenate([x for _, _, x in sorted(f, key=lambda e: e[:2])], axis=1)
            if len(shape) == 2
            else jnp.stack([x.reshape(NA, R, -1) for _, _, x in sorted(f, key=lambda e: e[:2])], 1)
        )
        for f, shape in zip(found, shapes)
    ]


def per_device(
    tokens_in,
    grad_out,
    keep_mask,
    adapter_index,
    ln_gain,
    ln_shift,
    w_qkv,
    bias_qv,
    w_proj,
    w_fc1,
    bias_fc1,
    w_fc2,
    bias_out,
    qkv_down,
    qkv_up,
    proj_down,
    proj_up,
    fc1_down,
    fc1_up,
    fc2_down,
    fc2_up,
):
    rows, cols = sizes()
    row, column = lax.axis_index("row"), lax.axis_index("col")
    assert adapter_index.shape[0] == cols and cols >= 4 and rows >= 2
    hid = D // cols
    n = 4 * hid
    blk = D // rows
    lead = lead_table(rows, cols)

    shard = jax.ShapeDtypeStruct((blk, n), BF)
    rows_in, shard_q = call(
        prep_q_kernel,
        [jax.ShapeDtypeStruct((cols, 2 * SEQ + EXTRA, hid), BF), shard],
        [tokens_in.reshape(cols, SEQ, hid), grad_out.reshape(cols, SEQ, hid), bias_qv]
        + [bias_fc1, w_qkv, w_proj],
        [VMEM] * 6,
        mib=56,
    )
    with jax.named_scope("q_high"):
        own_q, came_q = gather_high(shard_q)
    xa = lax.all_to_all(rows_in, "col", split_axis=0, concat_axis=0, tiled=True)
    adapter = lax.dynamic_index_in_dim(adapter_index, column, 0, keepdims=False)
    sc = jnp.stack([adapter, column, column % 2, row % 2]).astype(jnp.int32)
    up_qkv = jnp.swapaxes(lax.dynamic_index_in_dim(qkv_up, adapter, 0, keepdims=False), 0, 1)
    shard_a, shard_b, keep, closed = call(
        prep_f_kernel,
        [shard] * 2 + [jax.ShapeDtypeStruct((SEQ, 1), F32)] * 2,
        [sc, keep_mask, w_fc1, w_fc2],
        [pltpu.SMEM] + [VMEM] * 3,
    )

    own_q, shard_a, shard_b = after_all(
        (own_q, shard_a, shard_b), xa, keep, closed, sc, up_qkv, *came_q
    )
    with jax.named_scope("q_one"):
        one_q = swap(own_q, flip_one)
    with jax.named_scope("q_two"):
        two_q = swap(own_q, flip_two)
    with jax.named_scope("fa_high"):
        own_a, came_a = gather_high(shard_a)
    own_q, one_q, two_q = after_all((own_q, one_q, two_q), *came_a)
    with jax.named_scope("q_both"):
        both_q = swap(one_q, flip_two)
    with jax.named_scope("q_core"):
        away_q = [swap(p, flip_core) for p in (own_q, one_q, two_q)]
    own_a, shard_b = after_all((own_a, shard_b), *away_q)
    with jax.named_scope("q_core"):
        pieces_q = [own_q, one_q, two_q, both_q] + away_q + [swap(both_q, flip_core)]
    with jax.named_scope("fa_one"):
        one_a = swap(own_a, flip_one)
    with jax.named_scope("fa_two"):
        two_a = swap(own_a, flip_two)
    with jax.named_scope("fb_high"):
        own_b, came_b = gather_high(shard_b)

    def shaped(width, dtype, height=SEQ):
        return jax.ShapeDtypeStruct((height, width), dtype)

    big, small = shaped(D, BF), shaped(R, BF)
    scratch = weight_scratch(rows, cols, n)
    rows_space, bias_space = VMEM((cols, SEQ, hid), BF), VMEM((cols, EXTRA, hid), BF)
    any_space = [pl.ANY] * 8
    n1, lat1, q, k, v, lse, att, lat2, middle, n2, lat3 = call(
        functools.partial(front_kernel, lead, cols),
        [
            big,
            small,
            big,
            big,
            big,
            jax.ShapeDtypeStruct((H // 2, 1, 2 * SEQ), F32),
            big,
            small,
            shaped(D, F32),
            big,
            small,
        ],
        [sc, *pieces_q, xa, closed, ln_gain, ln_shift, qkv_down, up_qkv, proj_down]
        + [proj_up]
        + [fc1_down, bias_out],
        [pltpu.SMEM] + any_space + [pl.ANY] + [VMEM] * 3 + [pl.ANY, VMEM] + [pl.ANY] * 3 + [VMEM],
        scratch
        + [VMEM((SEQ, D), F32), VMEM((SEQ, D), F32), rows_space, bias_space]
        + [VMEM((R, D), BF)] * 4
        + [pltpu.SemaphoreType.DMA((6,))],
        mib=FRONT,
    )
    own_a, one_a, two_a = after_all((own_a, one_a, two_a), n1, *came_b)
    bits = list(reversed(range(bits_of(rows))))
    owners = after(adapter_index, n1)
    for bit in bits[:-1]:
        owners = owner_stack(owner_parts(owners, bit), bit)
    with jax.named_scope("fa_both"):
        both_a = swap(one_a, flip_two)
    with jax.named_scope("fa_core"):
        away_a = [swap(p, flip_core) for p in (own_a, one_a, two_a)]
    own_b, owners = after_all((own_b, owners), *away_a)
    owners = owner_parts(owners, 0)
    with jax.named_scope("fa_core"):
        pieces_a = [own_a, one_a, two_a, both_a] + away_a + [swap(both_a, flip_core)]
    with jax.named_scope("fb_one"):
        one_b = swap(own_b, flip_one)
    with jax.named_scope("fb_two"):
        two_b = swap(own_b, flip_two)
    wide = shaped(D, F32)
    thin = shaped(R, F32)
    res, gn2, lat4, glat3, gr, early_a = call(
        functools.partial(ffn_a_kernel, lead, cols),
        [wide, wide, thin, thin, big, jax.ShapeDtypeStruct((rows * cols, R, FF // (rows * cols)), BF)],
        [sc, *pieces_a, xa, keep, n2, lat3, fc1_up, fc2_down, fc2_up],
        [pltpu.SMEM] + any_space + [pl.ANY] + [VMEM] * 3 + [pl.ANY] * 3,
        scratch
        + [rows_space, bias_space, VMEM((R, FF), BF), VMEM((R, FF), BF), VMEM((R, D), BF)]
        + [pltpu.SemaphoreType.DMA((5,))],
        mib=FFN_A,
    )
    own_b, one_b, two_b, *owners = after_all((own_b, one_b, two_b, *owners), res)
    owners = owner_stack(owners, 0).transpose(tuple(bits) + (len(bits),)).reshape(-1)
    with jax.named_scope("fb_both"):
        both_b = swap(one_b, flip_two)
    with jax.named_scope("fb_core"):
        away_b = [swap(p, flip_core) for p in (own_b, one_b, two_b)]
        pieces_b = [own_b, one_b, two_b, both_b] + away_b + [swap(after(both_b, owners), flip_core)]
    *layer, gatt, gmid, grads_b = call(
        functools.partial(ffn_b_kernel, lead, cols),
        [shaped(hid, BF)] * cols + [big, wide]
        + [jax.ShapeDtypeStruct((rows * cols, R, 12 * D // (rows * cols)), BF)],
        [sc, *pieces_b, *pieces_q, xa, keep, ln_gain, n2, lat3, fc1_up, fc2_down, fc2_up]
        + [fc1_down, proj_down, proj_up, bias_out]
        + [middle, att, lat2, gr, res, gn2, lat4, glat3, early_a],
        [pltpu.SMEM]
        + any_space * 2
        + [pl.ANY, VMEM, VMEM, VMEM, VMEM]
        + [pl.ANY] * 6
        + [VMEM, pl.ANY, pl.ANY, VMEM, VMEM, pl.ANY, pl.ANY, VMEM, VMEM, pl.ANY],
        scratch
        + [VMEM((cols, D, hid), BF), scratch[1]]
        + [VMEM((SEQ, D), F32), VMEM((SEQ, D), F32), VMEM((SEQ, R), F32), VMEM((SEQ, R), F32)]
        + [bias_space, VMEM((R, FF), BF), VMEM((R, FF), BF)]
        + [VMEM((R, D), BF)] * 4
        + [VMEM((SEQ, D), F32), VMEM((SEQ, D), BF), VMEM((SEQ, D), F32), VMEM((SEQ, D), F32)]
        + [VMEM(early_a.shape, BF), pltpu.SemaphoreType.DMA((12,)), VMEM((SEQ, D), BF)],
        mib=FFN_B,
    )
    with jax.named_scope("grads_b_send"):
        mine_b = send_grads(grads_b)
    with jax.named_scope("layer_out"):
        layer = exchange_rows(layer)
    gq, gk, gv, glat1, late = call(
        functools.partial(attention_back_kernel, cols),
        [big, big, big, small, jax.ShapeDtypeStruct((rows * cols, R, 4 * D // (rows * cols)), BF)],
        [sc, closed, q, k, v, lse, gatt, lat1, n1, up_qkv],
        [pltpu.SMEM] + [VMEM] * 9,
        mib=ATT,
    )
    with jax.named_scope("grads_c_send"):
        mine_c = send_grads(late)
    with jax.named_scope("grads_b"):
        own_b, _ = gather_high(
            sum_grads(after(mine_b, late, *layer), owners, mine_b.shape[2]), 1
        )
        own_c, _ = gather_high(sum_grads(mine_c, owners, mine_c.shape[2]))
        order_b = tuple(lead.index(place) for place in lead_table(rows, cols, 1))
        own = lane_join([own_b, own_c], [order_b, tuple(range(len(lead)))])
    gmid = after(gmid, own)
    sent = call(
        functools.partial(back_kernel, lead, cols),
        [shaped(hid, BF)] * cols,
        [sc, *pieces_q, xa, ln_gain, gq, gk, gv, glat1, qkv_down, gmid],
        [pltpu.SMEM] + any_space + [pl.ANY] + [VMEM] * 5 + [pl.ANY] * 2,
        scratch
        + [VMEM((SEQ, D), F32), rows_space, VMEM((R, D), BF), VMEM((SEQ, D), F32)]
        + [pltpu.SemaphoreType.DMA((3,)), VMEM((SEQ, D), BF)],
        mib=BACK,
    )
    with jax.named_scope("grads"):
        one, two = swap(own, flip_one), swap(own, flip_two)
        own, one, two = after_all((own, one, two), *sent)
        layer_out = stacked(after_all(layer, one, two), column, pl.ANY)
        both = swap(one, flip_two)
        away = [swap(p, flip_core) for p in (own, one, two)]
        both = after(both, layer_out)
        pieces = [own, one, two, both] + away + [swap(both, flip_core)]
        half = FF // cols // 2
        map_a, map_b = (
            tuple(
                (out, None, (2 * block + part) * half, base + block * half, half)
                for out, base in ((0, 0), (1, FF // 2))
                for block in range(cols)
            )
            for part in (0, 1)
        )
        map_b = map_b + tuple((2 + i, None, 0, FF + i * D, D) for i in range(4))
        map_c = ((6, None, 0, 0, D),) + tuple((7, c, 0, (c + 1) * D, D) for c in range(3))
        parts = [early_a.shape[-1], mine_b.shape[-1] - early_a.shape[-1], mine_c.shape[-1]]
        shapes = [(NA * R, FF)] * 2 + [(NA * R, D)] * 5 + [(NA, 3, R, D)]
        sums = spread(sc, pieces, parts, [map_a, map_b, map_c], shapes)

    with jax.named_scope("rows_out"):
        grad_rows = exchange_rows(after_all(sent, *away))
        grad_in = stacked(after_all(grad_rows, sums[0]), column, pl.ANY)

    def split(table):
        return table.reshape((NA, R) + table.shape[1:])

    g_fc1_up, g_fc2_down, g_proj_down, g_proj_up, g_fc1_down, g_fc2_up = map(split, sums[:6])
    return (
        layer_out.reshape(cols * SEQ, hid),
        grad_in.reshape(cols * SEQ, hid),
        split(sums[6]),
        jnp.swapaxes(sums[7], 1, 2),
        g_proj_down,
        g_proj_up,
        g_fc1_down,
        g_fc1_up,
        g_fc2_down,
        g_fc2_up,
    )


def solution(mesh):
    return jax.shard_map(
        per_device,
        mesh=mesh,
        in_specs=(
            P("row", "col"),
            P("row", "col"),
            P("row", None),
            P("row"),
            P(),
            P(),
            P(None, "row", "col"),
            P(None, "col"),
            P("col", "row"),
            P("row", "col"),
            P("col"),
            P("col", "row"),
            P(),
            P(),
            P(),
            P(),
            P(),
            P(),
            P(),
            P(),
            P(),
        ),
        out_specs=(P("row", "col"), P("row", "col"), P(), P(), P(), P(), P(), P(), P(), P()),
        check_vma=False,
    )
```

```python
import functools

import jax
import jax.numpy as jnp
from jax import lax
from jax.experimental import pallas as pl
from jax.experimental.pallas import tpu as pltpu
from jax.sharding import PartitionSpec as P

D = 1024
H = 16
HD = 64
FF = 4096
BUF = 64
R = 16
NA = 8
SEQ = 320
PAIR = 2 * HD
EXTRA = 16
SPREAD = 56
FRONT, FFN_A, FFN_B, ATT, BACK = 56, 56, 56, 56, 56
BF = jnp.bfloat16
F32 = jnp.float32
BOTH = ("row", "col")
VMEM = pltpu.VMEM
NN = (((1,), (0,)), ((), ()))
NT = (((1,), (1,)), ((), ()))


def mm(left, right, dims=NN):
    return lax.dot_general(left, right, dims, preferred_element_type=F32)


def low(values):
    return values.astype(BF)


def norm_parts(values):
    row_mean = jnp.mean(values, axis=-1, keepdims=True)
    centered = values - row_mean
    variance = jnp.mean(centered * centered, axis=-1, keepdims=True)
    inverse = lax.rsqrt(variance + 1e-06)
    return (centered * inverse, inverse)


def norm_back(grad_normed, gain_row, unit_rows, inverse):
    scaled = grad_normed * gain_row
    first_mean = jnp.mean(scaled, axis=-1, keepdims=True)
    second_mean = jnp.mean(scaled * unit_rows, axis=-1, keepdims=True)
    return inverse * (scaled - first_mean - unit_rows * second_mean)


def call(kernel, outs, ins, spaces, scratch=(), out_space=VMEM, mib=4):
    return pl.pallas_call(
        kernel,
        out_shape=outs,
        in_specs=[pl.BlockSpec(memory_space=s) for s in spaces],
        out_specs=jax.tree.map(lambda _: pl.BlockSpec(memory_space=out_space), outs),
        scratch_shapes=list(scratch),
        compiler_params=pltpu.CompilerParams(vmem_limit_bytes=mib << 20),
        cost_estimate=pl.CostEstimate(flops=0, bytes_accessed=0, transcendentals=0),
    )(*ins)


def sizes():
    return lax.axis_size("row"), lax.axis_size("col")


def swap(block, flip):
    rows, cols = sizes()
    pairs = []
    for i in range(rows * cols):
        row, col = flip(i // cols, i % cols)
        pairs.append((i, row * cols + col))
    return lax.ppermute(block, BOTH, pairs)


def bits_of(size):
    return size.bit_length() - 1


def stack_kernel(which, *refs):
    parts, out, sems = refs[:-2], refs[-2], refs[-1]
    copies = [
        pltpu.make_async_copy(ref, out.at[which[0] ^ m], sems.at[m]) for m, ref in enumerate(parts)
    ]
    for copy in copies:
        copy.start()
    for copy in copies:
        copy.wait()


def stacked(parts, index, out_space=VMEM):
    shape = parts[0].shape
    flat = [p.reshape((-1, shape[-1])) for p in parts]
    out = jax.ShapeDtypeStruct((len(parts),) + flat[0].shape, flat[0].dtype)
    made = call(
        stack_kernel,
        out,
        [index.reshape(1).astype(jnp.int32)] + flat,
        [pltpu.SMEM] + [pl.ANY] * len(parts),
        [pltpu.SemaphoreType.DMA((len(parts),))],
        out_space,
    )
    return made.reshape((len(parts),) + shape)


def group_join(block, axis, low_bit, width):
    parts = [block]
    for m in range(1, 1 << width):
        step = m << low_bit
        if axis == "row":
            parts.append(swap(block, lambda r, c: (r ^ step, c)))
        else:
            parts.append(swap(block, lambda r, c: (r, c ^ step)))
    index = (lax.axis_index(axis) >> low_bit) & ((1 << width) - 1)
    return stacked(parts, index), parts


def groups(top, bottom, most):
    out = []
    while top > bottom:
        width = min(most, top - bottom)
        out.append((top - width, width))
        top -= width
    return out


def early_groups(rows, cols, most):
    return [("row",) + g for g in groups(bits_of(rows), 1, most)] + [
        ("col",) + g for g in groups(bits_of(cols), 2, most)
    ]


def lead_table(rows, cols, most=2):
    table = [(0, 0)]
    for axis, bit, width in early_groups(rows, cols, most):
        shift = bit - (1 if axis == "row" else 2)
        new = []
        for value in range(1 << width):
            for high_col, high_row in table:
                if axis == "row":
                    new.append((high_col, high_row + (value << shift)))
                else:
                    new.append((high_col + (value << shift), high_row))
        table = new
    return table


def after(value, *others):
    return lax.optimization_barrier((value,) + others)[0]


def after_all(values, *others):
    return lax.optimization_barrier(tuple(values) + others)[: len(values)]


def exchange_rows(parts):
    came = [parts[0]]
    for j in range(1, len(parts)):
        came.append(swap(parts[j], lambda r, c: (r, c ^ j)))
    return came


def gather_high(shard, most=2):
    rows, cols = sizes()
    block, parts = shard, []
    for axis, bit, width in early_groups(rows, cols, most):
        block, parts = group_join(block, axis, bit, width)
    return block.reshape((-1,) + shard.shape), parts[1:]


def lane_join_kernel(orders, *refs):
    parts, out, sems = refs[:-2], refs[-2], refs[-1]
    copies, lane = [], 0
    for i, (part, order) in enumerate(zip(parts, orders)):
        width = part.shape[-1]
        for n, put_at in enumerate(order):
            target = out.at[put_at, :, lane : lane + width]
            copies.append(pltpu.make_async_copy(part.at[n], target, sems.at[i, n]))
        lane += width
    for copy in copies:
        copy.start()
    for copy in copies:
        copy.wait()


def lane_join(parts, orders):
    if any(p.shape[-1] % 128 for p in parts):
        placed = [p[jnp.array(sorted(range(len(o)), key=o.index))] for p, o in zip(parts, orders)]
        return jnp.concatenate(placed, axis=-1)
    shape = parts[0].shape[:-1] + (sum(p.shape[-1] for p in parts),)
    return call(
        functools.partial(lane_join_kernel, orders),
        jax.ShapeDtypeStruct(shape, parts[0].dtype),
        parts,
        [pl.ANY] * len(parts),
        [pltpu.SemaphoreType.DMA((len(parts), shape[0]))],
    )


def flip_one(r, c):
    return (r, c ^ 2) if c % 2 == 0 else (r ^ 1, c)


def flip_two(r, c):
    return (r ^ 1, c) if c % 2 == 0 else (r, c ^ 2)


def flip_core(r, c):
    return (r, c ^ 1)


def with_cores(pieces):
    return pieces + [swap(p, flip_core) for p in pieces]


def owner_parts(block, bit):
    step = 1 << bit
    return [block, swap(block, lambda r, c: (r ^ step, c))]


def owner_stack(parts, bit):
    return jnp.stack(parts)[jnp.arange(2) ^ ((lax.axis_index("row") >> bit) & 1)]


def piece_place(sc, k):
    kind, away = k % 4, k // 4
    turn = (sc[2] + away) & 1
    return (0, 1 - turn, turn, 1)[kind], (0, turn, 1 - turn, 1)[kind], away


class Weights:
    def __init__(self, sc, pieces, w, sems, lead, first_lane=0):
        self.copies = []
        depth = pieces[0].shape[1]
        taken = pl.ds(first_lane, w.shape[2])
        for k, piece in enumerate(pieces):
            x_rel, y_rel, away = piece_place(sc, k)
            for n, (high_col, high_row) in enumerate(lead):
                slot = high_col * 4 + x_rel * 2 + away
                row = (high_row * 2 + ((sc[3] + y_rel) & 1)) * depth
                self.copies.append(
                    pltpu.make_async_copy(
                        piece.at[n, :, taken],
                        w.at[slot, pl.ds(pl.multiple_of(row, depth), depth), :],
                        sems.at[k, n],
                    )
                )

    def start(self):
        for copy in self.copies:
            copy.start()

    def wait(self, away=None):
        half = len(self.copies) // 2
        for copy in self.copies if away is None else self.copies[away * half : (away + 1) * half]:
            copy.wait()

    def slot(self, i, cols):
        half = cols // 2

        @pl.when(i == 0)
        def _():
            self.wait(0)

        @pl.when(i == half)
        def _():
            self.wait(1)

        return lax.rem(i, half) * 2 + i // half


def column_of(sc, slot):
    return (slot // 4) * 4 + ((sc[1] & 3) ^ (slot & 3))


def weight_scratch(rows, cols, n):
    lead = len(lead_table(rows, cols))
    return [VMEM((cols, D, n), BF), pltpu.SemaphoreType.DMA((8, lead))]


def put(ref, start, value, lane=0):
    part = ref.shape[-1] - lane
    for i in range(value.shape[-1] // part):
        ref[start // part + i, :, lane:] = value[:, i * part : (i + 1) * part]


def lanes(start, width):
    return pl.ds(pl.multiple_of(start, width), width)


def prep_q_kernel(tokens, grads, bias_qv, bias_f, wq, wp, rows, out):
    hid = wq.shape[2]
    seq = tokens.shape[1]
    for c in range(tokens.shape[0]):
        rows[c, :seq] = tokens[c]
        rows[c, seq : 2 * seq] = grads[c]
        rows[c, 2 * seq : 2 * seq + 2] = bias_qv[...]
        for i in range(4):
            rows[c, 2 * seq + 2 + i, :] = bias_f[pl.ds(i * hid, hid)]
    for c in range(3):
        out[:, c * hid : (c + 1) * hid] = wq[c]
    out[:, 3 * hid :] = low(wp[...].astype(F32).T)


def prep_f_kernel(sc, mask, w1, w2, out_a, out_b, keep, closed):
    row = mask[pl.ds(sc[1], 1), :].astype(F32)
    row = jnp.concatenate([jnp.ones((1, BUF), F32), row], axis=1)
    column = jnp.broadcast_to(row, (8, SEQ)).T[:, :1]
    keep[...] = column
    closed[...] = 1.0 - column
    half = w1.shape[1] // 2
    out_a[:, :half] = w1[:, :half]
    out_b[:, :half] = w1[:, half:]
    out_a[:, half:] = low(w2[:half].astype(F32).T)
    out_b[:, half:] = low(w2[half:].astype(F32).T)


def fetch(sems, *pairs):
    copies = [pltpu.make_async_copy(src, dst, sems.at[i]) for i, (src, dst) in enumerate(pairs)]
    for copy in copies:
        copy.start()
    return copies


def to_columns(sc, made, buffer, outs):
    hid = outs[0].shape[-1]
    buffer[...] = made
    for j, out in enumerate(outs):
        out[...] = buffer[:, lanes((sc[1] ^ j) * hid, hid)]


def rows_at(xa, start, height):
    return xa.at[:, pl.ds(start, height), :]


def across(ref, cols):
    return jnp.concatenate([ref[c] for c in range(cols)], axis=1).astype(F32)


def both_heads(pair):
    left = lax.broadcasted_iota(jnp.int32, (1, PAIR), 1) < HD
    zero = jnp.zeros_like(pair)
    return jnp.concatenate([jnp.where(left, pair, zero), jnp.where(left, zero, pair)], axis=0)


def own_heads(made, scale=1.0):
    both = jnp.concatenate([made[:HD, :SEQ], made[HD:, SEQ:]], axis=0)
    return low(both.T * scale)


def front_kernel(lead, cols, *refs):
    sc = refs[0]
    pieces = refs[1:9]
    (xa, closed, gain, shift, q_down, q_up, p_down, p_up, f_down, bias_out) = refs[9:19]
    (n1, lat1, q, k, v, lse, att, lat2, middle, n2, lat3) = refs[19:30]
    w, sems, hidden, branch, xs, bs, row_qd, row_pd, row_pu, row_fd, sems_f = refs[30:]
    a = sc[0]
    hid = D // cols
    first = fetch(
        sems_f,
        (rows_at(xa, 0, SEQ), xs),
        (q_down.at[a], row_qd),
        (rows_at(xa, 2 * SEQ, EXTRA), bs),
        (p_down.at[a], row_pd),
        (p_up.at[a], row_pu),
        (f_down.at[a], row_fd),
    )
    weights = Weights(sc, pieces, w, sems, lead)
    weights.start()
    first[0].wait()
    x = across(xs, cols)
    hidden[...] = x
    unit, _ = norm_parts(x)
    n1[...] = low(unit * gain[0:1] + shift[0:1])
    for copy in first[1:]:
        copy.wait()
    lat1[...] = low(mm(n1[...], row_qd[...], NT))

    def project(i, _):
        slot = weights.slot(i, cols)
        block = column_of(sc, slot)
        up = jnp.concatenate([q_up[c, :, lanes(block * hid, hid)] for c in range(3)], axis=1)
        made = mm(n1[...], w[slot, :, : 3 * hid]) + mm(lat1[...], up)
        bias_q = bs[block, 0:1, :].astype(F32)
        bias_v = bs[block, 1:2, :].astype(F32)
        at = lanes(slot * hid, hid)
        q[:, at] = low(made[:, :hid] + bias_q) * jnp.asarray(0.125, BF)
        k[:, at] = low(made[:, hid : 2 * hid])
        v[:, at] = low(made[:, 2 * hid :] + bias_v)
        return 0

    lax.fori_loop(0, cols, project, 0)
    shut = closed[...] > 0.5

    def attend(pair, _):
        at = lanes(pair * PAIR, PAIR)
        v_t = low(v[:, at].astype(F32).T)
        s = jnp.where(shut, -1e30, mm(k[:, at], both_heads(q[:, at]), NT))
        top = jnp.max(s, axis=0, keepdims=True)
        e = jnp.exp(s - top)
        total = jnp.sum(e, axis=0, keepdims=True)
        lse[pair] = top + jnp.log(total)
        att[:, at] = own_heads(mm(v_t, low(e * (1.0 / total))))
        return 0

    lax.fori_loop(0, H // 2, attend, 0, unroll=4)

    def down_two(slot, acc):
        block = column_of(sc, slot)
        return acc + mm(att[:, lanes(slot * hid, hid)], row_pd[:, lanes(block * hid, hid)], NT)

    lat2[...] = low(lax.fori_loop(0, cols, down_two, jnp.zeros((SEQ, R), F32)))
    branch[...] = mm(lat2[...], row_pu[...]) + bias_out[0:1].astype(F32)

    def out_proj(slot, _):
        branch[...] += mm(att[:, lanes(slot * hid, hid)], w[slot, :, 3 * hid :], NT)
        return 0

    lax.fori_loop(0, cols, out_proj, 0)
    mid = hidden[...] + branch[...]
    middle[...] = mid
    unit, _ = norm_parts(mid)
    n2[...] = low(unit * gain[1:2] + shift[1:2])
    lat3[...] = low(mm(n2[...], row_fd[...], NT))


def ffn_steps(weights, sc, part, cols, w, bs, n2, lat3, gr, glat4, up_1, down_2, acc, early, lane=0):
    res, gn2, lat4, glat3 = acc
    hid = D // cols
    ffn = FF // cols
    half = ffn // 2
    glat4_t = low(glat4.astype(F32).T)
    lat3_t = low(lat3[...].astype(F32).T)

    def step(i, _):
        slot = weights.slot(i, cols)
        block = column_of(sc, slot)
        at = pl.ds(pl.multiple_of(block * ffn + part * half, half), half)
        bias = jnp.concatenate(
            [bs[block, 2 + 2 * part + i : 3 + 2 * part + i, :] for i in range(2)], axis=1
        ).astype(F32)
        up, down = up_1[:, at], down_2[:, at]
        w1, w2 = w[slot, :, :half], w[slot, :, half:]
        pre = mm(n2[...], w1) + mm(lat3[...], up) + bias
        back = mm(gr[...], w2) + mm(glat4, down)
        cumulative = 0.5 * (1.0 + lax.erf(pre * 0.7071067811865476))
        activated = low(pre * cumulative)
        slope = cumulative + pre * jnp.exp(-0.5 * pre * pre) * 0.3989422804014327
        grad_pre = low(back * slope)
        lat4[...] += mm(activated, down, NT)
        glat3[...] += mm(grad_pre, up, NT)
        res[...] += mm(activated, w2, NT)
        gn2[...] += mm(grad_pre, w1, NT)
        put(early, block * half, low(mm(lat3_t, grad_pre)), lane)
        put(early, FF // 2 + block * half, low(mm(glat4_t, activated)), lane)
        return 0

    lax.fori_loop(0, cols, step, 0, unroll=2)


def ffn_a_kernel(lead, cols, *refs):
    sc = refs[0]
    pieces = refs[1:9]
    xa, keep, n2, lat3, up_1, down_2, up_2 = refs[9:16]
    res, gn2, lat4, glat3, gr, early = refs[16:22]
    w, sems, gs, bs, row_u1, row_d2, row_u2, sems_f = refs[22:]
    a = sc[0]
    first = fetch(
        sems_f,
        (rows_at(xa, SEQ, SEQ), gs),
        (up_2.at[a], row_u2),
        (rows_at(xa, 2 * SEQ, EXTRA), bs),
        (up_1.at[a], row_u1),
        (down_2.at[a], row_d2),
    )
    weights = Weights(sc, pieces, w, sems, lead)
    weights.start()
    first[0].wait()
    gr[...] = low(across(gs, cols) * keep[...])
    for copy in first[1:]:
        copy.wait()
    glat4 = low(mm(gr[...], row_u2[...], NT))
    res[...] = jnp.zeros_like(res)
    gn2[...] = jnp.zeros_like(gn2)
    lat4[...] = jnp.zeros_like(lat4)
    glat3[...] = jnp.zeros_like(glat3)
    ffn_steps(
        weights, sc, 0, cols, w, bs, n2, lat3, gr, glat4, row_u1, row_d2, (res, gn2, lat4, glat3), early
    )


def ffn_b_kernel(lead, cols, *refs):
    sc = refs[0]
    pieces = refs[1:9]
    own_q = refs[9:17]
    (xa, keep, gain, n2, lat3, up_1, down_2, up_2, f_down, p_down, p_up, bias_out) = refs[17:29]
    (middle, att, lat2, gr, res_in, gn2_in, lat4_in, glat3_in, early_in) = refs[29:38]
    layer, refs = refs[38 : 38 + cols], refs[:38] + refs[38 + cols :]
    gatt, gmid, early = refs[38:41]
    refs = refs[:41] + (None,) + refs[41:]
    w, sems, wp, sems_p, res, gn2, lat4, glat3 = refs[42:50]
    bs, row_u1, row_d2, row_u2, row_fd, row_pd, row_pu, mid_s, att_s, res_s, gn2_s, early_s = refs[50:62]
    sems_f, out_s = refs[62:]
    lane = early_in.shape[-1]
    a = sc[0]
    first = fetch(
        sems_f,
        (up_2.at[a], row_u2),
        (rows_at(xa, 2 * SEQ, EXTRA), bs),
        (up_1.at[a], row_u1),
        (down_2.at[a], row_d2),
    )
    weights = Weights(sc, pieces, w, sems, lead)
    weights.start()
    proj = Weights(sc, own_q, wp, sems_p, lead, 3 * D // cols)
    last = fetch(
        sems_f.at[pl.ds(4, 8)],
        (res_in, res_s),
        (middle, mid_s),
        (gn2_in, gn2_s),
        (f_down.at[a], row_fd),
        (p_up.at[a], row_pu),
        (p_down.at[a], row_pd),
        (att, att_s),
        (early_in, early_s),
    )
    proj.start()
    hid = D // cols
    for copy in first:
        copy.wait()
    glat4 = low(mm(gr[...], row_u2[...], NT))
    res[...] = jnp.zeros_like(res)
    gn2[...] = jnp.zeros_like(gn2)
    lat4[...] = lat4_in[...]
    glat3[...] = glat3_in[...]
    ffn_steps(
        weights, sc, 1, cols, w, bs, n2, lat3, gr, glat4, row_u1, row_d2, (res, gn2, lat4, glat3), early, lane
    )
    for copy in last:
        copy.wait()
    early[:, :, :lane] = early_s[...]
    mid = mid_s[...]
    lat4_low = low(lat4[...])
    out = low(
        keep[...]
        * (mid + (res_s[...] + res[...]) + mm(lat4_low, row_u2[...]) + bias_out[1:2].astype(F32))
    )
    to_columns(sc, out, out_s, layer)
    glat3_low = low(glat3[...])
    grad_normed = gn2_s[...] + gn2[...] + mm(glat3_low, row_fd[...])
    unit, inverse = norm_parts(mid)
    grad_middle = gr[...].astype(F32) + norm_back(grad_normed, gain[1:2], unit, inverse)
    gmid[...] = grad_middle
    gb = low(grad_middle)
    glat2 = low(mm(gb, row_pu[...], NT))
    glat2_t = low(glat2.astype(F32).T)
    put(early, FF + D, low(mm(low(lat2[...].astype(F32).T), gb)), lane)
    put(early, FF + 2 * D, low(mm(low(glat3_low.astype(F32).T), n2[...])), lane)
    put(early, FF + 3 * D, low(mm(low(lat4_low.astype(F32).T), gr[...])), lane)
    proj.wait()

    def step(slot, _):
        block = column_of(sc, slot)
        here = lanes(slot * hid, hid)
        there = lanes(block * hid, hid)
        gatt[:, here] = low(mm(gb, wp[slot]) + mm(glat2, row_pd[:, there]))
        put(early, FF + block * hid, low(mm(glat2_t, att_s[:, here])), lane)
        return 0

    for slot in range(cols):
        step(slot, 0)


def attention_back_kernel(cols, *refs):
    sc = refs[0]
    closed, q, k, v, lse, gatt, lat1, n1, q_up = refs[1:10]
    gq, gk, gv, glat1, late = refs[10:15]
    a = sc[0]
    hid = D // cols
    shut = closed[...] > 0.5

    def attend(pair, _):
        at = lanes(pair * PAIR, PAIR)
        kp = k[:, at]
        k_t = low(kp.astype(F32).T)
        q_both, g_both = both_heads(q[:, at]), both_heads(gatt[:, at])
        s = jnp.where(shut, -1e30, mm(kp, q_both, NT))
        soft = jnp.exp(s - lse[pair])
        grad_soft = mm(v[:, at], g_both, NT)
        total = jnp.sum(grad_soft * soft, axis=0, keepdims=True)
        grad_scores = low(soft * (grad_soft - total))
        gq[:, at] = own_heads(mm(k_t, grad_scores), 0.125)
        gk[:, at] = low(mm(grad_scores, q_both))
        gv[:, at] = low(mm(low(soft), g_both))
        return 0

    lax.fori_loop(0, H // 2, attend, 0, unroll=4)
    lat1_t = low(lat1[...].astype(F32).T)

    def step(slot, acc):
        block = column_of(sc, slot)
        here = lanes(slot * hid, hid)
        there = lanes(block * hid, hid)
        for c, g in enumerate((gq, gk, gv)):
            grad = g[:, here]
            acc = acc + mm(grad, q_up[c, :, there], NT)
            put(late, (c + 1) * D + block * hid, low(mm(lat1_t, grad)))
        return acc

    made = jnp.zeros((SEQ, R), F32)
    for slot in range(cols):
        made = step(slot, made)
    made = low(made)
    glat1[...] = made
    put(late, 0, low(mm(low(made.astype(F32).T), n1[...])))


def back_kernel(lead, cols, *refs):
    sc = refs[0]
    pieces = refs[1:9]
    xa, gain, gq, gk, gv, glat1, q_down, gmid = refs[9:17]
    outs = refs[17 : 17 + cols]
    w, sems, acc, xs, row_qd, gmid_s, sems_f, out_s = refs[17 + cols :]
    first = fetch(
        sems_f,
        (rows_at(xa, 0, SEQ), xs),
        (q_down.at[sc[0]], row_qd),
        (gmid, gmid_s),
    )
    weights = Weights(sc, pieces, w, sems, lead)
    weights.start()
    hid = D // cols
    for copy in first:
        copy.wait()
    acc[...] = mm(glat1[...], row_qd[...])
    x = across(xs, cols)
    unit, inverse = norm_parts(x)

    def step(i, _):
        slot = weights.slot(i, cols)
        here = lanes(slot * hid, hid)
        grad = jnp.concatenate([gq[:, here], gk[:, here], gv[:, here]], axis=1)
        acc[...] += mm(grad, w[slot, :, : 3 * hid], NT)
        return 0

    lax.fori_loop(0, cols, step, 0)
    made = low(gmid_s[...] + norm_back(acc[...], gain[0:1], unit, inverse))
    to_columns(sc, made, out_s, outs)


def sum_kernel(owners, mine, out, acc):
    acc[...] = jnp.zeros_like(acc)
    for d in range(mine.shape[0]):
        acc[owners[d]] += mine[d, :, : acc.shape[2]].astype(F32)
    out[...] = low(acc[...])


def spread_kernel(lead, cols, parts, maps, *refs):
    sc, pieces = refs[0], refs[1:9]
    count = (len(refs) - 11) // 2
    outs, whole, made = refs[9 : 9 + count], refs[9 + count], refs[10 + count : 10 + 2 * count]
    sems_in, sems_out = refs[10 + 2 * count :]
    copies = []
    for k, piece in enumerate(pieces):
        x_rel, y_rel, away = piece_place(sc, k)
        for n, (high_col, high_row) in enumerate(lead):
            row = high_row * 2 + ((sc[3] + y_rel) & 1)
            col = high_col * 4 + ((sc[1] & 3) ^ (x_rel * 2 + away))
            copies.append(
                pltpu.make_async_copy(piece.at[n], whole.at[row * cols + col], sems_in.at[k, n])
            )
    for copy in copies:
        copy.start()
    for copy in copies:
        copy.wait()
    found = [[] for _ in outs]
    base = 0
    for part, spans in zip(parts, maps):
        for out, section, there, start, width in spans:
            for lane in range(0, width, 128):
                at = start + lane
                found[out].append((section, there + lane, at // part, base + at % part))
        base += part
    leaving = []
    for i, (out, buffer) in enumerate(zip(outs, made)):
        for section, there, device, here in found[i]:
            block = whole[device, :, here : here + 128].astype(F32)
            if section is None:
                buffer[:, there : there + 128] = block
            else:
                buffer[:, section, :, there : there + 128] = block.reshape(NA, R, 128)
        leaving.append(pltpu.make_async_copy(buffer, out, sems_out.at[i]))
        leaving[-1].start()
    for copy in leaving:
        copy.wait()


def place_kernel(lead, cols, *refs):
    sc, pieces, out, sems = refs[0], refs[1:9], refs[9], refs[10]
    copies = []
    for k, piece in enumerate(pieces):
        x_rel, y_rel, away = piece_place(sc, k)
        for n, (high_col, high_row) in enumerate(lead):
            row = high_row * 2 + ((sc[3] + y_rel) & 1)
            col = high_col * 4 + ((sc[1] & 3) ^ (x_rel * 2 + away))
            copies.append(pltpu.make_async_copy(piece.at[n], out.at[row * cols + col], sems.at[k, n]))
    for copy in copies:
        copy.start()
    for copy in copies:
        copy.wait()


def send_grads(grads):
    return lax.all_to_all(grads, BOTH, split_axis=0, concat_axis=0, tiled=True)


def sum_grads(mine, owners, part):
    summed = call(
        sum_kernel,
        jax.ShapeDtypeStruct((NA, R, part), BF),
        [owners, mine],
        [pltpu.SMEM, VMEM],
        [VMEM((NA, R, part), F32)],
    )
    return summed.reshape(NA * R, part)


def spread(sc, pieces, parts, maps, shapes):
    rows, cols = sizes()
    devices = rows * cols
    lead = lead_table(rows, cols)
    arrivals = pltpu.SemaphoreType.DMA((8, len(lead)))
    whole = (devices, NA * R, sum(parts))
    ins, spaces = [sc, *pieces], [pltpu.SMEM] + [pl.ANY] * 8
    if all(p % 128 == 0 for p in parts):
        return call(
            functools.partial(spread_kernel, lead, cols, parts, maps),
            [jax.ShapeDtypeStruct(x, F32) for x in shapes],
            ins,
            spaces,
            [VMEM(whole, BF)]
            + [VMEM(x, F32) for x in shapes]
            + [arrivals, pltpu.SemaphoreType.DMA((len(shapes),))],
            pl.ANY,
            SPREAD,
        )
    whole = call(
        functools.partial(place_kernel, lead, cols),
        jax.ShapeDtypeStruct(whole, BF),
        ins,
        spaces,
        [arrivals],
    )
    found = [[] for _ in shapes]
    base = 0
    for part, spans in zip(parts, maps):
        flat = jnp.swapaxes(whole[:, :, base : base + part], 0, 1).reshape(NA * R, devices * part)
        for out, section, there, start, width in spans:
            found[out].append((section or 0, there, flat[:, start : start + width].astype(F32)))
        base += part
    return [
        (
            jnp.concatenate([x for _, _, x in sorted(f, key=lambda e: e[:2])], axis=1)
            if len(shape) == 2
            else jnp.stack([x.reshape(NA, R, -1) for _, _, x in sorted(f, key=lambda e: e[:2])], 1)
        )
        for f, shape in zip(found, shapes)
    ]


def per_device(
    tokens_in,
    grad_out,
    keep_mask,
    adapter_index,
    ln_gain,
    ln_shift,
    w_qkv,
    bias_qv,
    w_proj,
    w_fc1,
    bias_fc1,
    w_fc2,
    bias_out,
    qkv_down,
    qkv_up,
    proj_down,
    proj_up,
    fc1_down,
    fc1_up,
    fc2_down,
    fc2_up,
):
    rows, cols = sizes()
    row, column = lax.axis_index("row"), lax.axis_index("col")
    assert adapter_index.shape[0] == cols and cols >= 4 and rows >= 2
    hid = D // cols
    n = 4 * hid
    blk = D // rows
    lead = lead_table(rows, cols)

    shard = jax.ShapeDtypeStruct((blk, n), BF)
    rows_in, shard_q = call(
        prep_q_kernel,
        [jax.ShapeDtypeStruct((cols, 2 * SEQ + EXTRA, hid), BF), shard],
        [tokens_in.reshape(cols, SEQ, hid), grad_out.reshape(cols, SEQ, hid), bias_qv]
        + [bias_fc1, w_qkv, w_proj],
        [VMEM] * 6,
        mib=56,
    )
    with jax.named_scope("q_high"):
        own_q, came_q = gather_high(shard_q)
    xa = lax.all_to_all(rows_in, "col", split_axis=0, concat_axis=0, tiled=True)
    adapter = lax.dynamic_index_in_dim(adapter_index, column, 0, keepdims=False)
    sc = jnp.stack([adapter, column, column % 2, row % 2]).astype(jnp.int32)
    up_qkv = jnp.swapaxes(lax.dynamic_index_in_dim(qkv_up, adapter, 0, keepdims=False), 0, 1)
    shard_a, shard_b, keep, closed = call(
        prep_f_kernel,
        [shard] * 2 + [jax.ShapeDtypeStruct((SEQ, 1), F32)] * 2,
        [sc, keep_mask, w_fc1, w_fc2],
        [pltpu.SMEM] + [VMEM] * 3,
    )

    own_q, shard_a, shard_b = after_all(
        (own_q, shard_a, shard_b), xa, keep, closed, sc, up_qkv, *came_q
    )
    with jax.named_scope("q_one"):
        one_q = swap(own_q, flip_one)
    with jax.named_scope("q_two"):
        two_q = swap(own_q, flip_two)
    with jax.named_scope("fa_high"):
        own_a, came_a = gather_high(shard_a)
    own_q, one_q, two_q = after_all((own_q, one_q, two_q), *came_a)
    with jax.named_scope("q_both"):
        both_q = swap(one_q, flip_two)
    with jax.named_scope("q_core"):
        away_q = [swap(p, flip_core) for p in (own_q, one_q, two_q)]
    own_a, shard_b = after_all((own_a, shard_b), *away_q)
    with jax.named_scope("q_core"):
        pieces_q = [own_q, one_q, two_q, both_q] + away_q + [swap(both_q, flip_core)]
    with jax.named_scope("fa_one"):
        one_a = swap(own_a, flip_one)
    with jax.named_scope("fa_two"):
        two_a = swap(own_a, flip_two)
    with jax.named_scope("fb_high"):
        own_b, came_b = gather_high(shard_b)

    def shaped(width, dtype, height=SEQ):
        return jax.ShapeDtypeStruct((height, width), dtype)

    big, small = shaped(D, BF), shaped(R, BF)
    scratch = weight_scratch(rows, cols, n)
    rows_space, bias_space = VMEM((cols, SEQ, hid), BF), VMEM((cols, EXTRA, hid), BF)
    any_space = [pl.ANY] * 8
    n1, lat1, q, k, v, lse, att, lat2, middle, n2, lat3 = call(
        functools.partial(front_kernel, lead, cols),
        [
            big,
            small,
            big,
            big,
            big,
            jax.ShapeDtypeStruct((H // 2, 1, 2 * SEQ), F32),
            big,
            small,
            shaped(D, F32),
            big,
            small,
        ],
        [sc, *pieces_q, xa, closed, ln_gain, ln_shift, qkv_down, up_qkv, proj_down]
        + [proj_up]
        + [fc1_down, bias_out],
        [pltpu.SMEM] + any_space + [pl.ANY] + [VMEM] * 3 + [pl.ANY, VMEM] + [pl.ANY] * 3 + [VMEM],
        scratch
        + [VMEM((SEQ, D), F32), VMEM((SEQ, D), F32), rows_space, bias_space]
        + [VMEM((R, D), BF)] * 4
        + [pltpu.SemaphoreType.DMA((6,))],
        mib=FRONT,
    )
    own_a, one_a, two_a = after_all((own_a, one_a, two_a), n1, *came_b)
    bits = list(reversed(range(bits_of(rows))))
    owners = after(adapter_index, n1)
    for bit in bits[:-1]:
        owners = owner_stack(owner_parts(owners, bit), bit)
    with jax.named_scope("fa_both"):
        both_a = swap(one_a, flip_two)
    with jax.named_scope("fa_core"):
        away_a = [swap(p, flip_core) for p in (own_a, one_a, two_a)]
    own_b, owners = after_all((own_b, owners), *away_a)
    owners = owner_parts(owners, 0)
    with jax.named_scope("fa_core"):
        pieces_a = [own_a, one_a, two_a, both_a] + away_a + [swap(both_a, flip_core)]
    with jax.named_scope("fb_one"):
        one_b = swap(own_b, flip_one)
    with jax.named_scope("fb_two"):
        two_b = swap(own_b, flip_two)
    wide = shaped(D, F32)
    thin = shaped(R, F32)
    res, gn2, lat4, glat3, gr, early_a = call(
        functools.partial(ffn_a_kernel, lead, cols),
        [wide, wide, thin, thin, big, jax.ShapeDtypeStruct((rows * cols, R, FF // (rows * cols)), BF)],
        [sc, *pieces_a, xa, keep, n2, lat3, fc1_up, fc2_down, fc2_up],
        [pltpu.SMEM] + any_space + [pl.ANY] + [VMEM] * 3 + [pl.ANY] * 3,
        scratch
        + [rows_space, bias_space, VMEM((R, FF), BF), VMEM((R, FF), BF), VMEM((R, D), BF)]
        + [pltpu.SemaphoreType.DMA((5,))],
        mib=FFN_A,
    )
    own_b, one_b, two_b, *owners = after_all((own_b, one_b, two_b, *owners), res)
    owners = owner_stack(owners, 0).transpose(tuple(bits) + (len(bits),)).reshape(-1)
    with jax.named_scope("fb_both"):
        both_b = swap(one_b, flip_two)
    with jax.named_scope("fb_core"):
        away_b = [swap(p, flip_core) for p in (own_b, one_b, two_b)]
        pieces_b = [own_b, one_b, two_b, both_b] + away_b + [swap(after(both_b, owners), flip_core)]
    *layer, gatt, gmid, grads_b = call(
        functools.partial(ffn_b_kernel, lead, cols),
        [shaped(hid, BF)] * cols + [big, wide]
        + [jax.ShapeDtypeStruct((rows * cols, R, 12 * D // (rows * cols)), BF)],
        [sc, *pieces_b, *pieces_q, xa, keep, ln_gain, n2, lat3, fc1_up, fc2_down, fc2_up]
        + [fc1_down, proj_down, proj_up, bias_out]
        + [middle, att, lat2, gr, res, gn2, lat4, glat3, early_a],
        [pltpu.SMEM]
        + any_space * 2
        + [pl.ANY, VMEM, VMEM, VMEM, VMEM]
        + [pl.ANY] * 6
        + [VMEM, pl.ANY, pl.ANY, VMEM, VMEM, pl.ANY, pl.ANY, VMEM, VMEM, pl.ANY],
        scratch
        + [VMEM((cols, D, hid), BF), scratch[1]]
        + [VMEM((SEQ, D), F32), VMEM((SEQ, D), F32), VMEM((SEQ, R), F32), VMEM((SEQ, R), F32)]
        + [bias_space, VMEM((R, FF), BF), VMEM((R, FF), BF)]
        + [VMEM((R, D), BF)] * 4
        + [VMEM((SEQ, D), F32), VMEM((SEQ, D), BF), VMEM((SEQ, D), F32), VMEM((SEQ, D), F32)]
        + [VMEM(early_a.shape, BF), pltpu.SemaphoreType.DMA((12,)), VMEM((SEQ, D), BF)],
        mib=FFN_B,
    )
    with jax.named_scope("grads_b_send"):
        mine_b = send_grads(grads_b)
    with jax.named_scope("layer_out"):
        layer = exchange_rows(layer)
    gq, gk, gv, glat1, late = call(
        functools.partial(attention_back_kernel, cols),
        [big, big, big, small, jax.ShapeDtypeStruct((rows * cols, R, 4 * D // (rows * cols)), BF)],
        [sc, closed, q, k, v, lse, gatt, lat1, n1, up_qkv],
        [pltpu.SMEM] + [VMEM] * 9,
        mib=ATT,
    )
    with jax.named_scope("grads_c_send"):
        mine_c = send_grads(late)
    with jax.named_scope("grads_b"):
        own_b, _ = gather_high(
            sum_grads(after(mine_b, late, *layer), owners, mine_b.shape[2]), 1
        )
        own_c, _ = gather_high(sum_grads(mine_c, owners, mine_c.shape[2]))
        order_b = tuple(lead.index(place) for place in lead_table(rows, cols, 1))
        own = lane_join([own_b, own_c], [order_b, tuple(range(len(lead)))])
    gmid = after(gmid, own)
    sent = call(
        functools.partial(back_kernel, lead, cols),
        [shaped(hid, BF)] * cols,
        [sc, *pieces_q, xa, ln_gain, gq, gk, gv, glat1, qkv_down, gmid],
        [pltpu.SMEM] + any_space + [pl.ANY] + [VMEM] * 5 + [pl.ANY] * 2,
        scratch
        + [VMEM((SEQ, D), F32), rows_space, VMEM((R, D), BF), VMEM((SEQ, D), F32)]
        + [pltpu.SemaphoreType.DMA((3,)), VMEM((SEQ, D), BF)],
        mib=BACK,
    )
    with jax.named_scope("grads"):
        one, two = swap(own, flip_one), swap(own, flip_two)
        own, one, two = after_all((own, one, two), *sent)
        layer_out = stacked(after_all(layer, one, two), column, pl.ANY)
        both = swap(one, flip_two)
        away = [swap(p, flip_core) for p in (own, one, two)]
        both = after(both, layer_out)
        pieces = [own, one, two, both] + away + [swap(both, flip_core)]
        half = FF // cols // 2
        map_a, map_b = (
            tuple(
                (out, None, (2 * block + part) * half, base + block * half, half)
                for out, base in ((0, 0), (1, FF // 2))
                for block in range(cols)
            )
            for part in (0, 1)
        )
        map_b = map_b + tuple((2 + i, None, 0, FF + i * D, D) for i in range(4))
        map_c = ((6, None, 0, 0, D),) + tuple((7, c, 0, (c + 1) * D, D) for c in range(3))
        parts = [early_a.shape[-1], mine_b.shape[-1] - early_a.shape[-1], mine_c.shape[-1]]
        shapes = [(NA * R, FF)] * 2 + [(NA * R, D)] * 5 + [(NA, 3, R, D)]
        sums = spread(sc, pieces, parts, [map_a, map_b, map_c], shapes)

    with jax.named_scope("rows_out"):
        grad_rows = exchange_rows(after_all(sent, *away))
        grad_in = stacked(after_all(grad_rows, sums[0]), column, pl.ANY)

    def split(table):
        return table.reshape((NA, R) + table.shape[1:])

    g_fc1_up, g_fc2_down, g_proj_down, g_proj_up, g_fc1_down, g_fc2_up = map(split, sums[:6])
    return (
        layer_out.reshape(cols * SEQ, hid),
        grad_in.reshape(cols * SEQ, hid),
        split(sums[6]),
        jnp.swapaxes(sums[7], 1, 2),
        g_proj_down,
        g_proj_up,
        g_fc1_down,
        g_fc1_up,
        g_fc2_down,
        g_fc2_up,
    )


def solution(mesh):
    return jax.shard_map(
        per_device,
        mesh=mesh,
        in_specs=(
            P("row", "col"),
            P("row", "col"),
            P("row", None),
            P("row"),
            P(),
            P(),
            P(None, "row", "col"),
            P(None, "col"),
            P("col", "row"),
            P("row", "col"),
            P("col"),
            P("col", "row"),
            P(),
            P(),
            P(),
            P(),
            P(),
            P(),
            P(),
            P(),
            P(),
        ),
        out_specs=(P("row", "col"), P("row", "col"), P(), P(), P(), P(), P(), P(), P(), P()),
        check_vma=False,
    )
```

```python
import functools

import jax
import jax.numpy as jnp
from jax import lax
from jax.experimental import pallas as pl
from jax.experimental.pallas import tpu as pltpu
from jax.sharding import PartitionSpec as P

D = 1024
H = 16
HD = 64
FF = 4096
BUF = 64
R = 16
NA = 8
SEQ = 320
PAIR = 2 * HD
EXTRA = 16
SPREAD = 56
FRONT, FFN_A, FFN_B, ATT, BACK = 56, 56, 56, 56, 56
BF = jnp.bfloat16
F32 = jnp.float32
BOTH = ("row", "col")
VMEM = pltpu.VMEM
NN = (((1,), (0,)), ((), ()))
NT = (((1,), (1,)), ((), ()))


def mm(left, right, dims=NN):
    return lax.dot_general(left, right, dims, preferred_element_type=F32)


def low(values):
    return values.astype(BF)


def norm_parts(values):
    row_mean = jnp.mean(values, axis=-1, keepdims=True)
    centered = values - row_mean
    variance = jnp.mean(centered * centered, axis=-1, keepdims=True)
    inverse = lax.rsqrt(variance + 1e-06)
    return (centered * inverse, inverse)


def norm_back(grad_normed, gain_row, unit_rows, inverse):
    scaled = grad_normed * gain_row
    first_mean = jnp.mean(scaled, axis=-1, keepdims=True)
    second_mean = jnp.mean(scaled * unit_rows, axis=-1, keepdims=True)
    return inverse * (scaled - first_mean - unit_rows * second_mean)


def call(kernel, outs, ins, spaces, scratch=(), out_space=VMEM, mib=4):
    return pl.pallas_call(
        kernel,
        out_shape=outs,
        in_specs=[pl.BlockSpec(memory_space=s) for s in spaces],
        out_specs=jax.tree.map(lambda _: pl.BlockSpec(memory_space=out_space), outs),
        scratch_shapes=list(scratch),
        compiler_params=pltpu.CompilerParams(vmem_limit_bytes=mib << 20),
        cost_estimate=pl.CostEstimate(flops=0, bytes_accessed=0, transcendentals=0),
    )(*ins)


def sizes():
    return lax.axis_size("row"), lax.axis_size("col")


def swap(block, flip):
    rows, cols = sizes()
    pairs = []
    for i in range(rows * cols):
        row, col = flip(i // cols, i % cols)
        pairs.append((i, row * cols + col))
    return lax.ppermute(block, BOTH, pairs)


def bits_of(size):
    return size.bit_length() - 1


def stack_kernel(which, *refs):
    parts, out, sems = refs[:-2], refs[-2], refs[-1]
    copies = [
        pltpu.make_async_copy(ref, out.at[which[0] ^ m], sems.at[m]) for m, ref in enumerate(parts)
    ]
    for copy in copies:
        copy.start()
    for copy in copies:
        copy.wait()


def stacked(parts, index, out_space=VMEM):
    shape = parts[0].shape
    flat = [p.reshape((-1, shape[-1])) for p in parts]
    out = jax.ShapeDtypeStruct((len(parts),) + flat[0].shape, flat[0].dtype)
    made = call(
        stack_kernel,
        out,
        [index.reshape(1).astype(jnp.int32)] + flat,
        [pltpu.SMEM] + [pl.ANY] * len(parts),
        [pltpu.SemaphoreType.DMA((len(parts),))],
        out_space,
    )
    return made.reshape((len(parts),) + shape)


def group_join(block, axis, low_bit, width):
    parts = [block]
    for m in range(1, 1 << width):
        step = m << low_bit
        if axis == "row":
            parts.append(swap(block, lambda r, c: (r ^ step, c)))
        else:
            parts.append(swap(block, lambda r, c: (r, c ^ step)))
    index = (lax.axis_index(axis) >> low_bit) & ((1 << width) - 1)
    return stacked(parts, index), parts


def groups(top, bottom, most):
    out = []
    while top > bottom:
        width = min(most, top - bottom)
        out.append((top - width, width))
        top -= width
    return out


def early_groups(rows, cols, most):
    return [("row",) + g for g in groups(bits_of(rows), 1, most)] + [
        ("col",) + g for g in groups(bits_of(cols), 2, most)
    ]


def lead_table(rows, cols, most=2):
    table = [(0, 0)]
    for axis, bit, width in early_groups(rows, cols, most):
        shift = bit - (1 if axis == "row" else 2)
        new = []
        for value in range(1 << width):
            for high_col, high_row in table:
                if axis == "row":
                    new.append((high_col, high_row + (value << shift)))
                else:
                    new.append((high_col + (value << shift), high_row))
        table = new
    return table


def after(value, *others):
    return lax.optimization_barrier((value,) + others)[0]


def after_all(values, *others):
    return lax.optimization_barrier(tuple(values) + others)[: len(values)]


def exchange_rows(parts):
    came = [parts[0]]
    for j in range(1, len(parts)):
        came.append(swap(parts[j], lambda r, c: (r, c ^ j)))
    return came


def gather_high(shard, most=2):
    rows, cols = sizes()
    block, parts = shard, []
    for axis, bit, width in early_groups(rows, cols, most):
        block, parts = group_join(block, axis, bit, width)
    return block.reshape((-1,) + shard.shape), parts[1:]


def lane_join_kernel(orders, *refs):
    parts, out, sems = refs[:-2], refs[-2], refs[-1]
    copies, lane = [], 0
    for i, (part, order) in enumerate(zip(parts, orders)):
        width = part.shape[-1]
        for n, put_at in enumerate(order):
            target = out.at[put_at, :, lane : lane + width]
            copies.append(pltpu.make_async_copy(part.at[n], target, sems.at[i, n]))
        lane += width
    for copy in copies:
        copy.start()
    for copy in copies:
        copy.wait()


def lane_join(parts, orders):
    if any(p.shape[-1] % 128 for p in parts):
        placed = [p[jnp.array(sorted(range(len(o)), key=o.index))] for p, o in zip(parts, orders)]
        return jnp.concatenate(placed, axis=-1)
    shape = parts[0].shape[:-1] + (sum(p.shape[-1] for p in parts),)
    return call(
        functools.partial(lane_join_kernel, orders),
        jax.ShapeDtypeStruct(shape, parts[0].dtype),
        parts,
        [pl.ANY] * len(parts),
        [pltpu.SemaphoreType.DMA((len(parts), shape[0]))],
    )


def flip_one(r, c):
    return (r, c ^ 2) if c % 2 == 0 else (r ^ 1, c)


def flip_two(r, c):
    return (r ^ 1, c) if c % 2 == 0 else (r, c ^ 2)


def flip_core(r, c):
    return (r, c ^ 1)


def with_cores(pieces):
    return pieces + [swap(p, flip_core) for p in pieces]


def owner_parts(block, bit):
    step = 1 << bit
    return [block, swap(block, lambda r, c: (r ^ step, c))]


def owner_stack(parts, bit):
    return jnp.stack(parts)[jnp.arange(2) ^ ((lax.axis_index("row") >> bit) & 1)]


def piece_place(sc, k):
    kind, away = k % 4, k // 4
    turn = (sc[2] + away) & 1
    return (0, 1 - turn, turn, 1)[kind], (0, turn, 1 - turn, 1)[kind], away


class Weights:
    def __init__(self, sc, pieces, w, sems, lead, first_lane=0):
        self.copies = []
        depth = pieces[0].shape[1]
        taken = pl.ds(first_lane, w.shape[2])
        for k, piece in enumerate(pieces):
            x_rel, y_rel, away = piece_place(sc, k)
            for n, (high_col, high_row) in enumerate(lead):
                slot = high_col * 4 + x_rel * 2 + away
                row = (high_row * 2 + ((sc[3] + y_rel) & 1)) * depth
                self.copies.append(
                    pltpu.make_async_copy(
                        piece.at[n, :, taken],
                        w.at[slot, pl.ds(pl.multiple_of(row, depth), depth), :],
                        sems.at[k, n],
                    )
                )

    def start(self):
        for copy in self.copies:
            copy.start()

    def wait(self, away=None):
        half = len(self.copies) // 2
        for copy in self.copies if away is None else self.copies[away * half : (away + 1) * half]:
            copy.wait()

    def slot(self, i, cols):
        half = cols // 2

        @pl.when(i == 0)
        def _():
            self.wait(0)

        @pl.when(i == half)
        def _():
            self.wait(1)

        return lax.rem(i, half) * 2 + i // half


def column_of(sc, slot):
    return (slot // 4) * 4 + ((sc[1] & 3) ^ (slot & 3))


def weight_scratch(rows, cols, n):
    lead = len(lead_table(rows, cols))
    return [VMEM((cols, D, n), BF), pltpu.SemaphoreType.DMA((8, lead))]


def put(ref, start, value, lane=0):
    part = ref.shape[-1] - lane
    for i in range(value.shape[-1] // part):
        ref[start // part + i, :, lane:] = value[:, i * part : (i + 1) * part]


def lanes(start, width):
    return pl.ds(pl.multiple_of(start, width), width)


def prep_q_kernel(tokens, grads, bias_qv, bias_f, wq, wp, rows, out):
    hid = wq.shape[2]
    seq = tokens.shape[1]
    for c in range(tokens.shape[0]):
        rows[c, :seq] = tokens[c]
        rows[c, seq : 2 * seq] = grads[c]
        rows[c, 2 * seq : 2 * seq + 2] = bias_qv[...]
        for i in range(4):
            rows[c, 2 * seq + 2 + i, :] = bias_f[pl.ds(i * hid, hid)]
    for c in range(3):
        out[:, c * hid : (c + 1) * hid] = wq[c]
    out[:, 3 * hid :] = low(wp[...].astype(F32).T)


def prep_f_kernel(sc, mask, w1, w2, out_a, out_b, keep, closed):
    row = mask[pl.ds(sc[1], 1), :].astype(F32)
    row = jnp.concatenate([jnp.ones((1, BUF), F32), row], axis=1)
    column = jnp.broadcast_to(row, (8, SEQ)).T[:, :1]
    keep[...] = column
    closed[...] = 1.0 - column
    half = w1.shape[1] // 2
    out_a[:, :half] = w1[:, :half]
    out_b[:, :half] = w1[:, half:]
    out_a[:, half:] = low(w2[:half].astype(F32).T)
    out_b[:, half:] = low(w2[half:].astype(F32).T)


def fetch(sems, *pairs):
    copies = [pltpu.make_async_copy(src, dst, sems.at[i]) for i, (src, dst) in enumerate(pairs)]
    for copy in copies:
        copy.start()
    return copies


def to_columns(sc, made, buffer, outs):
    hid = outs[0].shape[-1]
    buffer[...] = made
    for j, out in enumerate(outs):
        out[...] = buffer[:, lanes((sc[1] ^ j) * hid, hid)]


def rows_at(xa, start, height):
    return xa.at[:, pl.ds(start, height), :]


def across(ref, cols):
    return jnp.concatenate([ref[c] for c in range(cols)], axis=1).astype(F32)


def both_heads(pair):
    left = lax.broadcasted_iota(jnp.int32, (1, PAIR), 1) < HD
    zero = jnp.zeros_like(pair)
    return jnp.concatenate([jnp.where(left, pair, zero), jnp.where(left, zero, pair)], axis=0)


def own_heads(made, scale=1.0):
    both = jnp.concatenate([made[:HD, :SEQ], made[HD:, SEQ:]], axis=0)
    return low(both.T * scale)


def front_kernel(lead, cols, *refs):
    sc = refs[0]
    pieces = refs[1:9]
    (xa, closed, gain, shift, q_down, q_up, p_down, p_up, f_down, bias_out) = refs[9:19]
    (n1, lat1, q, k, v, lse, att, lat2, middle, n2, lat3) = refs[19:30]
    w, sems, hidden, branch, xs, bs, row_qd, row_pd, row_pu, row_fd, sems_f = refs[30:]
    a = sc[0]
    hid = D // cols
    first = fetch(
        sems_f,
        (rows_at(xa, 0, SEQ), xs),
        (q_down.at[a], row_qd),
        (rows_at(xa, 2 * SEQ, EXTRA), bs),
        (p_down.at[a], row_pd),
        (p_up.at[a], row_pu),
        (f_down.at[a], row_fd),
    )
    weights = Weights(sc, pieces, w, sems, lead)
    weights.start()
    first[0].wait()
    x = across(xs, cols)
    hidden[...] = x
    unit, _ = norm_parts(x)
    n1[...] = low(unit * gain[0:1] + shift[0:1])
    for copy in first[1:]:
        copy.wait()
    lat1[...] = low(mm(n1[...], row_qd[...], NT))

    def project(i, _):
        slot = weights.slot(i, cols)
        block = column_of(sc, slot)
        up = jnp.concatenate([q_up[c, :, lanes(block * hid, hid)] for c in range(3)], axis=1)
        made = mm(n1[...], w[slot, :, : 3 * hid]) + mm(lat1[...], up)
        bias_q = bs[block, 0:1, :].astype(F32)
        bias_v = bs[block, 1:2, :].astype(F32)
        at = lanes(slot * hid, hid)
        q[:, at] = low(made[:, :hid] + bias_q) * jnp.asarray(0.125, BF)
        k[:, at] = low(made[:, hid : 2 * hid])
        v[:, at] = low(made[:, 2 * hid :] + bias_v)
        return 0

    lax.fori_loop(0, cols, project, 0)
    shut = closed[...] > 0.5

    def attend(pair, _):
        at = lanes(pair * PAIR, PAIR)
        v_t = low(v[:, at].astype(F32).T)
        s = jnp.where(shut, -1e30, mm(k[:, at], both_heads(q[:, at]), NT))
        top = jnp.max(s, axis=0, keepdims=True)
        e = jnp.exp(s - top)
        total = jnp.sum(e, axis=0, keepdims=True)
        lse[pair] = top + jnp.log(total)
        att[:, at] = own_heads(mm(v_t, low(e * (1.0 / total))))
        return 0

    lax.fori_loop(0, H // 2, attend, 0, unroll=4)

    def down_two(slot, acc):
        block = column_of(sc, slot)
        return acc + mm(att[:, lanes(slot * hid, hid)], row_pd[:, lanes(block * hid, hid)], NT)

    lat2[...] = low(lax.fori_loop(0, cols, down_two, jnp.zeros((SEQ, R), F32)))
    branch[...] = mm(lat2[...], row_pu[...]) + bias_out[0:1].astype(F32)

    def out_proj(slot, _):
        branch[...] += mm(att[:, lanes(slot * hid, hid)], w[slot, :, 3 * hid :], NT)
        return 0

    lax.fori_loop(0, cols, out_proj, 0)
    mid = hidden[...] + branch[...]
    middle[...] = mid
    unit, _ = norm_parts(mid)
    n2[...] = low(unit * gain[1:2] + shift[1:2])
    lat3[...] = low(mm(n2[...], row_fd[...], NT))


def ffn_steps(weights, sc, part, cols, w, bs, n2, lat3, gr, glat4, up_1, down_2, acc, early, lane=0):
    res, gn2, lat4, glat3 = acc
    hid = D // cols
    ffn = FF // cols
    half = ffn // 2
    glat4_t = low(glat4.astype(F32).T)
    lat3_t = low(lat3[...].astype(F32).T)

    def step(i, _):
        slot = weights.slot(i, cols)
        block = column_of(sc, slot)
        at = pl.ds(pl.multiple_of(block * ffn + part * half, half), half)
        bias = jnp.concatenate(
            [bs[block, 2 + 2 * part + i : 3 + 2 * part + i, :] for i in range(2)], axis=1
        ).astype(F32)
        up, down = up_1[:, at], down_2[:, at]
        w1, w2 = w[slot, :, :half], w[slot, :, half:]
        pre = mm(n2[...], w1) + mm(lat3[...], up) + bias
        back = mm(gr[...], w2) + mm(glat4, down)
        cumulative = 0.5 * (1.0 + lax.erf(pre * 0.7071067811865476))
        activated = low(pre * cumulative)
        slope = cumulative + pre * jnp.exp(-0.5 * pre * pre) * 0.3989422804014327
        grad_pre = low(back * slope)
        lat4[...] += mm(activated, down, NT)
        glat3[...] += mm(grad_pre, up, NT)
        res[...] += mm(activated, w2, NT)
        gn2[...] += mm(grad_pre, w1, NT)
        put(early, block * half, low(mm(lat3_t, grad_pre)), lane)
        put(early, FF // 2 + block * half, low(mm(glat4_t, activated)), lane)
        return 0

    lax.fori_loop(0, cols, step, 0, unroll=2)


def ffn_a_kernel(lead, cols, *refs):
    sc = refs[0]
    pieces = refs[1:9]
    xa, keep, n2, lat3, up_1, down_2, up_2 = refs[9:16]
    res, gn2, lat4, glat3, gr, early = refs[16:22]
    w, sems, gs, bs, row_u1, row_d2, row_u2, sems_f = refs[22:]
    a = sc[0]
    first = fetch(
        sems_f,
        (rows_at(xa, SEQ, SEQ), gs),
        (up_2.at[a], row_u2),
        (rows_at(xa, 2 * SEQ, EXTRA), bs),
        (up_1.at[a], row_u1),
        (down_2.at[a], row_d2),
    )
    weights = Weights(sc, pieces, w, sems, lead)
    weights.start()
    first[0].wait()
    gr[...] = low(across(gs, cols) * keep[...])
    for copy in first[1:]:
        copy.wait()
    glat4 = low(mm(gr[...], row_u2[...], NT))
    res[...] = jnp.zeros_like(res)
    gn2[...] = jnp.zeros_like(gn2)
    lat4[...] = jnp.zeros_like(lat4)
    glat3[...] = jnp.zeros_like(glat3)
    ffn_steps(
        weights, sc, 0, cols, w, bs, n2, lat3, gr, glat4, row_u1, row_d2, (res, gn2, lat4, glat3), early
    )


def ffn_b_kernel(lead, cols, *refs):
    sc = refs[0]
    pieces = refs[1:9]
    own_q = refs[9:17]
    (xa, keep, gain, n2, lat3, up_1, down_2, up_2, f_down, p_down, p_up, bias_out) = refs[17:29]
    (middle, att, lat2, gr, res_in, gn2_in, lat4_in, glat3_in, early_in) = refs[29:38]
    layer, refs = refs[38 : 38 + cols], refs[:38] + refs[38 + cols :]
    gatt, gmid, early = refs[38:41]
    refs = refs[:41] + (None,) + refs[41:]
    w, sems, wp, sems_p, res, gn2, lat4, glat3 = refs[42:50]
    bs, row_u1, row_d2, row_u2, row_fd, row_pd, row_pu, mid_s, att_s, res_s, gn2_s, early_s = refs[50:62]
    sems_f, out_s = refs[62:]
    lane = early_in.shape[-1]
    a = sc[0]
    first = fetch(
        sems_f,
        (up_2.at[a], row_u2),
        (rows_at(xa, 2 * SEQ, EXTRA), bs),
        (up_1.at[a], row_u1),
        (down_2.at[a], row_d2),
    )
    weights = Weights(sc, pieces, w, sems, lead)
    weights.start()
    proj = Weights(sc, own_q, wp, sems_p, lead, 3 * D // cols)
    last = fetch(
        sems_f.at[pl.ds(4, 8)],
        (res_in, res_s),
        (middle, mid_s),
        (gn2_in, gn2_s),
        (f_down.at[a], row_fd),
        (p_up.at[a], row_pu),
        (p_down.at[a], row_pd),
        (att, att_s),
        (early_in, early_s),
    )
    proj.start()
    hid = D // cols
    for copy in first:
        copy.wait()
    glat4 = low(mm(gr[...], row_u2[...], NT))
    res[...] = jnp.zeros_like(res)
    gn2[...] = jnp.zeros_like(gn2)
    lat4[...] = lat4_in[...]
    glat3[...] = glat3_in[...]
    ffn_steps(
        weights, sc, 1, cols, w, bs, n2, lat3, gr, glat4, row_u1, row_d2, (res, gn2, lat4, glat3), early, lane
    )
    for copy in last:
        copy.wait()
    early[:, :, :lane] = early_s[...]
    mid = mid_s[...]
    lat4_low = low(lat4[...])
    out = low(
        keep[...]
        * (mid + (res_s[...] + res[...]) + mm(lat4_low, row_u2[...]) + bias_out[1:2].astype(F32))
    )
    to_columns(sc, out, out_s, layer)
    glat3_low = low(glat3[...])
    grad_normed = gn2_s[...] + gn2[...] + mm(glat3_low, row_fd[...])
    unit, inverse = norm_parts(mid)
    grad_middle = gr[...].astype(F32) + norm_back(grad_normed, gain[1:2], unit, inverse)
    gmid[...] = grad_middle
    gb = low(grad_middle)
    glat2 = low(mm(gb, row_pu[...], NT))
    glat2_t = low(glat2.astype(F32).T)
    put(early, FF + D, low(mm(low(lat2[...].astype(F32).T), gb)), lane)
    put(early, FF + 2 * D, low(mm(low(glat3_low.astype(F32).T), n2[...])), lane)
    put(early, FF + 3 * D, low(mm(low(lat4_low.astype(F32).T), gr[...])), lane)
    proj.wait()

    def step(slot, _):
        block = column_of(sc, slot)
        here = lanes(slot * hid, hid)
        there = lanes(block * hid, hid)
        gatt[:, here] = low(mm(gb, wp[slot]) + mm(glat2, row_pd[:, there]))
        put(early, FF + block * hid, low(mm(glat2_t, att_s[:, here])), lane)
        return 0

    for slot in range(cols):
        step(slot, 0)


def attention_back_kernel(cols, *refs):
    sc = refs[0]
    closed, q, k, v, lse, gatt, lat1, n1, q_up = refs[1:10]
    gq, gk, gv, glat1, late = refs[10:15]
    a = sc[0]
    hid = D // cols
    shut = closed[...] > 0.5

    def attend(pair, _):
        at = lanes(pair * PAIR, PAIR)
        kp = k[:, at]
        k_t = low(kp.astype(F32).T)
        q_both, g_both = both_heads(q[:, at]), both_heads(gatt[:, at])
        s = jnp.where(shut, -1e30, mm(kp, q_both, NT))
        soft = jnp.exp(s - lse[pair])
        grad_soft = mm(v[:, at], g_both, NT)
        total = jnp.sum(grad_soft * soft, axis=0, keepdims=True)
        grad_scores = low(soft * (grad_soft - total))
        gq[:, at] = own_heads(mm(k_t, grad_scores), 0.125)
        gk[:, at] = low(mm(grad_scores, q_both))
        gv[:, at] = low(mm(low(soft), g_both))
        return 0

    lax.fori_loop(0, H // 2, attend, 0, unroll=4)
    lat1_t = low(lat1[...].astype(F32).T)

    def step(slot, acc):
        block = column_of(sc, slot)
        here = lanes(slot * hid, hid)
        there = lanes(block * hid, hid)
        for c, g in enumerate((gq, gk, gv)):
            grad = g[:, here]
            acc = acc + mm(grad, q_up[c, :, there], NT)
            put(late, (c + 1) * D + block * hid, low(mm(lat1_t, grad)))
        return acc

    made = jnp.zeros((SEQ, R), F32)
    for slot in range(cols):
        made = step(slot, made)
    made = low(made)
    glat1[...] = made
    put(late, 0, low(mm(low(made.astype(F32).T), n1[...])))


def back_kernel(lead, cols, *refs):
    sc = refs[0]
    pieces = refs[1:9]
    xa, gain, gq, gk, gv, glat1, q_down, gmid = refs[9:17]
    outs = refs[17 : 17 + cols]
    w, sems, acc, xs, row_qd, gmid_s, sems_f, out_s = refs[17 + cols :]
    first = fetch(
        sems_f,
        (rows_at(xa, 0, SEQ), xs),
        (q_down.at[sc[0]], row_qd),
        (gmid, gmid_s),
    )
    weights = Weights(sc, pieces, w, sems, lead)
    weights.start()
    hid = D // cols
    for copy in first:
        copy.wait()
    acc[...] = mm(glat1[...], row_qd[...])
    x = across(xs, cols)
    unit, inverse = norm_parts(x)

    def step(i, _):
        slot = weights.slot(i, cols)
        here = lanes(slot * hid, hid)
        grad = jnp.concatenate([gq[:, here], gk[:, here], gv[:, here]], axis=1)
        acc[...] += mm(grad, w[slot, :, : 3 * hid], NT)
        return 0

    lax.fori_loop(0, cols, step, 0)
    made = low(gmid_s[...] + norm_back(acc[...], gain[0:1], unit, inverse))
    to_columns(sc, made, out_s, outs)


def sum_kernel(owners, mine, out, acc):
    acc[...] = jnp.zeros_like(acc)
    for d in range(mine.shape[0]):
        acc[owners[d]] += mine[d, :, : acc.shape[2]].astype(F32)
    out[...] = low(acc[...])


def spread_kernel(lead, cols, parts, maps, *refs):
    sc, pieces = refs[0], refs[1:9]
    count = (len(refs) - 11) // 2
    outs, whole, made = refs[9 : 9 + count], refs[9 + count], refs[10 + count : 10 + 2 * count]
    sems_in, sems_out = refs[10 + 2 * count :]
    copies = []
    for k, piece in enumerate(pieces):
        x_rel, y_rel, away = piece_place(sc, k)
        for n, (high_col, high_row) in enumerate(lead):
            row = high_row * 2 + ((sc[3] + y_rel) & 1)
            col = high_col * 4 + ((sc[1] & 3) ^ (x_rel * 2 + away))
            copies.append(
                pltpu.make_async_copy(piece.at[n], whole.at[row * cols + col], sems_in.at[k, n])
            )
    for copy in copies:
        copy.start()
    for copy in copies:
        copy.wait()
    found = [[] for _ in outs]
    base = 0
    for part, spans in zip(parts, maps):
        for out, section, there, start, width in spans:
            for lane in range(0, width, 128):
                at = start + lane
                found[out].append((section, there + lane, at // part, base + at % part))
        base += part
    leaving = []
    for i, (out, buffer) in enumerate(zip(outs, made)):
        for section, there, device, here in found[i]:
            block = whole[device, :, here : here + 128].astype(F32)
            if section is None:
                buffer[:, there : there + 128] = block
            else:
                buffer[:, section, :, there : there + 128] = block.reshape(NA, R, 128)
        leaving.append(pltpu.make_async_copy(buffer, out, sems_out.at[i]))
        leaving[-1].start()
    for copy in leaving:
        copy.wait()


def place_kernel(lead, cols, *refs):
    sc, pieces, out, sems = refs[0], refs[1:9], refs[9], refs[10]
    copies = []
    for k, piece in enumerate(pieces):
        x_rel, y_rel, away = piece_place(sc, k)
        for n, (high_col, high_row) in enumerate(lead):
            row = high_row * 2 + ((sc[3] + y_rel) & 1)
            col = high_col * 4 + ((sc[1] & 3) ^ (x_rel * 2 + away))
            copies.append(pltpu.make_async_copy(piece.at[n], out.at[row * cols + col], sems.at[k, n]))
    for copy in copies:
        copy.start()
    for copy in copies:
        copy.wait()


def send_grads(grads):
    return lax.all_to_all(grads, BOTH, split_axis=0, concat_axis=0, tiled=True)


def sum_grads(mine, owners, part):
    summed = call(
        sum_kernel,
        jax.ShapeDtypeStruct((NA, R, part), BF),
        [owners, mine],
        [pltpu.SMEM, VMEM],
        [VMEM((NA, R, part), F32)],
    )
    return summed.reshape(NA * R, part)


def spread(sc, pieces, parts, maps, shapes):
    rows, cols = sizes()
    devices = rows * cols
    lead = lead_table(rows, cols)
    arrivals = pltpu.SemaphoreType.DMA((8, len(lead)))
    whole = (devices, NA * R, sum(parts))
    ins, spaces = [sc, *pieces], [pltpu.SMEM] + [pl.ANY] * 8
    if all(p % 128 == 0 for p in parts):
        return call(
            functools.partial(spread_kernel, lead, cols, parts, maps),
            [jax.ShapeDtypeStruct(x, F32) for x in shapes],
            ins,
            spaces,
            [VMEM(whole, BF)]
            + [VMEM(x, F32) for x in shapes]
            + [arrivals, pltpu.SemaphoreType.DMA((len(shapes),))],
            pl.ANY,
            SPREAD,
        )
    whole = call(
        functools.partial(place_kernel, lead, cols),
        jax.ShapeDtypeStruct(whole, BF),
        ins,
        spaces,
        [arrivals],
    )
    found = [[] for _ in shapes]
    base = 0
    for part, spans in zip(parts, maps):
        flat = jnp.swapaxes(whole[:, :, base : base + part], 0, 1).reshape(NA * R, devices * part)
        for out, section, there, start, width in spans:
            found[out].append((section or 0, there, flat[:, start : start + width].astype(F32)))
        base += part
    return [
        (
            jnp.concatenate([x for _, _, x in sorted(f, key=lambda e: e[:2])], axis=1)
            if len(shape) == 2
            else jnp.stack([x.reshape(NA, R, -1) for _, _, x in sorted(f, key=lambda e: e[:2])], 1)
        )
        for f, shape in zip(found, shapes)
    ]


def per_device(
    tokens_in,
    grad_out,
    keep_mask,
    adapter_index,
    ln_gain,
    ln_shift,
    w_qkv,
    bias_qv,
    w_proj,
    w_fc1,
    bias_fc1,
    w_fc2,
    bias_out,
    qkv_down,
    qkv_up,
    proj_down,
    proj_up,
    fc1_down,
    fc1_up,
    fc2_down,
    fc2_up,
):
    rows, cols = sizes()
    row, column = lax.axis_index("row"), lax.axis_index("col")
    assert adapter_index.shape[0] == cols and cols >= 4 and rows >= 2
    hid = D // cols
    n = 4 * hid
    blk = D // rows
    lead = lead_table(rows, cols)

    shard = jax.ShapeDtypeStruct((blk, n), BF)
    rows_in, shard_q = call(
        prep_q_kernel,
        [jax.ShapeDtypeStruct((cols, 2 * SEQ + EXTRA, hid), BF), shard],
        [tokens_in.reshape(cols, SEQ, hid), grad_out.reshape(cols, SEQ, hid), bias_qv]
        + [bias_fc1, w_qkv, w_proj],
        [VMEM] * 6,
        mib=56,
    )
    with jax.named_scope("q_high"):
        own_q, came_q = gather_high(shard_q)
    xa = lax.all_to_all(rows_in, "col", split_axis=0, concat_axis=0, tiled=True)
    adapter = lax.dynamic_index_in_dim(adapter_index, column, 0, keepdims=False)
    sc = jnp.stack([adapter, column, column % 2, row % 2]).astype(jnp.int32)
    up_qkv = jnp.swapaxes(lax.dynamic_index_in_dim(qkv_up, adapter, 0, keepdims=False), 0, 1)
    shard_a, shard_b, keep, closed = call(
        prep_f_kernel,
        [shard] * 2 + [jax.ShapeDtypeStruct((SEQ, 1), F32)] * 2,
        [sc, keep_mask, w_fc1, w_fc2],
        [pltpu.SMEM] + [VMEM] * 3,
    )

    own_q, shard_a, shard_b = after_all(
        (own_q, shard_a, shard_b), xa, keep, closed, sc, up_qkv, *came_q
    )
    with jax.named_scope("q_one"):
        one_q = swap(own_q, flip_one)
    with jax.named_scope("q_two"):
        two_q = swap(own_q, flip_two)
    with jax.named_scope("fa_high"):
        own_a, came_a = gather_high(shard_a)
    own_q, one_q, two_q = after_all((own_q, one_q, two_q), *came_a)
    with jax.named_scope("q_both"):
        both_q = swap(one_q, flip_two)
    with jax.named_scope("q_core"):
        away_q = [swap(p, flip_core) for p in (own_q, one_q, two_q)]
    own_a, shard_b = after_all((own_a, shard_b), *away_q)
    with jax.named_scope("q_core"):
        pieces_q = [own_q, one_q, two_q, both_q] + away_q + [swap(both_q, flip_core)]
    with jax.named_scope("fa_one"):
        one_a = swap(own_a, flip_one)
    with jax.named_scope("fa_two"):
        two_a = swap(own_a, flip_two)
    with jax.named_scope("fb_high"):
        own_b, came_b = gather_high(shard_b)

    def shaped(width, dtype, height=SEQ):
        return jax.ShapeDtypeStruct((height, width), dtype)

    big, small = shaped(D, BF), shaped(R, BF)
    scratch = weight_scratch(rows, cols, n)
    rows_space, bias_space = VMEM((cols, SEQ, hid), BF), VMEM((cols, EXTRA, hid), BF)
    any_space = [pl.ANY] * 8
    n1, lat1, q, k, v, lse, att, lat2, middle, n2, lat3 = call(
        functools.partial(front_kernel, lead, cols),
        [
            big,
            small,
            big,
            big,
            big,
            jax.ShapeDtypeStruct((H // 2, 1, 2 * SEQ), F32),
            big,
            small,
            shaped(D, F32),
            big,
            small,
        ],
        [sc, *pieces_q, xa, closed, ln_gain, ln_shift, qkv_down, up_qkv, proj_down]
        + [proj_up]
        + [fc1_down, bias_out],
        [pltpu.SMEM] + any_space + [pl.ANY] + [VMEM] * 3 + [pl.ANY, VMEM] + [pl.ANY] * 3 + [VMEM],
        scratch
        + [VMEM((SEQ, D), F32), VMEM((SEQ, D), F32), rows_space, bias_space]
        + [VMEM((R, D), BF)] * 4
        + [pltpu.SemaphoreType.DMA((6,))],
        mib=FRONT,
    )
    own_a, one_a, two_a = after_all((own_a, one_a, two_a), n1, *came_b)
    bits = list(reversed(range(bits_of(rows))))
    owners = after(adapter_index, n1)
    for bit in bits[:-1]:
        owners = owner_stack(owner_parts(owners, bit), bit)
    with jax.named_scope("fa_both"):
        both_a = swap(one_a, flip_two)
    with jax.named_scope("fa_core"):
        away_a = [swap(p, flip_core) for p in (own_a, one_a, two_a)]
    own_b, owners = after_all((own_b, owners), *away_a)
    owners = owner_parts(owners, 0)
    with jax.named_scope("fa_core"):
        pieces_a = [own_a, one_a, two_a, both_a] + away_a + [swap(both_a, flip_core)]
    with jax.named_scope("fb_one"):
        one_b = swap(own_b, flip_one)
    with jax.named_scope("fb_two"):
        two_b = swap(own_b, flip_two)
    wide = shaped(D, F32)
    thin = shaped(R, F32)
    res, gn2, lat4, glat3, gr, early_a = call(
        functools.partial(ffn_a_kernel, lead, cols),
        [wide, wide, thin, thin, big, jax.ShapeDtypeStruct((rows * cols, R, FF // (rows * cols)), BF)],
        [sc, *pieces_a, xa, keep, n2, lat3, fc1_up, fc2_down, fc2_up],
        [pltpu.SMEM] + any_space + [pl.ANY] + [VMEM] * 3 + [pl.ANY] * 3,
        scratch
        + [rows_space, bias_space, VMEM((R, FF), BF), VMEM((R, FF), BF), VMEM((R, D), BF)]
        + [pltpu.SemaphoreType.DMA((5,))],
        mib=FFN_A,
    )
    own_b, one_b, two_b, *owners = after_all((own_b, one_b, two_b, *owners), res)
    owners = owner_stack(owners, 0).transpose(tuple(bits) + (len(bits),)).reshape(-1)
    with jax.named_scope("fb_both"):
        both_b = swap(one_b, flip_two)
    with jax.named_scope("fb_core"):
        away_b = [swap(p, flip_core) for p in (own_b, one_b, two_b)]
        pieces_b = [own_b, one_b, two_b, both_b] + away_b + [swap(after(both_b, owners), flip_core)]
    *layer, gatt, gmid, grads_b = call(
        functools.partial(ffn_b_kernel, lead, cols),
        [shaped(hid, BF)] * cols + [big, wide]
        + [jax.ShapeDtypeStruct((rows * cols, R, 12 * D // (rows * cols)), BF)],
        [sc, *pieces_b, *pieces_q, xa, keep, ln_gain, n2, lat3, fc1_up, fc2_down, fc2_up]
        + [fc1_down, proj_down, proj_up, bias_out]
        + [middle, att, lat2, gr, res, gn2, lat4, glat3, early_a],
        [pltpu.SMEM]
        + any_space * 2
        + [pl.ANY, VMEM, VMEM, VMEM, VMEM]
        + [pl.ANY] * 6
        + [VMEM, pl.ANY, pl.ANY, VMEM, VMEM, pl.ANY, pl.ANY, VMEM, VMEM, pl.ANY],
        scratch
        + [VMEM((cols, D, hid), BF), scratch[1]]
        + [VMEM((SEQ, D), F32), VMEM((SEQ, D), F32), VMEM((SEQ, R), F32), VMEM((SEQ, R), F32)]
        + [bias_space, VMEM((R, FF), BF), VMEM((R, FF), BF)]
        + [VMEM((R, D), BF)] * 4
        + [VMEM((SEQ, D), F32), VMEM((SEQ, D), BF), VMEM((SEQ, D), F32), VMEM((SEQ, D), F32)]
        + [VMEM(early_a.shape, BF), pltpu.SemaphoreType.DMA((12,)), VMEM((SEQ, D), BF)],
        mib=FFN_B,
    )
    with jax.named_scope("grads_b_send"):
        mine_b = send_grads(grads_b)
    with jax.named_scope("layer_out"):
        layer = exchange_rows(layer)
    gq, gk, gv, glat1, late = call(
        functools.partial(attention_back_kernel, cols),
        [big, big, big, small, jax.ShapeDtypeStruct((rows * cols, R, 4 * D // (rows * cols)), BF)],
        [sc, closed, q, k, v, lse, gatt, lat1, n1, up_qkv],
        [pltpu.SMEM] + [VMEM] * 9,
        mib=ATT,
    )
    with jax.named_scope("grads_c_send"):
        mine_c = send_grads(late)
    with jax.named_scope("grads_b"):
        own_b, _ = gather_high(
            after(sum_grads(after(mine_b, late), owners, mine_b.shape[2]), *layer), 1
        )
        own_c, _ = gather_high(sum_grads(mine_c, owners, mine_c.shape[2]))
        order_b = tuple(lead.index(place) for place in lead_table(rows, cols, 1))
        own = lane_join([own_b, own_c], [order_b, tuple(range(len(lead)))])
    gmid = after(gmid, own)
    sent = call(
        functools.partial(back_kernel, lead, cols),
        [shaped(hid, BF)] * cols,
        [sc, *pieces_q, xa, ln_gain, gq, gk, gv, glat1, qkv_down, gmid],
        [pltpu.SMEM] + any_space + [pl.ANY] + [VMEM] * 5 + [pl.ANY] * 2,
        scratch
        + [VMEM((SEQ, D), F32), rows_space, VMEM((R, D), BF), VMEM((SEQ, D), F32)]
        + [pltpu.SemaphoreType.DMA((3,)), VMEM((SEQ, D), BF)],
        mib=BACK,
    )
    with jax.named_scope("grads"):
        one, two = swap(own, flip_one), swap(own, flip_two)
        own, one, two = after_all((own, one, two), *sent)
        layer_out = stacked(after_all(layer, one, two), column, pl.ANY)
        both = swap(one, flip_two)
        away = [swap(p, flip_core) for p in (own, one, two)]
        both = after(both, layer_out)
        pieces = [own, one, two, both] + away + [swap(both, flip_core)]
        half = FF // cols // 2
        map_a, map_b = (
            tuple(
                (out, None, (2 * block + part) * half, base + block * half, half)
                for out, base in ((0, 0), (1, FF // 2))
                for block in range(cols)
            )
            for part in (0, 1)
        )
        map_b = map_b + tuple((2 + i, None, 0, FF + i * D, D) for i in range(4))
        map_c = ((6, None, 0, 0, D),) + tuple((7, c, 0, (c + 1) * D, D) for c in range(3))
        parts = [early_a.shape[-1], mine_b.shape[-1] - early_a.shape[-1], mine_c.shape[-1]]
        shapes = [(NA * R, FF)] * 2 + [(NA * R, D)] * 5 + [(NA, 3, R, D)]
        sums = spread(sc, pieces, parts, [map_a, map_b, map_c], shapes)

    with jax.named_scope("rows_out"):
        grad_rows = exchange_rows(after_all(sent, *away))
        grad_in = stacked(after_all(grad_rows, sums[0]), column, pl.ANY)

    def split(table):
        return table.reshape((NA, R) + table.shape[1:])

    g_fc1_up, g_fc2_down, g_proj_down, g_proj_up, g_fc1_down, g_fc2_up = map(split, sums[:6])
    return (
        layer_out.reshape(cols * SEQ, hid),
        grad_in.reshape(cols * SEQ, hid),
        split(sums[6]),
        jnp.swapaxes(sums[7], 1, 2),
        g_proj_down,
        g_proj_up,
        g_fc1_down,
        g_fc1_up,
        g_fc2_down,
        g_fc2_up,
    )


def solution(mesh):
    return jax.shard_map(
        per_device,
        mesh=mesh,
        in_specs=(
            P("row", "col"),
            P("row", "col"),
            P("row", None),
            P("row"),
            P(),
            P(),
            P(None, "row", "col"),
            P(None, "col"),
            P("col", "row"),
            P("row", "col"),
            P("col"),
            P("col", "row"),
            P(),
            P(),
            P(),
            P(),
            P(),
            P(),
            P(),
            P(),
            P(),
        ),
        out_specs=(P("row", "col"), P("row", "col"), P(), P(), P(), P(), P(), P(), P(), P()),
        check_vma=False,
    )
```

```python
import functools

import jax
import jax.numpy as jnp
from jax import lax
from jax.experimental import pallas as pl
from jax.experimental.pallas import tpu as pltpu
from jax.sharding import PartitionSpec as P

D = 1024
H = 16
HD = 64
FF = 4096
BUF = 64
R = 16
NA = 8
SEQ = 320
PAIR = 2 * HD
EXTRA = 16
SPREAD = 56
FRONT, FFN_A, FFN_B, ATT, BACK = 56, 56, 56, 56, 56
BF = jnp.bfloat16
F32 = jnp.float32
BOTH = ("row", "col")
VMEM = pltpu.VMEM
NN = (((1,), (0,)), ((), ()))
NT = (((1,), (1,)), ((), ()))


def mm(left, right, dims=NN):
    return lax.dot_general(left, right, dims, preferred_element_type=F32)


def low(values):
    return values.astype(BF)


def norm_parts(values):
    row_mean = jnp.mean(values, axis=-1, keepdims=True)
    centered = values - row_mean
    variance = jnp.mean(centered * centered, axis=-1, keepdims=True)
    inverse = lax.rsqrt(variance + 1e-06)
    return (centered * inverse, inverse)


def norm_back(grad_normed, gain_row, unit_rows, inverse):
    scaled = grad_normed * gain_row
    first_mean = jnp.mean(scaled, axis=-1, keepdims=True)
    second_mean = jnp.mean(scaled * unit_rows, axis=-1, keepdims=True)
    return inverse * (scaled - first_mean - unit_rows * second_mean)


def call(kernel, outs, ins, spaces, scratch=(), out_space=VMEM, mib=4):
    return pl.pallas_call(
        kernel,
        out_shape=outs,
        in_specs=[pl.BlockSpec(memory_space=s) for s in spaces],
        out_specs=jax.tree.map(lambda _: pl.BlockSpec(memory_space=out_space), outs),
        scratch_shapes=list(scratch),
        compiler_params=pltpu.CompilerParams(vmem_limit_bytes=mib << 20),
        cost_estimate=pl.CostEstimate(flops=0, bytes_accessed=0, transcendentals=0),
    )(*ins)


def sizes():
    return lax.axis_size("row"), lax.axis_size("col")


def swap(block, flip):
    rows, cols = sizes()
    pairs = []
    for i in range(rows * cols):
        row, col = flip(i // cols, i % cols)
        pairs.append((i, row * cols + col))
    return lax.ppermute(block, BOTH, pairs)


def bits_of(size):
    return size.bit_length() - 1


def stack_kernel(which, *refs):
    parts, out, sems = refs[:-2], refs[-2], refs[-1]
    copies = [
        pltpu.make_async_copy(ref, out.at[which[0] ^ m], sems.at[m]) for m, ref in enumerate(parts)
    ]
    for copy in copies:
        copy.start()
    for copy in copies:
        copy.wait()


def stacked(parts, index, out_space=VMEM):
    shape = parts[0].shape
    flat = [p.reshape((-1, shape[-1])) for p in parts]
    out = jax.ShapeDtypeStruct((len(parts),) + flat[0].shape, flat[0].dtype)
    made = call(
        stack_kernel,
        out,
        [index.reshape(1).astype(jnp.int32)] + flat,
        [pltpu.SMEM] + [pl.ANY] * len(parts),
        [pltpu.SemaphoreType.DMA((len(parts),))],
        out_space,
    )
    return made.reshape((len(parts),) + shape)


def group_join(block, axis, low_bit, width):
    parts = [block]
    for m in range(1, 1 << width):
        step = m << low_bit
        if axis == "row":
            parts.append(swap(block, lambda r, c: (r ^ step, c)))
        else:
            parts.append(swap(block, lambda r, c: (r, c ^ step)))
    index = (lax.axis_index(axis) >> low_bit) & ((1 << width) - 1)
    return stacked(parts, index), parts


def groups(top, bottom, most):
    out = []
    while top > bottom:
        width = min(most, top - bottom)
        out.append((top - width, width))
        top -= width
    return out


def early_groups(rows, cols, most):
    return [("row",) + g for g in groups(bits_of(rows), 1, most)] + [
        ("col",) + g for g in groups(bits_of(cols), 2, most)
    ]


def lead_table(rows, cols, most=2):
    table = [(0, 0)]
    for axis, bit, width in early_groups(rows, cols, most):
        shift = bit - (1 if axis == "row" else 2)
        new = []
        for value in range(1 << width):
            for high_col, high_row in table:
                if axis == "row":
                    new.append((high_col, high_row + (value << shift)))
                else:
                    new.append((high_col + (value << shift), high_row))
        table = new
    return table


def after(value, *others):
    return lax.optimization_barrier((value,) + others)[0]


def after_all(values, *others):
    return lax.optimization_barrier(tuple(values) + others)[: len(values)]


def exchange_rows(parts):
    came = [parts[0]]
    for j in range(1, len(parts)):
        came.append(swap(parts[j], lambda r, c: (r, c ^ j)))
    return came


def gather_high(shard, most=2):
    rows, cols = sizes()
    block, parts = shard, []
    for axis, bit, width in early_groups(rows, cols, most):
        block, parts = group_join(block, axis, bit, width)
    return block.reshape((-1,) + shard.shape), parts[1:]


def lane_join_kernel(orders, *refs):
    parts, out, sems = refs[:-2], refs[-2], refs[-1]
    copies, lane = [], 0
    for i, (part, order) in enumerate(zip(parts, orders)):
        width = part.shape[-1]
        for n, put_at in enumerate(order):
            target = out.at[put_at, :, lane : lane + width]
            copies.append(pltpu.make_async_copy(part.at[n], target, sems.at[i, n]))
        lane += width
    for copy in copies:
        copy.start()
    for copy in copies:
        copy.wait()


def lane_join(parts, orders):
    if any(p.shape[-1] % 128 for p in parts):
        placed = [p[jnp.array(sorted(range(len(o)), key=o.index))] for p, o in zip(parts, orders)]
        return jnp.concatenate(placed, axis=-1)
    shape = parts[0].shape[:-1] + (sum(p.shape[-1] for p in parts),)
    return call(
        functools.partial(lane_join_kernel, orders),
        jax.ShapeDtypeStruct(shape, parts[0].dtype),
        parts,
        [pl.ANY] * len(parts),
        [pltpu.SemaphoreType.DMA((len(parts), shape[0]))],
    )


def flip_one(r, c):
    return (r, c ^ 2) if c % 2 == 0 else (r ^ 1, c)


def flip_two(r, c):
    return (r ^ 1, c) if c % 2 == 0 else (r, c ^ 2)


def flip_core(r, c):
    return (r, c ^ 1)


def with_cores(pieces):
    return pieces + [swap(p, flip_core) for p in pieces]


def owner_parts(block, bit):
    step = 1 << bit
    return [block, swap(block, lambda r, c: (r ^ step, c))]


def owner_stack(parts, bit):
    return jnp.stack(parts)[jnp.arange(2) ^ ((lax.axis_index("row") >> bit) & 1)]


def piece_place(sc, k):
    kind, away = k % 4, k // 4
    turn = (sc[2] + away) & 1
    return (0, 1 - turn, turn, 1)[kind], (0, turn, 1 - turn, 1)[kind], away


class Weights:
    def __init__(self, sc, pieces, w, sems, lead, first_lane=0):
        self.copies = []
        depth = pieces[0].shape[1]
        taken = pl.ds(first_lane, w.shape[2])
        for k, piece in enumerate(pieces):
            x_rel, y_rel, away = piece_place(sc, k)
            for n, (high_col, high_row) in enumerate(lead):
                slot = high_col * 4 + x_rel * 2 + away
                row = (high_row * 2 + ((sc[3] + y_rel) & 1)) * depth
                self.copies.append(
                    pltpu.make_async_copy(
                        piece.at[n, :, taken],
                        w.at[slot, pl.ds(pl.multiple_of(row, depth), depth), :],
                        sems.at[k, n],
                    )
                )

    def start(self):
        for copy in self.copies:
            copy.start()

    def wait(self, away=None):
        half = len(self.copies) // 2
        for copy in self.copies if away is None else self.copies[away * half : (away + 1) * half]:
            copy.wait()

    def slot(self, i, cols):
        half = cols // 2

        @pl.when(i == 0)
        def _():
            self.wait(0)

        @pl.when(i == half)
        def _():
            self.wait(1)

        return lax.rem(i, half) * 2 + i // half


def column_of(sc, slot):
    return (slot // 4) * 4 + ((sc[1] & 3) ^ (slot & 3))


def weight_scratch(rows, cols, n):
    lead = len(lead_table(rows, cols))
    return [VMEM((cols, D, n), BF), pltpu.SemaphoreType.DMA((8, lead))]


def put(ref, start, value, lane=0):
    part = ref.shape[-1] - lane
    for i in range(value.shape[-1] // part):
        ref[start // part + i, :, lane:] = value[:, i * part : (i + 1) * part]


def lanes(start, width):
    return pl.ds(pl.multiple_of(start, width), width)


def prep_q_kernel(tokens, grads, bias_qv, bias_f, wq, wp, rows, out):
    hid = wq.shape[2]
    seq = tokens.shape[1]
    for c in range(tokens.shape[0]):
        rows[c, :seq] = tokens[c]
        rows[c, seq : 2 * seq] = grads[c]
        rows[c, 2 * seq : 2 * seq + 2] = bias_qv[...]
        for i in range(4):
            rows[c, 2 * seq + 2 + i, :] = bias_f[pl.ds(i * hid, hid)]
    for c in range(3):
        out[:, c * hid : (c + 1) * hid] = wq[c]
    out[:, 3 * hid :] = low(wp[...].astype(F32).T)


def prep_f_kernel(sc, mask, w1, w2, out_a, out_b, keep, closed):
    row = mask[pl.ds(sc[1], 1), :].astype(F32)
    row = jnp.concatenate([jnp.ones((1, BUF), F32), row], axis=1)
    column = jnp.broadcast_to(row, (8, SEQ)).T[:, :1]
    keep[...] = column
    closed[...] = 1.0 - column
    half = w1.shape[1] // 2
    out_a[:, :half] = w1[:, :half]
    out_b[:, :half] = w1[:, half:]
    out_a[:, half:] = low(w2[:half].astype(F32).T)
    out_b[:, half:] = low(w2[half:].astype(F32).T)


def fetch(sems, *pairs):
    copies = [pltpu.make_async_copy(src, dst, sems.at[i]) for i, (src, dst) in enumerate(pairs)]
    for copy in copies:
        copy.start()
    return copies


def to_columns(sc, made, buffer, outs):
    hid = outs[0].shape[-1]
    buffer[...] = made
    for j, out in enumerate(outs):
        out[...] = buffer[:, lanes((sc[1] ^ j) * hid, hid)]


def rows_at(xa, start, height):
    return xa.at[:, pl.ds(start, height), :]


def across(ref, cols):
    return jnp.concatenate([ref[c] for c in range(cols)], axis=1).astype(F32)


def both_heads(pair):
    left = lax.broadcasted_iota(jnp.int32, (1, PAIR), 1) < HD
    zero = jnp.zeros_like(pair)
    return jnp.concatenate([jnp.where(left, pair, zero), jnp.where(left, zero, pair)], axis=0)


def own_heads(made, scale=1.0):
    both = jnp.concatenate([made[:HD, :SEQ], made[HD:, SEQ:]], axis=0)
    return low(both.T * scale)


def front_kernel(lead, cols, *refs):
    sc = refs[0]
    pieces = refs[1:9]
    (xa, closed, gain, shift, q_down, q_up, p_down, p_up, f_down, bias_out) = refs[9:19]
    (n1, lat1, q, k, v, lse, att, lat2, middle, n2, lat3) = refs[19:30]
    w, sems, hidden, branch, xs, bs, row_qd, row_pd, row_pu, row_fd, sems_f = refs[30:]
    a = sc[0]
    hid = D // cols
    first = fetch(
        sems_f,
        (rows_at(xa, 0, SEQ), xs),
        (q_down.at[a], row_qd),
        (rows_at(xa, 2 * SEQ, EXTRA), bs),
        (p_down.at[a], row_pd),
        (p_up.at[a], row_pu),
        (f_down.at[a], row_fd),
    )
    weights = Weights(sc, pieces, w, sems, lead)
    weights.start()
    first[0].wait()
    x = across(xs, cols)
    hidden[...] = x
    unit, _ = norm_parts(x)
    n1[...] = low(unit * gain[0:1] + shift[0:1])
    for copy in first[1:]:
        copy.wait()
    lat1[...] = low(mm(n1[...], row_qd[...], NT))

    def project(i, _):
        slot = weights.slot(i, cols)
        block = column_of(sc, slot)
        up = jnp.concatenate([q_up[c, :, lanes(block * hid, hid)] for c in range(3)], axis=1)
        made = mm(n1[...], w[slot, :, : 3 * hid]) + mm(lat1[...], up)
        bias_q = bs[block, 0:1, :].astype(F32)
        bias_v = bs[block, 1:2, :].astype(F32)
        at = lanes(slot * hid, hid)
        q[:, at] = low(made[:, :hid] + bias_q) * jnp.asarray(0.125, BF)
        k[:, at] = low(made[:, hid : 2 * hid])
        v[:, at] = low(made[:, 2 * hid :] + bias_v)
        return 0

    lax.fori_loop(0, cols, project, 0)
    shut = closed[...] > 0.5

    def attend(pair, _):
        at = lanes(pair * PAIR, PAIR)
        v_t = low(v[:, at].astype(F32).T)
        s = jnp.where(shut, -1e30, mm(k[:, at], both_heads(q[:, at]), NT))
        top = jnp.max(s, axis=0, keepdims=True)
        e = jnp.exp(s - top)
        total = jnp.sum(e, axis=0, keepdims=True)
        lse[pair] = top + jnp.log(total)
        att[:, at] = own_heads(mm(v_t, low(e * (1.0 / total))))
        return 0

    lax.fori_loop(0, H // 2, attend, 0, unroll=4)

    def down_two(slot, acc):
        block = column_of(sc, slot)
        return acc + mm(att[:, lanes(slot * hid, hid)], row_pd[:, lanes(block * hid, hid)], NT)

    lat2[...] = low(lax.fori_loop(0, cols, down_two, jnp.zeros((SEQ, R), F32)))
    branch[...] = mm(lat2[...], row_pu[...]) + bias_out[0:1].astype(F32)

    def out_proj(slot, _):
        branch[...] += mm(att[:, lanes(slot * hid, hid)], w[slot, :, 3 * hid :], NT)
        return 0

    lax.fori_loop(0, cols, out_proj, 0)
    mid = hidden[...] + branch[...]
    middle[...] = mid
    unit, _ = norm_parts(mid)
    n2[...] = low(unit * gain[1:2] + shift[1:2])
    lat3[...] = low(mm(n2[...], row_fd[...], NT))


def ffn_steps(weights, sc, part, cols, w, bs, n2, lat3, gr, glat4, up_1, down_2, acc, early, lane=0):
    res, gn2, lat4, glat3 = acc
    hid = D // cols
    ffn = FF // cols
    half = ffn // 2
    glat4_t = low(glat4.astype(F32).T)
    lat3_t = low(lat3[...].astype(F32).T)

    def step(i, _):
        slot = weights.slot(i, cols)
        block = column_of(sc, slot)
        at = pl.ds(pl.multiple_of(block * ffn + part * half, half), half)
        bias = jnp.concatenate(
            [bs[block, 2 + 2 * part + i : 3 + 2 * part + i, :] for i in range(2)], axis=1
        ).astype(F32)
        up, down = up_1[:, at], down_2[:, at]
        w1, w2 = w[slot, :, :half], w[slot, :, half:]
        pre = mm(n2[...], w1) + mm(lat3[...], up) + bias
        back = mm(gr[...], w2) + mm(glat4, down)
        cumulative = 0.5 * (1.0 + lax.erf(pre * 0.7071067811865476))
        activated = low(pre * cumulative)
        slope = cumulative + pre * jnp.exp(-0.5 * pre * pre) * 0.3989422804014327
        grad_pre = low(back * slope)
        lat4[...] += mm(activated, down, NT)
        glat3[...] += mm(grad_pre, up, NT)
        res[...] += mm(activated, w2, NT)
        gn2[...] += mm(grad_pre, w1, NT)
        put(early, block * half, low(mm(lat3_t, grad_pre)), lane)
        put(early, FF // 2 + block * half, low(mm(glat4_t, activated)), lane)
        return 0

    lax.fori_loop(0, cols, step, 0, unroll=2)


def ffn_a_kernel(lead, cols, *refs):
    sc = refs[0]
    pieces = refs[1:9]
    xa, keep, n2, lat3, up_1, down_2, up_2 = refs[9:16]
    res, gn2, lat4, glat3, gr, early = refs[16:22]
    w, sems, gs, bs, row_u1, row_d2, row_u2, sems_f = refs[22:]
    a = sc[0]
    first = fetch(
        sems_f,
        (rows_at(xa, SEQ, SEQ), gs),
        (up_2.at[a], row_u2),
        (rows_at(xa, 2 * SEQ, EXTRA), bs),
        (up_1.at[a], row_u1),
        (down_2.at[a], row_d2),
    )
    weights = Weights(sc, pieces, w, sems, lead)
    weights.start()
    first[0].wait()
    gr[...] = low(across(gs, cols) * keep[...])
    for copy in first[1:]:
        copy.wait()
    glat4 = low(mm(gr[...], row_u2[...], NT))
    res[...] = jnp.zeros_like(res)
    gn2[...] = jnp.zeros_like(gn2)
    lat4[...] = jnp.zeros_like(lat4)
    glat3[...] = jnp.zeros_like(glat3)
    ffn_steps(
        weights, sc, 0, cols, w, bs, n2, lat3, gr, glat4, row_u1, row_d2, (res, gn2, lat4, glat3), early
    )


def ffn_b_kernel(lead, cols, *refs):
    sc = refs[0]
    pieces = refs[1:9]
    own_q = refs[9:17]
    (xa, keep, gain, n2, lat3, up_1, down_2, up_2, f_down, p_down, p_up, bias_out) = refs[17:29]
    (middle, att, lat2, gr, res_in, gn2_in, lat4_in, glat3_in, early_in) = refs[29:38]
    layer, refs = refs[38 : 38 + cols], refs[:38] + refs[38 + cols :]
    gatt, gmid, early = refs[38:41]
    refs = refs[:41] + (None,) + refs[41:]
    w, sems, wp, sems_p, res, gn2, lat4, glat3 = refs[42:50]
    bs, row_u1, row_d2, row_u2, row_fd, row_pd, row_pu, mid_s, att_s, res_s, gn2_s, early_s = refs[50:62]
    sems_f, out_s = refs[62:]
    lane = early_in.shape[-1]
    a = sc[0]
    first = fetch(
        sems_f,
        (up_2.at[a], row_u2),
        (rows_at(xa, 2 * SEQ, EXTRA), bs),
        (up_1.at[a], row_u1),
        (down_2.at[a], row_d2),
    )
    weights = Weights(sc, pieces, w, sems, lead)
    weights.start()
    proj = Weights(sc, own_q, wp, sems_p, lead, 3 * D // cols)
    last = fetch(
        sems_f.at[pl.ds(4, 8)],
        (res_in, res_s),
        (middle, mid_s),
        (gn2_in, gn2_s),
        (f_down.at[a], row_fd),
        (p_up.at[a], row_pu),
        (p_down.at[a], row_pd),
        (att, att_s),
        (early_in, early_s),
    )
    proj.start()
    hid = D // cols
    for copy in first:
        copy.wait()
    glat4 = low(mm(gr[...], row_u2[...], NT))
    res[...] = jnp.zeros_like(res)
    gn2[...] = jnp.zeros_like(gn2)
    lat4[...] = lat4_in[...]
    glat3[...] = glat3_in[...]
    ffn_steps(
        weights, sc, 1, cols, w, bs, n2, lat3, gr, glat4, row_u1, row_d2, (res, gn2, lat4, glat3), early, lane
    )
    for copy in last:
        copy.wait()
    early[:, :, :lane] = early_s[...]
    mid = mid_s[...]
    lat4_low = low(lat4[...])
    out = low(
        keep[...]
        * (mid + (res_s[...] + res[...]) + mm(lat4_low, row_u2[...]) + bias_out[1:2].astype(F32))
    )
    to_columns(sc, out, out_s, layer)
    glat3_low = low(glat3[...])
    grad_normed = gn2_s[...] + gn2[...] + mm(glat3_low, row_fd[...])
    unit, inverse = norm_parts(mid)
    grad_middle = gr[...].astype(F32) + norm_back(grad_normed, gain[1:2], unit, inverse)
    gmid[...] = grad_middle
    gb = low(grad_middle)
    glat2 = low(mm(gb, row_pu[...], NT))
    glat2_t = low(glat2.astype(F32).T)
    put(early, FF + D, low(mm(low(lat2[...].astype(F32).T), gb)), lane)
    put(early, FF + 2 * D, low(mm(low(glat3_low.astype(F32).T), n2[...])), lane)
    put(early, FF + 3 * D, low(mm(low(lat4_low.astype(F32).T), gr[...])), lane)
    proj.wait()

    def step(slot, _):
        block = column_of(sc, slot)
        here = lanes(slot * hid, hid)
        there = lanes(block * hid, hid)
        gatt[:, here] = low(mm(gb, wp[slot]) + mm(glat2, row_pd[:, there]))
        put(early, FF + block * hid, low(mm(glat2_t, att_s[:, here])), lane)
        return 0

    for slot in range(cols):
        step(slot, 0)


def attention_back_kernel(cols, *refs):
    sc = refs[0]
    closed, q, k, v, lse, gatt, lat1, n1, q_up = refs[1:10]
    gq, gk, gv, glat1, late = refs[10:15]
    a = sc[0]
    hid = D // cols
    shut = closed[...] > 0.5

    def attend(pair, _):
        at = lanes(pair * PAIR, PAIR)
        kp = k[:, at]
        k_t = low(kp.astype(F32).T)
        q_both, g_both = both_heads(q[:, at]), both_heads(gatt[:, at])
        s = jnp.where(shut, -1e30, mm(kp, q_both, NT))
        soft = jnp.exp(s - lse[pair])
        grad_soft = mm(v[:, at], g_both, NT)
        total = jnp.sum(grad_soft * soft, axis=0, keepdims=True)
        grad_scores = low(soft * (grad_soft - total))
        gq[:, at] = own_heads(mm(k_t, grad_scores), 0.125)
        gk[:, at] = low(mm(grad_scores, q_both))
        gv[:, at] = low(mm(low(soft), g_both))
        return 0

    lax.fori_loop(0, H // 2, attend, 0, unroll=8)
    lat1_t = low(lat1[...].astype(F32).T)

    def step(slot, acc):
        block = column_of(sc, slot)
        here = lanes(slot * hid, hid)
        there = lanes(block * hid, hid)
        for c, g in enumerate((gq, gk, gv)):
            grad = g[:, here]
            acc = acc + mm(grad, q_up[c, :, there], NT)
            put(late, (c + 1) * D + block * hid, low(mm(lat1_t, grad)))
        return acc

    made = jnp.zeros((SEQ, R), F32)
    for slot in range(cols):
        made = step(slot, made)
    made = low(made)
    glat1[...] = made
    put(late, 0, low(mm(low(made.astype(F32).T), n1[...])))


def back_kernel(lead, cols, *refs):
    sc = refs[0]
    pieces = refs[1:9]
    xa, gain, gq, gk, gv, glat1, q_down, gmid = refs[9:17]
    outs = refs[17 : 17 + cols]
    w, sems, acc, xs, row_qd, gmid_s, sems_f, out_s = refs[17 + cols :]
    first = fetch(
        sems_f,
        (rows_at(xa, 0, SEQ), xs),
        (q_down.at[sc[0]], row_qd),
        (gmid, gmid_s),
    )
    weights = Weights(sc, pieces, w, sems, lead)
    weights.start()
    hid = D // cols
    for copy in first:
        copy.wait()
    acc[...] = mm(glat1[...], row_qd[...])
    x = across(xs, cols)
    unit, inverse = norm_parts(x)

    def step(i, _):
        slot = weights.slot(i, cols)
        here = lanes(slot * hid, hid)
        grad = jnp.concatenate([gq[:, here], gk[:, here], gv[:, here]], axis=1)
        acc[...] += mm(grad, w[slot, :, : 3 * hid], NT)
        return 0

    lax.fori_loop(0, cols, step, 0)
    made = low(gmid_s[...] + norm_back(acc[...], gain[0:1], unit, inverse))
    to_columns(sc, made, out_s, outs)


def sum_kernel(owners, mine, out, acc):
    acc[...] = jnp.zeros_like(acc)
    for d in range(mine.shape[0]):
        acc[owners[d]] += mine[d, :, : acc.shape[2]].astype(F32)
    out[...] = low(acc[...])


def spread_kernel(lead, cols, parts, maps, *refs):
    sc, pieces = refs[0], refs[1:9]
    count = (len(refs) - 11) // 2
    outs, whole, made = refs[9 : 9 + count], refs[9 + count], refs[10 + count : 10 + 2 * count]
    sems_in, sems_out = refs[10 + 2 * count :]
    copies = []
    for k, piece in enumerate(pieces):
        x_rel, y_rel, away = piece_place(sc, k)
        for n, (high_col, high_row) in enumerate(lead):
            row = high_row * 2 + ((sc[3] + y_rel) & 1)
            col = high_col * 4 + ((sc[1] & 3) ^ (x_rel * 2 + away))
            copies.append(
                pltpu.make_async_copy(piece.at[n], whole.at[row * cols + col], sems_in.at[k, n])
            )
    for copy in copies:
        copy.start()
    for copy in copies:
        copy.wait()
    found = [[] for _ in outs]
    base = 0
    for part, spans in zip(parts, maps):
        for out, section, there, start, width in spans:
            for lane in range(0, width, 128):
                at = start + lane
                found[out].append((section, there + lane, at // part, base + at % part))
        base += part
    leaving = []
    for i, (out, buffer) in enumerate(zip(outs, made)):
        for section, there, device, here in found[i]:
            block = whole[device, :, here : here + 128].astype(F32)
            if section is None:
                buffer[:, there : there + 128] = block
            else:
                buffer[:, section, :, there : there + 128] = block.reshape(NA, R, 128)
        leaving.append(pltpu.make_async_copy(buffer, out, sems_out.at[i]))
        leaving[-1].start()
    for copy in leaving:
        copy.wait()


def place_kernel(lead, cols, *refs):
    sc, pieces, out, sems = refs[0], refs[1:9], refs[9], refs[10]
    copies = []
    for k, piece in enumerate(pieces):
        x_rel, y_rel, away = piece_place(sc, k)
        for n, (high_col, high_row) in enumerate(lead):
            row = high_row * 2 + ((sc[3] + y_rel) & 1)
            col = high_col * 4 + ((sc[1] & 3) ^ (x_rel * 2 + away))
            copies.append(pltpu.make_async_copy(piece.at[n], out.at[row * cols + col], sems.at[k, n]))
    for copy in copies:
        copy.start()
    for copy in copies:
        copy.wait()


def send_grads(grads):
    return lax.all_to_all(grads, BOTH, split_axis=0, concat_axis=0, tiled=True)


def sum_grads(mine, owners, part):
    summed = call(
        sum_kernel,
        jax.ShapeDtypeStruct((NA, R, part), BF),
        [owners, mine],
        [pltpu.SMEM, VMEM],
        [VMEM((NA, R, part), F32)],
    )
    return summed.reshape(NA * R, part)


def spread(sc, pieces, parts, maps, shapes):
    rows, cols = sizes()
    devices = rows * cols
    lead = lead_table(rows, cols)
    arrivals = pltpu.SemaphoreType.DMA((8, len(lead)))
    whole = (devices, NA * R, sum(parts))
    ins, spaces = [sc, *pieces], [pltpu.SMEM] + [pl.ANY] * 8
    if all(p % 128 == 0 for p in parts):
        return call(
            functools.partial(spread_kernel, lead, cols, parts, maps),
            [jax.ShapeDtypeStruct(x, F32) for x in shapes],
            ins,
            spaces,
            [VMEM(whole, BF)]
            + [VMEM(x, F32) for x in shapes]
            + [arrivals, pltpu.SemaphoreType.DMA((len(shapes),))],
            pl.ANY,
            SPREAD,
        )
    whole = call(
        functools.partial(place_kernel, lead, cols),
        jax.ShapeDtypeStruct(whole, BF),
        ins,
        spaces,
        [arrivals],
    )
    found = [[] for _ in shapes]
    base = 0
    for part, spans in zip(parts, maps):
        flat = jnp.swapaxes(whole[:, :, base : base + part], 0, 1).reshape(NA * R, devices * part)
        for out, section, there, start, width in spans:
            found[out].append((section or 0, there, flat[:, start : start + width].astype(F32)))
        base += part
    return [
        (
            jnp.concatenate([x for _, _, x in sorted(f, key=lambda e: e[:2])], axis=1)
            if len(shape) == 2
            else jnp.stack([x.reshape(NA, R, -1) for _, _, x in sorted(f, key=lambda e: e[:2])], 1)
        )
        for f, shape in zip(found, shapes)
    ]


def per_device(
    tokens_in,
    grad_out,
    keep_mask,
    adapter_index,
    ln_gain,
    ln_shift,
    w_qkv,
    bias_qv,
    w_proj,
    w_fc1,
    bias_fc1,
    w_fc2,
    bias_out,
    qkv_down,
    qkv_up,
    proj_down,
    proj_up,
    fc1_down,
    fc1_up,
    fc2_down,
    fc2_up,
):
    rows, cols = sizes()
    row, column = lax.axis_index("row"), lax.axis_index("col")
    assert adapter_index.shape[0] == cols and cols >= 4 and rows >= 2
    hid = D // cols
    n = 4 * hid
    blk = D // rows
    lead = lead_table(rows, cols)

    shard = jax.ShapeDtypeStruct((blk, n), BF)
    rows_in, shard_q = call(
        prep_q_kernel,
        [jax.ShapeDtypeStruct((cols, 2 * SEQ + EXTRA, hid), BF), shard],
        [tokens_in.reshape(cols, SEQ, hid), grad_out.reshape(cols, SEQ, hid), bias_qv]
        + [bias_fc1, w_qkv, w_proj],
        [VMEM] * 6,
        mib=56,
    )
    with jax.named_scope("q_high"):
        own_q, came_q = gather_high(shard_q)
    xa = lax.all_to_all(rows_in, "col", split_axis=0, concat_axis=0, tiled=True)
    adapter = lax.dynamic_index_in_dim(adapter_index, column, 0, keepdims=False)
    sc = jnp.stack([adapter, column, column % 2, row % 2]).astype(jnp.int32)
    up_qkv = jnp.swapaxes(lax.dynamic_index_in_dim(qkv_up, adapter, 0, keepdims=False), 0, 1)
    shard_a, shard_b, keep, closed = call(
        prep_f_kernel,
        [shard] * 2 + [jax.ShapeDtypeStruct((SEQ, 1), F32)] * 2,
        [sc, keep_mask, w_fc1, w_fc2],
        [pltpu.SMEM] + [VMEM] * 3,
    )

    own_q, shard_a, shard_b = after_all(
        (own_q, shard_a, shard_b), xa, keep, closed, sc, up_qkv, *came_q
    )
    with jax.named_scope("q_one"):
        one_q = swap(own_q, flip_one)
    with jax.named_scope("q_two"):
        two_q = swap(own_q, flip_two)
    with jax.named_scope("fa_high"):
        own_a, came_a = gather_high(shard_a)
    own_q, one_q, two_q = after_all((own_q, one_q, two_q), *came_a)
    with jax.named_scope("q_both"):
        both_q = swap(one_q, flip_two)
    with jax.named_scope("q_core"):
        away_q = [swap(p, flip_core) for p in (own_q, one_q, two_q)]
    own_a, shard_b = after_all((own_a, shard_b), *away_q)
    with jax.named_scope("q_core"):
        pieces_q = [own_q, one_q, two_q, both_q] + away_q + [swap(both_q, flip_core)]
    with jax.named_scope("fa_one"):
        one_a = swap(own_a, flip_one)
    with jax.named_scope("fa_two"):
        two_a = swap(own_a, flip_two)
    with jax.named_scope("fb_high"):
        own_b, came_b = gather_high(shard_b)

    def shaped(width, dtype, height=SEQ):
        return jax.ShapeDtypeStruct((height, width), dtype)

    big, small = shaped(D, BF), shaped(R, BF)
    scratch = weight_scratch(rows, cols, n)
    rows_space, bias_space = VMEM((cols, SEQ, hid), BF), VMEM((cols, EXTRA, hid), BF)
    any_space = [pl.ANY] * 8
    n1, lat1, q, k, v, lse, att, lat2, middle, n2, lat3 = call(
        functools.partial(front_kernel, lead, cols),
        [
            big,
            small,
            big,
            big,
            big,
            jax.ShapeDtypeStruct((H // 2, 1, 2 * SEQ), F32),
            big,
            small,
            shaped(D, F32),
            big,
            small,
        ],
        [sc, *pieces_q, xa, closed, ln_gain, ln_shift, qkv_down, up_qkv, proj_down]
        + [proj_up]
        + [fc1_down, bias_out],
        [pltpu.SMEM] + any_space + [pl.ANY] + [VMEM] * 3 + [pl.ANY, VMEM] + [pl.ANY] * 3 + [VMEM],
        scratch
        + [VMEM((SEQ, D), F32), VMEM((SEQ, D), F32), rows_space, bias_space]
        + [VMEM((R, D), BF)] * 4
        + [pltpu.SemaphoreType.DMA((6,))],
        mib=FRONT,
    )
    own_a, one_a, two_a = after_all((own_a, one_a, two_a), n1, *came_b)
    bits = list(reversed(range(bits_of(rows))))
    owners = after(adapter_index, n1)
    for bit in bits[:-1]:
        owners = owner_stack(owner_parts(owners, bit), bit)
    with jax.named_scope("fa_both"):
        both_a = swap(one_a, flip_two)
    with jax.named_scope("fa_core"):
        away_a = [swap(p, flip_core) for p in (own_a, one_a, two_a)]
    own_b, owners = after_all((own_b, owners), *away_a)
    owners = owner_parts(owners, 0)
    with jax.named_scope("fa_core"):
        pieces_a = [own_a, one_a, two_a, both_a] + away_a + [swap(both_a, flip_core)]
    with jax.named_scope("fb_one"):
        one_b = swap(own_b, flip_one)
    with jax.named_scope("fb_two"):
        two_b = swap(own_b, flip_two)
    wide = shaped(D, F32)
    thin = shaped(R, F32)
    res, gn2, lat4, glat3, gr, early_a = call(
        functools.partial(ffn_a_kernel, lead, cols),
        [wide, wide, thin, thin, big, jax.ShapeDtypeStruct((rows * cols, R, FF // (rows * cols)), BF)],
        [sc, *pieces_a, xa, keep, n2, lat3, fc1_up, fc2_down, fc2_up],
        [pltpu.SMEM] + any_space + [pl.ANY] + [VMEM] * 3 + [pl.ANY] * 3,
        scratch
        + [rows_space, bias_space, VMEM((R, FF), BF), VMEM((R, FF), BF), VMEM((R, D), BF)]
        + [pltpu.SemaphoreType.DMA((5,))],
        mib=FFN_A,
    )
    own_b, one_b, two_b, *owners = after_all((own_b, one_b, two_b, *owners), res)
    owners = owner_stack(owners, 0).transpose(tuple(bits) + (len(bits),)).reshape(-1)
    with jax.named_scope("fb_both"):
        both_b = swap(one_b, flip_two)
    with jax.named_scope("fb_core"):
        away_b = [swap(p, flip_core) for p in (own_b, one_b, two_b)]
        pieces_b = [own_b, one_b, two_b, both_b] + away_b + [swap(after(both_b, owners), flip_core)]
    *layer, gatt, gmid, grads_b = call(
        functools.partial(ffn_b_kernel, lead, cols),
        [shaped(hid, BF)] * cols + [big, wide]
        + [jax.ShapeDtypeStruct((rows * cols, R, 12 * D // (rows * cols)), BF)],
        [sc, *pieces_b, *pieces_q, xa, keep, ln_gain, n2, lat3, fc1_up, fc2_down, fc2_up]
        + [fc1_down, proj_down, proj_up, bias_out]
        + [middle, att, lat2, gr, res, gn2, lat4, glat3, early_a],
        [pltpu.SMEM]
        + any_space * 2
        + [pl.ANY, VMEM, VMEM, VMEM, VMEM]
        + [pl.ANY] * 6
        + [VMEM, pl.ANY, pl.ANY, VMEM, VMEM, pl.ANY, pl.ANY, VMEM, VMEM, pl.ANY],
        scratch
        + [VMEM((cols, D, hid), BF), scratch[1]]
        + [VMEM((SEQ, D), F32), VMEM((SEQ, D), F32), VMEM((SEQ, R), F32), VMEM((SEQ, R), F32)]
        + [bias_space, VMEM((R, FF), BF), VMEM((R, FF), BF)]
        + [VMEM((R, D), BF)] * 4
        + [VMEM((SEQ, D), F32), VMEM((SEQ, D), BF), VMEM((SEQ, D), F32), VMEM((SEQ, D), F32)]
        + [VMEM(early_a.shape, BF), pltpu.SemaphoreType.DMA((12,)), VMEM((SEQ, D), BF)],
        mib=FFN_B,
    )
    with jax.named_scope("grads_b_send"):
        mine_b = send_grads(grads_b)
    with jax.named_scope("layer_out"):
        layer = exchange_rows(layer)
    gq, gk, gv, glat1, late = call(
        functools.partial(attention_back_kernel, cols),
        [big, big, big, small, jax.ShapeDtypeStruct((rows * cols, R, 4 * D // (rows * cols)), BF)],
        [sc, closed, q, k, v, lse, gatt, lat1, n1, up_qkv],
        [pltpu.SMEM] + [VMEM] * 9,
        mib=ATT,
    )
    with jax.named_scope("grads_c_send"):
        mine_c = send_grads(late)
    with jax.named_scope("grads_b"):
        own_b, _ = gather_high(
            after(sum_grads(after(mine_b, late), owners, mine_b.shape[2]), *layer), 1
        )
        own_c, _ = gather_high(sum_grads(mine_c, owners, mine_c.shape[2]))
        order_b = tuple(lead.index(place) for place in lead_table(rows, cols, 1))
        own = lane_join([own_b, own_c], [order_b, tuple(range(len(lead)))])
    gmid = after(gmid, own)
    sent = call(
        functools.partial(back_kernel, lead, cols),
        [shaped(hid, BF)] * cols,
        [sc, *pieces_q, xa, ln_gain, gq, gk, gv, glat1, qkv_down, gmid],
        [pltpu.SMEM] + any_space + [pl.ANY] + [VMEM] * 5 + [pl.ANY] * 2,
        scratch
        + [VMEM((SEQ, D), F32), rows_space, VMEM((R, D), BF), VMEM((SEQ, D), F32)]
        + [pltpu.SemaphoreType.DMA((3,)), VMEM((SEQ, D), BF)],
        mib=BACK,
    )
    with jax.named_scope("grads"):
        one, two = swap(own, flip_one), swap(own, flip_two)
        own, one, two = after_all((own, one, two), *sent)
        layer_out = stacked(after_all(layer, one, two), column, pl.ANY)
        both = swap(one, flip_two)
        away = [swap(p, flip_core) for p in (own, one, two)]
        both = after(both, layer_out)
        pieces = [own, one, two, both] + away + [swap(both, flip_core)]
        half = FF // cols // 2
        map_a, map_b = (
            tuple(
                (out, None, (2 * block + part) * half, base + block * half, half)
                for out, base in ((0, 0), (1, FF // 2))
                for block in range(cols)
            )
            for part in (0, 1)
        )
        map_b = map_b + tuple((2 + i, None, 0, FF + i * D, D) for i in range(4))
        map_c = ((6, None, 0, 0, D),) + tuple((7, c, 0, (c + 1) * D, D) for c in range(3))
        parts = [early_a.shape[-1], mine_b.shape[-1] - early_a.shape[-1], mine_c.shape[-1]]
        shapes = [(NA * R, FF)] * 2 + [(NA * R, D)] * 5 + [(NA, 3, R, D)]
        sums = spread(sc, pieces, parts, [map_a, map_b, map_c], shapes)

    with jax.named_scope("rows_out"):
        grad_rows = exchange_rows(after_all(sent, *away))
        grad_in = stacked(after_all(grad_rows, sums[0]), column, pl.ANY)

    def split(table):
        return table.reshape((NA, R) + table.shape[1:])

    g_fc1_up, g_fc2_down, g_proj_down, g_proj_up, g_fc1_down, g_fc2_up = map(split, sums[:6])
    return (
        layer_out.reshape(cols * SEQ, hid),
        grad_in.reshape(cols * SEQ, hid),
        split(sums[6]),
        jnp.swapaxes(sums[7], 1, 2),
        g_proj_down,
        g_proj_up,
        g_fc1_down,
        g_fc1_up,
        g_fc2_down,
        g_fc2_up,
    )


def solution(mesh):
    return jax.shard_map(
        per_device,
        mesh=mesh,
        in_specs=(
            P("row", "col"),
            P("row", "col"),
            P("row", None),
            P("row"),
            P(),
            P(),
            P(None, "row", "col"),
            P(None, "col"),
            P("col", "row"),
            P("row", "col"),
            P("col"),
            P("col", "row"),
            P(),
            P(),
            P(),
            P(),
            P(),
            P(),
            P(),
            P(),
            P(),
        ),
        out_specs=(P("row", "col"), P("row", "col"), P(), P(), P(), P(), P(), P(), P(), P()),
        check_vma=False,
    )
```
